32 devices in a mesh: rep: 8 (over y, x, core), grp: 4 (over z).
Axes of the slice: x: 2, y: 2, z: 4, core: 2. Of those that a mesh axis runs over, the one named last changes fastest.
Arguments:
- tokens: bfloat16 [16, 1024, 1024], P('rep', 'grp'), may hold values from -6 to 6
- positions: int32 [3, 16, 1024], P(None, 'rep', 'grp'), may hold values from 0 to 15
- ln1_gain: bfloat16 [1024], P('grp'), may hold values from 0.099609375 to 1.8984375
- ln1_bias: bfloat16 [1024], P('grp'), may hold values from -3 to 3
- w_qkv: bfloat16 [1024, 3072], P('grp'), may hold values from -0.1875 to 0.1875
- b_qkv: bfloat16 [3072], P('grp'), may hold values from -3 to 3
- w_out: bfloat16 [1024, 1024], P('grp'), may hold values from -0.75 to 0.75
- b_out: bfloat16 [1024], P('grp'), may hold values from -3 to 3
- ln2_gain: bfloat16 [1024], P('grp'), may hold values from 0.099609375 to 1.8984375
- ln2_bias: bfloat16 [1024], P('grp'), may hold values from -3 to 3
- w_up: bfloat16 [1024, 4096], P('grp'), may hold values from -0.1875 to 0.1875
- b_up: bfloat16 [4096], P('grp'), may hold values from -3 to 3
- w_down: bfloat16 [4096, 1024], P('grp'), may hold values from -0.09375 to 0.09375
- b_down: bfloat16 [1024], P('grp'), may hold values from -3 to 3
- cotangent: bfloat16 [16, 1024, 1024], P('rep', 'grp'), may hold values from -6 to 6
Outputs:
- output: bfloat16 [16, 1024, 1024], P('rep', 'grp')
- grad_tokens: bfloat16 [16, 1024, 1024], P('rep', 'grp')
- grad_ln1_gain: float32 [1024], P('grp')
- grad_ln1_bias: float32 [1024], P('grp')
- grad_w_qkv: float32 [1024, 3072], P('grp')
- grad_b_qkv: float32 [3072], P('grp')
- grad_w_out: float32 [1024, 1024], P('grp')
- grad_b_out: float32 [1024], P('grp')
- grad_ln2_gain: float32 [1024], P('grp')
- grad_ln2_bias: float32 [1024], P('grp')
- grad_w_up: float32 [1024, 4096], P('grp')
- grad_b_up: float32 [4096], P('grp')
- grad_w_down: float32 [4096, 1024], P('grp')
- grad_b_down: float32 [1024], P('grp')
The draws below stay inside these ranges and needn't reach their ends.
Inputs may be any that keep to these rules, and one draw needn't show every extreme that they name: `positions`: frame, row and column indices of a token.
All inputs are finite; a program needn't handle non-finite values.
Results may differ from the reference program's by a relative error of at most 0.02.
Values may be sent and summed in bfloat16 or wider, within the bound.
A program may use at most 320 MiB of HBM per device.

```python
import jax
import jax.numpy as jnp
from jax import lax

D = 1024
FF = 4096
LENGTH = 1024
CLIPS = 16


def place_ends(values, stream_key, low, high):
    longest = values.shape.index(max(values.shape))
    spots = []
    for shift in (0, 1):
        where = [jax.random.randint(jax.random.fold_in(stream_key, axis), (), 0, length) for axis, length in enumerate(values.shape)]
        where[longest] = (where[longest] + shift) % values.shape[longest]
        spots.append(tuple(where))
    return values.at[spots[0]].set(low).at[spots[1]].set(high)


def levels(stream_key, shape, pieces, low, high):
    loudness = 1.0
    for position, blocks in pieces:
        heights = jax.random.uniform(jax.random.fold_in(jax.random.fold_in(stream_key, 6), position), (blocks,), jnp.float32, low / len(pieces), high / len(pieces))
        loudness = loudness * jnp.repeat(jnp.exp(heights), shape[position] // blocks).reshape((-1,) + (1,) * (len(shape) - 1 - position))
    return loudness


def normal_values(rng, extent, deviation, limit, cuts=(), held_as=jnp.bfloat16):
    entries = jax.random.normal(rng, extent, jnp.float32) * deviation
    if len(cuts) > 0:
        entries = levels(rng, extent, cuts, -0.22, 0.18) * entries
    return jnp.clip(entries, min=-limit, max=limit).astype(held_as)


def setup_inputs(seed: int = 0) -> dict:
    seeds = jax.random.split(jax.random.key(seed), 16)
    tokens = normal_values(seeds[0], (CLIPS, LENGTH, D), 1.0, 6.0, ((0, 8), (1, 4)))
    positions = place_ends(jax.random.randint(seeds[1], (3, CLIPS, LENGTH), 0, 16), jax.random.fold_in(seeds[1], 1), 0, 15).astype(jnp.int32)
    ln1_gain = jnp.clip(1.0 + 0.18 * jax.random.normal(seeds[2], (D,), jnp.float32), 0.099609375, 1.8984375).astype(jnp.bfloat16)
    ln1_bias = normal_values(seeds[3], (D,), 0.3, 3.0, ((0, 4),))
    w_qkv = normal_values(seeds[4], (D, 3 * D), D ** -0.5, 0.1875, ((0, 4),))
    b_qkv = normal_values(seeds[5], (3 * D,), 0.5, 3.0, ((0, 4),))
    w_out = normal_values(seeds[6], (D, D), (D // 16) ** -0.5, 0.75, ((0, 4),))
    b_out = normal_values(seeds[7], (D,), 0.5, 3.0, ((0, 4),))
    ln2_gain = jnp.clip(1.0 + 0.18 * jax.random.normal(seeds[8], (D,), jnp.float32), 0.099609375, 1.8984375).astype(jnp.bfloat16)
    ln2_bias = normal_values(seeds[9], (D,), 0.3, 3.0, ((0, 4),))
    w_up = normal_values(seeds[10], (D, FF), D ** -0.5, 0.1875, ((0, 4),))
    b_up = normal_values(seeds[11], (FF,), 0.5, 3.0, ((0, 4),))
    w_down = normal_values(seeds[12], (FF, D), FF ** -0.5, 0.09375, ((0, 4),))
    b_down = normal_values(seeds[13], (D,), 0.5, 3.0, ((0, 4),))
    cotangent = normal_values(seeds[14], (CLIPS, LENGTH, D), 1.0, 6.0, ((0, 8), (1, 4)))
    return {"tokens": tokens, "positions": positions, "ln1_gain": ln1_gain, "ln1_bias": ln1_bias, "w_qkv": w_qkv, "b_qkv": b_qkv, "w_out": w_out, "b_out": b_out, "ln2_gain": ln2_gain, "ln2_bias": ln2_bias, "w_up": w_up, "b_up": b_up, "w_down": w_down, "b_down": b_down, "cotangent": cotangent}


@jax.custom_vjp
def low(v):
    return lax.optimization_barrier(v.astype(jnp.bfloat16)).astype(jnp.float32)

@jax.custom_vjp
def low_back(v):
    return v

def low_keep(v):
    return (low(v), None)

def low_pass(kept, grad):
    return (grad,)

def back_keep(v):
    return (v, None)

def back_low(kept, grad):
    return (low(grad),)
low.defvjp(low_keep, low_pass)
low_back.defvjp(back_keep, back_low)
SCALE = 0.125
EPS = 1e-06

def rotary_angles(positions):
    pair = jnp.arange(32)
    band = (pair >= 10).astype(jnp.int32) + (pair >= 21).astype(jnp.int32)
    start = jnp.where(band == 0, 0, jnp.where(band == 1, 10, 21))
    count = jnp.where(band == 0, 10, 11)
    freq = jnp.power(jnp.float32(10000.0), -(pair - start).astype(jnp.float32) / count.astype(jnp.float32))
    pos_f = positions.astype(jnp.float32)
    chosen = jnp.where(band[None, :] == 0, pos_f[0][:, None], jnp.where(band[None, :] == 1, pos_f[1][:, None], pos_f[2][:, None]))
    return chosen * freq[None, :]

def rotate(field, cosine, sine):
    first = field[..., :32]
    second = field[..., 32:]
    return jnp.concatenate([first * cosine - second * sine, first * sine + second * cosine], axis=-1)

def normalize(field):
    centred = field - lax.optimization_barrier(jnp.mean(field, axis=-1, keepdims=True))
    variance = lax.optimization_barrier(jnp.mean(centred * centred, axis=-1, keepdims=True))
    return centred * lax.rsqrt(variance + EPS)

def matmul(left, right):
    return jnp.dot(left, right, precision=lax.Precision.HIGHEST)

def forward(field, positions, params):
    g1, b1, wqkv, bqkv, wo, bo, g2, b2, w1, bu, w2, bd = params
    length, width = field.shape
    heads = width // 64
    angles = rotary_angles(positions)
    cosine = jnp.cos(angles)[:, None, :]
    sine = jnp.sin(angles)[:, None, :]
    h1 = low(normalize(field) * g1 + b1)
    qkv = low_back(matmul(h1, wqkv) + bqkv)
    query = qkv[:, :width].reshape(length, heads, 64)
    keys = qkv[:, width:2 * width].reshape(length, heads, 64)
    values = low(qkv[:, 2 * width:].reshape(length, heads, 64))
    query_rot = low(rotate(query, cosine, sine))
    keys_rot = low(rotate(keys, cosine, sine))
    scores = low_back(jnp.einsum('thd,shd->hts', query_rot, keys_rot, precision=lax.Precision.HIGHEST) * SCALE)
    probs = low(jax.nn.softmax(scores, axis=-1))
    mixed = jnp.einsum('hts,shd->thd', probs, values, precision=lax.Precision.HIGHEST).reshape(length, width)
    mixed = low(low_back(mixed))
    second = field + low_back(matmul(mixed, wo) + bo)
    h2 = low(normalize(second) * g2 + b2)
    hidden = low_back(matmul(h2, w1) + bu)
    active = low(jax.nn.gelu(hidden, approximate=False))
    return second + low_back(matmul(active, w2) + bd)

def reference(tokens, positions, ln1_gain, ln1_bias, w_qkv, b_qkv, w_out, b_out, ln2_gain, ln2_bias, w_up, b_up, w_down, b_down, cotangent):
    params = tuple((p.astype(jnp.float32) for p in (ln1_gain, ln1_bias, w_qkv, b_qkv, w_out, b_out, ln2_gain, ln2_bias, w_up, b_up, w_down, b_down)))
    clip_pos = jnp.moveaxis(positions, 1, 0)

    def one_clip(carry, clip):
        field, pos, grad_out = clip

        def run(inputs, *weights):
            return forward(inputs, pos, weights)
        result, pull = jax.vjp(run, field.astype(jnp.float32), *params)
        grads = pull(grad_out.astype(jnp.float32))
        carry = tuple((c + g for c, g in zip(carry, grads[1:])))
        return (carry, (result.astype(jnp.bfloat16), grads[0].astype(jnp.bfloat16)))
    zeros = tuple((jnp.zeros(p.shape, jnp.float32) for p in params))
    totals, (output, grad_tokens) = lax.scan(one_clip, zeros, (tokens, clip_pos, cotangent))
    return (output, grad_tokens, totals[0], totals[1], totals[2], totals[3], totals[4], totals[5], totals[6], totals[7], totals[8], totals[9], totals[10], totals[11])
```

```python
import functools

import jax
import jax.numpy as jnp
from jax import lax
from jax.experimental import pallas as pl
from jax.experimental.pallas import tpu as pltpu
from jax.sharding import Mesh
from jax.sharding import PartitionSpec as P

SCALE = 0.125
EPS = 1e-06
HEAD = 64
BF = jnp.bfloat16
F32 = jnp.float32
MESH = pl.DeviceIdType.MESH
ANY = pl.BlockSpec(memory_space=pl.ANY)
VM = pl.BlockSpec(memory_space=pltpu.VMEM)


def where_am_i():
    return lax.axis_index("rp"), lax.axis_index("core"), lax.axis_index("grp")


def remote(src, dst, send, recv, target):
    return pltpu.make_async_remote_copy(
        src_ref=src,
        dst_ref=dst,
        send_sem=send,
        recv_sem=recv,
        device_id=target,
        device_id_type=MESH,
    )


def enter(p, c, z, groups):
    barrier = pltpu.get_barrier_semaphore()
    for k in range(groups):
        for d in range(2):
            if k == 0 and d == 0:
                continue
            pl.semaphore_signal(
                barrier, inc=1, device_id=(p, c ^ d, lax.rem(z + k, groups)), device_id_type=MESH
            )
    for b in (1, 2):
        pl.semaphore_signal(barrier, inc=1, device_id=(p ^ b, c, z), device_id_type=MESH)
    pl.semaphore_wait(barrier, 2 * groups - 1 + 2)


def move_tokens(refs, outs, send, recv, p, c, z, clips):
    core, slot = lax.div(z, clips), lax.rem(z, clips)

    def route(i):
        return core, c * clips + i

    def here(i):
        return jnp.logical_and(core == c, c * clips + i == z)

    def start():
        for n, (src, dst) in enumerate(zip(refs, outs)):
            for i in range(clips):
                tc, tz = route(i)

                @pl.when(here(i))
                def _():
                    pltpu.make_async_copy(src.at[i], dst.at[slot], recv.at[n, slot]).start()

                @pl.when(jnp.logical_not(here(i)))
                def _():
                    remote(
                        src.at[i], dst.at[slot], send.at[n, i], recv.at[n, slot], (p, tc, tz)
                    ).start()

    def finish():
        for n, (src, dst) in enumerate(zip(refs, outs)):
            for i in range(clips):

                @pl.when(jnp.logical_not(here(i)))
                def _():
                    remote(
                        src.at[i], dst.at[slot], send.at[n, i], recv.at[n, slot], (p, c ^ 1, z)
                    ).wait_send()

            for m in range(clips):
                pltpu.make_async_copy(src.at[0], dst.at[m], recv.at[n, m]).wait()

    return start, finish


def gather_body(groups, clips, count, *refs):
    halves, (small, x, pos) = refs[:count], refs[count : count + 3]
    outs = refs[count + 3 : 2 * count + 3]
    small_o, x_o, pos_o = refs[2 * count + 3 : 2 * count + 6]
    zs, zr, xs, xr, ys, yr, fs, fr, ls, ss, sr, ts, tr = refs[2 * count + 6 :]
    p, c, z = where_am_i()
    enter(p, c, z, groups)
    col = [(p, c, lax.rem(z + k, groups)) for k in range(groups)]
    org = [lax.rem(z + groups - k, groups) for k in range(groups)]
    xn, yn = (p ^ 1, c, z), (p ^ 2, c, z)
    start, finish = move_tokens((x, pos), (x_o, pos_o), ts, tr, p, c, z, clips)
    start()
    smalls = [
        remote(small, small_o.at[z], ss.at[k], sr.at[k], col[k]) for k in range(1, groups)
    ]
    for s in smalls:
        s.start()
    keep = [pltpu.make_async_copy(small, small_o.at[z], ls.at[count])]
    for w in range(count):
        keep.append(pltpu.make_async_copy(halves[w], outs[w].at[z], ls.at[w]))
    for k in keep:
        k.start()
    first = {}
    for w in range(count):
        for k in range(1, groups):
            first[w, k] = remote(
                halves[w].at[p], outs[w].at[z, p], zs.at[w, k], zr.at[w, k], col[k]
            )
            first[w, k].start()
    units = [(w, k) for w in range(count) for k in range(1, groups)]
    xc, yc, fa, fb = {}, {}, {}, {}

    def plane(u):
        w, k = u
        o = outs[w].at[org[k]]
        remote(halves[w].at[p], o.at[p], zs.at[w, k], zr.at[w, k], col[k]).wait_recv()
        xc[u] = remote(o.at[p], o.at[p], xs.at[w, k], xr.at[w, k], xn)
        yc[u] = remote(o.at[p], o.at[p], ys.at[w, k], yr.at[w, k], yn)
        xc[u].start()
        yc[u].start()

    def forward(u):
        w, k = u
        o = outs[w].at[org[k]]
        q = p ^ 1
        remote(o.at[q], o.at[q], xs.at[w, k], xr.at[w, k], xn).wait_recv()
        fa[u] = remote(o.at[q, 0], o.at[q, 0], fs.at[w, k, 0], fr.at[w, k, 0], yn)
        fa[u].start()
        q = p ^ 2
        remote(o.at[q], o.at[q], ys.at[w, k], yr.at[w, k], yn).wait_recv()
        fb[u] = remote(o.at[q, 1], o.at[q, 1], fs.at[w, k, 1], fr.at[w, k, 1], xn)
        fb[u].start()

    lag = 2
    for n in range(len(units) + lag):
        if n < len(units):
            plane(units[n])
        if n >= lag:
            forward(units[n - lag])
    for u in units:
        w, k = u
        q = p ^ 3
        o = outs[w].at[org[k]]
        remote(o.at[q, 0], o.at[q, 0], fs.at[w, k, 0], fr.at[w, k, 0], yn).wait_recv()
        remote(o.at[q, 1], o.at[q, 1], fs.at[w, k, 1], fr.at[w, k, 1], xn).wait_recv()
    for k in range(1, groups):
        remote(small, small_o.at[org[k]], ss.at[k], sr.at[k], col[k]).wait_recv()
    for u in units:
        first[u].wait_send()
        xc[u].wait_send()
        yc[u].wait_send()
        fa[u].wait_send()
        fb[u].wait_send()
    for s in smalls:
        s.wait_send()
    for k in keep:
        k.wait()
    finish()


def gather(halves, small, x, pos, groups):
    count, clips = len(halves), x.shape[0]
    dma = pltpu.SemaphoreType.DMA
    shapes = [jax.ShapeDtypeStruct((groups,) + h.shape, h.dtype) for h in halves]
    shapes += [jax.ShapeDtypeStruct((groups,) + small.shape, small.dtype)]
    shapes += [jax.ShapeDtypeStruct(x.shape, x.dtype), jax.ShapeDtypeStruct(pos.shape, pos.dtype)]
    return pl.pallas_call(
        functools.partial(gather_body, groups, clips, count),
        out_shape=shapes,
        in_specs=[VM] * count + [VM, ANY, ANY],
        out_specs=[ANY] * len(shapes),
        scratch_shapes=[dma((count, groups))] * 6
        + [dma((count, groups, 2))] * 2
        + [dma((count + 1,)), dma((groups,)), dma((groups,)), dma((2, clips)), dma((2, clips))],
        compiler_params=pltpu.CompilerParams(collective_id=0, has_side_effects=True),
        name="gather",
    )(*halves, small, x, pos)


def reduce_body(groups, clips, count, *refs):
    grads, (small, gx) = refs[:count], refs[count : count + 2]
    outs = refs[count + 2 : 2 * count + 2]
    small_o, gx_o = refs[2 * count + 2 : 2 * count + 4]
    scratch = refs[2 * count + 4 :]
    own_a, own_b, one_a, one_b, two_a, two_b, mine, three, full = (
        scratch[i * count : (i + 1) * count] for i in range(9)
    )
    small_r, small_z = scratch[9 * count : 9 * count + 2]
    (os, s1, r1, s2, r2, s3, r3, s4, r4, s5, r5, cs, cr, ls, ss, sr, ts, tr) = scratch[9 * count + 2 :]
    p, c, z = where_am_i()
    hi, lo = lax.div(p, 2), lax.rem(p, 2)
    enter(p, c, z, groups)
    col = [(p, c, lax.rem(z + k, groups)) for k in range(groups)]
    xn, yn, cn = (p ^ 1, c, z), (p ^ 2, c, z), (p, c ^ 1, z)
    start, finish = move_tokens((gx,), (gx_o,), ts, tr, p, c, z, clips)
    start()
    small_o[...] = small[...]
    for n, target in enumerate((cn, xn, yn)):
        copy = remote(small_o, small_r.at[n], ss.at[n], sr.at[n], target)
        copy.start()
        copy.wait()
        small_o[...] += small_r[n]
    tails = [
        remote(small_o, small_z.at[k], ss.at[2 + k], sr.at[2 + k], col[k]) for k in range(1, groups)
    ]
    for t in tails:
        t.start()
    units = [(w, k) for w in range(count) for k in range(groups)]
    load, c1, c2, c3, c4, c5 = {}, {}, {}, {}, {}, {}
    for u in units:
        w, k = u
        g = grads[w].at[k]
        c1[u, 0] = remote(g.at[:, 1 - lo, 0], one_a[w].at[k], s1.at[w, k, 0], r1.at[w, k, 0], xn)
        c1[u, 1] = remote(g.at[1 - hi, :, 1], one_b[w].at[k], s1.at[w, k, 1], r1.at[w, k, 1], yn)
        load[u, 0] = pltpu.make_async_copy(g.at[:, lo, 0], own_a[w].at[k], os.at[w, k, 0])
        load[u, 1] = pltpu.make_async_copy(g.at[hi, :, 1], own_b[w].at[k], os.at[w, k, 1])
        c1[u, 0].start()
        c1[u, 1].start()
        load[u, 0].start()
        load[u, 1].start()

    def stage_one(u):
        w, k = u
        for n, (own, one, two, side, target) in enumerate(
            ((own_a, one_a, two_a, hi, yn), (own_b, one_b, two_b, lo, xn))
        ):
            load[u, n].wait()
            c1[u, n].wait_recv()
            o = own[w].at[k]
            o[...] = (o[...].astype(F32) + one[w][k].astype(F32)).astype(BF)
            c2[u, n] = remote(o.at[1 - side], two[w].at[k], s2.at[w, k, n], r2.at[w, k, n], target)
            c2[u, n].start()

    def stage_two(u):
        w, k = u
        for n, (own, two, side) in enumerate(((own_a, two_a, hi), (own_b, two_b, lo))):
            c2[u, n].wait_recv()
            mine[w][k, n] = (own[w][k, side].astype(F32) + two[w][k].astype(F32)).astype(BF)

        @pl.when(z != k)
        def _():
            remote(
                mine[w].at[k],
                three[w].at[lax.rem(k - z + groups, groups)],
                s3.at[w, k],
                r3.at[w, lax.rem(k - z + groups, groups)],
                (p, c, k),
            ).start()

    def stage_three(w):
        total = mine[w][z].astype(F32)
        for k in range(1, groups):
            remote(mine[w].at[0], three[w].at[k], s3.at[w, 0], r3.at[w, k], col[k]).wait_recv()
            total = total + three[w][k].astype(F32)
        full[w][p] = total.astype(BF)
        for n, target in enumerate((xn, yn)):
            f = full[w].at[p]
            c4[w, n] = remote(f, f, s4.at[w, n], r4.at[w, n], target)
            c4[w, n].start()

    def stage_four(w):
        for n, (q, target) in enumerate(((p ^ 1, yn), (p ^ 2, xn))):
            f = full[w].at[q]
            remote(f, f, s4.at[w, n], r4.at[w, n], target).wait_recv()
            f = full[w].at[q, n]
            c5[w, n] = remote(f, f, s5.at[w, n], r5.at[w, n], target)
            c5[w, n].start()

    def stage_five(w):
        for n in range(2):
            f = full[w].at[p ^ 3, n]
            remote(f, f, s5.at[w, n], r5.at[w, n], xn).wait_recv()
        pltpu.make_async_copy(full[w], outs[w].at[c], ls.at[w]).start()
        remote(full[w], outs[w].at[c], cs.at[w], cr.at[w], cn).start()

    lag = 3
    for n in range(len(units) + lag):
        if n < len(units):
            stage_one(units[n])
        if n >= lag:
            stage_two(units[n - lag])
    for w in range(count):
        stage_three(w)
        if w >= 1:
            stage_four(w - 1)
        if w >= 2:
            stage_five(w - 2)
    stage_four(count - 1)
    for w in range(max(count - 2, 0), count):
        stage_five(w)
    for k in range(1, groups):
        tails[k - 1].wait()
    for k in range(1, groups):
        small_o[...] += small_z[k]
    for u in units:
        w, k = u
        for n in range(2):
            c1[u, n].wait_send()
            c2[u, n].wait_send()

        @pl.when(z != k)
        def _():
            remote(mine[w].at[k], three[w].at[0], s3.at[w, k], r3.at[w, 0], xn).wait_send()

    for w in range(count):
        for n in range(2):
            c4[w, n].wait_send()
            c5[w, n].wait_send()
        pltpu.make_async_copy(full[w], outs[w].at[c], ls.at[w]).wait()
        remote(full[w], outs[w].at[1 - c], cs.at[w], cr.at[w], cn).wait()
    finish()


def reduce(grads, small, gx, groups):
    count, clips = len(grads), gx.shape[0]
    dma = pltpu.SemaphoreType.DMA
    tiles = [g.shape[4:] for g in grads]
    shapes = [jax.ShapeDtypeStruct((2, 4, 2) + t, BF) for t in tiles]
    shapes += [
        jax.ShapeDtypeStruct(small.shape, small.dtype),
        jax.ShapeDtypeStruct(gx.shape, gx.dtype),
    ]
    scratch = []
    for lead in (
        (groups, 2),
        (groups, 2),
        (groups, 2),
        (groups, 2),
        (groups,),
        (groups,),
        (groups, 2),
        (groups, 2),
        (4, 2),
    ):
        scratch += [pltpu.VMEM(lead + t, BF) for t in tiles]
    scratch += [pltpu.VMEM((3,) + small.shape, F32), pltpu.VMEM((groups,) + small.shape, F32)]
    pair = dma((count, groups, 2))
    scratch += [pair] * 5 + [dma((count, groups))] * 2 + [dma((count, 2))] * 4
    scratch += [dma((count,))] * 3 + [dma((2 + groups,))] * 2 + [dma((1, clips))] * 2
    return pl.pallas_call(
        functools.partial(reduce_body, groups, clips, count),
        out_shape=shapes,
        in_specs=[ANY] * count + [VM, ANY],
        out_specs=[ANY] * count + [VM, ANY],
        scratch_shapes=scratch,
        compiler_params=pltpu.CompilerParams(
            collective_id=1, has_side_effects=True, vmem_limit_bytes=60 * 1024 * 1024
        ),
        name="reduce",
    )(*grads, small, gx)


def turn(u, cosine, sine):
    half = HEAD // 2
    first, second = u[:half], u[half:]
    return jnp.concatenate(
        [first * cosine - second * sine, first * sine + second * cosine], axis=0
    )


def dot(a, b):
    return jnp.dot(a, b, preferred_element_type=F32)


def attention_body(step, q_ref, k_ref, v_ref, cos_ref, sin_ref, qs_ref, kr_ref, vb_ref, o_ref, l_ref):
    cosine, sine = cos_ref[...], sin_ref[...]
    length = cosine.shape[1]
    kr = turn(k_ref[...], cosine, sine).astype(BF)
    vb = v_ref[...].astype(BF)
    qs = (turn(q_ref[...], cosine, sine).astype(BF).astype(F32) * SCALE).astype(BF)
    kr_ref[...] = kr
    vb_ref[...] = vb
    qs_ref[...] = qs
    keys = kr.T
    for i in range(0, length, step):
        scores = dot(keys, qs[:, i : i + step])
        top = jnp.max(scores, axis=0, keepdims=True)
        e = jnp.exp(scores - top)
        total = jnp.sum(e, axis=0, keepdims=True)
        mixed = dot(vb, e.astype(BF))
        o_ref[:, i : i + step] = (mixed / total).astype(BF)
        l_ref[0, :, i : i + step] = top + jnp.log(total)


def attention(qkv, cosine, sine, step=256):
    rows, length = qkv.shape
    width = rows // 3
    heads = width // HEAD
    block = [pl.BlockSpec((HEAD, length), lambda h, n=n: (n * heads + h, 0)) for n in range(3)]
    table = pl.BlockSpec((HEAD // 2, length), lambda h: (0, 0))
    out = pl.BlockSpec((HEAD, length), lambda h: (h, 0))
    shape = jax.ShapeDtypeStruct((width, length), BF)
    return pl.pallas_call(
        functools.partial(attention_body, step),
        out_shape=[shape] * 4 + [jax.ShapeDtypeStruct((heads, 1, length), F32)],
        grid=(heads,),
        in_specs=block + [table, table],
        out_specs=[out] * 4 + [pl.BlockSpec((1, 1, length), lambda h: (h, 0, 0))],
        cost_estimate=pl.CostEstimate(
            flops=4 * width * length * length,
            transcendentals=heads * length * length,
            bytes_accessed=width * length * 24,
        ),
        name="attention",
    )(qkv, qkv, qkv, cosine, sine)


def attention_back_body(
    step, q_ref, k_ref, v_ref, o_ref, l_ref, g_ref, cos_ref, sin_ref, dq_ref, dk_ref, dv_ref, ak, av
):
    cosine, sine = cos_ref[...], sin_ref[...]
    length = cosine.shape[1]
    kt, keys, values = k_ref[...], k_ref[...].T, v_ref[...].T
    queries, grads = q_ref[...].T, g_ref[...].T
    for i in range(0, length, step):
        s = slice(i, i + step)
        g = g_ref[:, s]
        scores = dot(keys, q_ref[:, s])
        p = jnp.exp(scores - l_ref[0, :, s])
        dp = dot(values, g)
        delta = jnp.sum(o_ref[:, s].astype(F32) * g.astype(F32), axis=0, keepdims=True)
        ds = (p * (dp - delta)).astype(BF)
        dq = dot(kt, ds) * SCALE
        dq_ref[:, s] = turn(dq, cosine[:, s], -sine[:, s]).astype(BF)
        dv = dot(p.astype(BF), grads[s])
        dk = dot(ds, queries[s])
        if i == 0:
            ak[...] = dk
            av[...] = dv
        else:
            ak[...] += dk
            av[...] += dv
    dk_ref[...] = turn(ak[...].T, cosine, -sine).astype(BF)
    dv_ref[...] = av[...].T.astype(BF)


def attention_back(qs, kr, vb, out, lse, grad, cosine, sine, step=256):
    width, length = qs.shape
    heads = width // HEAD
    row = pl.BlockSpec((HEAD, length), lambda h: (h, 0))
    table = pl.BlockSpec((HEAD // 2, length), lambda h: (0, 0))
    line = pl.BlockSpec((1, 1, length), lambda h: (h, 0, 0))
    shape = jax.ShapeDtypeStruct((width, length), BF)
    return pl.pallas_call(
        functools.partial(attention_back_body, step),
        out_shape=[shape] * 3,
        grid=(heads,),
        in_specs=[row] * 4 + [line, row, table, table],
        out_specs=[row] * 3,
        scratch_shapes=[pltpu.VMEM((length, HEAD), F32)] * 2,
        cost_estimate=pl.CostEstimate(
            flops=10 * width * length * length,
            transcendentals=heads * length * length,
            bytes_accessed=width * length * 18,
        ),
        name="attention_back",
    )(qs, kr, vb, out, lse, grad, cosine, sine)


def swap(value):
    return lax.ppermute(value, "core", [(0, 1), (1, 0)])


def both(value):
    return jnp.concatenate([value, swap(value)], axis=0)


def contract(left, right, a, b):
    return lax.dot_general(left, right, (((a,), (b,)), ((), ())), preferred_element_type=F32)


def own_sum(partial):
    half = partial.shape[0] // 2
    return partial[:half] + swap(partial[half:].astype(BF)).astype(F32)


def move_blocks(x, clips, groups):
    c, z = lax.axis_index("core"), lax.axis_index("grp")
    got = []
    for t in range(clips):
        pairs = []
        for cc in range(2):
            for zz in range(groups):
                i = (t + zz) % clips
                pairs.append((cc * groups + zz, (zz // clips) * groups + cc * clips + i))
        block = lax.dynamic_index_in_dim(x, lax.rem(t + z, clips), 0, keepdims=False)
        got.append(lax.ppermute(block, ("core", "grp"), pairs))
    stacked = jnp.stack(got)
    return jnp.stack(
        [
            lax.dynamic_index_in_dim(stacked, lax.rem(z - m + clips, clips), 0, keepdims=False)
            for m in range(clips)
        ]
    )


def paired(
    tokens,
    positions,
    ln1_gain,
    ln1_bias,
    w_qkv,
    b_qkv,
    w_out,
    b_out,
    ln2_gain,
    ln2_bias,
    w_up,
    b_up,
    w_down,
    b_down,
    cotangent,
):
    groups = lax.axis_size("grp")
    clips, part, width = tokens.shape
    hidden = w_down.shape[0] * groups
    own = clips * part
    length = 2 * own
    c, z = lax.axis_index("core"), lax.axis_index("grp")
    wide = width // 2
    deep = hidden // 2
    row = width // groups

    def pick(value, axis):
        return lax.dynamic_index_in_dim(value, c, axis, keepdims=False)

    halves = [
        pick(w_qkv.reshape(row, 3, groups, 2, row // 2), 3).reshape(row, 3 * wide),
        pick(w_out.reshape(2, row // 2, width), 0),
        pick(w_up.reshape(row, groups, 2, deep // groups), 2).reshape(row, deep),
        pick(w_down.reshape(2, deep // groups, width), 0),
    ]
    halves = [h.reshape(4, 2, h.shape[0] // 8, h.shape[1]) for h in halves]
    bq, bu = b_qkv.shape[0] // row, b_up.shape[0] // row
    small = jnp.concatenate(
        [ln1_gain, ln1_bias, b_out, ln2_gain, ln2_bias, b_down, b_qkv, b_up]
    ).reshape(6 + bq + bu, row)
    lines = small.shape[0]
    small = jnp.pad(small, ((0, -lines % 16), (0, 0)))
    pos = jnp.pad(jnp.moveaxis(positions, 0, 1).astype(F32), ((0, 0), (0, 5), (0, 0)))
    wq, wo, w1, w2, small, x, pos = gather(halves, small, tokens, pos, groups)
    wq = wq.reshape(width, 3 * wide)
    wo = wo.reshape(wide, width)
    w1 = w1.reshape(width, deep)
    w2 = w2.reshape(deep, width)
    small = small.astype(F32)
    g1, b1, bo, g2, b2, bd = (small[:, n].reshape(1, width) for n in range(6))
    bq_own = pick(small[:, 6 : 6 + bq].reshape(3, groups, 2, row // 2), 2).reshape(3 * wide, 1)
    bu_own = pick(small[:, 6 + bq : lines].reshape(groups, 2, deep // groups), 1).reshape(1, deep)

    grad_out = move_blocks(cotangent, clips, groups).reshape(own, width)
    grad_all = both(grad_out)
    grad_f = grad_out.astype(F32)

    pos = jnp.moveaxis(pos[:, :3], 1, 0).reshape(3, own)
    pos = jnp.concatenate([pos, swap(pos)], axis=1)
    pair = jnp.arange(HEAD // 2)
    band = (pair >= 10).astype(jnp.int32) + (pair >= 21).astype(jnp.int32)
    begin = jnp.where(band == 0, 0, jnp.where(band == 1, 10, 21))
    count = jnp.where(band == 0, 10, 11)
    freq = jnp.power(F32(10000.0), -(pair - begin).astype(F32) / count.astype(F32))
    band = band[:, None]
    chosen = jnp.where(band == 0, pos[0:1], jnp.where(band == 1, pos[1:2], pos[2:3]))
    angles = chosen * freq[:, None]
    cosine, sine = jnp.cos(angles), jnp.sin(angles)

    x = x.reshape(own, width).astype(F32)
    n1, r1 = normalize(x)
    h1 = both((n1 * g1 + b1).astype(BF))
    qkv = contract(wq, h1, 0, 1) + bq_own
    qs, kr, vb, mixed, lse = attention(qkv, cosine, sine)
    x2 = x + own_sum(contract(mixed, wo, 0, 0)) + bo
    n2, r2 = normalize(x2)
    h2 = both((n2 * g2 + b2).astype(BF))
    u = contract(h2, w1, 1, 0) + bu_own
    cdf = 0.5 * (1.0 + lax.erf(u * F32(0.7071067811865476)))
    act = (u * cdf).astype(BF)
    slope = (cdf + u * jnp.exp(-0.5 * u * u) * F32(0.3989422804014327)).astype(BF)
    result = (x2 + own_sum(contract(act, w2, 1, 0)) + bd).astype(BF)
    output = move_blocks(result.reshape(clips, part, width), clips, groups)

    gw2 = contract(act, grad_all, 0, 0).astype(BF)
    gu = (contract(grad_all, w2, 1, 1) * slope.astype(F32)).astype(BF)
    gw1 = contract(h2, gu, 0, 0).astype(BF)
    gbu = jnp.sum(gu.astype(F32), axis=0)
    dh2 = own_sum(contract(gu, w1, 1, 1))
    gg2, gb2 = jnp.sum(dh2 * n2, axis=0), jnp.sum(dh2, axis=0)
    dx2 = grad_f + norm_back(dh2 * g2, n2, r2)
    low = dx2.astype(BF)
    low_all = both(low)
    gwo = contract(mixed, low_all, 1, 0).astype(BF)
    da = contract(wo, low_all, 1, 1).astype(BF)
    dqkv = jnp.concatenate(attention_back(qs, kr, vb, mixed, lse, da, cosine, sine), axis=0)
    gwq = contract(h1, dqkv, 0, 1).astype(BF)
    gbq = jnp.sum(dqkv.astype(F32), axis=1)
    dh1 = own_sum(contract(dqkv, wq, 0, 1))
    gg1, gb1 = jnp.sum(dh1 * n1, axis=0), jnp.sum(dh1, axis=0)
    gx = (dx2 + norm_back(dh1 * g1, n1, r1)).astype(BF)

    mine = (jnp.arange(2) == c).astype(F32)
    gbq = gbq.reshape(3, groups, 1, row // 2) * mine[None, None, :, None]
    gbu = gbu.reshape(groups, 1, deep // groups) * mine[None, :, None]
    sums = jnp.concatenate(
        [
            gg1,
            gb1,
            jnp.sum(low.astype(F32), axis=0),
            gg2,
            gb2,
            jnp.sum(grad_f, axis=0),
            gbq.reshape(-1),
            gbu.reshape(-1),
        ]
    ).reshape(lines, width)
    sums = jnp.pad(sums, ((0, -lines % 8), (0, 0)))
    grads = [g.reshape(groups, 2, 2, 2, g.shape[0] // (8 * groups), g.shape[1]) for g in (gwq, gwo, gw1, gw2)]
    gwq, gwo, gw1, gw2, sums, gx = reduce(grads, sums, gx.reshape(clips, part, width), groups)

    gwq = gwq.reshape(2, row, 3, groups, row // 2)
    gwq = jnp.transpose(gwq, (1, 2, 3, 0, 4)).reshape(row, 3 * width).astype(F32)
    gw1 = gw1.reshape(2, row, groups, deep // groups)
    gw1 = jnp.transpose(gw1, (1, 2, 0, 3)).reshape(row, hidden).astype(F32)
    gwo = gwo.reshape(row, width).astype(F32)
    gw2 = gw2.reshape(hidden // groups, width).astype(F32)
    cut = lambda v: lax.dynamic_index_in_dim(v.reshape(groups, -1), z, 0, keepdims=False)
    gg1, gb1, gbo, gg2, gb2, gbd = (cut(sums[n]) for n in range(6))
    return (
        output,
        gx,
        gg1,
        gb1,
        gwq,
        cut(sums[6 : 6 + bq]),
        gwo,
        gbo,
        gg2,
        gb2,
        gw1,
        cut(sums[6 + bq : lines]),
        gw2,
        gbd,
    )


def paired_specs():
    rep = ("rp", "core")
    ins = (P(rep, "grp", None), P(None, rep, "grp"))
    one, two = P("grp"), P("grp", None)
    ins += (one, one, two, one, two, one, one, one, two, one, two, one, P(rep, "grp", None))
    outs = (P(rep, "grp", None),) * 2
    outs += (one, one, two, one, two, one, one, one, two, one, two, one)
    return ins, outs


def rotary_angles(positions):
    pair = jnp.arange(32)
    band = (pair >= 10).astype(jnp.int32) + (pair >= 21).astype(jnp.int32)
    start = jnp.where(band == 0, 0, jnp.where(band == 1, 10, 21))
    count = jnp.where(band == 0, 10, 11)
    freq = jnp.power(
        jnp.float32(10000.0), -(pair - start).astype(jnp.float32) / count.astype(jnp.float32)
    )
    pos_f = positions.astype(jnp.float32)
    chosen = jnp.where(
        band[None, :] == 0,
        pos_f[0][:, None],
        jnp.where(band[None, :] == 1, pos_f[1][:, None], pos_f[2][:, None]),
    )
    return chosen * freq[None, :]


def rotate(field, cosine, sine):
    first = field[..., :32]
    second = field[..., 32:]
    return jnp.concatenate(
        [first * cosine - second * sine, first * sine + second * cosine], axis=-1
    )


def normalize(field):
    centred = field - jnp.mean(field, axis=-1, keepdims=True)
    variance = jnp.mean(centred * centred, axis=-1, keepdims=True)
    factor = lax.rsqrt(variance + EPS)
    return (centred * factor, factor)


def norm_back(grad_norm, normed, factor):
    return factor * (
        grad_norm
        - jnp.mean(grad_norm, axis=-1, keepdims=True)
        - normed * jnp.mean(grad_norm * normed, axis=-1, keepdims=True)
    )


def outer(left, right):
    return lax.dot_general(
        left, right, (((0,), (0,)), ((), ())), preferred_element_type=jnp.float32
    )


def back(left, right):
    return lax.dot_general(
        left, right, (((1,), (1,)), ((), ())), preferred_element_type=jnp.float32
    )


def exact_gelu(value):
    return jax.nn.gelu(value, approximate=False)


def column_sum(value):
    return jnp.sum(value.astype(jnp.float32), axis=0)


def forward_pass(params, field_in, positions):
    g1, b1, wqkv, bqkv, wo, bo, g2, b2, w1, bu, w2, bd = params
    field = field_in.astype(jnp.float32)
    count, width = field.shape
    heads = width // 64
    angles = rotary_angles(positions)
    cosine = jnp.cos(angles)[:, None, :]
    sine = jnp.sin(angles)[:, None, :]
    normed1, factor1 = normalize(field)
    h1 = (normed1 * g1.astype(jnp.float32) + b1.astype(jnp.float32)).astype(jnp.bfloat16)
    qkv = jnp.dot(h1, wqkv, preferred_element_type=jnp.float32) + bqkv.astype(jnp.float32)
    query_rot = rotate(qkv[:, :width].reshape(count, heads, 64), cosine, sine).astype(jnp.bfloat16)
    keys_rot = (
        rotate(qkv[:, width : 2 * width].reshape(count, heads, 64), cosine, sine)
        .astype(jnp.bfloat16)
        .reshape(count, width)
    )
    values = qkv[:, 2 * width :].astype(jnp.bfloat16)
    keys_all, values_all = (
        lax.all_gather(keys_rot, "grp", axis=0, tiled=True),
        lax.all_gather(values, "grp", axis=0, tiled=True),
    )
    total = keys_all.shape[0]
    keys_all = keys_all.reshape(total, heads, 64)
    values_all = values_all.reshape(total, heads, 64)
    scores = (
        jnp.einsum("thd,shd->hts", query_rot, keys_all, preferred_element_type=jnp.float32) * SCALE
    )
    top = jnp.max(scores, axis=-1, keepdims=True)
    lse = top + jnp.log(jnp.sum(jnp.exp(scores - top), axis=-1, keepdims=True))
    probs = jnp.exp(scores - lse).astype(jnp.bfloat16)
    mixed = (
        jnp.einsum("hts,shd->thd", probs, values_all, preferred_element_type=jnp.float32)
        .reshape(count, width)
        .astype(jnp.bfloat16)
    )
    second = field + jnp.dot(mixed, wo, preferred_element_type=jnp.float32) + bo.astype(jnp.float32)
    normed2, factor2 = normalize(second)
    h2 = (normed2 * g2.astype(jnp.float32) + b2.astype(jnp.float32)).astype(jnp.bfloat16)
    hidden = jnp.dot(h2, w1, preferred_element_type=jnp.float32) + bu.astype(jnp.float32)
    active = exact_gelu(hidden).astype(jnp.bfloat16)
    result = (
        second + jnp.dot(active, w2, preferred_element_type=jnp.float32) + bd.astype(jnp.float32)
    )
    saved = (
        normed1,
        factor1,
        h1,
        query_rot,
        keys_rot,
        values,
        lse,
        mixed,
        normed2,
        factor2,
        h2,
        hidden,
        active,
        cosine,
        sine,
    )
    return (saved, result.astype(jnp.bfloat16))


def backward_pass(params, saved, grad_in, totals):
    g1, b1, wqkv, bqkv, wo, bo, g2, b2, w1, bu, w2, bd = params
    (
        normed1,
        factor1,
        h1,
        query_rot,
        keys_rot,
        values,
        lse,
        mixed,
        normed2,
        factor2,
        h2,
        hidden,
        active,
        cosine,
        sine,
    ) = saved
    grad_out = grad_in.astype(jnp.float32)
    count, width = grad_out.shape
    heads = width // 64
    grad_y2 = grad_out.astype(jnp.bfloat16)
    grad_w2 = outer(active, grad_y2)
    grad_bd = column_sum(grad_y2)
    grad_act = back(grad_y2, w2)
    unused, pull = jax.vjp(exact_gelu, hidden)
    grad_hidden = pull(grad_act)[0].astype(jnp.bfloat16)
    grad_w1 = outer(h2, grad_hidden)
    grad_bu = column_sum(grad_hidden)
    grad_h2 = back(grad_hidden, w1)
    grad_g2 = jnp.sum(grad_h2 * normed2, axis=0)
    grad_b2 = jnp.sum(grad_h2, axis=0)
    grad_second = grad_out + norm_back(grad_h2 * g2.astype(jnp.float32), normed2, factor2)
    grad_y1 = grad_second.astype(jnp.bfloat16)
    grad_wo = outer(mixed, grad_y1)
    grad_bo = column_sum(grad_y1)
    grad_mixed = back(grad_y1, wo).astype(jnp.bfloat16).reshape(count, heads, 64)
    keys_all, values_all = (
        lax.all_gather(keys_rot, "grp", axis=0, tiled=True),
        lax.all_gather(values, "grp", axis=0, tiled=True),
    )
    total = keys_all.shape[0]
    keys_all = keys_all.reshape(total, heads, 64)
    values_all = values_all.reshape(total, heads, 64)
    scores = (
        jnp.einsum("thd,shd->hts", query_rot, keys_all, preferred_element_type=jnp.float32) * SCALE
    )
    probs = jnp.exp(scores - lse)
    grad_probs = jnp.einsum(
        "thd,shd->hts", grad_mixed, values_all, preferred_element_type=jnp.float32
    )
    delta = jnp.sum(probs * grad_probs, axis=-1, keepdims=True)
    grad_scores = (probs * (grad_probs - delta)).astype(jnp.bfloat16)
    grad_query = (
        jnp.einsum("hts,shd->thd", grad_scores, keys_all, preferred_element_type=jnp.float32)
        * SCALE
    )
    probs_low = probs.astype(jnp.bfloat16)
    grad_values = jnp.einsum(
        "hts,thd->shd", probs_low, grad_mixed, preferred_element_type=jnp.float32
    )
    grad_keys = (
        jnp.einsum("hts,thd->shd", grad_scores, query_rot, preferred_element_type=jnp.float32)
        * SCALE
    )
    keys_own, values_own = (
        lax.psum_scatter(
            grad_keys.reshape(total, width).astype(jnp.bfloat16),
            "grp",
            scatter_dimension=0,
            tiled=True,
        ).astype(jnp.float32),
        lax.psum_scatter(
            grad_values.reshape(total, width).astype(jnp.bfloat16),
            "grp",
            scatter_dimension=0,
            tiled=True,
        ).astype(jnp.float32),
    )
    query_back = rotate(grad_query, cosine, -sine).reshape(count, width)
    keys_back = rotate(keys_own.reshape(count, heads, 64), cosine, -sine).reshape(count, width)
    grad_qkv = jnp.concatenate([query_back, keys_back, values_own], axis=1).astype(jnp.bfloat16)
    grad_wqkv = outer(h1, grad_qkv)
    grad_bqkv = column_sum(grad_qkv)
    grad_h1 = back(grad_qkv, wqkv)
    grad_g1 = jnp.sum(grad_h1 * normed1, axis=0)
    grad_b1 = jnp.sum(grad_h1, axis=0)
    grad_field = grad_second + norm_back(grad_h1 * g1.astype(jnp.float32), normed1, factor1)
    terms = (
        grad_g1,
        grad_b1,
        grad_wqkv,
        grad_bqkv,
        grad_wo,
        grad_bo,
        grad_g2,
        grad_b2,
        grad_w1,
        grad_bu,
        grad_w2,
        grad_bd,
    )
    totals = tuple((a + b for a, b in zip(totals, terms)))
    return (grad_field.astype(jnp.bfloat16), totals)


def local(
    tokens,
    positions,
    ln1_gain,
    ln1_bias,
    w_qkv,
    b_qkv,
    w_out,
    b_out,
    ln2_gain,
    ln2_bias,
    w_up,
    b_up,
    w_down,
    b_down,
    cotangent,
):
    shards = (
        ln1_gain,
        ln1_bias,
        w_qkv,
        b_qkv,
        w_out,
        b_out,
        ln2_gain,
        ln2_bias,
        w_up,
        b_up,
        w_down,
        b_down,
    )
    groups = lax.axis_size("grp")
    totals = tuple((jnp.zeros((s.shape[0] * groups,) + s.shape[1:], jnp.float32) for s in shards))
    outputs = []
    gradients = []
    for index in range(tokens.shape[0]):
        forward_params = (
            lax.all_gather(ln1_gain, "grp", axis=0, tiled=True),
            lax.all_gather(ln1_bias, "grp", axis=0, tiled=True),
            lax.all_gather(w_qkv, "grp", axis=0, tiled=True),
            lax.all_gather(b_qkv, "grp", axis=0, tiled=True),
            lax.all_gather(w_out, "grp", axis=0, tiled=True),
            lax.all_gather(b_out, "grp", axis=0, tiled=True),
            lax.all_gather(ln2_gain, "grp", axis=0, tiled=True),
            lax.all_gather(ln2_bias, "grp", axis=0, tiled=True),
            lax.all_gather(w_up, "grp", axis=0, tiled=True),
            lax.all_gather(b_up, "grp", axis=0, tiled=True),
            lax.all_gather(w_down, "grp", axis=0, tiled=True),
            lax.all_gather(b_down, "grp", axis=0, tiled=True),
        )
        saved, result = forward_pass(forward_params, tokens[index], positions[:, index, :])
        outputs.append(result)
        backward_params = (
            lax.all_gather(ln1_gain, "grp", axis=0, tiled=True),
            lax.all_gather(ln1_bias, "grp", axis=0, tiled=True),
            lax.all_gather(w_qkv, "grp", axis=0, tiled=True),
            lax.all_gather(b_qkv, "grp", axis=0, tiled=True),
            lax.all_gather(w_out, "grp", axis=0, tiled=True),
            lax.all_gather(b_out, "grp", axis=0, tiled=True),
            lax.all_gather(ln2_gain, "grp", axis=0, tiled=True),
            lax.all_gather(ln2_bias, "grp", axis=0, tiled=True),
            lax.all_gather(w_up, "grp", axis=0, tiled=True),
            lax.all_gather(b_up, "grp", axis=0, tiled=True),
            lax.all_gather(w_down, "grp", axis=0, tiled=True),
            lax.all_gather(b_down, "grp", axis=0, tiled=True),
        )
        grad_field, totals = backward_pass(backward_params, saved, cotangent[index], totals)
        gradients.append(grad_field)
    owned = (
        lax.psum_scatter(
            totals[0].astype(jnp.bfloat16), "grp", scatter_dimension=0, tiled=True
        ).astype(jnp.float32),
        lax.psum_scatter(
            totals[1].astype(jnp.bfloat16), "grp", scatter_dimension=0, tiled=True
        ).astype(jnp.float32),
        lax.psum_scatter(
            totals[2].astype(jnp.bfloat16), "grp", scatter_dimension=0, tiled=True
        ).astype(jnp.float32),
        lax.psum_scatter(
            totals[3].astype(jnp.bfloat16), "grp", scatter_dimension=0, tiled=True
        ).astype(jnp.float32),
        lax.psum_scatter(
            totals[4].astype(jnp.bfloat16), "grp", scatter_dimension=0, tiled=True
        ).astype(jnp.float32),
        lax.psum_scatter(
            totals[5].astype(jnp.bfloat16), "grp", scatter_dimension=0, tiled=True
        ).astype(jnp.float32),
        lax.psum_scatter(
            totals[6].astype(jnp.bfloat16), "grp", scatter_dimension=0, tiled=True
        ).astype(jnp.float32),
        lax.psum_scatter(
            totals[7].astype(jnp.bfloat16), "grp", scatter_dimension=0, tiled=True
        ).astype(jnp.float32),
        lax.psum_scatter(
            totals[8].astype(jnp.bfloat16), "grp", scatter_dimension=0, tiled=True
        ).astype(jnp.float32),
        lax.psum_scatter(
            totals[9].astype(jnp.bfloat16), "grp", scatter_dimension=0, tiled=True
        ).astype(jnp.float32),
        lax.psum_scatter(
            totals[10].astype(jnp.bfloat16), "grp", scatter_dimension=0, tiled=True
        ).astype(jnp.float32),
        lax.psum_scatter(
            totals[11].astype(jnp.bfloat16), "grp", scatter_dimension=0, tiled=True
        ).astype(jnp.float32),
    )
    summed = (
        lax.psum(owned[0].astype(jnp.bfloat16), "rep").astype(jnp.float32),
        lax.psum(owned[1].astype(jnp.bfloat16), "rep").astype(jnp.float32),
        lax.psum(owned[2].astype(jnp.bfloat16), "rep").astype(jnp.float32),
        lax.psum(owned[3].astype(jnp.bfloat16), "rep").astype(jnp.float32),
        lax.psum(owned[4].astype(jnp.bfloat16), "rep").astype(jnp.float32),
        lax.psum(owned[5].astype(jnp.bfloat16), "rep").astype(jnp.float32),
        lax.psum(owned[6].astype(jnp.bfloat16), "rep").astype(jnp.float32),
        lax.psum(owned[7].astype(jnp.bfloat16), "rep").astype(jnp.float32),
        lax.psum(owned[8].astype(jnp.bfloat16), "rep").astype(jnp.float32),
        lax.psum(owned[9].astype(jnp.bfloat16), "rep").astype(jnp.float32),
        lax.psum(owned[10].astype(jnp.bfloat16), "rep").astype(jnp.float32),
        lax.psum(owned[11].astype(jnp.bfloat16), "rep").astype(jnp.float32),
    )
    output = jnp.stack(outputs, axis=0)
    grad_tokens = jnp.stack(gradients, axis=0)
    return (
        output,
        grad_tokens,
        summed[0],
        summed[1],
        summed[2],
        summed[3],
        summed[4],
        summed[5],
        summed[6],
        summed[7],
        summed[8],
        summed[9],
        summed[10],
        summed[11],
    )


def spread(mesh):
    placed = (
        P("rep", "grp", None),
        P(None, "rep", "grp"),
        P("grp"),
        P("grp"),
        P("grp", None),
        P("grp"),
        P("grp", None),
        P("grp"),
        P("grp"),
        P("grp"),
        P("grp", None),
        P("grp"),
        P("grp", None),
        P("grp"),
        P("rep", "grp", None),
    )
    return jax.shard_map(
        local,
        mesh=mesh,
        in_specs=placed,
        out_specs=(
            P("rep", "grp", None),
            P("rep", "grp", None),
            P("grp"),
            P("grp"),
            P("grp", None),
            P("grp"),
            P("grp", None),
            P("grp"),
            P("grp"),
            P("grp"),
            P("grp", None),
            P("grp"),
            P("grp", None),
            P("grp"),
        ),
        check_vma=False,
    )


def solution(mesh):
    reps, groups = mesh.devices.shape
    flat = mesh.devices.reshape(-1)

    def run(*args):
        clips = args[0].shape[0] // reps
        if reps == 8 and groups == 2 * clips:
            split = Mesh(flat.reshape(reps // 2, 2, groups), ("rp", "core", "grp"))
            ins, outs = paired_specs()
            return jax.shard_map(
                paired, mesh=split, in_specs=ins, out_specs=outs, check_vma=False
            )(*args)
        return spread(mesh)(*args)

    return run
```

```python
import functools

import jax
import jax.numpy as jnp
from jax import lax
from jax.experimental import pallas as pl
from jax.experimental.pallas import tpu as pltpu
from jax.sharding import Mesh
from jax.sharding import PartitionSpec as P

SCALE = 0.125
EPS = 1e-06
HEAD = 64
BF = jnp.bfloat16
F32 = jnp.float32
MESH = pl.DeviceIdType.MESH
ANY = pl.BlockSpec(memory_space=pl.ANY)
VM = pl.BlockSpec(memory_space=pltpu.VMEM)


def where_am_i():
    return lax.axis_index("rp"), lax.axis_index("core"), lax.axis_index("grp")


def remote(src, dst, send, recv, target):
    return pltpu.make_async_remote_copy(
        src_ref=src,
        dst_ref=dst,
        send_sem=send,
        recv_sem=recv,
        device_id=target,
        device_id_type=MESH,
    )


def enter(p, c, z, groups):
    barrier = pltpu.get_barrier_semaphore()
    for k in range(groups):
        for d in range(2):
            if k == 0 and d == 0:
                continue
            pl.semaphore_signal(
                barrier, inc=1, device_id=(p, c ^ d, lax.rem(z + k, groups)), device_id_type=MESH
            )
    for b in (1, 2):
        pl.semaphore_signal(barrier, inc=1, device_id=(p ^ b, c, z), device_id_type=MESH)
    pl.semaphore_wait(barrier, 2 * groups - 1 + 2)


def move_tokens(refs, outs, send, recv, p, c, z, clips):
    core, slot = lax.div(z, clips), lax.rem(z, clips)

    def route(i):
        return core, c * clips + i

    def here(i):
        return jnp.logical_and(core == c, c * clips + i == z)

    def start():
        for n, (src, dst) in enumerate(zip(refs, outs)):
            for i in range(clips):
                tc, tz = route(i)

                @pl.when(here(i))
                def _():
                    pltpu.make_async_copy(src.at[i], dst.at[slot], recv.at[n, slot]).start()

                @pl.when(jnp.logical_not(here(i)))
                def _():
                    remote(
                        src.at[i], dst.at[slot], send.at[n, i], recv.at[n, slot], (p, tc, tz)
                    ).start()

    def finish():
        for n, (src, dst) in enumerate(zip(refs, outs)):
            for i in range(clips):

                @pl.when(jnp.logical_not(here(i)))
                def _():
                    remote(
                        src.at[i], dst.at[slot], send.at[n, i], recv.at[n, slot], (p, c ^ 1, z)
                    ).wait_send()

            for m in range(clips):
                pltpu.make_async_copy(src.at[0], dst.at[m], recv.at[n, m]).wait()

    return start, finish


def cuts(whole, half, c, blocks):
    if blocks == 0:
        return [(whole.at[c], half)]
    size = half.shape[3] // blocks
    return [
        (
            whole.at[:, :, :, pl.ds(pl.multiple_of((2 * b + c) * size, size), size)],
            half.at[:, :, :, pl.ds(b * size, size)],
        )
        for b in range(blocks)
    ]


def gather_body(groups, clips, blocks, *refs):
    count = len(blocks)
    raw, (small, x, pos, dy) = refs[:count], refs[count : count + 4]
    outs = refs[count + 4 : 2 * count + 4]
    small_o, x_o, pos_o, dy_o = refs[2 * count + 4 : 2 * count + 8]
    halves = refs[2 * count + 8 : 3 * count + 8]
    zs, zr, xs, xr, ys, yr, fs, fr, hs, ls, ss, sr, ts, tr, us, ur = refs[3 * count + 8 :]
    p, c, z = where_am_i()
    for w in range(count):
        for src, dst in cuts(raw[w], halves[w], c, blocks[w]):
            pltpu.make_async_copy(src, dst, hs.at[w]).start()
    enter(p, c, z, groups)
    col = [(p, c, lax.rem(z + k, groups)) for k in range(groups)]
    org = [lax.rem(z + groups - k, groups) for k in range(groups)]
    xn, yn = (p ^ 1, c, z), (p ^ 2, c, z)
    start, finish = move_tokens((x, pos), (x_o, pos_o), ts, tr, p, c, z, clips)
    start()
    smalls = [
        remote(small, small_o.at[z], ss.at[k], sr.at[k], col[k]) for k in range(1, groups)
    ]
    for s in smalls:
        s.start()
    keep = [pltpu.make_async_copy(small, small_o.at[z], ls.at[count])]
    keep[0].start()
    first = {}
    for w in range(count):
        pltpu.make_async_copy(halves[w], halves[w], hs.at[w]).wait()
        keep.append(pltpu.make_async_copy(halves[w], outs[w].at[z], ls.at[w]))
        keep[-1].start()
        for k in range(1, groups):
            first[w, k] = remote(
                halves[w].at[p], outs[w].at[z, p], zs.at[w, k], zr.at[w, k], col[k]
            )
            first[w, k].start()
    start_dy, finish_dy = move_tokens((dy,), (dy_o,), us, ur, p, c, z, clips)
    start_dy()
    units = [(w, k) for w in range(count) for k in range(1, groups)]
    xc, yc, fa, fb = {}, {}, {}, {}

    def plane(u):
        w, k = u
        o = outs[w].at[org[k]]
        remote(halves[w].at[p], o.at[p], zs.at[w, k], zr.at[w, k], col[k]).wait_recv()
        xc[u] = remote(o.at[p], o.at[p], xs.at[w, k], xr.at[w, k], xn)
        yc[u] = remote(o.at[p], o.at[p], ys.at[w, k], yr.at[w, k], yn)
        xc[u].start()
        yc[u].start()

    def forward(u):
        w, k = u
        o = outs[w].at[org[k]]
        q = p ^ 1
        remote(o.at[q], o.at[q], xs.at[w, k], xr.at[w, k], xn).wait_recv()
        fa[u] = remote(o.at[q, 0], o.at[q, 0], fs.at[w, k, 0], fr.at[w, k, 0], yn)
        fa[u].start()
        q = p ^ 2
        remote(o.at[q], o.at[q], ys.at[w, k], yr.at[w, k], yn).wait_recv()
        fb[u] = remote(o.at[q, 1], o.at[q, 1], fs.at[w, k, 1], fr.at[w, k, 1], xn)
        fb[u].start()

    lag = 2
    for n in range(len(units) + lag):
        if n < len(units):
            plane(units[n])
        if n >= lag:
            forward(units[n - lag])
    for u in units:
        w, k = u
        q = p ^ 3
        o = outs[w].at[org[k]]
        remote(o.at[q, 0], o.at[q, 0], fs.at[w, k, 0], fr.at[w, k, 0], yn).wait_recv()
        remote(o.at[q, 1], o.at[q, 1], fs.at[w, k, 1], fr.at[w, k, 1], xn).wait_recv()
    for k in range(1, groups):
        remote(small, small_o.at[org[k]], ss.at[k], sr.at[k], col[k]).wait_recv()
    for u in units:
        first[u].wait_send()
        xc[u].wait_send()
        yc[u].wait_send()
        fa[u].wait_send()
        fb[u].wait_send()
    for s in smalls:
        s.wait_send()
    for k in keep:
        k.wait()
    finish()
    finish_dy()


def half_shape(raw, blocks):
    return raw.shape[1:] if blocks == 0 else raw.shape[:3] + (raw.shape[3] // 2,)


def gather(raw, blocks, small, x, pos, dy, groups):
    count, clips = len(raw), x.shape[0]
    dma = pltpu.SemaphoreType.DMA
    halves = [half_shape(r, b) for r, b in zip(raw, blocks)]
    shapes = [jax.ShapeDtypeStruct((groups,) + h, BF) for h in halves]
    shapes += [jax.ShapeDtypeStruct((groups,) + small.shape, small.dtype)]
    shapes += [jax.ShapeDtypeStruct(v.shape, v.dtype) for v in (x, pos, dy)]
    return pl.pallas_call(
        functools.partial(gather_body, groups, clips, blocks),
        out_shape=shapes,
        in_specs=[ANY] * count + [VM, ANY, ANY, ANY],
        out_specs=[ANY] * len(shapes),
        scratch_shapes=[pltpu.VMEM(h, BF) for h in halves]
        + [dma((count, groups))] * 6
        + [dma((count, groups, 2))] * 2
        + [dma((count,)), dma((count + 1,)), dma((groups,)), dma((groups,))]
        + [dma((2, clips))] * 2
        + [dma((1, clips))] * 2,
        compiler_params=pltpu.CompilerParams(collective_id=0, has_side_effects=True),
        name="gather",
    )(*raw, small, x, pos, dy)


def reduce_body(groups, clips, blocks, *refs):
    count = len(blocks)
    grads, (small, gx) = refs[:count], refs[count : count + 2]
    outs = refs[count + 2 : 2 * count + 2]
    small_o, gx_o = refs[2 * count + 2 : 2 * count + 4]
    scratch = refs[2 * count + 4 :]
    own_a, own_b, one_a, one_b, two_a, two_b, mine, three, full = (
        scratch[i * count : (i + 1) * count] for i in range(9)
    )
    small_s, small_r, small_z = scratch[9 * count : 9 * count + 3]
    (os, s1, r1, s2, r2, s3, r3, s4, r4, s5, r5, cs, cr, ls, ss, sr, ts, tr) = scratch[9 * count + 3 :]
    p, c, z = where_am_i()
    hi, lo = lax.div(p, 2), lax.rem(p, 2)
    enter(p, c, z, groups)
    col = [(p, c, lax.rem(z + k, groups)) for k in range(groups)]
    xn, yn, cn = (p ^ 1, c, z), (p ^ 2, c, z), (p, c ^ 1, z)
    start, finish = move_tokens((gx,), (gx_o,), ts, tr, p, c, z, clips)
    start()
    small_s[...] = small[...]
    for n, target in enumerate((cn, xn, yn)):
        copy = remote(small_s, small_r.at[n], ss.at[n], sr.at[n], target)
        copy.start()
        copy.wait()
        small_s[...] += small_r[n]
    tails = [
        remote(small_s.at[col[k][2]], small_z.at[k], ss.at[2 + k], sr.at[2 + k], col[k])
        for k in range(1, groups)
    ]
    for t in tails:
        t.start()
    units = [(w, k) for w in range(count) for k in range(groups)]
    load, c1, c2, c3, c4, c5 = {}, {}, {}, {}, {}, {}
    for u in units:
        w, k = u
        g = grads[w].at[k]
        c1[u, 0] = remote(g.at[:, 1 - lo, 0], one_a[w].at[k], s1.at[w, k, 0], r1.at[w, k, 0], xn)
        c1[u, 1] = remote(g.at[1 - hi, :, 1], one_b[w].at[k], s1.at[w, k, 1], r1.at[w, k, 1], yn)
        load[u, 0] = pltpu.make_async_copy(g.at[:, lo, 0], own_a[w].at[k], os.at[w, k, 0])
        load[u, 1] = pltpu.make_async_copy(g.at[hi, :, 1], own_b[w].at[k], os.at[w, k, 1])
        c1[u, 0].start()
        c1[u, 1].start()
        load[u, 0].start()
        load[u, 1].start()

    def stage_one(u):
        w, k = u
        for n, (own, one, two, side, target) in enumerate(
            ((own_a, one_a, two_a, hi, yn), (own_b, one_b, two_b, lo, xn))
        ):
            load[u, n].wait()
            c1[u, n].wait_recv()
            o = own[w].at[k]
            o[...] = (o[...].astype(F32) + one[w][k].astype(F32)).astype(BF)
            c2[u, n] = remote(o.at[1 - side], two[w].at[k], s2.at[w, k, n], r2.at[w, k, n], target)
            c2[u, n].start()

    def stage_two(u):
        w, k = u
        for n, (own, two, side) in enumerate(((own_a, two_a, hi), (own_b, two_b, lo))):
            c2[u, n].wait_recv()
            mine[w][k, n] = (own[w][k, side].astype(F32) + two[w][k].astype(F32)).astype(BF)

        @pl.when(z != k)
        def _():
            remote(
                mine[w].at[k],
                three[w].at[lax.rem(k - z + groups, groups)],
                s3.at[w, k],
                r3.at[w, lax.rem(k - z + groups, groups)],
                (p, c, k),
            ).start()

    def stage_three(w):
        total = mine[w][z].astype(F32)
        for k in range(1, groups):
            remote(mine[w].at[0], three[w].at[k], s3.at[w, 0], r3.at[w, k], col[k]).wait_recv()
            total = total + three[w][k].astype(F32)
        full[w][p] = total.astype(BF)
        for n, target in enumerate((xn, yn)):
            f = full[w].at[p]
            c4[w, n] = remote(f, f, s4.at[w, n], r4.at[w, n], target)
            c4[w, n].start()

    def stage_four(w):
        for n, (q, target) in enumerate(((p ^ 1, yn), (p ^ 2, xn))):
            f = full[w].at[q]
            remote(f, f, s4.at[w, n], r4.at[w, n], target).wait_recv()
            f = full[w].at[q, n]
            c5[w, n] = remote(f, f, s5.at[w, n], r5.at[w, n], target)
            c5[w, n].start()

    def stage_five(w):
        for n in range(2):
            f = full[w].at[p ^ 3, n]
            remote(f, f, s5.at[w, n], r5.at[w, n], xn).wait_recv()
        for dst, src in cuts(outs[w], full[w], c, blocks[w]):
            pltpu.make_async_copy(src, dst, ls.at[w]).start()
            remote(src, dst, cs.at[w], cr.at[w], cn).start()

    lag = 3
    for n in range(len(units) + lag):
        if n < len(units):
            stage_one(units[n])
        if n >= lag:
            stage_two(units[n - lag])
    for w in range(count):
        stage_three(w)
        if w >= 1:
            stage_four(w - 1)
        if w >= 2:
            stage_five(w - 2)
    stage_four(count - 1)
    for w in range(max(count - 2, 0), count):
        stage_five(w)
    for k in range(1, groups):
        tails[k - 1].wait()
    small_o[...] = small_s[z]
    for k in range(1, groups):
        small_o[...] += small_z[k]
    for u in units:
        w, k = u
        for n in range(2):
            c1[u, n].wait_send()
            c2[u, n].wait_send()

        @pl.when(z != k)
        def _():
            remote(mine[w].at[k], three[w].at[0], s3.at[w, k], r3.at[w, 0], xn).wait_send()

    for w in range(count):
        for n in range(2):
            c4[w, n].wait_send()
            c5[w, n].wait_send()
        pltpu.make_async_copy(full[w], full[w], ls.at[w]).wait()
        remote(full[w], full[w], cs.at[w], cr.at[w], cn).wait()
    finish()


def reduce(grads, blocks, small, gx, groups):
    count, clips = len(grads), gx.shape[0]
    dma = pltpu.SemaphoreType.DMA
    tiles = [g.shape[4:] for g in grads]
    shapes = [
        jax.ShapeDtypeStruct((4, 2, t[0], 2 * t[1]) if b else (2, 4, 2) + t, BF)
        for t, b in zip(tiles, blocks)
    ]
    shapes += [
        jax.ShapeDtypeStruct(small.shape[1:], small.dtype),
        jax.ShapeDtypeStruct(gx.shape, gx.dtype),
    ]
    scratch = []
    for lead in (
        (groups, 2),
        (groups, 2),
        (groups, 2),
        (groups, 2),
        (groups,),
        (groups,),
        (groups, 2),
        (groups, 2),
        (4, 2),
    ):
        scratch += [pltpu.VMEM(lead + t, BF) for t in tiles]
    scratch += [
        pltpu.VMEM(small.shape, F32),
        pltpu.VMEM((3,) + small.shape, F32),
        pltpu.VMEM(small.shape, F32),
    ]
    pair = dma((count, groups, 2))
    scratch += [pair] * 5 + [dma((count, groups))] * 2 + [dma((count, 2))] * 4
    scratch += [dma((count,))] * 3 + [dma((2 + groups,))] * 2 + [dma((1, clips))] * 2
    return pl.pallas_call(
        functools.partial(reduce_body, groups, clips, blocks),
        out_shape=shapes,
        in_specs=[ANY] * count + [VM, ANY],
        out_specs=[ANY] * count + [VM, ANY],
        scratch_shapes=scratch,
        compiler_params=pltpu.CompilerParams(
            collective_id=1, has_side_effects=True, vmem_limit_bytes=60 * 1024 * 1024
        ),
        name="reduce",
    )(*grads, small, gx)


def turn(u, cosine, sine):
    half = HEAD // 2
    first, second = u[:half], u[half:]
    return jnp.concatenate(
        [first * cosine - second * sine, first * sine + second * cosine], axis=0
    )


def dot(a, b):
    return jnp.dot(a, b, preferred_element_type=F32)


def attention_body(step, q_ref, k_ref, v_ref, cos_ref, sin_ref, qs_ref, kr_ref, vb_ref, o_ref, l_ref):
    cosine, sine = cos_ref[...], sin_ref[...]
    length = cosine.shape[1]
    kr = turn(k_ref[...], cosine, sine).astype(BF)
    vb = v_ref[...].astype(BF)
    qs = (turn(q_ref[...], cosine, sine).astype(BF).astype(F32) * SCALE).astype(BF)
    kr_ref[...] = kr
    vb_ref[...] = vb
    qs_ref[...] = qs
    keys = kr.T
    for i in range(0, length, step):
        scores = dot(keys, qs[:, i : i + step])
        top = jnp.max(scores, axis=0, keepdims=True)
        e = jnp.exp(scores - top)
        total = jnp.sum(e, axis=0, keepdims=True)
        mixed = dot(vb, e.astype(BF))
        o_ref[:, i : i + step] = (mixed / total).astype(BF)
        l_ref[0, :, i : i + step] = top + jnp.log(total)


def attention(qkv, cosine, sine, step=256):
    rows, length = qkv.shape
    width = rows // 3
    heads = width // HEAD
    block = [pl.BlockSpec((HEAD, length), lambda h, n=n: (n * heads + h, 0)) for n in range(3)]
    table = pl.BlockSpec((HEAD // 2, length), lambda h: (0, 0))
    out = pl.BlockSpec((HEAD, length), lambda h: (h, 0))
    shape = jax.ShapeDtypeStruct((width, length), BF)
    return pl.pallas_call(
        functools.partial(attention_body, step),
        out_shape=[shape] * 4 + [jax.ShapeDtypeStruct((heads, 1, length), F32)],
        grid=(heads,),
        in_specs=block + [table, table],
        out_specs=[out] * 4 + [pl.BlockSpec((1, 1, length), lambda h: (h, 0, 0))],
        cost_estimate=pl.CostEstimate(
            flops=4 * width * length * length,
            transcendentals=heads * length * length,
            bytes_accessed=width * length * 24,
        ),
        name="attention",
    )(qkv, qkv, qkv, cosine, sine)


def attention_back_body(
    step, q_ref, k_ref, v_ref, o_ref, l_ref, g_ref, cos_ref, sin_ref, dq_ref, dk_ref, dv_ref, ak, av
):
    cosine, sine = cos_ref[...], sin_ref[...]
    length = cosine.shape[1]
    kt, keys, values = k_ref[...], k_ref[...].T, v_ref[...].T
    queries, grads = q_ref[...].T, g_ref[...].T
    for i in range(0, length, step):
        s = slice(i, i + step)
        g = g_ref[:, s]
        scores = dot(keys, q_ref[:, s])
        p = jnp.exp(scores - l_ref[0, :, s])
        dp = dot(values, g)
        delta = jnp.sum(o_ref[:, s].astype(F32) * g.astype(F32), axis=0, keepdims=True)
        ds = (p * (dp - delta)).astype(BF)
        dq = dot(kt, ds) * SCALE
        dq_ref[:, s] = turn(dq, cosine[:, s], -sine[:, s]).astype(BF)
        dv = dot(p.astype(BF), grads[s])
        dk = dot(ds, queries[s])
        if i == 0:
            ak[...] = dk
            av[...] = dv
        else:
            ak[...] += dk
            av[...] += dv
    dk_ref[...] = turn(ak[...].T, cosine, -sine).astype(BF)
    dv_ref[...] = av[...].T.astype(BF)


def attention_back(qs, kr, vb, out, lse, grad, cosine, sine, step=256):
    width, length = qs.shape
    heads = width // HEAD
    row = pl.BlockSpec((HEAD, length), lambda h: (h, 0))
    table = pl.BlockSpec((HEAD // 2, length), lambda h: (0, 0))
    line = pl.BlockSpec((1, 1, length), lambda h: (h, 0, 0))
    shape = jax.ShapeDtypeStruct((width, length), BF)
    return pl.pallas_call(
        functools.partial(attention_back_body, step),
        out_shape=[shape] * 3,
        grid=(heads,),
        in_specs=[row] * 4 + [line, row, table, table],
        out_specs=[row] * 3,
        scratch_shapes=[pltpu.VMEM((length, HEAD), F32)] * 2,
        cost_estimate=pl.CostEstimate(
            flops=10 * width * length * length,
            transcendentals=heads * length * length,
            bytes_accessed=width * length * 18,
        ),
        name="attention_back",
    )(qs, kr, vb, out, lse, grad, cosine, sine)


def swap(value):
    return lax.ppermute(value, "core", [(0, 1), (1, 0)])


def both(value):
    return jnp.concatenate([value, swap(value)], axis=0)


def contract(left, right, a, b):
    return lax.dot_general(left, right, (((a,), (b,)), ((), ())), preferred_element_type=F32)


def own_sum(partial):
    half = partial.shape[0] // 2
    return partial[:half] + swap(partial[half:].astype(BF)).astype(F32)


def move_blocks(x, clips, groups):
    c, z = lax.axis_index("core"), lax.axis_index("grp")
    got = []
    for t in range(clips):
        pairs = []
        for cc in range(2):
            for zz in range(groups):
                i = (t + zz) % clips
                pairs.append((cc * groups + zz, (zz // clips) * groups + cc * clips + i))
        block = lax.dynamic_index_in_dim(x, lax.rem(t + z, clips), 0, keepdims=False)
        got.append(lax.ppermute(block, ("core", "grp"), pairs))
    stacked = jnp.stack(got)
    return jnp.stack(
        [
            lax.dynamic_index_in_dim(stacked, lax.rem(z - m + clips, clips), 0, keepdims=False)
            for m in range(clips)
        ]
    )


def paired(
    tokens,
    positions,
    ln1_gain,
    ln1_bias,
    w_qkv,
    b_qkv,
    w_out,
    b_out,
    ln2_gain,
    ln2_bias,
    w_up,
    b_up,
    w_down,
    b_down,
    cotangent,
):
    groups = lax.axis_size("grp")
    clips, part, width = tokens.shape
    hidden = w_down.shape[0] * groups
    own = clips * part
    length = 2 * own
    c, z = lax.axis_index("core"), lax.axis_index("grp")
    wide = width // 2
    deep = hidden // 2
    row = width // groups

    def pick(value, axis):
        return lax.dynamic_index_in_dim(value, c, axis, keepdims=False)

    blocks = (3 * groups, 0, groups, 0)
    raw = [
        w.reshape(((4, 2) if b else (2, 4, 2)) + (w.shape[0] // (8 if b else 16), w.shape[1]))
        for w, b in zip((w_qkv, w_out, w_up, w_down), blocks)
    ]
    bq, bu = b_qkv.shape[0] // row, b_up.shape[0] // row
    vectors = [ln1_gain, ln1_bias, b_out, ln2_gain, ln2_bias, b_down]
    vectors += [b_qkv[n * row : (n + 1) * row] for n in range(bq)]
    vectors += [b_up[n * row : (n + 1) * row] for n in range(bu)]
    lines = len(vectors)
    place = lax.broadcasted_iota(jnp.int32, (lines + -lines % 8, row), 0)
    small = jnp.zeros(place.shape, F32)
    for n, v in enumerate(vectors):
        small = jnp.where(place == n, v.astype(F32)[None, :], small)
    pos = jnp.pad(jnp.moveaxis(positions, 0, 1).astype(F32), ((0, 0), (0, 5), (0, 0)))
    wq, wo, w1, w2, small, x, pos, dy = gather(raw, blocks, small, tokens, pos, cotangent, groups)
    wq = wq.reshape(width, 3 * wide)
    wo = wo.reshape(wide, width)
    w1 = w1.reshape(width, deep)
    w2 = w2.reshape(deep, width)
    g1, b1, bo, g2, b2, bd = (small[:, n].reshape(1, width) for n in range(6))
    bq_own = pick(small[:, 6 : 6 + bq].reshape(3, groups, 2, row // 2), 2).reshape(3 * wide, 1)
    bu_own = pick(small[:, 6 + bq : lines].reshape(groups, 2, deep // groups), 1).reshape(1, deep)

    grad_out = dy.reshape(own, width)
    grad_all = both(grad_out)
    grad_f = grad_out.astype(F32)

    pos = jnp.moveaxis(pos[:, :3], 1, 0).reshape(3, own)
    pos = jnp.concatenate([pos, swap(pos)], axis=1)
    pair = jnp.arange(HEAD // 2)
    band = (pair >= 10).astype(jnp.int32) + (pair >= 21).astype(jnp.int32)
    begin = jnp.where(band == 0, 0, jnp.where(band == 1, 10, 21))
    count = jnp.where(band == 0, 10, 11)
    freq = jnp.power(F32(10000.0), -(pair - begin).astype(F32) / count.astype(F32))
    band = band[:, None]
    chosen = jnp.where(band == 0, pos[0:1], jnp.where(band == 1, pos[1:2], pos[2:3]))
    angles = chosen * freq[:, None]
    cosine, sine = jnp.cos(angles), jnp.sin(angles)

    x = x.reshape(own, width).astype(F32)
    n1, r1 = normalize(x)
    h1 = both((n1 * g1 + b1).astype(BF))
    qkv = contract(wq, h1, 0, 1) + bq_own
    qs, kr, vb, mixed, lse = attention(qkv, cosine, sine)
    x2 = x + own_sum(contract(mixed, wo, 0, 0)) + bo
    n2, r2 = normalize(x2)
    h2 = both((n2 * g2 + b2).astype(BF))
    u = contract(h2, w1, 1, 0) + bu_own
    cdf = 0.5 * (1.0 + lax.erf(u * F32(0.7071067811865476)))
    act = (u * cdf).astype(BF)
    slope = (cdf + u * jnp.exp(-0.5 * u * u) * F32(0.3989422804014327)).astype(BF)
    result = (x2 + own_sum(contract(act, w2, 1, 0)) + bd).astype(BF)
    output = move_blocks(result.reshape(clips, part, width), clips, groups)

    gw2 = contract(act, grad_all, 0, 0).astype(BF)
    gu = (contract(grad_all, w2, 1, 1) * slope.astype(F32)).astype(BF)
    gw1 = contract(h2, gu, 0, 0).astype(BF)
    gbu = jnp.sum(gu.astype(F32), axis=0)
    dh2 = own_sum(contract(gu, w1, 1, 1))
    gg2, gb2 = jnp.sum(dh2 * n2, axis=0), jnp.sum(dh2, axis=0)
    dx2 = grad_f + norm_back(dh2 * g2, n2, r2)
    low = dx2.astype(BF)
    low_all = both(low)
    gwo = contract(mixed, low_all, 1, 0).astype(BF)
    da = contract(wo, low_all, 1, 1).astype(BF)
    dqkv = jnp.concatenate(attention_back(qs, kr, vb, mixed, lse, da, cosine, sine), axis=0)
    gwq = contract(h1, dqkv, 0, 1).astype(BF)
    gbq = jnp.sum(dqkv.astype(F32), axis=1)
    dh1 = own_sum(contract(dqkv, wq, 0, 1))
    gg1, gb1 = jnp.sum(dh1 * n1, axis=0), jnp.sum(dh1, axis=0)
    gx = (dx2 + norm_back(dh1 * g1, n1, r1)).astype(BF)

    mine = (jnp.arange(2) == c).astype(F32)
    gbq = gbq.reshape(bq * groups, 1, row // 2) * mine[None, :, None]
    gbu = gbu.reshape(groups, 1, deep // groups) * mine[None, :, None]
    vectors = (gg1, gb1, jnp.sum(low.astype(F32), axis=0), gg2, gb2, jnp.sum(grad_f, axis=0), gbq, gbu)
    sums = jnp.concatenate([v.reshape(groups, -1, row) for v in vectors], axis=1)
    sums = jnp.pad(sums, ((0, 0), (0, -lines % 8), (0, 0)))
    grads = [g.reshape(groups, 2, 2, 2, g.shape[0] // (8 * groups), g.shape[1]) for g in (gwq, gwo, gw1, gw2)]
    gwq, gwo, gw1, gw2, sums, gx = reduce(
        grads, blocks, sums, gx.reshape(clips, part, width), groups
    )
    gwq, gwo, gw1, gw2 = (
        g.reshape(shard.shape).astype(F32)
        for g, shard in zip((gwq, gwo, gw1, gw2), (w_qkv, w_out, w_up, w_down))
    )
    gg1, gb1, gbo, gg2, gb2, gbd = (sums[n] for n in range(6))
    gbq, gbu = sums[6 : 6 + bq].reshape(-1), sums[6 + bq : lines].reshape(-1)
    return (output, gx, gg1, gb1, gwq, gbq, gwo, gbo, gg2, gb2, gw1, gbu, gw2, gbd)


def paired_specs():
    rep = ("rp", "core")
    ins = (P(rep, "grp", None), P(None, rep, "grp"))
    one, two = P("grp"), P("grp", None)
    ins += (one, one, two, one, two, one, one, one, two, one, two, one, P(rep, "grp", None))
    outs = (P(rep, "grp", None),) * 2
    outs += (one, one, two, one, two, one, one, one, two, one, two, one)
    return ins, outs


def rotary_angles(positions):
    pair = jnp.arange(32)
    band = (pair >= 10).astype(jnp.int32) + (pair >= 21).astype(jnp.int32)
    start = jnp.where(band == 0, 0, jnp.where(band == 1, 10, 21))
    count = jnp.where(band == 0, 10, 11)
    freq = jnp.power(
        jnp.float32(10000.0), -(pair - start).astype(jnp.float32) / count.astype(jnp.float32)
    )
    pos_f = positions.astype(jnp.float32)
    chosen = jnp.where(
        band[None, :] == 0,
        pos_f[0][:, None],
        jnp.where(band[None, :] == 1, pos_f[1][:, None], pos_f[2][:, None]),
    )
    return chosen * freq[None, :]


def rotate(field, cosine, sine):
    first = field[..., :32]
    second = field[..., 32:]
    return jnp.concatenate(
        [first * cosine - second * sine, first * sine + second * cosine], axis=-1
    )


def normalize(field):
    centred = field - jnp.mean(field, axis=-1, keepdims=True)
    variance = jnp.mean(centred * centred, axis=-1, keepdims=True)
    factor = lax.rsqrt(variance + EPS)
    return (centred * factor, factor)


def norm_back(grad_norm, normed, factor):
    return factor * (
        grad_norm
        - jnp.mean(grad_norm, axis=-1, keepdims=True)
        - normed * jnp.mean(grad_norm * normed, axis=-1, keepdims=True)
    )


def outer(left, right):
    return lax.dot_general(
        left, right, (((0,), (0,)), ((), ())), preferred_element_type=jnp.float32
    )


def back(left, right):
    return lax.dot_general(
        left, right, (((1,), (1,)), ((), ())), preferred_element_type=jnp.float32
    )


def exact_gelu(value):
    return jax.nn.gelu(value, approximate=False)


def column_sum(value):
    return jnp.sum(value.astype(jnp.float32), axis=0)


def forward_pass(params, field_in, positions):
    g1, b1, wqkv, bqkv, wo, bo, g2, b2, w1, bu, w2, bd = params
    field = field_in.astype(jnp.float32)
    count, width = field.shape
    heads = width // 64
    angles = rotary_angles(positions)
    cosine = jnp.cos(angles)[:, None, :]
    sine = jnp.sin(angles)[:, None, :]
    normed1, factor1 = normalize(field)
    h1 = (normed1 * g1.astype(jnp.float32) + b1.astype(jnp.float32)).astype(jnp.bfloat16)
    qkv = jnp.dot(h1, wqkv, preferred_element_type=jnp.float32) + bqkv.astype(jnp.float32)
    query_rot = rotate(qkv[:, :width].reshape(count, heads, 64), cosine, sine).astype(jnp.bfloat16)
    keys_rot = (
        rotate(qkv[:, width : 2 * width].reshape(count, heads, 64), cosine, sine)
        .astype(jnp.bfloat16)
        .reshape(count, width)
    )
    values = qkv[:, 2 * width :].astype(jnp.bfloat16)
    keys_all, values_all = (
        lax.all_gather(keys_rot, "grp", axis=0, tiled=True),
        lax.all_gather(values, "grp", axis=0, tiled=True),
    )
    total = keys_all.shape[0]
    keys_all = keys_all.reshape(total, heads, 64)
    values_all = values_all.reshape(total, heads, 64)
    scores = (
        jnp.einsum("thd,shd->hts", query_rot, keys_all, preferred_element_type=jnp.float32) * SCALE
    )
    top = jnp.max(scores, axis=-1, keepdims=True)
    lse = top + jnp.log(jnp.sum(jnp.exp(scores - top), axis=-1, keepdims=True))
    probs = jnp.exp(scores - lse).astype(jnp.bfloat16)
    mixed = (
        jnp.einsum("hts,shd->thd", probs, values_all, preferred_element_type=jnp.float32)
        .reshape(count, width)
        .astype(jnp.bfloat16)
    )
    second = field + jnp.dot(mixed, wo, preferred_element_type=jnp.float32) + bo.astype(jnp.float32)
    normed2, factor2 = normalize(second)
    h2 = (normed2 * g2.astype(jnp.float32) + b2.astype(jnp.float32)).astype(jnp.bfloat16)
    hidden = jnp.dot(h2, w1, preferred_element_type=jnp.float32) + bu.astype(jnp.float32)
    active = exact_gelu(hidden).astype(jnp.bfloat16)
    result = (
        second + jnp.dot(active, w2, preferred_element_type=jnp.float32) + bd.astype(jnp.float32)
    )
    saved = (
        normed1,
        factor1,
        h1,
        query_rot,
        keys_rot,
        values,
        lse,
        mixed,
        normed2,
        factor2,
        h2,
        hidden,
        active,
        cosine,
        sine,
    )
    return (saved, result.astype(jnp.bfloat16))


def backward_pass(params, saved, grad_in, totals):
    g1, b1, wqkv, bqkv, wo, bo, g2, b2, w1, bu, w2, bd = params
    (
        normed1,
        factor1,
        h1,
        query_rot,
        keys_rot,
        values,
        lse,
        mixed,
        normed2,
        factor2,
        h2,
        hidden,
        active,
        cosine,
        sine,
    ) = saved
    grad_out = grad_in.astype(jnp.float32)
    count, width = grad_out.shape
    heads = width // 64
    grad_y2 = grad_out.astype(jnp.bfloat16)
    grad_w2 = outer(active, grad_y2)
    grad_bd = column_sum(grad_y2)
    grad_act = back(grad_y2, w2)
    unused, pull = jax.vjp(exact_gelu, hidden)
    grad_hidden = pull(grad_act)[0].astype(jnp.bfloat16)
    grad_w1 = outer(h2, grad_hidden)
    grad_bu = column_sum(grad_hidden)
    grad_h2 = back(grad_hidden, w1)
    grad_g2 = jnp.sum(grad_h2 * normed2, axis=0)
    grad_b2 = jnp.sum(grad_h2, axis=0)
    grad_second = grad_out + norm_back(grad_h2 * g2.astype(jnp.float32), normed2, factor2)
    grad_y1 = grad_second.astype(jnp.bfloat16)
    grad_wo = outer(mixed, grad_y1)
    grad_bo = column_sum(grad_y1)
    grad_mixed = back(grad_y1, wo).astype(jnp.bfloat16).reshape(count, heads, 64)
    keys_all, values_all = (
        lax.all_gather(keys_rot, "grp", axis=0, tiled=True),
        lax.all_gather(values, "grp", axis=0, tiled=True),
    )
    total = keys_all.shape[0]
    keys_all = keys_all.reshape(total, heads, 64)
    values_all = values_all.reshape(total, heads, 64)
    scores = (
        jnp.einsum("thd,shd->hts", query_rot, keys_all, preferred_element_type=jnp.float32) * SCALE
    )
    probs = jnp.exp(scores - lse)
    grad_probs = jnp.einsum(
        "thd,shd->hts", grad_mixed, values_all, preferred_element_type=jnp.float32
    )
    delta = jnp.sum(probs * grad_probs, axis=-1, keepdims=True)
    grad_scores = (probs * (grad_probs - delta)).astype(jnp.bfloat16)
    grad_query = (
        jnp.einsum("hts,shd->thd", grad_scores, keys_all, preferred_element_type=jnp.float32)
        * SCALE
    )
    probs_low = probs.astype(jnp.bfloat16)
    grad_values = jnp.einsum(
        "hts,thd->shd", probs_low, grad_mixed, preferred_element_type=jnp.float32
    )
    grad_keys = (
        jnp.einsum("hts,thd->shd", grad_scores, query_rot, preferred_element_type=jnp.float32)
        * SCALE
    )
    keys_own, values_own = (
        lax.psum_scatter(
            grad_keys.reshape(total, width).astype(jnp.bfloat16),
            "grp",
            scatter_dimension=0,
            tiled=True,
        ).astype(jnp.float32),
        lax.psum_scatter(
            grad_values.reshape(total, width).astype(jnp.bfloat16),
            "grp",
            scatter_dimension=0,
            tiled=True,
        ).astype(jnp.float32),
    )
    query_back = rotate(grad_query, cosine, -sine).reshape(count, width)
    keys_back = rotate(keys_own.reshape(count, heads, 64), cosine, -sine).reshape(count, width)
    grad_qkv = jnp.concatenate([query_back, keys_back, values_own], axis=1).astype(jnp.bfloat16)
    grad_wqkv = outer(h1, grad_qkv)
    grad_bqkv = column_sum(grad_qkv)
    grad_h1 = back(grad_qkv, wqkv)
    grad_g1 = jnp.sum(grad_h1 * normed1, axis=0)
    grad_b1 = jnp.sum(grad_h1, axis=0)
    grad_field = grad_second + norm_back(grad_h1 * g1.astype(jnp.float32), normed1, factor1)
    terms = (
        grad_g1,
        grad_b1,
        grad_wqkv,
        grad_bqkv,
        grad_wo,
        grad_bo,
        grad_g2,
        grad_b2,
        grad_w1,
        grad_bu,
        grad_w2,
        grad_bd,
    )
    totals = tuple((a + b for a, b in zip(totals, terms)))
    return (grad_field.astype(jnp.bfloat16), totals)


def local(
    tokens,
    positions,
    ln1_gain,
    ln1_bias,
    w_qkv,
    b_qkv,
    w_out,
    b_out,
    ln2_gain,
    ln2_bias,
    w_up,
    b_up,
    w_down,
    b_down,
    cotangent,
):
    shards = (
        ln1_gain,
        ln1_bias,
        w_qkv,
        b_qkv,
        w_out,
        b_out,
        ln2_gain,
        ln2_bias,
        w_up,
        b_up,
        w_down,
        b_down,
    )
    groups = lax.axis_size("grp")
    totals = tuple((jnp.zeros((s.shape[0] * groups,) + s.shape[1:], jnp.float32) for s in shards))
    outputs = []
    gradients = []
    for index in range(tokens.shape[0]):
        forward_params = (
            lax.all_gather(ln1_gain, "grp", axis=0, tiled=True),
            lax.all_gather(ln1_bias, "grp", axis=0, tiled=True),
            lax.all_gather(w_qkv, "grp", axis=0, tiled=True),
            lax.all_gather(b_qkv, "grp", axis=0, tiled=True),
            lax.all_gather(w_out, "grp", axis=0, tiled=True),
            lax.all_gather(b_out, "grp", axis=0, tiled=True),
            lax.all_gather(ln2_gain, "grp", axis=0, tiled=True),
            lax.all_gather(ln2_bias, "grp", axis=0, tiled=True),
            lax.all_gather(w_up, "grp", axis=0, tiled=True),
            lax.all_gather(b_up, "grp", axis=0, tiled=True),
            lax.all_gather(w_down, "grp", axis=0, tiled=True),
            lax.all_gather(b_down, "grp", axis=0, tiled=True),
        )
        saved, result = forward_pass(forward_params, tokens[index], positions[:, index, :])
        outputs.append(result)
        backward_params = (
            lax.all_gather(ln1_gain, "grp", axis=0, tiled=True),
            lax.all_gather(ln1_bias, "grp", axis=0, tiled=True),
            lax.all_gather(w_qkv, "grp", axis=0, tiled=True),
            lax.all_gather(b_qkv, "grp", axis=0, tiled=True),
            lax.all_gather(w_out, "grp", axis=0, tiled=True),
            lax.all_gather(b_out, "grp", axis=0, tiled=True),
            lax.all_gather(ln2_gain, "grp", axis=0, tiled=True),
            lax.all_gather(ln2_bias, "grp", axis=0, tiled=True),
            lax.all_gather(w_up, "grp", axis=0, tiled=True),
            lax.all_gather(b_up, "grp", axis=0, tiled=True),
            lax.all_gather(w_down, "grp", axis=0, tiled=True),
            lax.all_gather(b_down, "grp", axis=0, tiled=True),
        )
        grad_field, totals = backward_pass(backward_params, saved, cotangent[index], totals)
        gradients.append(grad_field)
    owned = (
        lax.psum_scatter(
            totals[0].astype(jnp.bfloat16), "grp", scatter_dimension=0, tiled=True
        ).astype(jnp.float32),
        lax.psum_scatter(
            totals[1].astype(jnp.bfloat16), "grp", scatter_dimension=0, tiled=True
        ).astype(jnp.float32),
        lax.psum_scatter(
            totals[2].astype(jnp.bfloat16), "grp", scatter_dimension=0, tiled=True
        ).astype(jnp.float32),
        lax.psum_scatter(
            totals[3].astype(jnp.bfloat16), "grp", scatter_dimension=0, tiled=True
        ).astype(jnp.float32),
        lax.psum_scatter(
            totals[4].astype(jnp.bfloat16), "grp", scatter_dimension=0, tiled=True
        ).astype(jnp.float32),
        lax.psum_scatter(
            totals[5].astype(jnp.bfloat16), "grp", scatter_dimension=0, tiled=True
        ).astype(jnp.float32),
        lax.psum_scatter(
            totals[6].astype(jnp.bfloat16), "grp", scatter_dimension=0, tiled=True
        ).astype(jnp.float32),
        lax.psum_scatter(
            totals[7].astype(jnp.bfloat16), "grp", scatter_dimension=0, tiled=True
        ).astype(jnp.float32),
        lax.psum_scatter(
            totals[8].astype(jnp.bfloat16), "grp", scatter_dimension=0, tiled=True
        ).astype(jnp.float32),
        lax.psum_scatter(
            totals[9].astype(jnp.bfloat16), "grp", scatter_dimension=0, tiled=True
        ).astype(jnp.float32),
        lax.psum_scatter(
            totals[10].astype(jnp.bfloat16), "grp", scatter_dimension=0, tiled=True
        ).astype(jnp.float32),
        lax.psum_scatter(
            totals[11].astype(jnp.bfloat16), "grp", scatter_dimension=0, tiled=True
        ).astype(jnp.float32),
    )
    summed = (
        lax.psum(owned[0].astype(jnp.bfloat16), "rep").astype(jnp.float32),
        lax.psum(owned[1].astype(jnp.bfloat16), "rep").astype(jnp.float32),
        lax.psum(owned[2].astype(jnp.bfloat16), "rep").astype(jnp.float32),
        lax.psum(owned[3].astype(jnp.bfloat16), "rep").astype(jnp.float32),
        lax.psum(owned[4].astype(jnp.bfloat16), "rep").astype(jnp.float32),
        lax.psum(owned[5].astype(jnp.bfloat16), "rep").astype(jnp.float32),
        lax.psum(owned[6].astype(jnp.bfloat16), "rep").astype(jnp.float32),
        lax.psum(owned[7].astype(jnp.bfloat16), "rep").astype(jnp.float32),
        lax.psum(owned[8].astype(jnp.bfloat16), "rep").astype(jnp.float32),
        lax.psum(owned[9].astype(jnp.bfloat16), "rep").astype(jnp.float32),
        lax.psum(owned[10].astype(jnp.bfloat16), "rep").astype(jnp.float32),
        lax.psum(owned[11].astype(jnp.bfloat16), "rep").astype(jnp.float32),
    )
    output = jnp.stack(outputs, axis=0)
    grad_tokens = jnp.stack(gradients, axis=0)
    return (
        output,
        grad_tokens,
        summed[0],
        summed[1],
        summed[2],
        summed[3],
        summed[4],
        summed[5],
        summed[6],
        summed[7],
        summed[8],
        summed[9],
        summed[10],
        summed[11],
    )


def spread(mesh):
    placed = (
        P("rep", "grp", None),
        P(None, "rep", "grp"),
        P("grp"),
        P("grp"),
        P("grp", None),
        P("grp"),
        P("grp", None),
        P("grp"),
        P("grp"),
        P("grp"),
        P("grp", None),
        P("grp"),
        P("grp", None),
        P("grp"),
        P("rep", "grp", None),
    )
    return jax.shard_map(
        local,
        mesh=mesh,
        in_specs=placed,
        out_specs=(
            P("rep", "grp", None),
            P("rep", "grp", None),
            P("grp"),
            P("grp"),
            P("grp", None),
            P("grp"),
            P("grp", None),
            P("grp"),
            P("grp"),
            P("grp"),
            P("grp", None),
            P("grp"),
            P("grp", None),
            P("grp"),
        ),
        check_vma=False,
    )


def solution(mesh):
    reps, groups = mesh.devices.shape
    flat = mesh.devices.reshape(-1)

    def run(*args):
        clips = args[0].shape[0] // reps
        if reps == 8 and groups == 2 * clips:
            split = Mesh(flat.reshape(reps // 2, 2, groups), ("rp", "core", "grp"))
            ins, outs = paired_specs()
            return jax.shard_map(
                paired, mesh=split, in_specs=ins, out_specs=outs, check_vma=False
            )(*args)
        return spread(mesh)(*args)

    return run
```

```python
import functools

import jax
import jax.numpy as jnp
from jax import lax
from jax.experimental import pallas as pl
from jax.experimental.pallas import tpu as pltpu
from jax.sharding import Mesh
from jax.sharding import PartitionSpec as P

SCALE = 0.125
EPS = 1e-06
HEAD = 64
BF = jnp.bfloat16
F32 = jnp.float32
MESH = pl.DeviceIdType.MESH
ANY = pl.BlockSpec(memory_space=pl.ANY)
VM = pl.BlockSpec(memory_space=pltpu.VMEM)


def where_am_i():
    return lax.axis_index("rp"), lax.axis_index("core"), lax.axis_index("grp")


def remote(src, dst, send, recv, target):
    return pltpu.make_async_remote_copy(
        src_ref=src,
        dst_ref=dst,
        send_sem=send,
        recv_sem=recv,
        device_id=target,
        device_id_type=MESH,
    )


def enter(p, c, z, groups):
    barrier = pltpu.get_barrier_semaphore()
    for k in range(groups):
        for d in range(2):
            if k == 0 and d == 0:
                continue
            pl.semaphore_signal(
                barrier, inc=1, device_id=(p, c ^ d, lax.rem(z + k, groups)), device_id_type=MESH
            )
    for b in (1, 2):
        pl.semaphore_signal(barrier, inc=1, device_id=(p ^ b, c, z), device_id_type=MESH)
    pl.semaphore_wait(barrier, 2 * groups - 1 + 2)


def move_tokens(refs, outs, send, recv, p, c, z, clips):
    core, slot = lax.div(z, clips), lax.rem(z, clips)

    def route(i):
        return core, c * clips + i

    def here(i):
        return jnp.logical_and(core == c, c * clips + i == z)

    def start():
        for n, (src, dst) in enumerate(zip(refs, outs)):
            for i in range(clips):
                tc, tz = route(i)

                @pl.when(here(i))
                def _():
                    pltpu.make_async_copy(src.at[i], dst.at[slot], recv.at[n, slot]).start()

                @pl.when(jnp.logical_not(here(i)))
                def _():
                    remote(
                        src.at[i], dst.at[slot], send.at[n, i], recv.at[n, slot], (p, tc, tz)
                    ).start()

    def finish():
        for n, (src, dst) in enumerate(zip(refs, outs)):
            for i in range(clips):

                @pl.when(jnp.logical_not(here(i)))
                def _():
                    remote(
                        src.at[i], dst.at[slot], send.at[n, i], recv.at[n, slot], (p, c ^ 1, z)
                    ).wait_send()

            for m in range(clips):
                pltpu.make_async_copy(src.at[0], dst.at[m], recv.at[n, m]).wait()

    return start, finish


def cuts(whole, half, c, blocks):
    if blocks == 0:
        return [(whole.at[c], half)]
    size = half.shape[3] // blocks
    return [
        (
            whole.at[:, :, :, pl.ds(pl.multiple_of((2 * b + c) * size, size), size)],
            half.at[:, :, :, pl.ds(b * size, size)],
        )
        for b in range(blocks)
    ]


def gather_body(groups, clips, blocks, *refs):
    count = len(blocks)
    raw, (small, x, pos, dy) = refs[:count], refs[count : count + 4]
    outs = refs[count + 4 : 2 * count + 4]
    small_o, x_o, pos_o, dy_o = refs[2 * count + 4 : 2 * count + 8]
    halves = refs[2 * count + 8 : 3 * count + 8]
    zs, zr, xs, xr, ys, yr, fs, fr, hs, ls, ss, sr, ts, tr, us, ur = refs[3 * count + 8 :]
    p, c, z = where_am_i()
    for w in range(count):
        for src, dst in cuts(raw[w], halves[w], c, blocks[w]):
            pltpu.make_async_copy(src, dst, hs.at[w]).start()
    enter(p, c, z, groups)
    col = [(p, c, lax.rem(z + k, groups)) for k in range(groups)]
    org = [lax.rem(z + groups - k, groups) for k in range(groups)]
    xn, yn = (p ^ 1, c, z), (p ^ 2, c, z)
    start, finish = move_tokens((x, pos), (x_o, pos_o), ts, tr, p, c, z, clips)
    start()
    smalls = [
        remote(small, small_o.at[z], ss.at[k], sr.at[k], col[k]) for k in range(1, groups)
    ]
    for s in smalls:
        s.start()
    keep = [pltpu.make_async_copy(small, small_o.at[z], ls.at[count])]
    keep[0].start()
    start_dy, finish_dy = move_tokens((dy,), (dy_o,), us, ur, p, c, z, clips)
    units = [(w, d, side) for w in range(count) for d in range(1, groups) for side in range(2)]

    def origin(d, side):
        return z - d if side == 0 else z + d

    def arrives(d, side):
        return z >= d if side == 0 else z + d < groups

    def leaves(d, side):
        if side == 0:
            return jnp.logical_and(z + 1 < groups, z + 1 >= d)
        return jnp.logical_and(z >= 1, z - 1 + d < groups)

    def hop(w, d, side, src):
        o = origin(d - 1, side)
        target = (p, c, lax.rem(z + 1 if side == 0 else z + groups - 1, groups))
        return remote(src, outs[w].at[o, p], zs.at[w, side, d], zr.at[w, side, d], target)

    def own(w):
        pltpu.make_async_copy(halves[w], halves[w], hs.at[w]).wait()
        keep.append(pltpu.make_async_copy(halves[w], outs[w].at[z], ls.at[w]))
        keep[-1].start()
        for side in range(2):

            @pl.when(leaves(1, side))
            def _():
                hop(w, 1, side, halves[w].at[p]).start()

    def links(u):
        w, d, side = u
        o = outs[w].at[lax.rem(origin(d, side) + groups, groups)]
        e, f = xs.at[w, side, d], xr.at[w, side, d]
        g, h = ys.at[w, side, d], yr.at[w, side, d]
        a, b = fs.at[w, side, d, 0], fr.at[w, side, d, 0]
        m, n = fs.at[w, side, d, 1], fr.at[w, side, d, 1]
        across = lambda q: remote(o.at[q], o.at[q], e, f, xn)
        along = lambda q: remote(o.at[q], o.at[q], g, h, yn)
        first = lambda q: remote(o.at[q, 0], o.at[q, 0], a, b, yn)
        second = lambda q: remote(o.at[q, 1], o.at[q, 1], m, n, xn)
        return o, across, along, first, second

    def plane(u):
        w, d, side = u
        o, across, along, first, second = links(u)

        @pl.when(arrives(d, side))
        def _():
            remote(o.at[p], o.at[p], zs.at[w, side, d], zr.at[w, side, d], xn).wait_recv()
            if d + 1 < groups:

                @pl.when(leaves(d + 1, side))
                def _():
                    hop(w, d + 1, side, o.at[p]).start()

            across(p).start()
            along(p).start()

    def forward(u):
        w, d, side = u
        o, across, along, first, second = links(u)

        @pl.when(arrives(d, side))
        def _():
            across(p ^ 1).wait_recv()
            first(p ^ 1).start()
            along(p ^ 2).wait_recv()
            second(p ^ 2).start()

    def settle(u):
        w, d, side = u
        o, across, along, first, second = links(u)

        @pl.when(arrives(d, side))
        def _():
            first(p ^ 3).wait_recv()
            second(p ^ 3).wait_recv()
            across(p).wait_send()
            along(p).wait_send()
            first(p).wait_send()
            second(p).wait_send()

        @pl.when(leaves(d, side))
        def _():
            hop(w, d, side, halves[w].at[p]).wait_send()

    own(0)
    own(1)
    lag = 3
    for n in range(len(units) + lag):
        if n < len(units):
            plane(units[n])
            w, d, side = units[n]
            if (d, side) == (1, 1) and w + 2 < count:
                own(w + 2)
            if n + 1 == len(units):
                start_dy()
        if n >= lag:
            forward(units[n - lag])
    for u in units:
        settle(u)
    for k in range(1, groups):
        remote(small, small_o.at[org[k]], ss.at[k], sr.at[k], col[k]).wait_recv()
    for s in smalls:
        s.wait_send()
    for k in keep:
        k.wait()
    finish()
    finish_dy()


def half_shape(raw, blocks):
    return raw.shape[1:] if blocks == 0 else raw.shape[:3] + (raw.shape[3] // 2,)


def gather(raw, blocks, small, x, pos, dy, groups):
    count, clips = len(raw), x.shape[0]
    dma = pltpu.SemaphoreType.DMA
    halves = [half_shape(r, b) for r, b in zip(raw, blocks)]
    shapes = [jax.ShapeDtypeStruct((groups,) + h, BF) for h in halves]
    shapes += [jax.ShapeDtypeStruct((groups,) + small.shape, small.dtype)]
    shapes += [jax.ShapeDtypeStruct(v.shape, v.dtype) for v in (x, pos, dy)]
    return pl.pallas_call(
        functools.partial(gather_body, groups, clips, blocks),
        out_shape=shapes,
        in_specs=[ANY] * count + [VM, ANY, ANY, ANY],
        out_specs=[ANY] * len(shapes),
        scratch_shapes=[pltpu.VMEM(h, BF) for h in halves]
        + [dma((count, 2, groups))] * 6
        + [dma((count, 2, groups, 2))] * 2
        + [dma((count,)), dma((count + 1,)), dma((groups,)), dma((groups,))]
        + [dma((2, clips))] * 2
        + [dma((1, clips))] * 2,
        compiler_params=pltpu.CompilerParams(collective_id=0, has_side_effects=True),
        name="gather",
    )(*raw, small, x, pos, dy)


def reduce_body(groups, clips, blocks, *refs):
    count = len(blocks)
    grads, (small, gx) = refs[:count], refs[count : count + 2]
    outs = refs[count + 2 : 2 * count + 2]
    small_o, gx_o = refs[2 * count + 2 : 2 * count + 4]
    scratch = refs[2 * count + 4 :]
    own_a, own_b, one_a, one_b, two_a, two_b, mine, three, full = (
        scratch[i * count : (i + 1) * count] for i in range(9)
    )
    small_s, small_r, small_z = scratch[9 * count : 9 * count + 3]
    (os, s1, r1, s2, r2, s3, r3, s4, r4, s5, r5, cs, cr, ls, ss, sr, ts, tr) = scratch[9 * count + 3 :]
    p, c, z = where_am_i()
    hi, lo = lax.div(p, 2), lax.rem(p, 2)
    enter(p, c, z, groups)
    col = [(p, c, lax.rem(z + k, groups)) for k in range(groups)]
    xn, yn, cn = (p ^ 1, c, z), (p ^ 2, c, z), (p, c ^ 1, z)
    start, finish = move_tokens((gx,), (gx_o,), ts, tr, p, c, z, clips)
    start()
    small_s[...] = small[...]
    for n, target in enumerate((cn, xn, yn)):
        copy = remote(small_s, small_r.at[n], ss.at[n], sr.at[n], target)
        copy.start()
        copy.wait()
        small_s[...] += small_r[n]
    tails = [
        remote(small_s.at[col[k][2]], small_z.at[k], ss.at[2 + k], sr.at[2 + k], col[k])
        for k in range(1, groups)
    ]
    for t in tails:
        t.start()
    order = sorted(range(count), key=lambda w: -mine[w].shape[3] * mine[w].shape[2])
    units = [(w, j) for w in order for j in [*range(1, groups), 0]]
    load, c1, c2, c4, c5 = {}, {}, {}, {}, {}

    def stage_zero(u):
        w, j = u
        g = grads[w].at[lax.rem(z + j, groups)]
        c1[u, 0] = remote(g.at[:, 1 - lo, 0], one_a[w].at[j], s1.at[w, j, 0], r1.at[w, j, 0], xn)
        c1[u, 1] = remote(g.at[1 - hi, :, 1], one_b[w].at[j], s1.at[w, j, 1], r1.at[w, j, 1], yn)
        load[u, 0] = pltpu.make_async_copy(g.at[:, lo, 0], own_a[w].at[j], os.at[w, j, 0])
        load[u, 1] = pltpu.make_async_copy(g.at[hi, :, 1], own_b[w].at[j], os.at[w, j, 1])
        for copy in (c1[u, 0], c1[u, 1], load[u, 0], load[u, 1]):
            copy.start()

    def stage_one(u):
        w, j = u
        for n, (own, one, two, side, target) in enumerate(
            ((own_a, one_a, two_a, hi, yn), (own_b, one_b, two_b, lo, xn))
        ):
            load[u, n].wait()
            c1[u, n].wait_recv()
            o = own[w].at[j]
            o[...] = (o[...].astype(F32) + one[w][j].astype(F32)).astype(BF)
            c2[u, n] = remote(o.at[1 - side], two[w].at[j], s2.at[w, j, n], r2.at[w, j, n], target)
            c2[u, n].start()

    def third(w, j):
        return remote(mine[w].at[j], three[w].at[j], s3.at[w, j], r3.at[w, j], col[j])

    def stage_two(u):
        w, j = u
        for n, (own, two, side) in enumerate(((own_a, two_a, hi), (own_b, two_b, lo))):
            c2[u, n].wait_recv()
            mine[w][j, n] = (own[w][j, side].astype(F32) + two[w][j].astype(F32)).astype(BF)
        if j:
            third(w, j).start()

    def stage_three(w):
        total = mine[w][0].astype(F32)
        for j in range(1, groups):
            third(w, j).wait_recv()
            total = total + three[w][j].astype(F32)
        full[w][p] = total.astype(BF)
        for n, target in enumerate((xn, yn)):
            f = full[w].at[p]
            c4[w, n] = remote(f, f, s4.at[w, n], r4.at[w, n], target)
            c4[w, n].start()

    def stage_four(w):
        for n, (q, target) in enumerate(((p ^ 1, yn), (p ^ 2, xn))):
            f = full[w].at[q]
            remote(f, f, s4.at[w, n], r4.at[w, n], target).wait_recv()
            f = full[w].at[q, n]
            c5[w, n] = remote(f, f, s5.at[w, n], r5.at[w, n], target)
            c5[w, n].start()

    def stage_five(w):
        for n in range(2):
            f = full[w].at[p ^ 3, n]
            remote(f, f, s5.at[w, n], r5.at[w, n], xn).wait_recv()
        for dst, src in cuts(outs[w], full[w], c, blocks[w]):
            pltpu.make_async_copy(src, dst, ls.at[w]).start()
            remote(src, dst, cs.at[w], cr.at[w], cn).start()

    ahead, lag = 2, 2
    todo = {}
    for n, u in enumerate(units):
        todo.setdefault(max(n - ahead, -1), []).append((stage_zero, u))
        todo.setdefault(n, []).append((stage_one, u))
        todo.setdefault(n + lag, []).append((stage_two, u))
    for i, w in enumerate(order):
        last = (i + 1) * groups - 1 + lag
        for at, stage in ((2, stage_three), (3, stage_four), (4, stage_five)):
            todo.setdefault(last + at, []).append((stage, w))
    for n in sorted(todo):
        for stage, what in todo[n]:
            stage(what)
    for k in range(1, groups):
        tails[k - 1].wait()
    small_o[...] = small_s[z]
    for k in range(1, groups):
        small_o[...] += small_z[k]
    for u in units:
        w, j = u
        for n in range(2):
            c1[u, n].wait_send()
            c2[u, n].wait_send()
        if j:
            third(w, j).wait_send()
    for w in range(count):
        for n in range(2):
            c4[w, n].wait_send()
            c5[w, n].wait_send()
        pltpu.make_async_copy(full[w], full[w], ls.at[w]).wait()
        remote(full[w], full[w], cs.at[w], cr.at[w], cn).wait()
    finish()


def reduce(grads, blocks, small, gx, groups):
    count, clips = len(grads), gx.shape[0]
    dma = pltpu.SemaphoreType.DMA
    tiles = [g.shape[4:] for g in grads]
    shapes = [
        jax.ShapeDtypeStruct((4, 2, t[0], 2 * t[1]) if b else (2, 4, 2) + t, BF)
        for t, b in zip(tiles, blocks)
    ]
    shapes += [
        jax.ShapeDtypeStruct(small.shape[1:], small.dtype),
        jax.ShapeDtypeStruct(gx.shape, gx.dtype),
    ]
    scratch = []
    for lead in (
        (groups, 2),
        (groups, 2),
        (groups, 2),
        (groups, 2),
        (groups,),
        (groups,),
        (groups, 2),
        (groups, 2),
        (4, 2),
    ):
        scratch += [pltpu.VMEM(lead + t, BF) for t in tiles]
    scratch += [
        pltpu.VMEM(small.shape, F32),
        pltpu.VMEM((3,) + small.shape, F32),
        pltpu.VMEM(small.shape, F32),
    ]
    pair = dma((count, groups, 2))
    scratch += [pair] * 5 + [dma((count, groups))] * 2 + [dma((count, 2))] * 4
    scratch += [dma((count,))] * 3 + [dma((2 + groups,))] * 2 + [dma((1, clips))] * 2
    return pl.pallas_call(
        functools.partial(reduce_body, groups, clips, blocks),
        out_shape=shapes,
        in_specs=[ANY] * count + [VM, ANY],
        out_specs=[ANY] * count + [VM, ANY],
        scratch_shapes=scratch,
        compiler_params=pltpu.CompilerParams(
            collective_id=1, has_side_effects=True, vmem_limit_bytes=60 * 1024 * 1024
        ),
        name="reduce",
    )(*grads, small, gx)


def turn(u, cosine, sine):
    half = HEAD // 2
    first, second = u[:half], u[half:]
    return jnp.concatenate(
        [first * cosine - second * sine, first * sine + second * cosine], axis=0
    )


def dot(a, b):
    return jnp.dot(a, b, preferred_element_type=F32)


def attention_body(step, q_ref, k_ref, v_ref, cos_ref, sin_ref, qs_ref, kr_ref, vb_ref, o_ref, l_ref):
    cosine, sine = cos_ref[...], sin_ref[...]
    length = cosine.shape[1]
    kr = turn(k_ref[...], cosine, sine).astype(BF)
    vb = v_ref[...].astype(BF)
    qs = (turn(q_ref[...], cosine, sine).astype(BF).astype(F32) * SCALE).astype(BF)
    kr_ref[...] = kr
    vb_ref[...] = vb
    qs_ref[...] = qs
    keys = kr.T
    for i in range(0, length, step):
        scores = dot(keys, qs[:, i : i + step])
        top = jnp.max(scores, axis=0, keepdims=True)
        e = jnp.exp(scores - top)
        total = jnp.sum(e, axis=0, keepdims=True)
        mixed = dot(vb, e.astype(BF))
        o_ref[:, i : i + step] = (mixed / total).astype(BF)
        l_ref[0, :, i : i + step] = top + jnp.log(total)


def attention(qkv, cosine, sine, step=256):
    rows, length = qkv.shape
    width = rows // 3
    heads = width // HEAD
    block = [pl.BlockSpec((HEAD, length), lambda h, n=n: (n * heads + h, 0)) for n in range(3)]
    table = pl.BlockSpec((HEAD // 2, length), lambda h: (0, 0))
    out = pl.BlockSpec((HEAD, length), lambda h: (h, 0))
    shape = jax.ShapeDtypeStruct((width, length), BF)
    return pl.pallas_call(
        functools.partial(attention_body, step),
        out_shape=[shape] * 4 + [jax.ShapeDtypeStruct((heads, 1, length), F32)],
        grid=(heads,),
        in_specs=block + [table, table],
        out_specs=[out] * 4 + [pl.BlockSpec((1, 1, length), lambda h: (h, 0, 0))],
        cost_estimate=pl.CostEstimate(
            flops=4 * width * length * length,
            transcendentals=heads * length * length,
            bytes_accessed=width * length * 24,
        ),
        name="attention",
    )(qkv, qkv, qkv, cosine, sine)


def attention_back_body(
    step, q_ref, k_ref, v_ref, o_ref, l_ref, g_ref, cos_ref, sin_ref, dq_ref, dk_ref, dv_ref, ak, av
):
    cosine, sine = cos_ref[...], sin_ref[...]
    length = cosine.shape[1]
    kt, keys, values = k_ref[...], k_ref[...].T, v_ref[...].T
    queries, grads = q_ref[...].T, g_ref[...].T
    for i in range(0, length, step):
        s = slice(i, i + step)
        g = g_ref[:, s]
        scores = dot(keys, q_ref[:, s])
        p = jnp.exp(scores - l_ref[0, :, s])
        dp = dot(values, g)
        delta = jnp.sum(o_ref[:, s].astype(F32) * g.astype(F32), axis=0, keepdims=True)
        ds = (p * (dp - delta)).astype(BF)
        dq = dot(kt, ds) * SCALE
        dq_ref[:, s] = turn(dq, cosine[:, s], -sine[:, s]).astype(BF)
        dv = dot(p.astype(BF), grads[s])
        dk = dot(ds, queries[s])
        if i == 0:
            ak[...] = dk
            av[...] = dv
        else:
            ak[...] += dk
            av[...] += dv
    dk_ref[...] = turn(ak[...].T, cosine, -sine).astype(BF)
    dv_ref[...] = av[...].T.astype(BF)


def attention_back(qs, kr, vb, out, lse, grad, cosine, sine, step=256):
    width, length = qs.shape
    heads = width // HEAD
    row = pl.BlockSpec((HEAD, length), lambda h: (h, 0))
    table = pl.BlockSpec((HEAD // 2, length), lambda h: (0, 0))
    line = pl.BlockSpec((1, 1, length), lambda h: (h, 0, 0))
    shape = jax.ShapeDtypeStruct((width, length), BF)
    return pl.pallas_call(
        functools.partial(attention_back_body, step),
        out_shape=[shape] * 3,
        grid=(heads,),
        in_specs=[row] * 4 + [line, row, table, table],
        out_specs=[row] * 3,
        scratch_shapes=[pltpu.VMEM((length, HEAD), F32)] * 2,
        cost_estimate=pl.CostEstimate(
            flops=10 * width * length * length,
            transcendentals=heads * length * length,
            bytes_accessed=width * length * 18,
        ),
        name="attention_back",
    )(qs, kr, vb, out, lse, grad, cosine, sine)


def swap(value):
    return lax.ppermute(value, "core", [(0, 1), (1, 0)])


def both(value):
    return jnp.concatenate([value, swap(value)], axis=0)


def contract(left, right, a, b):
    return lax.dot_general(left, right, (((a,), (b,)), ((), ())), preferred_element_type=F32)


def own_sum(partial):
    half = partial.shape[0] // 2
    return partial[:half] + swap(partial[half:].astype(BF)).astype(F32)


def move_blocks(x, clips, groups):
    c, z = lax.axis_index("core"), lax.axis_index("grp")
    got = []
    for t in range(clips):
        pairs = []
        for cc in range(2):
            for zz in range(groups):
                i = (t + zz) % clips
                pairs.append((cc * groups + zz, (zz // clips) * groups + cc * clips + i))
        block = lax.dynamic_index_in_dim(x, lax.rem(t + z, clips), 0, keepdims=False)
        got.append(lax.ppermute(block, ("core", "grp"), pairs))
    stacked = jnp.stack(got)
    return jnp.stack(
        [
            lax.dynamic_index_in_dim(stacked, lax.rem(z - m + clips, clips), 0, keepdims=False)
            for m in range(clips)
        ]
    )


def paired(
    tokens,
    positions,
    ln1_gain,
    ln1_bias,
    w_qkv,
    b_qkv,
    w_out,
    b_out,
    ln2_gain,
    ln2_bias,
    w_up,
    b_up,
    w_down,
    b_down,
    cotangent,
):
    groups = lax.axis_size("grp")
    clips, part, width = tokens.shape
    hidden = w_down.shape[0] * groups
    own = clips * part
    length = 2 * own
    c, z = lax.axis_index("core"), lax.axis_index("grp")
    wide = width // 2
    deep = hidden // 2
    row = width // groups

    def pick(value, axis):
        return lax.dynamic_index_in_dim(value, c, axis, keepdims=False)

    blocks = (3 * groups, 0, groups, 0)
    raw = [
        w.reshape(((4, 2) if b else (2, 4, 2)) + (w.shape[0] // (8 if b else 16), w.shape[1]))
        for w, b in zip((w_qkv, w_out, w_up, w_down), blocks)
    ]
    bq, bu = b_qkv.shape[0] // row, b_up.shape[0] // row
    vectors = [ln1_gain, ln1_bias, b_out, ln2_gain, ln2_bias, b_down]
    vectors += [b_qkv[n * row : (n + 1) * row] for n in range(bq)]
    vectors += [b_up[n * row : (n + 1) * row] for n in range(bu)]
    lines = len(vectors)
    place = lax.broadcasted_iota(jnp.int32, (lines + -lines % 8, row), 0)
    small = jnp.zeros(place.shape, F32)
    for n, v in enumerate(vectors):
        small = jnp.where(place == n, v.astype(F32)[None, :], small)
    pos = jnp.pad(jnp.moveaxis(positions, 0, 1).astype(F32), ((0, 0), (0, 5), (0, 0)))
    wq, wo, w1, w2, small, x, pos, dy = gather(raw, blocks, small, tokens, pos, cotangent, groups)
    wq = wq.reshape(width, 3 * wide)
    wo = wo.reshape(wide, width)
    w1 = w1.reshape(width, deep)
    w2 = w2.reshape(deep, width)
    g1, b1, bo, g2, b2, bd = (small[:, n].reshape(1, width) for n in range(6))
    bq_own = pick(small[:, 6 : 6 + bq].reshape(3, groups, 2, row // 2), 2).reshape(3 * wide, 1)
    bu_own = pick(small[:, 6 + bq : lines].reshape(groups, 2, deep // groups), 1).reshape(1, deep)

    grad_out = dy.reshape(own, width)
    grad_all = both(grad_out)
    grad_f = grad_out.astype(F32)

    pos = jnp.moveaxis(pos[:, :3], 1, 0).reshape(3, own)
    pos = jnp.concatenate([pos, swap(pos)], axis=1)
    pair = jnp.arange(HEAD // 2)
    band = (pair >= 10).astype(jnp.int32) + (pair >= 21).astype(jnp.int32)
    begin = jnp.where(band == 0, 0, jnp.where(band == 1, 10, 21))
    count = jnp.where(band == 0, 10, 11)
    freq = jnp.power(F32(10000.0), -(pair - begin).astype(F32) / count.astype(F32))
    band = band[:, None]
    chosen = jnp.where(band == 0, pos[0:1], jnp.where(band == 1, pos[1:2], pos[2:3]))
    angles = chosen * freq[:, None]
    cosine, sine = jnp.cos(angles), jnp.sin(angles)

    x = x.reshape(own, width).astype(F32)
    n1, r1 = normalize(x)
    h1 = both((n1 * g1 + b1).astype(BF))
    qkv = contract(wq, h1, 0, 1) + bq_own
    qs, kr, vb, mixed, lse = attention(qkv, cosine, sine)
    x2 = x + own_sum(contract(mixed, wo, 0, 0)) + bo
    n2, r2 = normalize(x2)
    h2 = both((n2 * g2 + b2).astype(BF))
    u = contract(h2, w1, 1, 0) + bu_own
    cdf = 0.5 * (1.0 + lax.erf(u * F32(0.7071067811865476)))
    act = (u * cdf).astype(BF)
    slope = (cdf + u * jnp.exp(-0.5 * u * u) * F32(0.3989422804014327)).astype(BF)
    result = (x2 + own_sum(contract(act, w2, 1, 0)) + bd).astype(BF)
    output = move_blocks(result.reshape(clips, part, width), clips, groups)

    gw2 = contract(act, grad_all, 0, 0).astype(BF)
    gu = (contract(grad_all, w2, 1, 1) * slope.astype(F32)).astype(BF)
    gw1 = contract(h2, gu, 0, 0).astype(BF)
    gbu = jnp.sum(gu.astype(F32), axis=0)
    dh2 = own_sum(contract(gu, w1, 1, 1))
    gg2, gb2 = jnp.sum(dh2 * n2, axis=0), jnp.sum(dh2, axis=0)
    dx2 = grad_f + norm_back(dh2 * g2, n2, r2)
    low = dx2.astype(BF)
    low_all = both(low)
    gwo = contract(mixed, low_all, 1, 0).astype(BF)
    da = contract(wo, low_all, 1, 1).astype(BF)
    dqkv = jnp.concatenate(attention_back(qs, kr, vb, mixed, lse, da, cosine, sine), axis=0)
    gwq = contract(h1, dqkv, 0, 1).astype(BF)
    gbq = jnp.sum(dqkv.astype(F32), axis=1)
    dh1 = own_sum(contract(dqkv, wq, 0, 1))
    gg1, gb1 = jnp.sum(dh1 * n1, axis=0), jnp.sum(dh1, axis=0)
    gx = (dx2 + norm_back(dh1 * g1, n1, r1)).astype(BF)

    mine = (jnp.arange(2) == c).astype(F32)
    gbq = gbq.reshape(bq * groups, 1, row // 2) * mine[None, :, None]
    gbu = gbu.reshape(groups, 1, deep // groups) * mine[None, :, None]
    vectors = (gg1, gb1, jnp.sum(low.astype(F32), axis=0), gg2, gb2, jnp.sum(grad_f, axis=0), gbq, gbu)
    sums = jnp.concatenate([v.reshape(groups, -1, row) for v in vectors], axis=1)
    sums = jnp.pad(sums, ((0, 0), (0, -lines % 8), (0, 0)))
    grads = [g.reshape(groups, 2, 2, 2, g.shape[0] // (8 * groups), g.shape[1]) for g in (gwq, gwo, gw1, gw2)]
    gwq, gwo, gw1, gw2, sums, gx = reduce(
        grads, blocks, sums, gx.reshape(clips, part, width), groups
    )
    gwq, gwo, gw1, gw2 = (
        g.reshape(shard.shape).astype(F32)
        for g, shard in zip((gwq, gwo, gw1, gw2), (w_qkv, w_out, w_up, w_down))
    )
    gg1, gb1, gbo, gg2, gb2, gbd = (sums[n] for n in range(6))
    gbq, gbu = sums[6 : 6 + bq].reshape(-1), sums[6 + bq : lines].reshape(-1)
    return (output, gx, gg1, gb1, gwq, gbq, gwo, gbo, gg2, gb2, gw1, gbu, gw2, gbd)


def paired_specs():
    rep = ("rp", "core")
    ins = (P(rep, "grp", None), P(None, rep, "grp"))
    one, two = P("grp"), P("grp", None)
    ins += (one, one, two, one, two, one, one, one, two, one, two, one, P(rep, "grp", None))
    outs = (P(rep, "grp", None),) * 2
    outs += (one, one, two, one, two, one, one, one, two, one, two, one)
    return ins, outs


def rotary_angles(positions):
    pair = jnp.arange(32)
    band = (pair >= 10).astype(jnp.int32) + (pair >= 21).astype(jnp.int32)
    start = jnp.where(band == 0, 0, jnp.where(band == 1, 10, 21))
    count = jnp.where(band == 0, 10, 11)
    freq = jnp.power(
        jnp.float32(10000.0), -(pair - start).astype(jnp.float32) / count.astype(jnp.float32)
    )
    pos_f = positions.astype(jnp.float32)
    chosen = jnp.where(
        band[None, :] == 0,
        pos_f[0][:, None],
        jnp.where(band[None, :] == 1, pos_f[1][:, None], pos_f[2][:, None]),
    )
    return chosen * freq[None, :]


def rotate(field, cosine, sine):
    first = field[..., :32]
    second = field[..., 32:]
    return jnp.concatenate(
        [first * cosine - second * sine, first * sine + second * cosine], axis=-1
    )


def normalize(field):
    centred = field - jnp.mean(field, axis=-1, keepdims=True)
    variance = jnp.mean(centred * centred, axis=-1, keepdims=True)
    factor = lax.rsqrt(variance + EPS)
    return (centred * factor, factor)


def norm_back(grad_norm, normed, factor):
    return factor * (
        grad_norm
        - jnp.mean(grad_norm, axis=-1, keepdims=True)
        - normed * jnp.mean(grad_norm * normed, axis=-1, keepdims=True)
    )


def outer(left, right):
    return lax.dot_general(
        left, right, (((0,), (0,)), ((), ())), preferred_element_type=jnp.float32
    )


def back(left, right):
    return lax.dot_general(
        left, right, (((1,), (1,)), ((), ())), preferred_element_type=jnp.float32
    )


def exact_gelu(value):
    return jax.nn.gelu(value, approximate=False)


def column_sum(value):
    return jnp.sum(value.astype(jnp.float32), axis=0)


def forward_pass(params, field_in, positions):
    g1, b1, wqkv, bqkv, wo, bo, g2, b2, w1, bu, w2, bd = params
    field = field_in.astype(jnp.float32)
    count, width = field.shape
    heads = width // 64
    angles = rotary_angles(positions)
    cosine = jnp.cos(angles)[:, None, :]
    sine = jnp.sin(angles)[:, None, :]
    normed1, factor1 = normalize(field)
    h1 = (normed1 * g1.astype(jnp.float32) + b1.astype(jnp.float32)).astype(jnp.bfloat16)
    qkv = jnp.dot(h1, wqkv, preferred_element_type=jnp.float32) + bqkv.astype(jnp.float32)
    query_rot = rotate(qkv[:, :width].reshape(count, heads, 64), cosine, sine).astype(jnp.bfloat16)
    keys_rot = (
        rotate(qkv[:, width : 2 * width].reshape(count, heads, 64), cosine, sine)
        .astype(jnp.bfloat16)
        .reshape(count, width)
    )
    values = qkv[:, 2 * width :].astype(jnp.bfloat16)
    keys_all, values_all = (
        lax.all_gather(keys_rot, "grp", axis=0, tiled=True),
        lax.all_gather(values, "grp", axis=0, tiled=True),
    )
    total = keys_all.shape[0]
    keys_all = keys_all.reshape(total, heads, 64)
    values_all = values_all.reshape(total, heads, 64)
    scores = (
        jnp.einsum("thd,shd->hts", query_rot, keys_all, preferred_element_type=jnp.float32) * SCALE
    )
    top = jnp.max(scores, axis=-1, keepdims=True)
    lse = top + jnp.log(jnp.sum(jnp.exp(scores - top), axis=-1, keepdims=True))
    probs = jnp.exp(scores - lse).astype(jnp.bfloat16)
    mixed = (
        jnp.einsum("hts,shd->thd", probs, values_all, preferred_element_type=jnp.float32)
        .reshape(count, width)
        .astype(jnp.bfloat16)
    )
    second = field + jnp.dot(mixed, wo, preferred_element_type=jnp.float32) + bo.astype(jnp.float32)
    normed2, factor2 = normalize(second)
    h2 = (normed2 * g2.astype(jnp.float32) + b2.astype(jnp.float32)).astype(jnp.bfloat16)
    hidden = jnp.dot(h2, w1, preferred_element_type=jnp.float32) + bu.astype(jnp.float32)
    active = exact_gelu(hidden).astype(jnp.bfloat16)
    result = (
        second + jnp.dot(active, w2, preferred_element_type=jnp.float32) + bd.astype(jnp.float32)
    )
    saved = (
        normed1,
        factor1,
        h1,
        query_rot,
        keys_rot,
        values,
        lse,
        mixed,
        normed2,
        factor2,
        h2,
        hidden,
        active,
        cosine,
        sine,
    )
    return (saved, result.astype(jnp.bfloat16))


def backward_pass(params, saved, grad_in, totals):
    g1, b1, wqkv, bqkv, wo, bo, g2, b2, w1, bu, w2, bd = params
    (
        normed1,
        factor1,
        h1,
        query_rot,
        keys_rot,
        values,
        lse,
        mixed,
        normed2,
        factor2,
        h2,
        hidden,
        active,
        cosine,
        sine,
    ) = saved
    grad_out = grad_in.astype(jnp.float32)
    count, width = grad_out.shape
    heads = width // 64
    grad_y2 = grad_out.astype(jnp.bfloat16)
    grad_w2 = outer(active, grad_y2)
    grad_bd = column_sum(grad_y2)
    grad_act = back(grad_y2, w2)
    unused, pull = jax.vjp(exact_gelu, hidden)
    grad_hidden = pull(grad_act)[0].astype(jnp.bfloat16)
    grad_w1 = outer(h2, grad_hidden)
    grad_bu = column_sum(grad_hidden)
    grad_h2 = back(grad_hidden, w1)
    grad_g2 = jnp.sum(grad_h2 * normed2, axis=0)
    grad_b2 = jnp.sum(grad_h2, axis=0)
    grad_second = grad_out + norm_back(grad_h2 * g2.astype(jnp.float32), normed2, factor2)
    grad_y1 = grad_second.astype(jnp.bfloat16)
    grad_wo = outer(mixed, grad_y1)
    grad_bo = column_sum(grad_y1)
    grad_mixed = back(grad_y1, wo).astype(jnp.bfloat16).reshape(count, heads, 64)
    keys_all, values_all = (
        lax.all_gather(keys_rot, "grp", axis=0, tiled=True),
        lax.all_gather(values, "grp", axis=0, tiled=True),
    )
    total = keys_all.shape[0]
    keys_all = keys_all.reshape(total, heads, 64)
    values_all = values_all.reshape(total, heads, 64)
    scores = (
        jnp.einsum("thd,shd->hts", query_rot, keys_all, preferred_element_type=jnp.float32) * SCALE
    )
    probs = jnp.exp(scores - lse)
    grad_probs = jnp.einsum(
        "thd,shd->hts", grad_mixed, values_all, preferred_element_type=jnp.float32
    )
    delta = jnp.sum(probs * grad_probs, axis=-1, keepdims=True)
    grad_scores = (probs * (grad_probs - delta)).astype(jnp.bfloat16)
    grad_query = (
        jnp.einsum("hts,shd->thd", grad_scores, keys_all, preferred_element_type=jnp.float32)
        * SCALE
    )
    probs_low = probs.astype(jnp.bfloat16)
    grad_values = jnp.einsum(
        "hts,thd->shd", probs_low, grad_mixed, preferred_element_type=jnp.float32
    )
    grad_keys = (
        jnp.einsum("hts,thd->shd", grad_scores, query_rot, preferred_element_type=jnp.float32)
        * SCALE
    )
    keys_own, values_own = (
        lax.psum_scatter(
            grad_keys.reshape(total, width).astype(jnp.bfloat16),
            "grp",
            scatter_dimension=0,
            tiled=True,
        ).astype(jnp.float32),
        lax.psum_scatter(
            grad_values.reshape(total, width).astype(jnp.bfloat16),
            "grp",
            scatter_dimension=0,
            tiled=True,
        ).astype(jnp.float32),
    )
    query_back = rotate(grad_query, cosine, -sine).reshape(count, width)
    keys_back = rotate(keys_own.reshape(count, heads, 64), cosine, -sine).reshape(count, width)
    grad_qkv = jnp.concatenate([query_back, keys_back, values_own], axis=1).astype(jnp.bfloat16)
    grad_wqkv = outer(h1, grad_qkv)
    grad_bqkv = column_sum(grad_qkv)
    grad_h1 = back(grad_qkv, wqkv)
    grad_g1 = jnp.sum(grad_h1 * normed1, axis=0)
    grad_b1 = jnp.sum(grad_h1, axis=0)
    grad_field = grad_second + norm_back(grad_h1 * g1.astype(jnp.float32), normed1, factor1)
    terms = (
        grad_g1,
        grad_b1,
        grad_wqkv,
        grad_bqkv,
        grad_wo,
        grad_bo,
        grad_g2,
        grad_b2,
        grad_w1,
        grad_bu,
        grad_w2,
        grad_bd,
    )
    totals = tuple((a + b for a, b in zip(totals, terms)))
    return (grad_field.astype(jnp.bfloat16), totals)


def local(
    tokens,
    positions,
    ln1_gain,
    ln1_bias,
    w_qkv,
    b_qkv,
    w_out,
    b_out,
    ln2_gain,
    ln2_bias,
    w_up,
    b_up,
    w_down,
    b_down,
    cotangent,
):
    shards = (
        ln1_gain,
        ln1_bias,
        w_qkv,
        b_qkv,
        w_out,
        b_out,
        ln2_gain,
        ln2_bias,
        w_up,
        b_up,
        w_down,
        b_down,
    )
    groups = lax.axis_size("grp")
    totals = tuple((jnp.zeros((s.shape[0] * groups,) + s.shape[1:], jnp.float32) for s in shards))
    outputs = []
    gradients = []
    for index in range(tokens.shape[0]):
        forward_params = (
            lax.all_gather(ln1_gain, "grp", axis=0, tiled=True),
            lax.all_gather(ln1_bias, "grp", axis=0, tiled=True),
            lax.all_gather(w_qkv, "grp", axis=0, tiled=True),
            lax.all_gather(b_qkv, "grp", axis=0, tiled=True),
            lax.all_gather(w_out, "grp", axis=0, tiled=True),
            lax.all_gather(b_out, "grp", axis=0, tiled=True),
            lax.all_gather(ln2_gain, "grp", axis=0, tiled=True),
            lax.all_gather(ln2_bias, "grp", axis=0, tiled=True),
            lax.all_gather(w_up, "grp", axis=0, tiled=True),
            lax.all_gather(b_up, "grp", axis=0, tiled=True),
            lax.all_gather(w_down, "grp", axis=0, tiled=True),
            lax.all_gather(b_down, "grp", axis=0, tiled=True),
        )
        saved, result = forward_pass(forward_params, tokens[index], positions[:, index, :])
        outputs.append(result)
        backward_params = (
            lax.all_gather(ln1_gain, "grp", axis=0, tiled=True),
            lax.all_gather(ln1_bias, "grp", axis=0, tiled=True),
            lax.all_gather(w_qkv, "grp", axis=0, tiled=True),
            lax.all_gather(b_qkv, "grp", axis=0, tiled=True),
            lax.all_gather(w_out, "grp", axis=0, tiled=True),
            lax.all_gather(b_out, "grp", axis=0, tiled=True),
            lax.all_gather(ln2_gain, "grp", axis=0, tiled=True),
            lax.all_gather(ln2_bias, "grp", axis=0, tiled=True),
            lax.all_gather(w_up, "grp", axis=0, tiled=True),
            lax.all_gather(b_up, "grp", axis=0, tiled=True),
            lax.all_gather(w_down, "grp", axis=0, tiled=True),
            lax.all_gather(b_down, "grp", axis=0, tiled=True),
        )
        grad_field, totals = backward_pass(backward_params, saved, cotangent[index], totals)
        gradients.append(grad_field)
    owned = (
        lax.psum_scatter(
            totals[0].astype(jnp.bfloat16), "grp", scatter_dimension=0, tiled=True
        ).astype(jnp.float32),
        lax.psum_scatter(
            totals[1].astype(jnp.bfloat16), "grp", scatter_dimension=0, tiled=True
        ).astype(jnp.float32),
        lax.psum_scatter(
            totals[2].astype(jnp.bfloat16), "grp", scatter_dimension=0, tiled=True
        ).astype(jnp.float32),
        lax.psum_scatter(
            totals[3].astype(jnp.bfloat16), "grp", scatter_dimension=0, tiled=True
        ).astype(jnp.float32),
        lax.psum_scatter(
            totals[4].astype(jnp.bfloat16), "grp", scatter_dimension=0, tiled=True
        ).astype(jnp.float32),
        lax.psum_scatter(
            totals[5].astype(jnp.bfloat16), "grp", scatter_dimension=0, tiled=True
        ).astype(jnp.float32),
        lax.psum_scatter(
            totals[6].astype(jnp.bfloat16), "grp", scatter_dimension=0, tiled=True
        ).astype(jnp.float32),
        lax.psum_scatter(
            totals[7].astype(jnp.bfloat16), "grp", scatter_dimension=0, tiled=True
        ).astype(jnp.float32),
        lax.psum_scatter(
            totals[8].astype(jnp.bfloat16), "grp", scatter_dimension=0, tiled=True
        ).astype(jnp.float32),
        lax.psum_scatter(
            totals[9].astype(jnp.bfloat16), "grp", scatter_dimension=0, tiled=True
        ).astype(jnp.float32),
        lax.psum_scatter(
            totals[10].astype(jnp.bfloat16), "grp", scatter_dimension=0, tiled=True
        ).astype(jnp.float32),
        lax.psum_scatter(
            totals[11].astype(jnp.bfloat16), "grp", scatter_dimension=0, tiled=True
        ).astype(jnp.float32),
    )
    summed = (
        lax.psum(owned[0].astype(jnp.bfloat16), "rep").astype(jnp.float32),
        lax.psum(owned[1].astype(jnp.bfloat16), "rep").astype(jnp.float32),
        lax.psum(owned[2].astype(jnp.bfloat16), "rep").astype(jnp.float32),
        lax.psum(owned[3].astype(jnp.bfloat16), "rep").astype(jnp.float32),
        lax.psum(owned[4].astype(jnp.bfloat16), "rep").astype(jnp.float32),
        lax.psum(owned[5].astype(jnp.bfloat16), "rep").astype(jnp.float32),
        lax.psum(owned[6].astype(jnp.bfloat16), "rep").astype(jnp.float32),
        lax.psum(owned[7].astype(jnp.bfloat16), "rep").astype(jnp.float32),
        lax.psum(owned[8].astype(jnp.bfloat16), "rep").astype(jnp.float32),
        lax.psum(owned[9].astype(jnp.bfloat16), "rep").astype(jnp.float32),
        lax.psum(owned[10].astype(jnp.bfloat16), "rep").astype(jnp.float32),
        lax.psum(owned[11].astype(jnp.bfloat16), "rep").astype(jnp.float32),
    )
    output = jnp.stack(outputs, axis=0)
    grad_tokens = jnp.stack(gradients, axis=0)
    return (
        output,
        grad_tokens,
        summed[0],
        summed[1],
        summed[2],
        summed[3],
        summed[4],
        summed[5],
        summed[6],
        summed[7],
        summed[8],
        summed[9],
        summed[10],
        summed[11],
    )


def spread(mesh):
    placed = (
        P("rep", "grp", None),
        P(None, "rep", "grp"),
        P("grp"),
        P("grp"),
        P("grp", None),
        P("grp"),
        P("grp", None),
        P("grp"),
        P("grp"),
        P("grp"),
        P("grp", None),
        P("grp"),
        P("grp", None),
        P("grp"),
        P("rep", "grp", None),
    )
    return jax.shard_map(
        local,
        mesh=mesh,
        in_specs=placed,
        out_specs=(
            P("rep", "grp", None),
            P("rep", "grp", None),
            P("grp"),
            P("grp"),
            P("grp", None),
            P("grp"),
            P("grp", None),
            P("grp"),
            P("grp"),
            P("grp"),
            P("grp", None),
            P("grp"),
            P("grp", None),
            P("grp"),
        ),
        check_vma=False,
    )


def solution(mesh):
    reps, groups = mesh.devices.shape
    flat = mesh.devices.reshape(-1)

    def run(*args):
        clips = args[0].shape[0] // reps
        if reps == 8 and groups == 2 * clips:
            split = Mesh(flat.reshape(reps // 2, 2, groups), ("rp", "core", "grp"))
            ins, outs = paired_specs()
            return jax.shard_map(
                paired, mesh=split, in_specs=ins, out_specs=outs, check_vma=False
            )(*args)
        return spread(mesh)(*args)

    return run
```

```python
import functools

import jax
import jax.numpy as jnp
from jax import lax
from jax.experimental import pallas as pl
from jax.experimental.pallas import tpu as pltpu
from jax.sharding import Mesh
from jax.sharding import PartitionSpec as P

SCALE = 0.125
EPS = 1e-06
HEAD = 64
BF = jnp.bfloat16
F32 = jnp.float32
MESH = pl.DeviceIdType.MESH
ANY = pl.BlockSpec(memory_space=pl.ANY)
VM = pl.BlockSpec(memory_space=pltpu.VMEM)


def where_am_i():
    return lax.axis_index("rp"), lax.axis_index("core"), lax.axis_index("grp")


def remote(src, dst, send, recv, target):
    return pltpu.make_async_remote_copy(
        src_ref=src,
        dst_ref=dst,
        send_sem=send,
        recv_sem=recv,
        device_id=target,
        device_id_type=MESH,
    )


def enter(p, c, z, groups):
    barrier = pltpu.get_barrier_semaphore()
    for k in range(groups):
        for d in range(2):
            if k == 0 and d == 0:
                continue
            pl.semaphore_signal(
                barrier, inc=1, device_id=(p, c ^ d, lax.rem(z + k, groups)), device_id_type=MESH
            )
    for b in (1, 2):
        pl.semaphore_signal(barrier, inc=1, device_id=(p ^ b, c, z), device_id_type=MESH)
    pl.semaphore_wait(barrier, 2 * groups - 1 + 2)


def move_tokens(refs, outs, send, recv, p, c, z, clips):
    core, slot = lax.div(z, clips), lax.rem(z, clips)

    def route(i):
        return core, c * clips + i

    def here(i):
        return jnp.logical_and(core == c, c * clips + i == z)

    def start():
        for n, (src, dst) in enumerate(zip(refs, outs)):
            for i in range(clips):
                tc, tz = route(i)

                @pl.when(here(i))
                def _():
                    pltpu.make_async_copy(src.at[i], dst.at[slot], recv.at[n, slot]).start()

                @pl.when(jnp.logical_not(here(i)))
                def _():
                    remote(
                        src.at[i], dst.at[slot], send.at[n, i], recv.at[n, slot], (p, tc, tz)
                    ).start()

    def finish():
        for n, (src, dst) in enumerate(zip(refs, outs)):
            for i in range(clips):

                @pl.when(jnp.logical_not(here(i)))
                def _():
                    remote(
                        src.at[i], dst.at[slot], send.at[n, i], recv.at[n, slot], (p, c ^ 1, z)
                    ).wait_send()

            for m in range(clips):
                pltpu.make_async_copy(src.at[0], dst.at[m], recv.at[n, m]).wait()

    return start, finish


def cuts(whole, half, c, blocks):
    if blocks == 0:
        return [(whole.at[c], half)]
    size = half.shape[3] // blocks
    return [
        (
            whole.at[:, :, :, pl.ds(pl.multiple_of((2 * b + c) * size, size), size)],
            half.at[:, :, :, pl.ds(b * size, size)],
        )
        for b in range(blocks)
    ]


def gather_body(groups, clips, blocks, *refs):
    count = len(blocks)
    raw, (small, x, pos, dy) = refs[:count], refs[count : count + 4]
    outs = refs[count + 4 : 2 * count + 4]
    small_o, x_o, pos_o, dy_o = refs[2 * count + 4 : 2 * count + 8]
    halves = refs[2 * count + 8 : 3 * count + 8]
    zs, zr, xs, xr, ys, yr, fs, fr, hs, ls, ss, sr, ts, tr, us, ur = refs[3 * count + 8 :]
    p, c, z = where_am_i()
    for w in range(count):
        for src, dst in cuts(raw[w], halves[w], c, blocks[w]):
            pltpu.make_async_copy(src, dst, hs.at[w]).start()
    enter(p, c, z, groups)
    col = [(p, c, lax.rem(z + k, groups)) for k in range(groups)]
    org = [lax.rem(z + groups - k, groups) for k in range(groups)]
    xn, yn = (p ^ 1, c, z), (p ^ 2, c, z)
    start, finish = move_tokens((x, pos), (x_o, pos_o), ts, tr, p, c, z, clips)
    start()
    smalls = [
        remote(small, small_o.at[z], ss.at[k], sr.at[k], col[k]) for k in range(1, groups)
    ]
    for s in smalls:
        s.start()
    keep = [pltpu.make_async_copy(small, small_o.at[z], ls.at[count])]
    keep[0].start()
    start_dy, finish_dy = move_tokens((dy,), (dy_o,), us, ur, p, c, z, clips)
    units = [(w, d, side) for w in range(count) for d in range(1, groups) for side in range(2)]

    def origin(d, side):
        return z - d if side == 0 else z + d

    def arrives(d, side):
        return z >= d if side == 0 else z + d < groups

    def leaves(d, side):
        if side == 0:
            return jnp.logical_and(z + 1 < groups, z + 1 >= d)
        return jnp.logical_and(z >= 1, z - 1 + d < groups)

    def hop(w, d, side, src):
        o = origin(d - 1, side)
        target = (p, c, lax.rem(z + 1 if side == 0 else z + groups - 1, groups))
        return remote(src, outs[w].at[o, p], zs.at[w, side, d], zr.at[w, side, d], target)

    def own(w):
        pltpu.make_async_copy(halves[w], halves[w], hs.at[w]).wait()
        keep.append(pltpu.make_async_copy(halves[w], outs[w].at[z], ls.at[w]))
        keep[-1].start()
        for side in range(2):

            @pl.when(leaves(1, side))
            def _():
                hop(w, 1, side, halves[w].at[p]).start()

    def links(u):
        w, d, side = u
        o = outs[w].at[lax.rem(origin(d, side) + groups, groups)]
        e, f = xs.at[w, side, d], xr.at[w, side, d]
        g, h = ys.at[w, side, d], yr.at[w, side, d]
        a, b = fs.at[w, side, d, 0], fr.at[w, side, d, 0]
        m, n = fs.at[w, side, d, 1], fr.at[w, side, d, 1]
        across = lambda q: remote(o.at[q], o.at[q], e, f, xn)
        along = lambda q: remote(o.at[q], o.at[q], g, h, yn)
        first = lambda q: remote(o.at[q, 0], o.at[q, 0], a, b, yn)
        second = lambda q: remote(o.at[q, 1], o.at[q, 1], m, n, xn)
        return o, across, along, first, second

    def plane(u):
        w, d, side = u
        o, across, along, first, second = links(u)

        @pl.when(arrives(d, side))
        def _():
            remote(o.at[p], o.at[p], zs.at[w, side, d], zr.at[w, side, d], xn).wait_recv()
            if d + 1 < groups:

                @pl.when(leaves(d + 1, side))
                def _():
                    hop(w, d + 1, side, o.at[p]).start()

            across(p).start()
            along(p).start()

    def forward(u):
        w, d, side = u
        o, across, along, first, second = links(u)

        @pl.when(arrives(d, side))
        def _():
            across(p ^ 1).wait_recv()
            first(p ^ 1).start()
            along(p ^ 2).wait_recv()
            second(p ^ 2).start()

    def settle(u):
        w, d, side = u
        o, across, along, first, second = links(u)

        @pl.when(arrives(d, side))
        def _():
            first(p ^ 3).wait_recv()
            second(p ^ 3).wait_recv()
            across(p).wait_send()
            along(p).wait_send()
            first(p).wait_send()
            second(p).wait_send()

        @pl.when(leaves(d, side))
        def _():
            hop(w, d, side, halves[w].at[p]).wait_send()

    own(0)
    own(1)
    lag = 3
    for n in range(len(units) + lag):
        if n < len(units):
            plane(units[n])
            w, d, side = units[n]
            if (d, side) == (1, 1) and w + 2 < count:
                own(w + 2)
            if n + 1 == len(units):
                start_dy()
        if n >= lag:
            forward(units[n - lag])
    for u in units:
        settle(u)
    for k in range(1, groups):
        remote(small, small_o.at[org[k]], ss.at[k], sr.at[k], col[k]).wait_recv()
    for s in smalls:
        s.wait_send()
    for k in keep:
        k.wait()
    finish()
    finish_dy()


def half_shape(raw, blocks):
    return raw.shape[1:] if blocks == 0 else raw.shape[:3] + (raw.shape[3] // 2,)


def gather(raw, blocks, small, x, pos, dy, groups):
    count, clips = len(raw), x.shape[0]
    dma = pltpu.SemaphoreType.DMA
    halves = [half_shape(r, b) for r, b in zip(raw, blocks)]
    shapes = [jax.ShapeDtypeStruct((groups,) + h, BF) for h in halves]
    shapes += [jax.ShapeDtypeStruct((groups,) + small.shape, small.dtype)]
    shapes += [jax.ShapeDtypeStruct(v.shape, v.dtype) for v in (x, pos, dy)]
    return pl.pallas_call(
        functools.partial(gather_body, groups, clips, blocks),
        out_shape=shapes,
        in_specs=[ANY] * count + [VM, ANY, ANY, ANY],
        out_specs=[ANY] * len(shapes),
        scratch_shapes=[pltpu.VMEM(h, BF) for h in halves]
        + [dma((count, 2, groups))] * 6
        + [dma((count, 2, groups, 2))] * 2
        + [dma((count,)), dma((count + 1,)), dma((groups,)), dma((groups,))]
        + [dma((2, clips))] * 2
        + [dma((1, clips))] * 2,
        compiler_params=pltpu.CompilerParams(collective_id=0, has_side_effects=True),
        name="gather",
    )(*raw, small, x, pos, dy)


def turn(u, cosine, sine):
    half = HEAD // 2
    first, second = u[:half], u[half:]
    return jnp.concatenate(
        [first * cosine - second * sine, first * sine + second * cosine], axis=0
    )


def dot(a, b):
    return jnp.dot(a, b, preferred_element_type=F32)


def dot_t(a, b):
    return lax.dot_general(a, b, (((1,), (1,)), ((), ())), preferred_element_type=F32)


def tile(i, size):
    return pl.ds(pl.multiple_of(i * size, size), size)


def backward_body(groups, clips, blocks, *refs):
    count = len(blocks)
    (gw2, gw1, gu, w1, wo, wq, mix, qs, kr, vb, h1, x2, x, dy, base, rest) = refs[:16]
    (lse, cosine, sine, g1, g2, gbu) = refs[16:22]
    outs = refs[22 : 22 + count]
    small_o, gx_o, y_o = refs[22 + count : 25 + count]
    (gu_b, w1_b, wo_b, mix_b, qs_b, kr_b, vb_b, h1_b, x2_b, x_b, dy_b) = refs[25 + count : 36 + count]
    (own_f, give, take, y_take, dx2, low, da, gwo, gwq, ak, av, dq2, dk2, acc, gx) = refs[
        36 + count : 51 + count
    ]
    ld, es, er = refs[51 + count : 54 + count]
    grads = (gwq, gwo, gw1, gw2)
    scratch = refs[54 + count :]
    own_a, own_b, one_a, one_b, two_a, two_b, three, full = (
        scratch[i * count : (i + 1) * count] for i in range(8)
    )
    small_s, small_r, small_z = scratch[8 * count : 8 * count + 3]
    (os, s1, r1, s2, r2, s3, r3, s4, r4, s5, r5, cs, cr, ls, ss, sr, ts, tr, us, ur) = scratch[
        8 * count + 3 :
    ]
    own, width = own_f.shape
    inner = mix_b.shape[0]
    third_width = wq.shape[1]
    pairs = ((gu, gu_b), (w1, w1_b), (wo, wo_b), (mix, mix_b), (qs, qs_b), (kr, kr_b), (vb, vb_b))
    pairs += ((h1, h1_b), (x2, x2_b), (x, x_b), (dy, dy_b))
    loads = [pltpu.make_async_copy(a, b, ld.at[n]) for n, (a, b) in enumerate(pairs)]
    for copy in loads:
        copy.start()
    p, c, z = where_am_i()
    hi, lo = lax.div(p, 2), lax.rem(p, 2)
    enter(p, c, z, groups)
    col = [(p, c, lax.rem(z + k, groups)) for k in range(groups)]
    xn, yn, cn = (p ^ 1, c, z), (p ^ 2, c, z), (p, c ^ 1, z)
    order = (3, 2, 1, 0)
    units = [(w, j) for w in order for j in [*range(1, groups), 0]]
    sides = ((own_a, one_a, two_a, hi, yn), (own_b, one_b, two_b, lo, xn))

    def c1(u, n):
        w, j = u
        g = grads[w].at[lax.rem(z + j, groups)]
        src, target = (g.at[:, 1 - lo, 0], xn) if n == 0 else (g.at[1 - hi, :, 1], yn)
        return remote(src, sides[n][1][w].at[j], s1.at[w, j, n], r1.at[w, j, n], target)

    def load(u, n):
        w, j = u
        g = grads[w].at[lax.rem(z + j, groups)]
        src = g.at[:, lo, 0] if n == 0 else g.at[hi, :, 1]
        return pltpu.make_async_copy(src, sides[n][0][w].at[j], os.at[w, j, n])

    def c2(u, n):
        w, j = u
        own, one, two, side, target = sides[n]
        return remote(own[w].at[j, 1 - side], two[w].at[j], s2.at[w, j, n], r2.at[w, j, n], target)

    def c3(u, n):
        w, j = u
        src = sides[n][0][w].at[j, sides[n][3]]
        return remote(src, three[w].at[j, n], s3.at[w, j, n], r3.at[w, j, n], col[j])

    def c4(w, n):
        f = full[w].at[p]
        return remote(f, f, s4.at[w, n], r4.at[w, n], (xn, yn)[n])

    def c5(w, n):
        f = full[w].at[(p ^ 1, p ^ 2)[n], n]
        return remote(f, f, s5.at[w, n], r5.at[w, n], (yn, xn)[n])

    def stage_zero(u):
        for n in range(2):
            c1(u, n).start()
            load(u, n).start()

    def stage_one(u):
        w, j = u
        for n, (own, one, two, side, target) in enumerate(sides):
            load(u, n).wait()
            c1(u, n).wait_recv()
            own[w][j] = (own[w][j].astype(F32) + one[w][j].astype(F32)).astype(BF)
            c2(u, n).start()

    def stage_two(u):
        w, j = u
        for n, (own, one, two, side, target) in enumerate(sides):
            c2(u, n).wait_recv()
            own[w][j, side] = (own[w][j, side].astype(F32) + two[w][j].astype(F32)).astype(BF)
            if j:
                c3(u, n).start()

    def stage_three(w):
        for n, (own, one, two, side, target) in enumerate(sides):
            total = own[w][0, side].astype(F32)
            for j in range(1, groups):
                c3((w, j), n).wait_recv()
                total = total + three[w][j, n].astype(F32)
            full[w][p, n] = total.astype(BF)
        for n in range(2):
            c4(w, n).start()

    def stage_four(w):
        for n, target in enumerate((yn, xn)):
            f = full[w].at[(p ^ 1, p ^ 2)[n]]
            remote(f, f, s4.at[w, n], r4.at[w, n], target).wait_recv()
            c5(w, n).start()

    def stage_five(w):
        for n in range(2):
            f = full[w].at[p ^ 3, n]
            remote(f, f, s5.at[w, n], r5.at[w, n], xn).wait_recv()
        for dst, src in cuts(outs[w], full[w], c, blocks[w]):
            pltpu.make_async_copy(src, dst, ls.at[w]).start()
            remote(src, dst, cs.at[w], cr.at[w], cn).start()

    ahead, lag = 3, 2
    todo = {}
    for n, u in enumerate(units):
        todo.setdefault(max(n - ahead, -1), []).append((stage_zero, u))
        todo.setdefault(n, []).append((stage_one, u))
        todo.setdefault(n + lag, []).append((stage_two, u))
    for i, w in enumerate(order):
        last = (i + 1) * groups - 1 + lag
        for at, stage in ((2, stage_three), (3, stage_four), (4, stage_five)):
            todo.setdefault(last + at, []).append((stage, w))
    steps = sorted(todo)

    def run(step):
        for stage, what in todo[step]:
            stage(what)

    def tick():
        run(steps.pop(0))

    def half_sum(n, left, right, depth):
        def other(i, carry):
            part = dot_t(left[own:, :depth], right[tile(i, 256), :depth])
            give[:, tile(i, 256)] = part.astype(BF)
            return carry

        def self(i, carry):
            own_f[:, tile(i, 256)] = dot_t(left[:own, :depth], right[tile(i, 256), :depth])
            return carry

        lax.fori_loop(0, width // 256, other, 0)
        copy = remote(give, take, es.at[n], er.at[n], cn)
        copy.start()
        lax.fori_loop(0, width // 256, self, 0)
        return copy

    def part(i):
        per = own // clips // 128
        return lax.div(i, per), tile(lax.rem(i, per), 128)

    def norm_step(i, field, gain, grad, row):
        at = tile(i, 128)
        d = own_f[at] + take[at].astype(F32)
        v = field[at].astype(F32)
        v = v - jnp.mean(v, axis=1, keepdims=True)
        r = lax.rsqrt(jnp.mean(v * v, axis=1, keepdims=True) + EPS)
        v = v * r
        acc[row : row + 1] += jnp.sum(d * v, axis=0, keepdims=True)
        acc[row + 1 : row + 2] += jnp.sum(d, axis=0, keepdims=True)
        e = d * gain[...]
        mean = jnp.mean(e, axis=1, keepdims=True)
        e = e - mean - v * jnp.mean(e * v, axis=1, keepdims=True)
        return grad + r * e

    tick()
    y_copy = remote(rest, y_take, es.at[3], er.at[3], cn)
    y_copy.start()
    acc[...] = jnp.zeros_like(acc)
    loads[0].wait()
    loads[1].wait()
    swap = half_sum(0, gu_b, w1_b, w1.shape[1])
    wq_b = w1_b.at[:, :third_width]
    dqkv = gu_b.at[:, :third_width]
    late = pltpu.make_async_copy(wq, wq_b, ld.at[len(loads)])
    late.start()
    tick()
    for copy in loads[2:]:
        copy.wait()
    swap.wait()

    def second_norm(i, carry):
        at = tile(i, 128)
        g = dy_b[part(i)].astype(F32)
        d = norm_step(i, x2_b, g2, g, 3)
        dx2[at] = d
        acc[5:6] += jnp.sum(g, axis=0, keepdims=True)
        low[at] = d.astype(BF)
        acc[2:3] += jnp.sum(d.astype(BF).astype(F32), axis=0, keepdims=True)
        return carry

    lax.fori_loop(0, own // 128, second_norm, 0)
    swap = remote(low.at[:own], low.at[own:], es.at[1], er.at[1], cn)
    swap.start()
    y_base = pltpu.make_async_copy(base, x2_b, ld.at[len(loads) + 1])
    y_base.start()
    tick()
    swap.wait()

    def out_grad(i, carry):
        at = tile(i, 256)
        gwo[..., at] = dot(mix_b[...], low[:, at]).astype(BF).reshape(gwo.shape[:-1] + (256,))
        return carry

    lax.fori_loop(0, width // 256, out_grad, 0)

    def attn_grad(i, carry):
        at = tile(i, 256)
        da[:, at] = dot_t(wo_b[...], low[at]).astype(BF)
        return carry

    lax.fori_loop(0, 2 * own // 256, attn_grad, 0)
    tick()

    def head(h, side):
        rows = tile(h, HEAD)
        place = tile(side, HEAD)
        co, si = cosine[...], sine[...]
        kt = kr_b[rows]
        keys, values = kt.T, vb_b[rows].T
        queries, outer_grads = qs_b[rows].T, da[rows].T
        step = 256
        for i in range(0, 2 * own, step):
            s = slice(i, i + step)
            g = da[rows, s]
            p = jnp.exp(dot(keys, qs_b[rows, s]) - lse[h, :, s])
            delta = jnp.sum(mix_b[rows, s].astype(F32) * g.astype(F32), axis=0, keepdims=True)
            ds = (p * (dot(values, g) - delta)).astype(BF)
            dq2[place, s] = turn(dot(kt, ds) * SCALE, co[:, s], -si[:, s]).astype(BF)
            dv = dot(p.astype(BF), outer_grads[s])
            dk = dot(ds, queries[s])
            if i == 0:
                ak[...] = dk
                av[side] = dv
            else:
                ak[...] += dk
                av[side] += dv
        dk2[place] = turn(ak[...].T, co, -si).astype(BF)

    heads = inner // HEAD
    during = [steps.pop(0) for _ in range(4)]

    def two_heads(i, carry):
        lax.fori_loop(0, 2, lambda side, _: head(2 * i + side, side), None)
        for n, value in enumerate(
            (dq2[...].T, dk2[...].T, jnp.concatenate([av[0], av[1]], axis=1).astype(BF))
        ):
            at = pl.ds(pl.multiple_of(n * inner + i * 2 * HEAD, 2 * HEAD), 2 * HEAD)
            dqkv[:, at] = value
        for n, step in enumerate(during):
            pl.when(i == n * heads // 8)(functools.partial(run, step))
        return carry

    lax.fori_loop(0, heads // 2, two_heads, 0)
    y_base.wait()
    y_copy.wait()

    def last_add(i, carry):
        at = tile(i, 128)
        dy_b[part(i)] = (x2_b[at] + y_take[at].astype(F32)).astype(BF)
        return carry

    lax.fori_loop(0, own // 128, last_add, 0)
    y_start, y_finish = move_tokens((dy_b,), (y_o,), us, ur, p, c, z, clips)
    y_start()
    row = width // groups
    for g in range(groups):
        left = h1_b[:, g * row : (g + 1) * row].T

        def in_grad(i, carry):
            at = tile(i, 512)
            gwq[g, ..., at] = dot(left, dqkv[:, at]).astype(BF).reshape(gwq.shape[1:-1] + (512,))
            return carry

        lax.fori_loop(0, third_width // 512, in_grad, 0)
    tick()
    late.wait()
    swap = half_sum(2, dqkv, wq_b, third_width)
    tick()
    swap.wait()

    def first_norm(i, carry):
        gx[part(i)] = norm_step(i, x_b, g1, dx2[tile(i, 128)], 0).astype(BF)
        return carry

    lax.fori_loop(0, own // 128, first_norm, 0)
    start, finish = move_tokens((gx,), (gx_o,), ts, tr, p, c, z, clips)
    start()
    tick()
    small_s[...] = jnp.zeros_like(small_s)
    for n in range(6):
        for g in range(groups):
            small_s[g, n : n + 1] = acc[n : n + 1, g * row : (g + 1) * row]
    half = row // 2
    mine_at = pl.ds(pl.multiple_of(c * half, half), half)
    for b in range(3 * groups):
        line = jnp.sum(dqkv[:, b * half : (b + 1) * half].astype(F32), axis=0, keepdims=True)
        small_s[b // 3, 6 + b % 3 : 7 + b % 3, mine_at] = line
    deep = gbu.shape[1] // groups
    for g in range(groups):
        for n in range(deep // row):
            at = pl.ds(9 + c * (deep // row) + n, 1)
            small_s[g, at] = gbu[:, g * deep + n * row : g * deep + (n + 1) * row]
    tick()
    for n, target in enumerate((cn, xn, yn)):
        copy = remote(small_s, small_r.at[n], ss.at[n], sr.at[n], target)
        copy.start()
        tick()
        copy.wait()
        small_s[...] += small_r[n]
    tails = [
        remote(small_s.at[col[k][2]], small_z.at[k], ss.at[2 + k], sr.at[2 + k], col[k])
        for k in range(1, groups)
    ]
    for t in tails:
        t.start()
    while steps:
        tick()
    for k in range(1, groups):
        tails[k - 1].wait()
    small_o[...] = small_s[z]
    for k in range(1, groups):
        small_o[...] += small_z[k]
    for u in units:
        w, j = u
        for n in range(2):
            c1(u, n).wait_send()
            c2(u, n).wait_send()
            if j:
                c3(u, n).wait_send()
    for w in range(count):
        for n in range(2):
            c4(w, n).wait_send()
            c5(w, n).wait_send()
        pltpu.make_async_copy(full[w], full[w], ls.at[w]).wait()
        remote(full[w], full[w], cs.at[w], cr.at[w], cn).wait()
    finish()
    y_finish()


def backward(gw2, gw1, arrays, tables, lines, groups, blocks):
    gu, w1, wo, wq, mix, qs, kr, vb, h1, x2, x, dy, base, rest = arrays
    (own, width), clips = x.shape, dy.shape[0]
    small = jax.ShapeDtypeStruct((groups, lines + -lines % 8, width // groups), F32)
    count = len(blocks)
    dma = pltpu.SemaphoreType.DMA
    split = lambda v: (groups, 2, 2, 2, v.shape[0] // (8 * groups), v.shape[1])
    tiles = [split(wq)[4:], split(wo)[4:], gw1.shape[4:], gw2.shape[4:]]
    shapes = [
        jax.ShapeDtypeStruct((4, 2, t[0], 2 * t[1]) if b else (2, 4, 2) + t, BF)
        for t, b in zip(tiles, blocks)
    ]
    shapes += [
        jax.ShapeDtypeStruct(small.shape[1:], F32),
        jax.ShapeDtypeStruct(dy.shape, BF),
        jax.ShapeDtypeStruct(dy.shape, BF),
    ]
    scratch = [pltpu.VMEM(v.shape, v.dtype) for v in (gu, w1, wo, mix, qs, kr, vb, h1, x2, x, dy)]
    half, low = (own, width), pltpu.VMEM((2 * own, width), BF)
    scratch += [pltpu.VMEM(half, F32)] + [pltpu.VMEM(half, BF)] * 3
    scratch += [pltpu.VMEM(half, F32), low, pltpu.VMEM(mix.shape, BF)]
    scratch += [pltpu.VMEM(split(wo), BF), pltpu.VMEM(split(wq), BF)]
    scratch += [pltpu.VMEM((2 * own, HEAD), F32), pltpu.VMEM((2, 2 * own, HEAD), F32)]
    scratch += [pltpu.VMEM((2 * HEAD, 2 * own), BF)] * 2
    scratch += [pltpu.VMEM((8, width), F32), pltpu.VMEM(dy.shape, BF)]
    scratch += [dma((13,)), dma((4,)), dma((4,))]
    for lead in (
        (groups, 2),
        (groups, 2),
        (groups, 2),
        (groups, 2),
        (groups,),
        (groups,),
        (groups, 2),
        (4, 2),
    ):
        scratch += [pltpu.VMEM(lead + t, BF) for t in tiles]
    scratch += [
        pltpu.VMEM(small.shape, F32),
        pltpu.VMEM((3,) + small.shape, F32),
        pltpu.VMEM(small.shape, F32),
    ]
    pair = dma((count, groups, 2))
    scratch += [pair] * 7 + [dma((count, 2))] * 4
    scratch += [dma((count,))] * 3 + [dma((2 + groups,))] * 2 + [dma((1, clips))] * 4
    return pl.pallas_call(
        functools.partial(backward_body, groups, clips, blocks),
        out_shape=shapes,
        in_specs=[ANY] * (2 + len(arrays)) + [VM] * len(tables),
        out_specs=[ANY] * count + [VM, ANY, ANY],
        scratch_shapes=scratch,
        compiler_params=pltpu.CompilerParams(
            collective_id=1, has_side_effects=True, vmem_limit_bytes=67043328
        ),
        name="backward",
    )(gw2, gw1, *arrays, *tables)


def attention_body(step, q_ref, k_ref, v_ref, cos_ref, sin_ref, qs_ref, kr_ref, vb_ref, o_ref, l_ref):
    cosine, sine = cos_ref[...], sin_ref[...]
    length = cosine.shape[1]
    kr = turn(k_ref[...], cosine, sine).astype(BF)
    vb = v_ref[...].astype(BF)
    qs = (turn(q_ref[...], cosine, sine).astype(BF).astype(F32) * SCALE).astype(BF)
    kr_ref[...] = kr
    vb_ref[...] = vb
    qs_ref[...] = qs
    keys = kr.T
    for i in range(0, length, step):
        scores = dot(keys, qs[:, i : i + step])
        top = jnp.max(scores, axis=0, keepdims=True)
        e = jnp.exp(scores - top)
        total = jnp.sum(e, axis=0, keepdims=True)
        mixed = dot(vb, e.astype(BF))
        o_ref[:, i : i + step] = (mixed / total).astype(BF)
        l_ref[0, :, i : i + step] = top + jnp.log(total)


def attention(qkv, cosine, sine, step=256):
    rows, length = qkv.shape
    width = rows // 3
    heads = width // HEAD
    block = [pl.BlockSpec((HEAD, length), lambda h, n=n: (n * heads + h, 0)) for n in range(3)]
    table = pl.BlockSpec((HEAD // 2, length), lambda h: (0, 0))
    out = pl.BlockSpec((HEAD, length), lambda h: (h, 0))
    shape = jax.ShapeDtypeStruct((width, length), BF)
    return pl.pallas_call(
        functools.partial(attention_body, step),
        out_shape=[shape] * 4 + [jax.ShapeDtypeStruct((heads, 1, length), F32)],
        grid=(heads,),
        in_specs=block + [table, table],
        out_specs=[out] * 4 + [pl.BlockSpec((1, 1, length), lambda h: (h, 0, 0))],
        cost_estimate=pl.CostEstimate(
            flops=4 * width * length * length,
            transcendentals=heads * length * length,
            bytes_accessed=width * length * 24,
        ),
        name="attention",
    )(qkv, qkv, qkv, cosine, sine)


def swap(value):
    return lax.ppermute(value, "core", [(0, 1), (1, 0)])


def both(value):
    return jnp.concatenate([value, swap(value)], axis=0)


def contract(left, right, a, b):
    return lax.dot_general(left, right, (((a,), (b,)), ((), ())), preferred_element_type=F32)


def own_sum(partial):
    half = partial.shape[0] // 2
    return partial[:half] + swap(partial[half:].astype(BF)).astype(F32)


def paired(
    tokens,
    positions,
    ln1_gain,
    ln1_bias,
    w_qkv,
    b_qkv,
    w_out,
    b_out,
    ln2_gain,
    ln2_bias,
    w_up,
    b_up,
    w_down,
    b_down,
    cotangent,
):
    groups = lax.axis_size("grp")
    clips, part, width = tokens.shape
    hidden = w_down.shape[0] * groups
    own = clips * part
    length = 2 * own
    c, z = lax.axis_index("core"), lax.axis_index("grp")
    wide = width // 2
    deep = hidden // 2
    row = width // groups

    def pick(value, axis):
        return lax.dynamic_index_in_dim(value, c, axis, keepdims=False)

    blocks = (3 * groups, 0, groups, 0)
    raw = [
        w.reshape(((4, 2) if b else (2, 4, 2)) + (w.shape[0] // (8 if b else 16), w.shape[1]))
        for w, b in zip((w_qkv, w_out, w_up, w_down), blocks)
    ]
    bq, bu = b_qkv.shape[0] // row, b_up.shape[0] // row
    vectors = [ln1_gain, ln1_bias, b_out, ln2_gain, ln2_bias, b_down]
    vectors += [b_qkv[n * row : (n + 1) * row] for n in range(bq)]
    vectors += [b_up[n * row : (n + 1) * row] for n in range(bu)]
    lines = len(vectors)
    place = lax.broadcasted_iota(jnp.int32, (lines + -lines % 8, row), 0)
    small = jnp.zeros(place.shape, F32)
    for n, v in enumerate(vectors):
        small = jnp.where(place == n, v.astype(F32)[None, :], small)
    pos = jnp.pad(jnp.moveaxis(positions, 0, 1).astype(F32), ((0, 0), (0, 5), (0, 0)))
    wq, wo, w1, w2, small, x, pos, dy = gather(raw, blocks, small, tokens, pos, cotangent, groups)
    wq = wq.reshape(width, 3 * wide)
    wo = wo.reshape(wide, width)
    w1 = w1.reshape(width, deep)
    w2 = w2.reshape(deep, width)
    g1, b1, bo, g2, b2, bd = (small[:, n].reshape(1, width) for n in range(6))
    bq_own = pick(small[:, 6 : 6 + bq].reshape(3, groups, 2, row // 2), 2).reshape(3 * wide, 1)
    bu_own = pick(small[:, 6 + bq : lines].reshape(groups, 2, deep // groups), 1).reshape(1, deep)

    grad_out = dy.reshape(own, width)
    grad_all = both(grad_out)

    pos = jnp.moveaxis(pos[:, :3], 1, 0).reshape(3, own)
    pos = jnp.concatenate([pos, swap(pos)], axis=1)
    pair = jnp.arange(HEAD // 2)
    band = (pair >= 10).astype(jnp.int32) + (pair >= 21).astype(jnp.int32)
    begin = jnp.where(band == 0, 0, jnp.where(band == 1, 10, 21))
    count = jnp.where(band == 0, 10, 11)
    freq = jnp.power(F32(10000.0), -(pair - begin).astype(F32) / count.astype(F32))
    band = band[:, None]
    chosen = jnp.where(band == 0, pos[0:1], jnp.where(band == 1, pos[1:2], pos[2:3]))
    angles = chosen * freq[:, None]
    cosine, sine = jnp.cos(angles), jnp.sin(angles)

    tokens = x.reshape(own, width)
    x = tokens.astype(F32)
    h1 = both((normalize(x)[0] * g1 + b1).astype(BF))
    qkv = contract(wq, h1, 0, 1) + bq_own
    qs, kr, vb, mixed, lse = attention(qkv, cosine, sine)
    x2 = x + own_sum(contract(mixed, wo, 0, 0)) + bo
    h2 = both((normalize(x2)[0] * g2 + b2).astype(BF))
    u = contract(h2, w1, 1, 0) + bu_own
    cdf = 0.5 * (1.0 + lax.erf(u * F32(0.7071067811865476)))
    act = (u * cdf).astype(BF)
    slope = (cdf + u * jnp.exp(-0.5 * u * u) * F32(0.3989422804014327)).astype(BF)
    result = contract(act, w2, 1, 0)
    base, rest = x2 + result[:own] + bd, result[own:].astype(BF)

    gw2 = contract(act, grad_all, 0, 0).astype(BF)
    gu = (contract(grad_all, w2, 1, 1) * slope.astype(F32)).astype(BF)
    gw1 = contract(h2, gu, 0, 0).astype(BF)
    gbu = jnp.sum(gu.astype(F32), axis=0)
    gw2, gw1 = (
        g.reshape(groups, 2, 2, 2, g.shape[0] // (8 * groups), g.shape[1]) for g in (gw2, gw1)
    )
    arrays = (gu, w1, wo, wq, mixed, qs, kr, vb, h1, x2, tokens, dy, base, rest)
    tables = (lse, cosine, sine, g1, g2, gbu.reshape(1, deep))
    gwq, gwo, gw1, gw2, sums, gx, output = backward(gw2, gw1, arrays, tables, lines, groups, blocks)
    gwq, gwo, gw1, gw2 = (
        g.reshape(shard.shape).astype(F32)
        for g, shard in zip((gwq, gwo, gw1, gw2), (w_qkv, w_out, w_up, w_down))
    )
    gg1, gb1, gbo, gg2, gb2, gbd = (sums[n] for n in range(6))
    gbq, gbu = sums[6 : 6 + bq].reshape(-1), sums[6 + bq : lines].reshape(-1)
    return (output, gx, gg1, gb1, gwq, gbq, gwo, gbo, gg2, gb2, gw1, gbu, gw2, gbd)


def paired_specs():
    rep = ("rp", "core")
    ins = (P(rep, "grp", None), P(None, rep, "grp"))
    one, two = P("grp"), P("grp", None)
    ins += (one, one, two, one, two, one, one, one, two, one, two, one, P(rep, "grp", None))
    outs = (P(rep, "grp", None),) * 2
    outs += (one, one, two, one, two, one, one, one, two, one, two, one)
    return ins, outs


def rotary_angles(positions):
    pair = jnp.arange(32)
    band = (pair >= 10).astype(jnp.int32) + (pair >= 21).astype(jnp.int32)
    start = jnp.where(band == 0, 0, jnp.where(band == 1, 10, 21))
    count = jnp.where(band == 0, 10, 11)
    freq = jnp.power(
        jnp.float32(10000.0), -(pair - start).astype(jnp.float32) / count.astype(jnp.float32)
    )
    pos_f = positions.astype(jnp.float32)
    chosen = jnp.where(
        band[None, :] == 0,
        pos_f[0][:, None],
        jnp.where(band[None, :] == 1, pos_f[1][:, None], pos_f[2][:, None]),
    )
    return chosen * freq[None, :]


def rotate(field, cosine, sine):
    first = field[..., :32]
    second = field[..., 32:]
    return jnp.concatenate(
        [first * cosine - second * sine, first * sine + second * cosine], axis=-1
    )


def normalize(field):
    centred = field - jnp.mean(field, axis=-1, keepdims=True)
    variance = jnp.mean(centred * centred, axis=-1, keepdims=True)
    factor = lax.rsqrt(variance + EPS)
    return (centred * factor, factor)


def norm_back(grad_norm, normed, factor):
    return factor * (
        grad_norm
        - jnp.mean(grad_norm, axis=-1, keepdims=True)
        - normed * jnp.mean(grad_norm * normed, axis=-1, keepdims=True)
    )


def outer(left, right):
    return lax.dot_general(
        left, right, (((0,), (0,)), ((), ())), preferred_element_type=jnp.float32
    )


def back(left, right):
    return lax.dot_general(
        left, right, (((1,), (1,)), ((), ())), preferred_element_type=jnp.float32
    )


def exact_gelu(value):
    return jax.nn.gelu(value, approximate=False)


def column_sum(value):
    return jnp.sum(value.astype(jnp.float32), axis=0)


def forward_pass(params, field_in, positions):
    g1, b1, wqkv, bqkv, wo, bo, g2, b2, w1, bu, w2, bd = params
    field = field_in.astype(jnp.float32)
    count, width = field.shape
    heads = width // 64
    angles = rotary_angles(positions)
    cosine = jnp.cos(angles)[:, None, :]
    sine = jnp.sin(angles)[:, None, :]
    normed1, factor1 = normalize(field)
    h1 = (normed1 * g1.astype(jnp.float32) + b1.astype(jnp.float32)).astype(jnp.bfloat16)
    qkv = jnp.dot(h1, wqkv, preferred_element_type=jnp.float32) + bqkv.astype(jnp.float32)
    query_rot = rotate(qkv[:, :width].reshape(count, heads, 64), cosine, sine).astype(jnp.bfloat16)
    keys_rot = (
        rotate(qkv[:, width : 2 * width].reshape(count, heads, 64), cosine, sine)
        .astype(jnp.bfloat16)
        .reshape(count, width)
    )
    values = qkv[:, 2 * width :].astype(jnp.bfloat16)
    keys_all, values_all = (
        lax.all_gather(keys_rot, "grp", axis=0, tiled=True),
        lax.all_gather(values, "grp", axis=0, tiled=True),
    )
    total = keys_all.shape[0]
    keys_all = keys_all.reshape(total, heads, 64)
    values_all = values_all.reshape(total, heads, 64)
    scores = (
        jnp.einsum("thd,shd->hts", query_rot, keys_all, preferred_element_type=jnp.float32) * SCALE
    )
    top = jnp.max(scores, axis=-1, keepdims=True)
    lse = top + jnp.log(jnp.sum(jnp.exp(scores - top), axis=-1, keepdims=True))
    probs = jnp.exp(scores - lse).astype(jnp.bfloat16)
    mixed = (
        jnp.einsum("hts,shd->thd", probs, values_all, preferred_element_type=jnp.float32)
        .reshape(count, width)
        .astype(jnp.bfloat16)
    )
    second = field + jnp.dot(mixed, wo, preferred_element_type=jnp.float32) + bo.astype(jnp.float32)
    normed2, factor2 = normalize(second)
    h2 = (normed2 * g2.astype(jnp.float32) + b2.astype(jnp.float32)).astype(jnp.bfloat16)
    hidden = jnp.dot(h2, w1, preferred_element_type=jnp.float32) + bu.astype(jnp.float32)
    active = exact_gelu(hidden).astype(jnp.bfloat16)
    result = (
        second + jnp.dot(active, w2, preferred_element_type=jnp.float32) + bd.astype(jnp.float32)
    )
    saved = (
        normed1,
        factor1,
        h1,
        query_rot,
        keys_rot,
        values,
        lse,
        mixed,
        normed2,
        factor2,
        h2,
        hidden,
        active,
        cosine,
        sine,
    )
    return (saved, result.astype(jnp.bfloat16))


def backward_pass(params, saved, grad_in, totals):
    g1, b1, wqkv, bqkv, wo, bo, g2, b2, w1, bu, w2, bd = params
    (
        normed1,
        factor1,
        h1,
        query_rot,
        keys_rot,
        values,
        lse,
        mixed,
        normed2,
        factor2,
        h2,
        hidden,
        active,
        cosine,
        sine,
    ) = saved
    grad_out = grad_in.astype(jnp.float32)
    count, width = grad_out.shape
    heads = width // 64
    grad_y2 = grad_out.astype(jnp.bfloat16)
    grad_w2 = outer(active, grad_y2)
    grad_bd = column_sum(grad_y2)
    grad_act = back(grad_y2, w2)
    unused, pull = jax.vjp(exact_gelu, hidden)
    grad_hidden = pull(grad_act)[0].astype(jnp.bfloat16)
    grad_w1 = outer(h2, grad_hidden)
    grad_bu = column_sum(grad_hidden)
    grad_h2 = back(grad_hidden, w1)
    grad_g2 = jnp.sum(grad_h2 * normed2, axis=0)
    grad_b2 = jnp.sum(grad_h2, axis=0)
    grad_second = grad_out + norm_back(grad_h2 * g2.astype(jnp.float32), normed2, factor2)
    grad_y1 = grad_second.astype(jnp.bfloat16)
    grad_wo = outer(mixed, grad_y1)
    grad_bo = column_sum(grad_y1)
    grad_mixed = back(grad_y1, wo).astype(jnp.bfloat16).reshape(count, heads, 64)
    keys_all, values_all = (
        lax.all_gather(keys_rot, "grp", axis=0, tiled=True),
        lax.all_gather(values, "grp", axis=0, tiled=True),
    )
    total = keys_all.shape[0]
    keys_all = keys_all.reshape(total, heads, 64)
    values_all = values_all.reshape(total, heads, 64)
    scores = (
        jnp.einsum("thd,shd->hts", query_rot, keys_all, preferred_element_type=jnp.float32) * SCALE
    )
    probs = jnp.exp(scores - lse)
    grad_probs = jnp.einsum(
        "thd,shd->hts", grad_mixed, values_all, preferred_element_type=jnp.float32
    )
    delta = jnp.sum(probs * grad_probs, axis=-1, keepdims=True)
    grad_scores = (probs * (grad_probs - delta)).astype(jnp.bfloat16)
    grad_query = (
        jnp.einsum("hts,shd->thd", grad_scores, keys_all, preferred_element_type=jnp.float32)
        * SCALE
    )
    probs_low = probs.astype(jnp.bfloat16)
    grad_values = jnp.einsum(
        "hts,thd->shd", probs_low, grad_mixed, preferred_element_type=jnp.float32
    )
    grad_keys = (
        jnp.einsum("hts,thd->shd", grad_scores, query_rot, preferred_element_type=jnp.float32)
        * SCALE
    )
    keys_own, values_own = (
        lax.psum_scatter(
            grad_keys.reshape(total, width).astype(jnp.bfloat16),
            "grp",
            scatter_dimension=0,
            tiled=True,
        ).astype(jnp.float32),
        lax.psum_scatter(
            grad_values.reshape(total, width).astype(jnp.bfloat16),
            "grp",
            scatter_dimension=0,
            tiled=True,
        ).astype(jnp.float32),
    )
    query_back = rotate(grad_query, cosine, -sine).reshape(count, width)
    keys_back = rotate(keys_own.reshape(count, heads, 64), cosine, -sine).reshape(count, width)
    grad_qkv = jnp.concatenate([query_back, keys_back, values_own], axis=1).astype(jnp.bfloat16)
    grad_wqkv = outer(h1, grad_qkv)
    grad_bqkv = column_sum(grad_qkv)
    grad_h1 = back(grad_qkv, wqkv)
    grad_g1 = jnp.sum(grad_h1 * normed1, axis=0)
    grad_b1 = jnp.sum(grad_h1, axis=0)
    grad_field = grad_second + norm_back(grad_h1 * g1.astype(jnp.float32), normed1, factor1)
    terms = (
        grad_g1,
        grad_b1,
        grad_wqkv,
        grad_bqkv,
        grad_wo,
        grad_bo,
        grad_g2,
        grad_b2,
        grad_w1,
        grad_bu,
        grad_w2,
        grad_bd,
    )
    totals = tuple((a + b for a, b in zip(totals, terms)))
    return (grad_field.astype(jnp.bfloat16), totals)


def local(
    tokens,
    positions,
    ln1_gain,
    ln1_bias,
    w_qkv,
    b_qkv,
    w_out,
    b_out,
    ln2_gain,
    ln2_bias,
    w_up,
    b_up,
    w_down,
    b_down,
    cotangent,
):
    shards = (
        ln1_gain,
        ln1_bias,
        w_qkv,
        b_qkv,
        w_out,
        b_out,
        ln2_gain,
        ln2_bias,
        w_up,
        b_up,
        w_down,
        b_down,
    )
    groups = lax.axis_size("grp")
    totals = tuple((jnp.zeros((s.shape[0] * groups,) + s.shape[1:], jnp.float32) for s in shards))
    outputs = []
    gradients = []
    for index in range(tokens.shape[0]):
        forward_params = (
            lax.all_gather(ln1_gain, "grp", axis=0, tiled=True),
            lax.all_gather(ln1_bias, "grp", axis=0, tiled=True),
            lax.all_gather(w_qkv, "grp", axis=0, tiled=True),
            lax.all_gather(b_qkv, "grp", axis=0, tiled=True),
            lax.all_gather(w_out, "grp", axis=0, tiled=True),
            lax.all_gather(b_out, "grp", axis=0, tiled=True),
            lax.all_gather(ln2_gain, "grp", axis=0, tiled=True),
            lax.all_gather(ln2_bias, "grp", axis=0, tiled=True),
            lax.all_gather(w_up, "grp", axis=0, tiled=True),
            lax.all_gather(b_up, "grp", axis=0, tiled=True),
            lax.all_gather(w_down, "grp", axis=0, tiled=True),
            lax.all_gather(b_down, "grp", axis=0, tiled=True),
        )
        saved, result = forward_pass(forward_params, tokens[index], positions[:, index, :])
        outputs.append(result)
        backward_params = (
            lax.all_gather(ln1_gain, "grp", axis=0, tiled=True),
            lax.all_gather(ln1_bias, "grp", axis=0, tiled=True),
            lax.all_gather(w_qkv, "grp", axis=0, tiled=True),
            lax.all_gather(b_qkv, "grp", axis=0, tiled=True),
            lax.all_gather(w_out, "grp", axis=0, tiled=True),
            lax.all_gather(b_out, "grp", axis=0, tiled=True),
            lax.all_gather(ln2_gain, "grp", axis=0, tiled=True),
            lax.all_gather(ln2_bias, "grp", axis=0, tiled=True),
            lax.all_gather(w_up, "grp", axis=0, tiled=True),
            lax.all_gather(b_up, "grp", axis=0, tiled=True),
            lax.all_gather(w_down, "grp", axis=0, tiled=True),
            lax.all_gather(b_down, "grp", axis=0, tiled=True),
        )
        grad_field, totals = backward_pass(backward_params, saved, cotangent[index], totals)
        gradients.append(grad_field)
    owned = (
        lax.psum_scatter(
            totals[0].astype(jnp.bfloat16), "grp", scatter_dimension=0, tiled=True
        ).astype(jnp.float32),
        lax.psum_scatter(
            totals[1].astype(jnp.bfloat16), "grp", scatter_dimension=0, tiled=True
        ).astype(jnp.float32),
        lax.psum_scatter(
            totals[2].astype(jnp.bfloat16), "grp", scatter_dimension=0, tiled=True
        ).astype(jnp.float32),
        lax.psum_scatter(
            totals[3].astype(jnp.bfloat16), "grp", scatter_dimension=0, tiled=True
        ).astype(jnp.float32),
        lax.psum_scatter(
            totals[4].astype(jnp.bfloat16), "grp", scatter_dimension=0, tiled=True
        ).astype(jnp.float32),
        lax.psum_scatter(
            totals[5].astype(jnp.bfloat16), "grp", scatter_dimension=0, tiled=True
        ).astype(jnp.float32),
        lax.psum_scatter(
            totals[6].astype(jnp.bfloat16), "grp", scatter_dimension=0, tiled=True
        ).astype(jnp.float32),
        lax.psum_scatter(
            totals[7].astype(jnp.bfloat16), "grp", scatter_dimension=0, tiled=True
        ).astype(jnp.float32),
        lax.psum_scatter(
            totals[8].astype(jnp.bfloat16), "grp", scatter_dimension=0, tiled=True
        ).astype(jnp.float32),
        lax.psum_scatter(
            totals[9].astype(jnp.bfloat16), "grp", scatter_dimension=0, tiled=True
        ).astype(jnp.float32),
        lax.psum_scatter(
            totals[10].astype(jnp.bfloat16), "grp", scatter_dimension=0, tiled=True
        ).astype(jnp.float32),
        lax.psum_scatter(
            totals[11].astype(jnp.bfloat16), "grp", scatter_dimension=0, tiled=True
        ).astype(jnp.float32),
    )
    summed = (
        lax.psum(owned[0].astype(jnp.bfloat16), "rep").astype(jnp.float32),
        lax.psum(owned[1].astype(jnp.bfloat16), "rep").astype(jnp.float32),
        lax.psum(owned[2].astype(jnp.bfloat16), "rep").astype(jnp.float32),
        lax.psum(owned[3].astype(jnp.bfloat16), "rep").astype(jnp.float32),
        lax.psum(owned[4].astype(jnp.bfloat16), "rep").astype(jnp.float32),
        lax.psum(owned[5].astype(jnp.bfloat16), "rep").astype(jnp.float32),
        lax.psum(owned[6].astype(jnp.bfloat16), "rep").astype(jnp.float32),
        lax.psum(owned[7].astype(jnp.bfloat16), "rep").astype(jnp.float32),
        lax.psum(owned[8].astype(jnp.bfloat16), "rep").astype(jnp.float32),
        lax.psum(owned[9].astype(jnp.bfloat16), "rep").astype(jnp.float32),
        lax.psum(owned[10].astype(jnp.bfloat16), "rep").astype(jnp.float32),
        lax.psum(owned[11].astype(jnp.bfloat16), "rep").astype(jnp.float32),
    )
    output = jnp.stack(outputs, axis=0)
    grad_tokens = jnp.stack(gradients, axis=0)
    return (
        output,
        grad_tokens,
        summed[0],
        summed[1],
        summed[2],
        summed[3],
        summed[4],
        summed[5],
        summed[6],
        summed[7],
        summed[8],
        summed[9],
        summed[10],
        summed[11],
    )


def spread(mesh):
    placed = (
        P("rep", "grp", None),
        P(None, "rep", "grp"),
        P("grp"),
        P("grp"),
        P("grp", None),
        P("grp"),
        P("grp", None),
        P("grp"),
        P("grp"),
        P("grp"),
        P("grp", None),
        P("grp"),
        P("grp", None),
        P("grp"),
        P("rep", "grp", None),
    )
    return jax.shard_map(
        local,
        mesh=mesh,
        in_specs=placed,
        out_specs=(
            P("rep", "grp", None),
            P("rep", "grp", None),
            P("grp"),
            P("grp"),
            P("grp", None),
            P("grp"),
            P("grp", None),
            P("grp"),
            P("grp"),
            P("grp"),
            P("grp", None),
            P("grp"),
            P("grp", None),
            P("grp"),
        ),
        check_vma=False,
    )


def solution(mesh):
    reps, groups = mesh.devices.shape
    flat = mesh.devices.reshape(-1)

    def run(*args):
        clips = args[0].shape[0] // reps
        if reps == 8 and groups == 2 * clips:
            split = Mesh(flat.reshape(reps // 2, 2, groups), ("rp", "core", "grp"))
            ins, outs = paired_specs()
            return jax.shard_map(
                paired, mesh=split, in_specs=ins, out_specs=outs, check_vma=False
            )(*args)
        return spread(mesh)(*args)

    return run
```

```python
import functools

import jax
import jax.numpy as jnp
from jax import lax
from jax.experimental import pallas as pl
from jax.experimental.pallas import tpu as pltpu
from jax.sharding import Mesh
from jax.sharding import PartitionSpec as P

SCALE = 0.125
EPS = 1e-06
HEAD = 64
BF = jnp.bfloat16
F32 = jnp.float32
MESH = pl.DeviceIdType.MESH
ANY = pl.BlockSpec(memory_space=pl.ANY)
VM = pl.BlockSpec(memory_space=pltpu.VMEM)


def where_am_i():
    return lax.axis_index("rp"), lax.axis_index("core"), lax.axis_index("grp")


def remote(src, dst, send, recv, target):
    return pltpu.make_async_remote_copy(
        src_ref=src,
        dst_ref=dst,
        send_sem=send,
        recv_sem=recv,
        device_id=target,
        device_id_type=MESH,
    )


def enter(p, c, z, groups):
    barrier = pltpu.get_barrier_semaphore()
    for k in range(groups):
        for d in range(2):
            if k == 0 and d == 0:
                continue
            pl.semaphore_signal(
                barrier, inc=1, device_id=(p, c ^ d, lax.rem(z + k, groups)), device_id_type=MESH
            )
    for b in (1, 2):
        pl.semaphore_signal(barrier, inc=1, device_id=(p ^ b, c, z), device_id_type=MESH)
    pl.semaphore_wait(barrier, 2 * groups - 1 + 2)


def move_tokens(refs, outs, send, recv, p, c, z, clips):
    core, slot = lax.div(z, clips), lax.rem(z, clips)

    def route(i):
        return core, c * clips + i

    def here(i):
        return jnp.logical_and(core == c, c * clips + i == z)

    def start(k, pieces):
        for n, (src, dst) in enumerate(zip(refs, outs)):
            rows = src.shape[1] // pieces
            rows = pl.ds(k * rows, rows)
            for i in range(clips):
                tc, tz = route(i)

                @pl.when(here(i))
                def _():
                    pltpu.make_async_copy(
                        src.at[i, rows], dst.at[slot, rows], recv.at[n, slot]
                    ).start()

                @pl.when(jnp.logical_not(here(i)))
                def _():
                    remote(
                        src.at[i, rows],
                        dst.at[slot, rows],
                        send.at[n, i],
                        recv.at[n, slot],
                        (p, tc, tz),
                    ).start()

    def finish():
        for n, (src, dst) in enumerate(zip(refs, outs)):
            for i in range(clips):

                @pl.when(jnp.logical_not(here(i)))
                def _():
                    remote(
                        src.at[i], dst.at[slot], send.at[n, i], recv.at[n, slot], (p, c ^ 1, z)
                    ).wait_send()

            for m in range(clips):
                pltpu.make_async_copy(src.at[0], dst.at[m], recv.at[n, m]).wait()

    return start, finish


def cuts(whole, half, c, blocks):
    if blocks == 0:
        return [(whole.at[c], half)]
    size = half.shape[3] // blocks
    return [
        (
            whole.at[:, :, :, pl.ds(pl.multiple_of((2 * b + c) * size, size), size)],
            half.at[:, :, :, pl.ds(b * size, size)],
        )
        for b in range(blocks)
    ]


def gather_body(groups, clips, blocks, *refs):
    count = len(blocks)
    raw, (small, x, pos, dy) = refs[:count], refs[count : count + 4]
    outs = refs[count + 4 : 2 * count + 4]
    small_o, x_o, pos_o, dy_o = refs[2 * count + 4 : 2 * count + 8]
    halves = refs[2 * count + 8 : 3 * count + 8]
    zs, zr, xs, xr, ys, yr, fs, fr, hs, ls, ss, sr, ts, tr, us, ur, vs, vr = refs[
        3 * count + 8 :
    ]
    p, c, z = where_am_i()
    for w in range(count):
        for src, dst in cuts(raw[w], halves[w], c, blocks[w]):
            pltpu.make_async_copy(src, dst, hs.at[w]).start()
    enter(p, c, z, groups)
    col = [(p, c, lax.rem(z + k, groups)) for k in range(groups)]
    org = [lax.rem(z + groups - k, groups) for k in range(groups)]
    xn, yn = (p ^ 1, c, z), (p ^ 2, c, z)
    start_pos, finish_pos = move_tokens((pos,), (pos_o,), vs, vr, p, c, z, clips)
    start_x, finish_x = move_tokens((x,), (x_o,), ts, tr, p, c, z, clips)
    smalls = [
        remote(small, small_o.at[z], ss.at[k], sr.at[k], col[k]) for k in range(1, groups)
    ]
    for s in smalls:
        s.start()
    keep = [pltpu.make_async_copy(small, small_o.at[z], ls.at[count])]
    keep[0].start()
    start_dy, finish_dy = move_tokens((dy,), (dy_o,), us, ur, p, c, z, clips)
    units = [(w, d, side) for w in range(count) for d in range(1, groups) for side in range(2)]

    def origin(d, side):
        return z - d if side == 0 else z + d

    def arrives(d, side):
        return z >= d if side == 0 else z + d < groups

    def leaves(d, side):
        if side == 0:
            return jnp.logical_and(z + 1 < groups, z + 1 >= d)
        return jnp.logical_and(z >= 1, z - 1 + d < groups)

    def hop(w, d, side, src):
        o = origin(d - 1, side)
        target = (p, c, lax.rem(z + 1 if side == 0 else z + groups - 1, groups))
        return remote(src, outs[w].at[o, p], zs.at[w, side, d], zr.at[w, side, d], target)

    def own(w):
        pltpu.make_async_copy(halves[w], halves[w], hs.at[w]).wait()
        keep.append(pltpu.make_async_copy(halves[w], outs[w].at[z], ls.at[w]))
        keep[-1].start()
        for side in range(2):

            @pl.when(leaves(1, side))
            def _():
                hop(w, 1, side, halves[w].at[p]).start()

    def links(u):
        w, d, side = u
        o = outs[w].at[lax.rem(origin(d, side) + groups, groups)]
        e, f = xs.at[w, side, d], xr.at[w, side, d]
        g, h = ys.at[w, side, d], yr.at[w, side, d]
        a, b = fs.at[w, side, d, 0], fr.at[w, side, d, 0]
        m, n = fs.at[w, side, d, 1], fr.at[w, side, d, 1]
        across = lambda q: remote(o.at[q], o.at[q], e, f, xn)
        along = lambda q: remote(o.at[q], o.at[q], g, h, yn)
        first = lambda q: remote(o.at[q, 0], o.at[q, 0], a, b, yn)
        second = lambda q: remote(o.at[q, 1], o.at[q, 1], m, n, xn)
        return o, across, along, first, second

    def plane(u):
        w, d, side = u
        o, across, along, first, second = links(u)

        @pl.when(arrives(d, side))
        def _():
            remote(o.at[p], o.at[p], zs.at[w, side, d], zr.at[w, side, d], xn).wait_recv()
            if d + 1 < groups:

                @pl.when(leaves(d + 1, side))
                def _():
                    hop(w, d + 1, side, o.at[p]).start()

            across(p).start()
            along(p).start()

    def forward(u):
        w, d, side = u
        o, across, along, first, second = links(u)

        @pl.when(arrives(d, side))
        def _():
            across(p ^ 1).wait_recv()
            first(p ^ 1).start()
            along(p ^ 2).wait_recv()
            second(p ^ 2).start()

    def settle(u):
        w, d, side = u
        o, across, along, first, second = links(u)

        @pl.when(arrives(d, side))
        def _():
            first(p ^ 3).wait_recv()
            second(p ^ 3).wait_recv()
            across(p).wait_send()
            along(p).wait_send()
            first(p).wait_send()
            second(p).wait_send()

        @pl.when(leaves(d, side))
        def _():
            hop(w, d, side, halves[w].at[p]).wait_send()

    own(0)
    start_pos(0, 1)
    own(1)
    moves = {2 * k: (start_x, k) for k in range(4)}
    moves.update({10 + 3 * k: (start_dy, k) for k in range(4)})
    lag = 3
    for n in range(len(units) + lag):
        if n < len(units):
            plane(units[n])
            w, d, side = units[n]
            if (d, side) == (1, 1) and w + 2 < count:
                own(w + 2)
            if n in moves:
                moves[n][0](moves[n][1], 4)
        if n >= lag:
            forward(units[n - lag])
    for u in units:
        settle(u)
    for k in range(1, groups):
        remote(small, small_o.at[org[k]], ss.at[k], sr.at[k], col[k]).wait_recv()
    for s in smalls:
        s.wait_send()
    for k in keep:
        k.wait()
    finish_pos()
    finish_x()
    finish_dy()


def half_shape(raw, blocks):
    return raw.shape[1:] if blocks == 0 else raw.shape[:3] + (raw.shape[3] // 2,)


def gather(raw, blocks, small, x, pos, dy, groups):
    count, clips = len(raw), x.shape[0]
    dma = pltpu.SemaphoreType.DMA
    halves = [half_shape(r, b) for r, b in zip(raw, blocks)]
    shapes = [jax.ShapeDtypeStruct((groups,) + h, BF) for h in halves]
    shapes += [jax.ShapeDtypeStruct((groups,) + small.shape, small.dtype)]
    shapes += [jax.ShapeDtypeStruct(v.shape, v.dtype) for v in (x, pos, dy)]
    return pl.pallas_call(
        functools.partial(gather_body, groups, clips, blocks),
        out_shape=shapes,
        in_specs=[ANY] * count + [VM, ANY, ANY, ANY],
        out_specs=[ANY] * len(shapes),
        scratch_shapes=[pltpu.VMEM(h, BF) for h in halves]
        + [dma((count, 2, groups))] * 6
        + [dma((count, 2, groups, 2))] * 2
        + [dma((count,)), dma((count + 1,)), dma((groups,)), dma((groups,))]
        + [dma((1, clips))] * 6,
        compiler_params=pltpu.CompilerParams(collective_id=0, has_side_effects=True),
        name="gather",
    )(*raw, small, x, pos, dy)


def turn(u, cosine, sine):
    half = HEAD // 2
    first, second = u[:half], u[half:]
    return jnp.concatenate(
        [first * cosine - second * sine, first * sine + second * cosine], axis=0
    )


def dot(a, b):
    return jnp.dot(a, b, preferred_element_type=F32)


def dot_t(a, b):
    return lax.dot_general(a, b, (((1,), (1,)), ((), ())), preferred_element_type=F32)


def tile(i, size):
    return pl.ds(pl.multiple_of(i * size, size), size)


def backward_body(groups, clips, blocks, *refs):
    count = len(blocks)
    (gw2, gw1, gu, w1, wo, wq, mix, qs, kr, vb, h1, x2, x, dy, base, rest) = refs[:16]
    (lse, cosine, sine, g1, g2, gbu) = refs[16:22]
    outs = refs[22 : 22 + count]
    small_o, gx_o, y_o = refs[22 + count : 25 + count]
    (gu_b, w1_b, wo_b, mix_b, qs_b, kr_b, vb_b, h1_b, x2_b, x_b, dy_b) = refs[25 + count : 36 + count]
    (own_f, give, take, y_take, dx2, low, da, gwo, gwq, ak, av, dq2, dk2, acc, gx) = refs[
        36 + count : 51 + count
    ]
    ld, es, er = refs[51 + count : 54 + count]
    grads = (gwq, gwo, gw1, gw2)
    scratch = refs[54 + count :]
    own_a, own_b, one_a, one_b, two_a, two_b, three, full = (
        scratch[i * count : (i + 1) * count] for i in range(8)
    )
    small_s, small_r, small_z = scratch[8 * count : 8 * count + 3]
    (os, s1, r1, s2, r2, s3, r3, s4, r4, s5, r5, cs, cr, ls, ss, sr, ts, tr, us, ur) = scratch[
        8 * count + 3 :
    ]
    own, width = own_f.shape
    inner = mix_b.shape[0]
    third_width = wq.shape[1]
    pairs = ((gu, gu_b), (w1, w1_b), (wo, wo_b), (mix, mix_b), (qs, qs_b), (kr, kr_b), (vb, vb_b))
    pairs += ((h1, h1_b), (x2, x2_b), (x, x_b), (dy, dy_b))
    loads = [pltpu.make_async_copy(a, b, ld.at[n]) for n, (a, b) in enumerate(pairs)]
    for copy in loads:
        copy.start()
    p, c, z = where_am_i()
    hi, lo = lax.div(p, 2), lax.rem(p, 2)
    enter(p, c, z, groups)
    col = [(p, c, lax.rem(z + k, groups)) for k in range(groups)]
    xn, yn, cn = (p ^ 1, c, z), (p ^ 2, c, z), (p, c ^ 1, z)
    order = (3, 2, 1, 0)
    units = [(w, j) for w in order for j in [*range(1, groups), 0]]
    sides = ((own_a, one_a, two_a, hi, yn), (own_b, one_b, two_b, lo, xn))

    def c1(u, n):
        w, j = u
        g = grads[w].at[lax.rem(z + j, groups)]
        src, target = (g.at[:, 1 - lo, 0], xn) if n == 0 else (g.at[1 - hi, :, 1], yn)
        return remote(src, sides[n][1][w].at[j], s1.at[w, j, n], r1.at[w, j, n], target)

    def load(u, n):
        w, j = u
        g = grads[w].at[lax.rem(z + j, groups)]
        src = g.at[:, lo, 0] if n == 0 else g.at[hi, :, 1]
        return pltpu.make_async_copy(src, sides[n][0][w].at[j], os.at[w, j, n])

    def c2(u, n):
        w, j = u
        own, one, two, side, target = sides[n]
        return remote(own[w].at[j, 1 - side], two[w].at[j], s2.at[w, j, n], r2.at[w, j, n], target)

    def c3(u, n):
        w, j = u
        src = sides[n][0][w].at[j, sides[n][3]]
        return remote(src, three[w].at[j, n], s3.at[w, j, n], r3.at[w, j, n], col[j])

    def c4(w, n):
        f = full[w].at[p]
        return remote(f, f, s4.at[w, n], r4.at[w, n], (xn, yn)[n])

    def c5(w, n):
        f = full[w].at[(p ^ 1, p ^ 2)[n], n]
        return remote(f, f, s5.at[w, n], r5.at[w, n], (yn, xn)[n])

    def stage_zero(u):
        for n in range(2):
            c1(u, n).start()
            load(u, n).start()

    def stage_one(u):
        w, j = u
        for n, (own, one, two, side, target) in enumerate(sides):
            load(u, n).wait()
            c1(u, n).wait_recv()
            own[w][j] = (own[w][j].astype(F32) + one[w][j].astype(F32)).astype(BF)
            c2(u, n).start()

    def stage_two(u):
        w, j = u
        for n, (own, one, two, side, target) in enumerate(sides):
            c2(u, n).wait_recv()
            own[w][j, side] = (own[w][j, side].astype(F32) + two[w][j].astype(F32)).astype(BF)
            if j:
                c3(u, n).start()

    def stage_three(w):
        for n, (own, one, two, side, target) in enumerate(sides):
            total = own[w][0, side].astype(F32)
            for j in range(1, groups):
                c3((w, j), n).wait_recv()
                total = total + three[w][j, n].astype(F32)
            full[w][p, n] = total.astype(BF)
        for n in range(2):
            c4(w, n).start()

    def stage_four(w):
        for n, target in enumerate((yn, xn)):
            f = full[w].at[(p ^ 1, p ^ 2)[n]]
            remote(f, f, s4.at[w, n], r4.at[w, n], target).wait_recv()
            c5(w, n).start()

    def stage_five(w):
        for n in range(2):
            f = full[w].at[p ^ 3, n]
            remote(f, f, s5.at[w, n], r5.at[w, n], xn).wait_recv()
        for dst, src in cuts(outs[w], full[w], c, blocks[w]):
            pltpu.make_async_copy(src, dst, ls.at[w]).start()
            remote(src, dst, cs.at[w], cr.at[w], cn).start()

    ahead, lag = 3, 2
    todo = {}
    for n, u in enumerate(units):
        todo.setdefault(max(n - ahead, -1), []).append((stage_zero, u))
        todo.setdefault(n, []).append((stage_one, u))
        todo.setdefault(n + lag, []).append((stage_two, u))
    for i, w in enumerate(order):
        last = (i + 1) * groups - 1 + lag
        for at, stage in ((2, stage_three), (3, stage_four), (4, stage_five)):
            todo.setdefault(last + at, []).append((stage, w))
    steps = sorted(todo)

    def run(step):
        for stage, what in todo[step]:
            stage(what)

    def tick():
        run(steps.pop(0))

    def half_sum(n, left, right, depth):
        def other(i, carry):
            part = dot_t(left[own:, :depth], right[tile(i, 256), :depth])
            give[:, tile(i, 256)] = part.astype(BF)
            return carry

        def self(i, carry):
            own_f[:, tile(i, 256)] = dot_t(left[:own, :depth], right[tile(i, 256), :depth])
            return carry

        lax.fori_loop(0, width // 256, other, 0)
        copy = remote(give, take, es.at[n], er.at[n], cn)
        copy.start()
        lax.fori_loop(0, width // 256, self, 0)
        return copy

    def part(i):
        per = own // clips // 128
        return lax.div(i, per), tile(lax.rem(i, per), 128)

    def norm_step(i, field, gain, grad, row):
        at = tile(i, 128)
        d = own_f[at] + take[at].astype(F32)
        v = field[at].astype(F32)
        v = v - jnp.mean(v, axis=1, keepdims=True)
        r = lax.rsqrt(jnp.mean(v * v, axis=1, keepdims=True) + EPS)
        v = v * r
        acc[row : row + 1] += jnp.sum(d * v, axis=0, keepdims=True)
        acc[row + 1 : row + 2] += jnp.sum(d, axis=0, keepdims=True)
        e = d * gain[...]
        mean = jnp.mean(e, axis=1, keepdims=True)
        e = e - mean - v * jnp.mean(e * v, axis=1, keepdims=True)
        return grad + r * e

    tick()
    y_copy = remote(rest, y_take, es.at[3], er.at[3], cn)
    y_copy.start()
    y_base = pltpu.make_async_copy(base, dx2, ld.at[len(loads) + 1])
    y_base.start()
    acc[...] = jnp.zeros_like(acc)
    loads[0].wait()
    loads[1].wait()
    swap = half_sum(0, gu_b, w1_b, w1.shape[1])
    wq_b = w1_b.at[:, :third_width]
    dqkv = gu_b.at[:, :third_width]
    late = pltpu.make_async_copy(wq, wq_b, ld.at[len(loads)])
    late.start()
    tick()
    y_base.wait()
    y_copy.wait()

    def last_add(i, carry):
        at = tile(i, 128)
        gx[part(i)] = (dx2[at] + y_take[at].astype(F32)).astype(BF)
        return carry

    lax.fori_loop(0, own // 128, last_add, 0)
    y_start, y_finish = move_tokens((gx,), (y_o,), us, ur, p, c, z, clips)
    y_start(0, 2)
    y_start(1, 2)
    for copy in loads[2:]:
        copy.wait()
    swap.wait()

    def second_norm(i, carry):
        at = tile(i, 128)
        g = dy_b[part(i)].astype(F32)
        d = norm_step(i, x2_b, g2, g, 3)
        dx2[at] = d
        acc[5:6] += jnp.sum(g, axis=0, keepdims=True)
        low[at] = d.astype(BF)
        acc[2:3] += jnp.sum(d.astype(BF).astype(F32), axis=0, keepdims=True)
        return carry

    lax.fori_loop(0, own // 128, second_norm, 0)
    swap = remote(low.at[:own], low.at[own:], es.at[1], er.at[1], cn)
    swap.start()
    tick()
    swap.wait()

    def out_grad(i, carry):
        at = tile(i, 256)
        gwo[..., at] = dot(mix_b[...], low[:, at]).astype(BF).reshape(gwo.shape[:-1] + (256,))
        return carry

    lax.fori_loop(0, width // 256, out_grad, 0)

    def attn_grad(i, carry):
        at = tile(i, 256)
        da[:, at] = dot_t(wo_b[...], low[at]).astype(BF)
        return carry

    lax.fori_loop(0, 2 * own // 256, attn_grad, 0)
    tick()

    def head(h, side):
        rows = tile(h, HEAD)
        place = tile(side, HEAD)
        co, si = cosine[...], sine[...]
        kt = kr_b[rows]
        keys, values = kt.T, vb_b[rows].T
        queries, outer_grads = qs_b[rows].T, da[rows].T
        step = 256
        for i in range(0, 2 * own, step):
            s = slice(i, i + step)
            g = da[rows, s]
            p = jnp.exp(dot(keys, qs_b[rows, s]) - lse[h, :, s])
            delta = jnp.sum(mix_b[rows, s].astype(F32) * g.astype(F32), axis=0, keepdims=True)
            ds = (p * (dot(values, g) - delta)).astype(BF)
            dq2[place, s] = turn(dot(kt, ds) * SCALE, co[:, s], -si[:, s]).astype(BF)
            dv = dot(p.astype(BF), outer_grads[s])
            dk = dot(ds, queries[s])
            if i == 0:
                ak[...] = dk
                av[side] = dv
            else:
                ak[...] += dk
                av[side] += dv
        dk2[place] = turn(ak[...].T, co, -si).astype(BF)

    heads = inner // HEAD
    during = [steps.pop(0) for _ in range(4)]

    def two_heads(i, carry):
        lax.fori_loop(0, 2, lambda side, _: head(2 * i + side, side), None)
        for n, value in enumerate(
            (dq2[...].T, dk2[...].T, jnp.concatenate([av[0], av[1]], axis=1).astype(BF))
        ):
            at = pl.ds(pl.multiple_of(n * inner + i * 2 * HEAD, 2 * HEAD), 2 * HEAD)
            dqkv[:, at] = value
        for n, step in enumerate(during):
            pl.when(i == n * heads // 8)(functools.partial(run, step))
        return carry

    lax.fori_loop(0, heads // 2, two_heads, 0)
    row = width // groups
    for g in range(groups):
        left = h1_b[:, g * row : (g + 1) * row].T

        def in_grad(i, carry):
            at = tile(i, 512)
            gwq[g, ..., at] = dot(left, dqkv[:, at]).astype(BF).reshape(gwq.shape[1:-1] + (512,))
            return carry

        lax.fori_loop(0, third_width // 512, in_grad, 0)
    tick()
    late.wait()
    swap = half_sum(2, dqkv, wq_b, third_width)
    tick()
    swap.wait()
    y_finish()

    def first_norm(i, carry):
        gx[part(i)] = norm_step(i, x_b, g1, dx2[tile(i, 128)], 0).astype(BF)
        return carry

    lax.fori_loop(0, own // 128, first_norm, 0)
    start, finish = move_tokens((gx,), (gx_o,), ts, tr, p, c, z, clips)
    start(0, 4)
    tick()
    small_s[...] = jnp.zeros_like(small_s)
    for n in range(6):
        for g in range(groups):
            small_s[g, n : n + 1] = acc[n : n + 1, g * row : (g + 1) * row]
    half = row // 2
    mine_at = pl.ds(pl.multiple_of(c * half, half), half)
    for b in range(3 * groups):
        line = jnp.sum(dqkv[:, b * half : (b + 1) * half].astype(F32), axis=0, keepdims=True)
        small_s[b // 3, 6 + b % 3 : 7 + b % 3, mine_at] = line
    deep = gbu.shape[1] // groups
    for g in range(groups):
        for n in range(deep // row):
            at = pl.ds(9 + c * (deep // row) + n, 1)
            small_s[g, at] = gbu[:, g * deep + n * row : g * deep + (n + 1) * row]
    tick()
    for n, target in enumerate((cn, xn, yn)):
        copy = remote(small_s, small_r.at[n], ss.at[n], sr.at[n], target)
        copy.start()
        start(n + 1, 4)
        for _ in range(1 if n == 0 else 3):
            tick()
        copy.wait()
        small_s[...] += small_r[n]
    tails = [
        remote(small_s.at[col[k][2]], small_z.at[k], ss.at[2 + k], sr.at[2 + k], col[k])
        for k in range(1, groups)
    ]
    for t in tails:
        t.start()
    while steps:
        tick()
    for k in range(1, groups):
        tails[k - 1].wait()
    small_o[...] = small_s[z]
    for k in range(1, groups):
        small_o[...] += small_z[k]
    for u in units:
        w, j = u
        for n in range(2):
            c1(u, n).wait_send()
            c2(u, n).wait_send()
            if j:
                c3(u, n).wait_send()
    for w in range(count):
        for n in range(2):
            c4(w, n).wait_send()
            c5(w, n).wait_send()
        pltpu.make_async_copy(full[w], full[w], ls.at[w]).wait()
        remote(full[w], full[w], cs.at[w], cr.at[w], cn).wait()
    finish()


def backward(gw2, gw1, arrays, tables, lines, groups, blocks):
    gu, w1, wo, wq, mix, qs, kr, vb, h1, x2, x, dy, base, rest = arrays
    (own, width), clips = x.shape, dy.shape[0]
    small = jax.ShapeDtypeStruct((groups, lines + -lines % 8, width // groups), F32)
    count = len(blocks)
    dma = pltpu.SemaphoreType.DMA
    split = lambda v: (groups, 2, 2, 2, v.shape[0] // (8 * groups), v.shape[1])
    tiles = [split(wq)[4:], split(wo)[4:], gw1.shape[4:], gw2.shape[4:]]
    shapes = [
        jax.ShapeDtypeStruct((4, 2, t[0], 2 * t[1]) if b else (2, 4, 2) + t, BF)
        for t, b in zip(tiles, blocks)
    ]
    shapes += [
        jax.ShapeDtypeStruct(small.shape[1:], F32),
        jax.ShapeDtypeStruct(dy.shape, BF),
        jax.ShapeDtypeStruct(dy.shape, BF),
    ]
    scratch = [pltpu.VMEM(v.shape, v.dtype) for v in (gu, w1, wo, mix, qs, kr, vb, h1, x2, x, dy)]
    half, low = (own, width), pltpu.VMEM((2 * own, width), BF)
    scratch += [pltpu.VMEM(half, F32)] + [pltpu.VMEM(half, BF)] * 3
    scratch += [pltpu.VMEM(half, F32), low, pltpu.VMEM(mix.shape, BF)]
    scratch += [pltpu.VMEM(split(wo), BF), pltpu.VMEM(split(wq), BF)]
    scratch += [pltpu.VMEM((2 * own, HEAD), F32), pltpu.VMEM((2, 2 * own, HEAD), F32)]
    scratch += [pltpu.VMEM((2 * HEAD, 2 * own), BF)] * 2
    scratch += [pltpu.VMEM((8, width), F32), pltpu.VMEM(dy.shape, BF)]
    scratch += [dma((13,)), dma((4,)), dma((4,))]
    for lead in (
        (groups, 2),
        (groups, 2),
        (groups, 2),
        (groups, 2),
        (groups,),
        (groups,),
        (groups, 2),
        (4, 2),
    ):
        scratch += [pltpu.VMEM(lead + t, BF) for t in tiles]
    scratch += [
        pltpu.VMEM(small.shape, F32),
        pltpu.VMEM((3,) + small.shape, F32),
        pltpu.VMEM(small.shape, F32),
    ]
    pair = dma((count, groups, 2))
    scratch += [pair] * 7 + [dma((count, 2))] * 4
    scratch += [dma((count,))] * 3 + [dma((2 + groups,))] * 2 + [dma((1, clips))] * 4
    return pl.pallas_call(
        functools.partial(backward_body, groups, clips, blocks),
        out_shape=shapes,
        in_specs=[ANY] * (2 + len(arrays)) + [VM] * len(tables),
        out_specs=[ANY] * count + [VM, ANY, ANY],
        scratch_shapes=scratch,
        compiler_params=pltpu.CompilerParams(
            collective_id=1, has_side_effects=True, vmem_limit_bytes=67043328
        ),
        name="backward",
    )(gw2, gw1, *arrays, *tables)


def attention_body(step, q_ref, k_ref, v_ref, cos_ref, sin_ref, qs_ref, kr_ref, vb_ref, o_ref, l_ref):
    cosine, sine = cos_ref[...], sin_ref[...]
    length = cosine.shape[1]
    kr = turn(k_ref[...], cosine, sine).astype(BF)
    vb = v_ref[...].astype(BF)
    qs = (turn(q_ref[...], cosine, sine).astype(BF).astype(F32) * SCALE).astype(BF)
    kr_ref[...] = kr
    vb_ref[...] = vb
    qs_ref[...] = qs
    keys = kr.T
    for i in range(0, length, step):
        scores = dot(keys, qs[:, i : i + step])
        top = jnp.max(scores, axis=0, keepdims=True)
        e = jnp.exp(scores - top)
        total = jnp.sum(e, axis=0, keepdims=True)
        mixed = dot(vb, e.astype(BF))
        o_ref[:, i : i + step] = (mixed / total).astype(BF)
        l_ref[0, :, i : i + step] = top + jnp.log(total)


def attention(qkv, cosine, sine, step=256):
    rows, length = qkv.shape
    width = rows // 3
    heads = width // HEAD
    block = [pl.BlockSpec((HEAD, length), lambda h, n=n: (n * heads + h, 0)) for n in range(3)]
    table = pl.BlockSpec((HEAD // 2, length), lambda h: (0, 0))
    out = pl.BlockSpec((HEAD, length), lambda h: (h, 0))
    shape = jax.ShapeDtypeStruct((width, length), BF)
    return pl.pallas_call(
        functools.partial(attention_body, step),
        out_shape=[shape] * 4 + [jax.ShapeDtypeStruct((heads, 1, length), F32)],
        grid=(heads,),
        in_specs=block + [table, table],
        out_specs=[out] * 4 + [pl.BlockSpec((1, 1, length), lambda h: (h, 0, 0))],
        cost_estimate=pl.CostEstimate(
            flops=4 * width * length * length,
            transcendentals=heads * length * length,
            bytes_accessed=width * length * 24,
        ),
        name="attention",
    )(qkv, qkv, qkv, cosine, sine)


def swap(value):
    return lax.ppermute(value, "core", [(0, 1), (1, 0)])


def both(value):
    return jnp.concatenate([value, swap(value)], axis=0)


def contract(left, right, a, b):
    return lax.dot_general(left, right, (((a,), (b,)), ((), ())), preferred_element_type=F32)


def own_sum(partial):
    half = partial.shape[0] // 2
    return partial[:half] + swap(partial[half:].astype(BF)).astype(F32)


def paired(
    tokens,
    positions,
    ln1_gain,
    ln1_bias,
    w_qkv,
    b_qkv,
    w_out,
    b_out,
    ln2_gain,
    ln2_bias,
    w_up,
    b_up,
    w_down,
    b_down,
    cotangent,
):
    groups = lax.axis_size("grp")
    clips, part, width = tokens.shape
    hidden = w_down.shape[0] * groups
    own = clips * part
    length = 2 * own
    c, z = lax.axis_index("core"), lax.axis_index("grp")
    wide = width // 2
    deep = hidden // 2
    row = width // groups

    def pick(value, axis):
        return lax.dynamic_index_in_dim(value, c, axis, keepdims=False)

    blocks = (3 * groups, 0, groups, 0)
    raw = [
        w.reshape(((4, 2) if b else (2, 4, 2)) + (w.shape[0] // (8 if b else 16), w.shape[1]))
        for w, b in zip((w_qkv, w_out, w_up, w_down), blocks)
    ]
    bq, bu = b_qkv.shape[0] // row, b_up.shape[0] // row
    vectors = [ln1_gain, ln1_bias, b_out, ln2_gain, ln2_bias, b_down]
    vectors += [b_qkv[n * row : (n + 1) * row] for n in range(bq)]
    vectors += [b_up[n * row : (n + 1) * row] for n in range(bu)]
    lines = len(vectors)
    place = lax.broadcasted_iota(jnp.int32, (lines + -lines % 8, row), 0)
    small = jnp.zeros(place.shape, F32)
    for n, v in enumerate(vectors):
        small = jnp.where(place == n, v.astype(F32)[None, :], small)
    pos = jnp.pad(jnp.moveaxis(positions, 0, 1).astype(F32), ((0, 0), (0, 5), (0, 0)))
    wq, wo, w1, w2, small, x, pos, dy = gather(raw, blocks, small, tokens, pos, cotangent, groups)
    wq = wq.reshape(width, 3 * wide)
    wo = wo.reshape(wide, width)
    w1 = w1.reshape(width, deep)
    w2 = w2.reshape(deep, width)
    g1, b1, bo, g2, b2, bd = (small[:, n].reshape(1, width) for n in range(6))
    bq_own = pick(small[:, 6 : 6 + bq].reshape(3, groups, 2, row // 2), 2).reshape(3 * wide, 1)
    bu_own = pick(small[:, 6 + bq : lines].reshape(groups, 2, deep // groups), 1).reshape(1, deep)

    grad_out = dy.reshape(own, width)
    grad_all = both(grad_out)

    pos = jnp.moveaxis(pos[:, :3], 1, 0).reshape(3, own)
    pos = jnp.concatenate([pos, swap(pos)], axis=1)
    pair = jnp.arange(HEAD // 2)
    band = (pair >= 10).astype(jnp.int32) + (pair >= 21).astype(jnp.int32)
    begin = jnp.where(band == 0, 0, jnp.where(band == 1, 10, 21))
    count = jnp.where(band == 0, 10, 11)
    freq = jnp.power(F32(10000.0), -(pair - begin).astype(F32) / count.astype(F32))
    band = band[:, None]
    chosen = jnp.where(band == 0, pos[0:1], jnp.where(band == 1, pos[1:2], pos[2:3]))
    angles = chosen * freq[:, None]
    cosine, sine = jnp.cos(angles), jnp.sin(angles)

    tokens = x.reshape(own, width)
    x = tokens.astype(F32)
    h1 = both((normalize(x)[0] * g1 + b1).astype(BF))
    qkv = contract(wq, h1, 0, 1) + bq_own
    qs, kr, vb, mixed, lse = attention(qkv, cosine, sine)
    x2 = x + own_sum(contract(mixed, wo, 0, 0)) + bo
    h2 = both((normalize(x2)[0] * g2 + b2).astype(BF))
    u = contract(h2, w1, 1, 0) + bu_own
    cdf = 0.5 * (1.0 + lax.erf(u * F32(0.7071067811865476)))
    act = (u * cdf).astype(BF)
    slope = (cdf + u * jnp.exp(-0.5 * u * u) * F32(0.3989422804014327)).astype(BF)
    result = contract(act, w2, 1, 0)
    base, rest = x2 + result[:own] + bd, result[own:].astype(BF)

    gw2 = contract(act, grad_all, 0, 0).astype(BF)
    gu = (contract(grad_all, w2, 1, 1) * slope.astype(F32)).astype(BF)
    gw1 = contract(h2, gu, 0, 0).astype(BF)
    gbu = jnp.sum(gu.astype(F32), axis=0)
    gw2, gw1 = (
        g.reshape(groups, 2, 2, 2, g.shape[0] // (8 * groups), g.shape[1]) for g in (gw2, gw1)
    )
    arrays = (gu, w1, wo, wq, mixed, qs, kr, vb, h1, x2, tokens, dy, base, rest)
    tables = (lse, cosine, sine, g1, g2, gbu.reshape(1, deep))
    gwq, gwo, gw1, gw2, sums, gx, output = backward(gw2, gw1, arrays, tables, lines, groups, blocks)
    gwq, gwo, gw1, gw2 = (
        g.reshape(shard.shape).astype(F32)
        for g, shard in zip((gwq, gwo, gw1, gw2), (w_qkv, w_out, w_up, w_down))
    )
    gg1, gb1, gbo, gg2, gb2, gbd = (sums[n] for n in range(6))
    gbq, gbu = sums[6 : 6 + bq].reshape(-1), sums[6 + bq : lines].reshape(-1)
    return (output, gx, gg1, gb1, gwq, gbq, gwo, gbo, gg2, gb2, gw1, gbu, gw2, gbd)


def paired_specs():
    rep = ("rp", "core")
    ins = (P(rep, "grp", None), P(None, rep, "grp"))
    one, two = P("grp"), P("grp", None)
    ins += (one, one, two, one, two, one, one, one, two, one, two, one, P(rep, "grp", None))
    outs = (P(rep, "grp", None),) * 2
    outs += (one, one, two, one, two, one, one, one, two, one, two, one)
    return ins, outs


def rotary_angles(positions):
    pair = jnp.arange(32)
    band = (pair >= 10).astype(jnp.int32) + (pair >= 21).astype(jnp.int32)
    start = jnp.where(band == 0, 0, jnp.where(band == 1, 10, 21))
    count = jnp.where(band == 0, 10, 11)
    freq = jnp.power(
        jnp.float32(10000.0), -(pair - start).astype(jnp.float32) / count.astype(jnp.float32)
    )
    pos_f = positions.astype(jnp.float32)
    chosen = jnp.where(
        band[None, :] == 0,
        pos_f[0][:, None],
        jnp.where(band[None, :] == 1, pos_f[1][:, None], pos_f[2][:, None]),
    )
    return chosen * freq[None, :]


def rotate(field, cosine, sine):
    first = field[..., :32]
    second = field[..., 32:]
    return jnp.concatenate(
        [first * cosine - second * sine, first * sine + second * cosine], axis=-1
    )


def normalize(field):
    centred = field - jnp.mean(field, axis=-1, keepdims=True)
    variance = jnp.mean(centred * centred, axis=-1, keepdims=True)
    factor = lax.rsqrt(variance + EPS)
    return (centred * factor, factor)


def norm_back(grad_norm, normed, factor):
    return factor * (
        grad_norm
        - jnp.mean(grad_norm, axis=-1, keepdims=True)
        - normed * jnp.mean(grad_norm * normed, axis=-1, keepdims=True)
    )


def outer(left, right):
    return lax.dot_general(
        left, right, (((0,), (0,)), ((), ())), preferred_element_type=jnp.float32
    )


def back(left, right):
    return lax.dot_general(
        left, right, (((1,), (1,)), ((), ())), preferred_element_type=jnp.float32
    )


def exact_gelu(value):
    return jax.nn.gelu(value, approximate=False)


def column_sum(value):
    return jnp.sum(value.astype(jnp.float32), axis=0)


def forward_pass(params, field_in, positions):
    g1, b1, wqkv, bqkv, wo, bo, g2, b2, w1, bu, w2, bd = params
    field = field_in.astype(jnp.float32)
    count, width = field.shape
    heads = width // 64
    angles = rotary_angles(positions)
    cosine = jnp.cos(angles)[:, None, :]
    sine = jnp.sin(angles)[:, None, :]
    normed1, factor1 = normalize(field)
    h1 = (normed1 * g1.astype(jnp.float32) + b1.astype(jnp.float32)).astype(jnp.bfloat16)
    qkv = jnp.dot(h1, wqkv, preferred_element_type=jnp.float32) + bqkv.astype(jnp.float32)
    query_rot = rotate(qkv[:, :width].reshape(count, heads, 64), cosine, sine).astype(jnp.bfloat16)
    keys_rot = (
        rotate(qkv[:, width : 2 * width].reshape(count, heads, 64), cosine, sine)
        .astype(jnp.bfloat16)
        .reshape(count, width)
    )
    values = qkv[:, 2 * width :].astype(jnp.bfloat16)
    keys_all, values_all = (
        lax.all_gather(keys_rot, "grp", axis=0, tiled=True),
        lax.all_gather(values, "grp", axis=0, tiled=True),
    )
    total = keys_all.shape[0]
    keys_all = keys_all.reshape(total, heads, 64)
    values_all = values_all.reshape(total, heads, 64)
    scores = (
        jnp.einsum("thd,shd->hts", query_rot, keys_all, preferred_element_type=jnp.float32) * SCALE
    )
    top = jnp.max(scores, axis=-1, keepdims=True)
    lse = top + jnp.log(jnp.sum(jnp.exp(scores - top), axis=-1, keepdims=True))
    probs = jnp.exp(scores - lse).astype(jnp.bfloat16)
    mixed = (
        jnp.einsum("hts,shd->thd", probs, values_all, preferred_element_type=jnp.float32)
        .reshape(count, width)
        .astype(jnp.bfloat16)
    )
    second = field + jnp.dot(mixed, wo, preferred_element_type=jnp.float32) + bo.astype(jnp.float32)
    normed2, factor2 = normalize(second)
    h2 = (normed2 * g2.astype(jnp.float32) + b2.astype(jnp.float32)).astype(jnp.bfloat16)
    hidden = jnp.dot(h2, w1, preferred_element_type=jnp.float32) + bu.astype(jnp.float32)
    active = exact_gelu(hidden).astype(jnp.bfloat16)
    result = (
        second + jnp.dot(active, w2, preferred_element_type=jnp.float32) + bd.astype(jnp.float32)
    )
    saved = (
        normed1,
        factor1,
        h1,
        query_rot,
        keys_rot,
        values,
        lse,
        mixed,
        normed2,
        factor2,
        h2,
        hidden,
        active,
        cosine,
        sine,
    )
    return (saved, result.astype(jnp.bfloat16))


def backward_pass(params, saved, grad_in, totals):
    g1, b1, wqkv, bqkv, wo, bo, g2, b2, w1, bu, w2, bd = params
    (
        normed1,
        factor1,
        h1,
        query_rot,
        keys_rot,
        values,
        lse,
        mixed,
        normed2,
        factor2,
        h2,
        hidden,
        active,
        cosine,
        sine,
    ) = saved
    grad_out = grad_in.astype(jnp.float32)
    count, width = grad_out.shape
    heads = width // 64
    grad_y2 = grad_out.astype(jnp.bfloat16)
    grad_w2 = outer(active, grad_y2)
    grad_bd = column_sum(grad_y2)
    grad_act = back(grad_y2, w2)
    unused, pull = jax.vjp(exact_gelu, hidden)
    grad_hidden = pull(grad_act)[0].astype(jnp.bfloat16)
    grad_w1 = outer(h2, grad_hidden)
    grad_bu = column_sum(grad_hidden)
    grad_h2 = back(grad_hidden, w1)
    grad_g2 = jnp.sum(grad_h2 * normed2, axis=0)
    grad_b2 = jnp.sum(grad_h2, axis=0)
    grad_second = grad_out + norm_back(grad_h2 * g2.astype(jnp.float32), normed2, factor2)
    grad_y1 = grad_second.astype(jnp.bfloat16)
    grad_wo = outer(mixed, grad_y1)
    grad_bo = column_sum(grad_y1)
    grad_mixed = back(grad_y1, wo).astype(jnp.bfloat16).reshape(count, heads, 64)
    keys_all, values_all = (
        lax.all_gather(keys_rot, "grp", axis=0, tiled=True),
        lax.all_gather(values, "grp", axis=0, tiled=True),
    )
    total = keys_all.shape[0]
    keys_all = keys_all.reshape(total, heads, 64)
    values_all = values_all.reshape(total, heads, 64)
    scores = (
        jnp.einsum("thd,shd->hts", query_rot, keys_all, preferred_element_type=jnp.float32) * SCALE
    )
    probs = jnp.exp(scores - lse)
    grad_probs = jnp.einsum(
        "thd,shd->hts", grad_mixed, values_all, preferred_element_type=jnp.float32
    )
    delta = jnp.sum(probs * grad_probs, axis=-1, keepdims=True)
    grad_scores = (probs * (grad_probs - delta)).astype(jnp.bfloat16)
    grad_query = (
        jnp.einsum("hts,shd->thd", grad_scores, keys_all, preferred_element_type=jnp.float32)
        * SCALE
    )
    probs_low = probs.astype(jnp.bfloat16)
    grad_values = jnp.einsum(
        "hts,thd->shd", probs_low, grad_mixed, preferred_element_type=jnp.float32
    )
    grad_keys = (
        jnp.einsum("hts,thd->shd", grad_scores, query_rot, preferred_element_type=jnp.float32)
        * SCALE
    )
    keys_own, values_own = (
        lax.psum_scatter(
            grad_keys.reshape(total, width).astype(jnp.bfloat16),
            "grp",
            scatter_dimension=0,
            tiled=True,
        ).astype(jnp.float32),
        lax.psum_scatter(
            grad_values.reshape(total, width).astype(jnp.bfloat16),
            "grp",
            scatter_dimension=0,
            tiled=True,
        ).astype(jnp.float32),
    )
    query_back = rotate(grad_query, cosine, -sine).reshape(count, width)
    keys_back = rotate(keys_own.reshape(count, heads, 64), cosine, -sine).reshape(count, width)
    grad_qkv = jnp.concatenate([query_back, keys_back, values_own], axis=1).astype(jnp.bfloat16)
    grad_wqkv = outer(h1, grad_qkv)
    grad_bqkv = column_sum(grad_qkv)
    grad_h1 = back(grad_qkv, wqkv)
    grad_g1 = jnp.sum(grad_h1 * normed1, axis=0)
    grad_b1 = jnp.sum(grad_h1, axis=0)
    grad_field = grad_second + norm_back(grad_h1 * g1.astype(jnp.float32), normed1, factor1)
    terms = (
        grad_g1,
        grad_b1,
        grad_wqkv,
        grad_bqkv,
        grad_wo,
        grad_bo,
        grad_g2,
        grad_b2,
        grad_w1,
        grad_bu,
        grad_w2,
        grad_bd,
    )
    totals = tuple((a + b for a, b in zip(totals, terms)))
    return (grad_field.astype(jnp.bfloat16), totals)


def local(
    tokens,
    positions,
    ln1_gain,
    ln1_bias,
    w_qkv,
    b_qkv,
    w_out,
    b_out,
    ln2_gain,
    ln2_bias,
    w_up,
    b_up,
    w_down,
    b_down,
    cotangent,
):
    shards = (
        ln1_gain,
        ln1_bias,
        w_qkv,
        b_qkv,
        w_out,
        b_out,
        ln2_gain,
        ln2_bias,
        w_up,
        b_up,
        w_down,
        b_down,
    )
    groups = lax.axis_size("grp")
    totals = tuple((jnp.zeros((s.shape[0] * groups,) + s.shape[1:], jnp.float32) for s in shards))
    outputs = []
    gradients = []
    for index in range(tokens.shape[0]):
        forward_params = (
            lax.all_gather(ln1_gain, "grp", axis=0, tiled=True),
            lax.all_gather(ln1_bias, "grp", axis=0, tiled=True),
            lax.all_gather(w_qkv, "grp", axis=0, tiled=True),
            lax.all_gather(b_qkv, "grp", axis=0, tiled=True),
            lax.all_gather(w_out, "grp", axis=0, tiled=True),
            lax.all_gather(b_out, "grp", axis=0, tiled=True),
            lax.all_gather(ln2_gain, "grp", axis=0, tiled=True),
            lax.all_gather(ln2_bias, "grp", axis=0, tiled=True),
            lax.all_gather(w_up, "grp", axis=0, tiled=True),
            lax.all_gather(b_up, "grp", axis=0, tiled=True),
            lax.all_gather(w_down, "grp", axis=0, tiled=True),
            lax.all_gather(b_down, "grp", axis=0, tiled=True),
        )
        saved, result = forward_pass(forward_params, tokens[index], positions[:, index, :])
        outputs.append(result)
        backward_params = (
            lax.all_gather(ln1_gain, "grp", axis=0, tiled=True),
            lax.all_gather(ln1_bias, "grp", axis=0, tiled=True),
            lax.all_gather(w_qkv, "grp", axis=0, tiled=True),
            lax.all_gather(b_qkv, "grp", axis=0, tiled=True),
            lax.all_gather(w_out, "grp", axis=0, tiled=True),
            lax.all_gather(b_out, "grp", axis=0, tiled=True),
            lax.all_gather(ln2_gain, "grp", axis=0, tiled=True),
            lax.all_gather(ln2_bias, "grp", axis=0, tiled=True),
            lax.all_gather(w_up, "grp", axis=0, tiled=True),
            lax.all_gather(b_up, "grp", axis=0, tiled=True),
            lax.all_gather(w_down, "grp", axis=0, tiled=True),
            lax.all_gather(b_down, "grp", axis=0, tiled=True),
        )
        grad_field, totals = backward_pass(backward_params, saved, cotangent[index], totals)
        gradients.append(grad_field)
    owned = (
        lax.psum_scatter(
            totals[0].astype(jnp.bfloat16), "grp", scatter_dimension=0, tiled=True
        ).astype(jnp.float32),
        lax.psum_scatter(
            totals[1].astype(jnp.bfloat16), "grp", scatter_dimension=0, tiled=True
        ).astype(jnp.float32),
        lax.psum_scatter(
            totals[2].astype(jnp.bfloat16), "grp", scatter_dimension=0, tiled=True
        ).astype(jnp.float32),
        lax.psum_scatter(
            totals[3].astype(jnp.bfloat16), "grp", scatter_dimension=0, tiled=True
        ).astype(jnp.float32),
        lax.psum_scatter(
            totals[4].astype(jnp.bfloat16), "grp", scatter_dimension=0, tiled=True
        ).astype(jnp.float32),
        lax.psum_scatter(
            totals[5].astype(jnp.bfloat16), "grp", scatter_dimension=0, tiled=True
        ).astype(jnp.float32),
        lax.psum_scatter(
            totals[6].astype(jnp.bfloat16), "grp", scatter_dimension=0, tiled=True
        ).astype(jnp.float32),
        lax.psum_scatter(
            totals[7].astype(jnp.bfloat16), "grp", scatter_dimension=0, tiled=True
        ).astype(jnp.float32),
        lax.psum_scatter(
            totals[8].astype(jnp.bfloat16), "grp", scatter_dimension=0, tiled=True
        ).astype(jnp.float32),
        lax.psum_scatter(
            totals[9].astype(jnp.bfloat16), "grp", scatter_dimension=0, tiled=True
        ).astype(jnp.float32),
        lax.psum_scatter(
            totals[10].astype(jnp.bfloat16), "grp", scatter_dimension=0, tiled=True
        ).astype(jnp.float32),
        lax.psum_scatter(
            totals[11].astype(jnp.bfloat16), "grp", scatter_dimension=0, tiled=True
        ).astype(jnp.float32),
    )
    summed = (
        lax.psum(owned[0].astype(jnp.bfloat16), "rep").astype(jnp.float32),
        lax.psum(owned[1].astype(jnp.bfloat16), "rep").astype(jnp.float32),
        lax.psum(owned[2].astype(jnp.bfloat16), "rep").astype(jnp.float32),
        lax.psum(owned[3].astype(jnp.bfloat16), "rep").astype(jnp.float32),
        lax.psum(owned[4].astype(jnp.bfloat16), "rep").astype(jnp.float32),
        lax.psum(owned[5].astype(jnp.bfloat16), "rep").astype(jnp.float32),
        lax.psum(owned[6].astype(jnp.bfloat16), "rep").astype(jnp.float32),
        lax.psum(owned[7].astype(jnp.bfloat16), "rep").astype(jnp.float32),
        lax.psum(owned[8].astype(jnp.bfloat16), "rep").astype(jnp.float32),
        lax.psum(owned[9].astype(jnp.bfloat16), "rep").astype(jnp.float32),
        lax.psum(owned[10].astype(jnp.bfloat16), "rep").astype(jnp.float32),
        lax.psum(owned[11].astype(jnp.bfloat16), "rep").astype(jnp.float32),
    )
    output = jnp.stack(outputs, axis=0)
    grad_tokens = jnp.stack(gradients, axis=0)
    return (
        output,
        grad_tokens,
        summed[0],
        summed[1],
        summed[2],
        summed[3],
        summed[4],
        summed[5],
        summed[6],
        summed[7],
        summed[8],
        summed[9],
        summed[10],
        summed[11],
    )


def spread(mesh):
    placed = (
        P("rep", "grp", None),
        P(None, "rep", "grp"),
        P("grp"),
        P("grp"),
        P("grp", None),
        P("grp"),
        P("grp", None),
        P("grp"),
        P("grp"),
        P("grp"),
        P("grp", None),
        P("grp"),
        P("grp", None),
        P("grp"),
        P("rep", "grp", None),
    )
    return jax.shard_map(
        local,
        mesh=mesh,
        in_specs=placed,
        out_specs=(
            P("rep", "grp", None),
            P("rep", "grp", None),
            P("grp"),
            P("grp"),
            P("grp", None),
            P("grp"),
            P("grp", None),
            P("grp"),
            P("grp"),
            P("grp"),
            P("grp", None),
            P("grp"),
            P("grp", None),
            P("grp"),
        ),
        check_vma=False,
    )


def solution(mesh):
    reps, groups = mesh.devices.shape
    flat = mesh.devices.reshape(-1)

    def run(*args):
        clips = args[0].shape[0] // reps
        if reps == 8 and groups == 2 * clips:
            split = Mesh(flat.reshape(reps // 2, 2, groups), ("rp", "core", "grp"))
            ins, outs = paired_specs()
            return jax.shard_map(
                paired, mesh=split, in_specs=ins, out_specs=outs, check_vma=False
            )(*args)
        return spread(mesh)(*args)

    return run
```

```python
import functools

import jax
import jax.numpy as jnp
from jax import lax
from jax.experimental import pallas as pl
from jax.experimental.pallas import tpu as pltpu
from jax.sharding import Mesh
from jax.sharding import PartitionSpec as P

SCALE = 0.125
EPS = 1e-06
HEAD = 64
BF = jnp.bfloat16
F32 = jnp.float32
MESH = pl.DeviceIdType.MESH
ANY = pl.BlockSpec(memory_space=pl.ANY)
VM = pl.BlockSpec(memory_space=pltpu.VMEM)


def where_am_i():
    return lax.axis_index("rp"), lax.axis_index("core"), lax.axis_index("grp")


def remote(src, dst, send, recv, target):
    return pltpu.make_async_remote_copy(
        src_ref=src,
        dst_ref=dst,
        send_sem=send,
        recv_sem=recv,
        device_id=target,
        device_id_type=MESH,
    )


def enter(p, c, z, groups):
    barrier = pltpu.get_barrier_semaphore()
    for k in range(groups):
        for d in range(2):
            if k == 0 and d == 0:
                continue
            pl.semaphore_signal(
                barrier, inc=1, device_id=(p, c ^ d, lax.rem(z + k, groups)), device_id_type=MESH
            )
    for b in (1, 2):
        pl.semaphore_signal(barrier, inc=1, device_id=(p ^ b, c, z), device_id_type=MESH)
    pl.semaphore_wait(barrier, 2 * groups - 1 + 2)


def move_tokens(refs, outs, send, recv, p, c, z, clips):
    core, slot = lax.div(z, clips), lax.rem(z, clips)

    def route(i):
        return core, c * clips + i

    def here(i):
        return jnp.logical_and(core == c, c * clips + i == z)

    def start(k, pieces):
        for n, (src, dst) in enumerate(zip(refs, outs)):
            rows = src.shape[1] // pieces
            rows = pl.ds(k * rows, rows)
            for i in range(clips):
                tc, tz = route(i)

                @pl.when(here(i))
                def _():
                    pltpu.make_async_copy(
                        src.at[i, rows], dst.at[slot, rows], recv.at[n, slot]
                    ).start()

                @pl.when(jnp.logical_not(here(i)))
                def _():
                    remote(
                        src.at[i, rows],
                        dst.at[slot, rows],
                        send.at[n, i],
                        recv.at[n, slot],
                        (p, tc, tz),
                    ).start()

    def sent():
        for n, (src, dst) in enumerate(zip(refs, outs)):
            for i in range(clips):

                @pl.when(jnp.logical_not(here(i)))
                def _():
                    remote(
                        src.at[i], dst.at[slot], send.at[n, i], recv.at[n, slot], (p, c ^ 1, z)
                    ).wait_send()

    def arrive():
        for n, (src, dst) in enumerate(zip(refs, outs)):
            for m in range(clips):
                pltpu.make_async_copy(src.at[0], dst.at[m], recv.at[n, m]).wait()

    def finish():
        sent()
        arrive()

    return start, finish, sent, arrive


def turn(u, cosine, sine):
    half = HEAD // 2
    first, second = u[:half], u[half:]
    return jnp.concatenate(
        [first * cosine - second * sine, first * sine + second * cosine], axis=0
    )


def dot(a, b):
    return jnp.dot(a, b, preferred_element_type=F32)


def dot_t(a, b):
    return lax.dot_general(a, b, (((1,), (1,)), ((), ())), preferred_element_type=F32)


def tile(i, size):
    return pl.ds(pl.multiple_of(i * size, size), size)


def cuts(whole, half, c, blocks):
    if blocks == 0:
        return [(whole.at[c], half)]
    size = half.shape[3] // blocks
    return [
        (
            whole.at[:, :, :, pl.ds(pl.multiple_of((2 * b + c) * size, size), size)],
            half.at[:, :, :, pl.ds(b * size, size)],
        )
        for b in range(blocks)
    ]


def forward_body(groups, clips, blocks, *refs):
    count = len(blocks)
    raw, (small, x, tab, dy) = refs[:count], refs[count : count + 4]
    (wq_o, *outs) = refs[count + 4 : 2 * count + 4]
    (small_o, x_o, tab_o, dy_o, h1_o, qs_o, kr_o, vb_o, mix_o, lse_o) = refs[2 * count + 4 : 2 * count + 14]
    halves = refs[2 * count + 14 : 3 * count + 14]
    (wq_v, small_v, x_v, tab_v, tab_w, h1, qs, kr, vb, mix, qkv, gain, bias) = refs[
        3 * count + 14 : 3 * count + 27
    ]
    (zs, zr, xs, xr, ys, yr, fs, fr, hs, ls, ss, sr, ts, tr, us, ur, vs, vr, es, er, ks) = refs[
        3 * count + 27 :
    ]
    outs = [wq_v, *outs]
    p, c, z = where_am_i()
    for w in range(count):
        for src, dst in cuts(raw[w], halves[w], c, blocks[w]):
            pltpu.make_async_copy(src, dst, hs.at[w]).start()
    enter(p, c, z, groups)
    col = [(p, c, lax.rem(z + k, groups)) for k in range(groups)]
    org = [lax.rem(z + groups - k, groups) for k in range(groups)]
    xn, yn, cn = (p ^ 1, c, z), (p ^ 2, c, z), (p, c ^ 1, z)
    smalls = [
        remote(small, small_v.at[z], ss.at[k], sr.at[k], col[k]) for k in range(1, groups)
    ]
    for s in smalls:
        s.start()
    keep = [pltpu.make_async_copy(small, small_v.at[z], ls.at[count])]
    keep[0].start()
    start_tab, _, sent_tab, arrive_tab = move_tokens((tab,), (tab_v,), vs, vr, p, c, z, clips)
    start_x, _, sent_x, arrive_x = move_tokens((x,), (x_v,), ts, tr, p, c, z, clips)
    start_dy, finish_dy, *_ = move_tokens((dy,), (dy_o,), us, ur, p, c, z, clips)
    units = [(w, d, side) for w in range(count) for d in range(1, groups) for side in range(2)]

    def origin(d, side):
        return z - d if side == 0 else z + d

    def arrives(d, side):
        return z >= d if side == 0 else z + d < groups

    def leaves(d, side):
        if side == 0:
            return jnp.logical_and(z + 1 < groups, z + 1 >= d)
        return jnp.logical_and(z >= 1, z - 1 + d < groups)

    def hop(w, d, side, src):
        o = origin(d - 1, side)
        target = (p, c, lax.rem(z + 1 if side == 0 else z + groups - 1, groups))
        return remote(src, outs[w].at[o, p], zs.at[w, side, d], zr.at[w, side, d], target)

    def own(w):
        pltpu.make_async_copy(halves[w], halves[w], hs.at[w]).wait()
        keep.append(pltpu.make_async_copy(halves[w], outs[w].at[z], ls.at[w]))
        keep[-1].start()
        for side in range(2):

            @pl.when(leaves(1, side))
            def _():
                hop(w, 1, side, halves[w].at[p]).start()

    def links(u):
        w, d, side = u
        o = outs[w].at[lax.rem(origin(d, side) + groups, groups)]
        e, f = xs.at[w, side, d], xr.at[w, side, d]
        g, h = ys.at[w, side, d], yr.at[w, side, d]
        a, b = fs.at[w, side, d, 0], fr.at[w, side, d, 0]
        m, n = fs.at[w, side, d, 1], fr.at[w, side, d, 1]
        across = lambda q: remote(o.at[q], o.at[q], e, f, xn)
        along = lambda q: remote(o.at[q], o.at[q], g, h, yn)
        first = lambda q: remote(o.at[q, 0], o.at[q, 0], a, b, yn)
        second = lambda q: remote(o.at[q, 1], o.at[q, 1], m, n, xn)
        return o, across, along, first, second

    def plane(u):
        w, d, side = u
        o, across, along, first, second = links(u)

        @pl.when(arrives(d, side))
        def _():
            remote(o.at[p], o.at[p], zs.at[w, side, d], zr.at[w, side, d], xn).wait_recv()
            if d + 1 < groups:

                @pl.when(leaves(d + 1, side))
                def _():
                    hop(w, d + 1, side, o.at[p]).start()

            across(p).start()
            along(p).start()

    def forward(u):
        w, d, side = u
        o, across, along, first, second = links(u)

        @pl.when(arrives(d, side))
        def _():
            across(p ^ 1).wait_recv()
            first(p ^ 1).start()
            along(p ^ 2).wait_recv()
            second(p ^ 2).start()

    def complete(u):
        w, d, side = u
        o, across, along, first, second = links(u)

        @pl.when(arrives(d, side))
        def _():
            first(p ^ 3).wait_recv()
            second(p ^ 3).wait_recv()

    def settle(u):
        w, d, side = u
        o, across, along, first, second = links(u)

        @pl.when(arrives(d, side))
        def _():
            across(p).wait_send()
            along(p).wait_send()
            first(p).wait_send()
            second(p).wait_send()

        @pl.when(leaves(d, side))
        def _():
            hop(w, d, side, halves[w].at[p]).wait_send()

    own(0)
    start_tab(0, 1)
    own(1)
    moves = {2 * k: (start_x, k) for k in range(4)}
    moves.update({10 + 3 * k: (start_dy, k) for k in range(4)})
    lag = 3

    def step(n):
        if n < len(units):
            plane(units[n])
            w, d, side = units[n]
            if (d, side) == (1, 1) and w + 2 < count:
                own(w + 2)
            if n in moves:
                moves[n][0](moves[n][1], 4)
        if n >= lag:
            forward(units[n - lag])

    steps = list(range(len(units) + lag))
    early = 2 * (groups - 1) + lag
    for _ in range(early):
        step(steps.pop(0))
    for k in range(1, groups):
        remote(small, small_v.at[org[k]], ss.at[k], sr.at[k], col[k]).wait_recv()
    keep[0].wait()
    row = small_v.shape[2]
    half = row // 2
    mine = pl.ds(pl.multiple_of(c * half, half), half)
    for g in range(groups):
        gain[0:2, g * row : (g + 1) * row] = small_v[g, 0:2]
        for r in range(3):
            bias[3 * g + r : 3 * g + r + 1] = small_v[g, 6 + r : 7 + r, mine]
    small_o[...] = small_v[...]
    own_count = h1.shape[0] // 2
    arrive_x()
    saves = [pltpu.make_async_copy(x_v, x_o, ks.at[0])]
    saves[0].start()

    def norm(i, carry):
        per = own_count // clips // 128
        v = x_v[lax.div(i, per), tile(lax.rem(i, per), 128)].astype(F32)
        v = v - jnp.mean(v, axis=1, keepdims=True)
        v = v * lax.rsqrt(jnp.mean(v * v, axis=1, keepdims=True) + EPS)
        h1[tile(i, 128)] = (v * gain[0:1] + gain[1:2]).astype(BF)
        return carry

    lax.fori_loop(0, own_count // 128, norm, 0)
    swap = remote(h1.at[:own_count], h1.at[own_count:], es.at[0], er.at[0], cn)
    swap.start()
    arrive_tab()
    swap_tab = remote(tab_v, tab_w, es.at[1], er.at[1], cn)
    swap_tab.start()
    step(steps.pop(0))
    swap_tab.wait()
    part = tab_v.shape[2]
    for m in range(clips):
        tab_o[:, m * part : (m + 1) * part] = tab_v[m]
        tab_o[:, own_count + m * part : own_count + (m + 1) * part] = tab_w[m]
    for u in units[: 2 * (groups - 1)]:
        complete(u)
    keep[1].wait()
    saves.append(pltpu.make_async_copy(wq_v, wq_o, ks.at[1]))
    saves[1].start()
    swap.wait()
    saves.append(pltpu.make_async_copy(h1, h1_o, ks.at[2]))
    saves[2].start()
    inner = qs.shape[0]
    heads = inner // HEAD
    pairs = heads // 2

    def head(h, side):
        rows, place = tile(h, HEAD), tile(side, HEAD)
        co, si = tab_o[: HEAD // 2], tab_o[HEAD // 2 :]
        k = turn(qkv[1, place], co, si).astype(BF)
        v = qkv[2, place].astype(BF)
        q = (turn(qkv[0, place], co, si).astype(BF).astype(F32) * SCALE).astype(BF)
        kr[rows] = k
        vb[rows] = v
        qs[rows] = q
        keys = k.T
        size = 256
        for i in range(0, 2 * own_count, size):
            scores = dot(keys, q[:, i : i + size])
            top = jnp.max(scores, axis=0, keepdims=True)
            e = jnp.exp(scores - top)
            total = jnp.sum(e, axis=0, keepdims=True)
            mixed = dot(v, e.astype(BF))
            mix[rows, i : i + size] = (mixed / total).astype(BF)
            lse_o[h, :, i : i + size] = top + jnp.log(total)

    during = [steps.pop(0) for _ in range(heads + heads // 2)]

    def two_heads(i, carry):
        def project(n, carry):
            at = pl.ds(pl.multiple_of(n * inner + i * 2 * HEAD, 2 * HEAD), 2 * HEAD)
            w = wq_v[..., at].reshape(h1.shape[1], 2 * HEAD)
            qkv[n] = (dot(h1[...], w) + bias[pl.ds(n * pairs + i, 1)]).T
            return carry

        lax.fori_loop(0, 3, project, 0)
        for n in range(pairs):

            @pl.when(i == n)
            def _():
                step(during[3 * n])

        def one(side, carry):
            head(2 * i + side, side)
            for n in range(heads):

                @pl.when(2 * i + side == n)
                def _():
                    step(during[3 * (n // 2) + 1 + n % 2])

            return carry

        lax.fori_loop(0, 2, one, 0)
        return carry

    lax.fori_loop(0, pairs, two_heads, 0)
    for n, (a, b) in enumerate(((qs, qs_o), (kr, kr_o), (vb, vb_o), (mix, mix_o))):
        saves.append(pltpu.make_async_copy(a, b, ks.at[3 + n]))
        saves[-1].start()
    while steps:
        step(steps.pop(0))
    for u in units[2 * (groups - 1) :]:
        complete(u)
    for u in units:
        settle(u)
    for s in smalls:
        s.wait_send()
    for k in keep[2:] + saves:
        k.wait()
    sent_tab()
    sent_x()
    finish_dy()


def half_shape(raw, blocks):
    return raw.shape[1:] if blocks == 0 else raw.shape[:3] + (raw.shape[3] // 2,)


def forward(raw, blocks, small, x, tab, dy, groups):
    count, clips = len(raw), x.shape[0]
    own, width = clips * x.shape[1], x.shape[2]
    halves = [half_shape(r, b) for r, b in zip(raw, blocks)]
    inner = halves[0][-1] // 3
    dma = pltpu.SemaphoreType.DMA
    of = jax.ShapeDtypeStruct
    feature = (inner, 2 * own)
    shapes = [of((groups,) + h, BF) for h in halves]
    shapes += [of((groups,) + small.shape, F32), of(x.shape, BF), of((HEAD, 2 * own), F32)]
    shapes += [of(x.shape, BF), of((2 * own, width), BF)] + [of(feature, BF)] * 4
    shapes += [of((inner // HEAD, 1, 2 * own), F32)]
    vm = pltpu.VMEM
    scratch = [vm(h, BF) for h in halves]
    scratch += [vm((groups,) + halves[0], BF), vm((groups,) + small.shape, F32), vm(x.shape, BF)]
    scratch += [vm(tab.shape, F32)] * 2 + [vm((2 * own, width), BF)] + [vm(feature, BF)] * 4
    scratch += [vm((3, 2 * HEAD, 2 * own), F32), vm((8, width), F32)]
    scratch += [vm((3 * groups + -3 * groups % 8, width // groups // 2), F32)]
    return pl.pallas_call(
        functools.partial(forward_body, groups, clips, blocks),
        out_shape=shapes,
        in_specs=[ANY] * count + [VM, ANY, ANY, ANY],
        out_specs=[ANY] * count + [VM, ANY, VM] + [ANY] * 6 + [VM],
        scratch_shapes=scratch
        + [dma((count, 2, groups))] * 6
        + [dma((count, 2, groups, 2))] * 2
        + [dma((count,)), dma((count + 1,)), dma((groups,)), dma((groups,))]
        + [dma((1, clips))] * 6
        + [dma((2,)), dma((2,)), dma((7,))],
        compiler_params=pltpu.CompilerParams(
            collective_id=0, has_side_effects=True, vmem_limit_bytes=60 * 1024 * 1024
        ),
        name="forward",
    )(*raw, small, x, tab, dy)


def backward_body(groups, clips, blocks, *refs):
    count = len(blocks)
    (gw2, gw1, gu, w1, wo, wq, mix, qs, kr, vb, h1, x2, x, dy, base, rest) = refs[:16]
    (lse, cosine, sine, g1, g2, gbu) = refs[16:22]
    outs = refs[22 : 22 + count]
    small_o, gx_o, y_o = refs[22 + count : 25 + count]
    (gu_b, w1_b, wo_b, mix_b, qs_b, kr_b, vb_b, h1_b, x2_b, x_b, dy_b) = refs[25 + count : 36 + count]
    (own_f, give, take, y_take, dx2, low, da, gwo, gwq, ak, av, dq2, dk2, acc, gx) = refs[
        36 + count : 51 + count
    ]
    ld, es, er = refs[51 + count : 54 + count]
    grads = (gwq, gwo, gw1, gw2)
    scratch = refs[54 + count :]
    own_a, own_b, one_a, one_b, two_a, two_b, three, full = (
        scratch[i * count : (i + 1) * count] for i in range(8)
    )
    small_s, small_r, small_z = scratch[8 * count : 8 * count + 3]
    (os, s1, r1, s2, r2, s3, r3, s4, r4, s5, r5, cs, cr, ls, ss, sr, ts, tr, us, ur) = scratch[
        8 * count + 3 :
    ]
    own, width = own_f.shape
    inner = mix_b.shape[0]
    third_width = wq.shape[1]
    pairs = ((gu, gu_b), (w1, w1_b), (wo, wo_b), (mix, mix_b), (qs, qs_b), (kr, kr_b), (vb, vb_b))
    pairs += ((h1, h1_b), (x2, x2_b), (x, x_b), (dy, dy_b))
    loads = [pltpu.make_async_copy(a, b, ld.at[n]) for n, (a, b) in enumerate(pairs)]
    for copy in loads:
        copy.start()
    p, c, z = where_am_i()
    hi, lo = lax.div(p, 2), lax.rem(p, 2)
    enter(p, c, z, groups)
    col = [(p, c, lax.rem(z + k, groups)) for k in range(groups)]
    xn, yn, cn = (p ^ 1, c, z), (p ^ 2, c, z), (p, c ^ 1, z)
    order = (3, 2, 1, 0)
    units = [(w, j) for w in order for j in [*range(1, groups), 0]]
    sides = ((own_a, one_a, two_a, hi, yn), (own_b, one_b, two_b, lo, xn))

    def c1(u, n):
        w, j = u
        g = grads[w].at[lax.rem(z + j, groups)]
        src, target = (g.at[:, 1 - lo, 0], xn) if n == 0 else (g.at[1 - hi, :, 1], yn)
        return remote(src, sides[n][1][w].at[j], s1.at[w, j, n], r1.at[w, j, n], target)

    def load(u, n):
        w, j = u
        g = grads[w].at[lax.rem(z + j, groups)]
        src = g.at[:, lo, 0] if n == 0 else g.at[hi, :, 1]
        return pltpu.make_async_copy(src, sides[n][0][w].at[j], os.at[w, j, n])

    def c2(u, n):
        w, j = u
        own, one, two, side, target = sides[n]
        return remote(own[w].at[j, 1 - side], two[w].at[j], s2.at[w, j, n], r2.at[w, j, n], target)

    def c3(u, n):
        w, j = u
        src = sides[n][0][w].at[j, sides[n][3]]
        return remote(src, three[w].at[j, n], s3.at[w, j, n], r3.at[w, j, n], col[j])

    def c4(w, n):
        f = full[w].at[p]
        return remote(f, f, s4.at[w, n], r4.at[w, n], (xn, yn)[n])

    def c5(w, n):
        f = full[w].at[(p ^ 1, p ^ 2)[n], n]
        return remote(f, f, s5.at[w, n], r5.at[w, n], (yn, xn)[n])

    def stage_zero(u):
        for n in range(2):
            c1(u, n).start()
            load(u, n).start()

    def stage_one(u):
        w, j = u
        for n, (own, one, two, side, target) in enumerate(sides):
            load(u, n).wait()
            c1(u, n).wait_recv()
            own[w][j] = (own[w][j].astype(F32) + one[w][j].astype(F32)).astype(BF)
            c2(u, n).start()

    def stage_two(u):
        w, j = u
        for n, (own, one, two, side, target) in enumerate(sides):
            c2(u, n).wait_recv()
            own[w][j, side] = (own[w][j, side].astype(F32) + two[w][j].astype(F32)).astype(BF)
            if j:
                c3(u, n).start()

    def stage_three(w):
        for n, (own, one, two, side, target) in enumerate(sides):
            total = own[w][0, side].astype(F32)
            for j in range(1, groups):
                c3((w, j), n).wait_recv()
                total = total + three[w][j, n].astype(F32)
            full[w][p, n] = total.astype(BF)
        for n in range(2):
            c4(w, n).start()

    def stage_four(w):
        for n, target in enumerate((yn, xn)):
            f = full[w].at[(p ^ 1, p ^ 2)[n]]
            remote(f, f, s4.at[w, n], r4.at[w, n], target).wait_recv()
            c5(w, n).start()

    def stage_five(w):
        for n in range(2):
            f = full[w].at[p ^ 3, n]
            remote(f, f, s5.at[w, n], r5.at[w, n], xn).wait_recv()
        for dst, src in cuts(outs[w], full[w], c, blocks[w]):
            pltpu.make_async_copy(src, dst, ls.at[w]).start()
            remote(src, dst, cs.at[w], cr.at[w], cn).start()

    ahead, lag = 3, 2
    todo = {}
    for n, u in enumerate(units):
        todo.setdefault(max(n - ahead, -1), []).append((stage_zero, u))
        todo.setdefault(n, []).append((stage_one, u))
        todo.setdefault(n + lag, []).append((stage_two, u))
    for i, w in enumerate(order):
        last = (i + 1) * groups - 1 + lag
        for at, stage in ((2, stage_three), (3, stage_four), (4, stage_five)):
            todo.setdefault(last + at, []).append((stage, w))
    steps = sorted(todo)

    def run(step):
        for stage, what in todo[step]:
            stage(what)

    def tick():
        run(steps.pop(0))

    def half_sum(n, left, right, depth):
        def other(i, carry):
            part = dot_t(left[own:, :depth], right[tile(i, 256), :depth])
            give[:, tile(i, 256)] = part.astype(BF)
            return carry

        def self(i, carry):
            own_f[:, tile(i, 256)] = dot_t(left[:own, :depth], right[tile(i, 256), :depth])
            return carry

        lax.fori_loop(0, width // 256, other, 0)
        copy = remote(give, take, es.at[n], er.at[n], cn)
        copy.start()
        lax.fori_loop(0, width // 256, self, 0)
        return copy

    def part(i):
        per = own // clips // 128
        return lax.div(i, per), tile(lax.rem(i, per), 128)

    def norm_step(i, field, gain, grad, row):
        at = tile(i, 128)
        d = own_f[at] + take[at].astype(F32)
        v = field[at].astype(F32)
        v = v - jnp.mean(v, axis=1, keepdims=True)
        r = lax.rsqrt(jnp.mean(v * v, axis=1, keepdims=True) + EPS)
        v = v * r
        acc[row : row + 1] += jnp.sum(d * v, axis=0, keepdims=True)
        acc[row + 1 : row + 2] += jnp.sum(d, axis=0, keepdims=True)
        e = d * gain[...]
        mean = jnp.mean(e, axis=1, keepdims=True)
        e = e - mean - v * jnp.mean(e * v, axis=1, keepdims=True)
        return grad + r * e

    tick()
    y_copy = remote(rest, y_take, es.at[3], er.at[3], cn)
    y_copy.start()
    y_base = pltpu.make_async_copy(base, dx2, ld.at[len(loads) + 1])
    y_base.start()
    acc[...] = jnp.zeros_like(acc)
    loads[0].wait()
    loads[1].wait()
    swap = half_sum(0, gu_b, w1_b, w1.shape[1])
    wq_b = w1_b.at[:, :third_width]
    dqkv = gu_b.at[:, :third_width]
    late = pltpu.make_async_copy(wq, wq_b, ld.at[len(loads)])
    late.start()
    tick()
    y_base.wait()
    y_copy.wait()

    def last_add(i, carry):
        at = tile(i, 128)
        gx[part(i)] = (dx2[at] + y_take[at].astype(F32)).astype(BF)
        return carry

    lax.fori_loop(0, own // 128, last_add, 0)
    y_start, y_finish, *_ = move_tokens((gx,), (y_o,), us, ur, p, c, z, clips)
    y_start(0, 2)
    y_start(1, 2)
    for copy in loads[2:]:
        copy.wait()
    swap.wait()

    def second_norm(i, carry):
        at = tile(i, 128)
        g = dy_b[part(i)].astype(F32)
        d = norm_step(i, x2_b, g2, g, 3)
        dx2[at] = d
        acc[5:6] += jnp.sum(g, axis=0, keepdims=True)
        low[at] = d.astype(BF)
        acc[2:3] += jnp.sum(d.astype(BF).astype(F32), axis=0, keepdims=True)
        return carry

    lax.fori_loop(0, own // 128, second_norm, 0)
    swap = remote(low.at[:own], low.at[own:], es.at[1], er.at[1], cn)
    swap.start()
    tick()
    swap.wait()

    def out_grad(i, carry):
        at = tile(i, 256)
        gwo[..., at] = dot(mix_b[...], low[:, at]).astype(BF).reshape(gwo.shape[:-1] + (256,))
        return carry

    lax.fori_loop(0, width // 256, out_grad, 0)

    def attn_grad(i, carry):
        at = tile(i, 256)
        da[:, at] = dot_t(wo_b[...], low[at]).astype(BF)
        return carry

    lax.fori_loop(0, 2 * own // 256, attn_grad, 0)
    tick()

    def head(h, side):
        rows = tile(h, HEAD)
        place = tile(side, HEAD)
        co, si = cosine[...], sine[...]
        kt = kr_b[rows]
        keys, values = kt.T, vb_b[rows].T
        queries, outer_grads = qs_b[rows].T, da[rows].T
        step = 256
        for i in range(0, 2 * own, step):
            s = slice(i, i + step)
            g = da[rows, s]
            p = jnp.exp(dot(keys, qs_b[rows, s]) - lse[h, :, s])
            delta = jnp.sum(mix_b[rows, s].astype(F32) * g.astype(F32), axis=0, keepdims=True)
            ds = (p * (dot(values, g) - delta)).astype(BF)
            dq2[place, s] = turn(dot(kt, ds) * SCALE, co[:, s], -si[:, s]).astype(BF)
            dv = dot(p.astype(BF), outer_grads[s])
            dk = dot(ds, queries[s])
            if i == 0:
                ak[...] = dk
                av[side] = dv
            else:
                ak[...] += dk
                av[side] += dv
        dk2[place] = turn(ak[...].T, co, -si).astype(BF)

    heads = inner // HEAD
    during = [steps.pop(0) for _ in range(4)]

    def two_heads(i, carry):
        lax.fori_loop(0, 2, lambda side, _: head(2 * i + side, side), None)
        for n, value in enumerate(
            (dq2[...].T, dk2[...].T, jnp.concatenate([av[0], av[1]], axis=1).astype(BF))
        ):
            at = pl.ds(pl.multiple_of(n * inner + i * 2 * HEAD, 2 * HEAD), 2 * HEAD)
            dqkv[:, at] = value
        for n, step in enumerate(during):
            pl.when(i == n * heads // 8)(functools.partial(run, step))
        return carry

    lax.fori_loop(0, heads // 2, two_heads, 0)
    row = width // groups
    for g in range(groups):
        left = h1_b[:, g * row : (g + 1) * row].T

        def in_grad(i, carry):
            at = tile(i, 512)
            gwq[g, ..., at] = dot(left, dqkv[:, at]).astype(BF).reshape(gwq.shape[1:-1] + (512,))
            return carry

        lax.fori_loop(0, third_width // 512, in_grad, 0)
    tick()
    late.wait()
    swap = half_sum(2, dqkv, wq_b, third_width)
    tick()
    swap.wait()
    y_finish()

    def first_norm(i, carry):
        gx[part(i)] = norm_step(i, x_b, g1, dx2[tile(i, 128)], 0).astype(BF)
        return carry

    lax.fori_loop(0, own // 128, first_norm, 0)
    start, finish, *_ = move_tokens((gx,), (gx_o,), ts, tr, p, c, z, clips)
    start(0, 4)
    tick()
    small_s[...] = jnp.zeros_like(small_s)
    for n in range(6):
        for g in range(groups):
            small_s[g, n : n + 1] = acc[n : n + 1, g * row : (g + 1) * row]
    half = row // 2
    mine_at = pl.ds(pl.multiple_of(c * half, half), half)
    for b in range(3 * groups):
        line = jnp.sum(dqkv[:, b * half : (b + 1) * half].astype(F32), axis=0, keepdims=True)
        small_s[b // 3, 6 + b % 3 : 7 + b % 3, mine_at] = line
    deep = gbu.shape[1] // groups
    for g in range(groups):
        for n in range(deep // row):
            at = pl.ds(9 + c * (deep // row) + n, 1)
            small_s[g, at] = gbu[:, g * deep + n * row : g * deep + (n + 1) * row]
    tick()
    for n, target in enumerate((cn, xn, yn)):
        copy = remote(small_s, small_r.at[n], ss.at[n], sr.at[n], target)
        copy.start()
        start(n + 1, 4)
        for _ in range(1 if n == 0 else 3):
            tick()
        copy.wait()
        small_s[...] += small_r[n]
    tails = [
        remote(small_s.at[col[k][2]], small_z.at[k], ss.at[2 + k], sr.at[2 + k], col[k])
        for k in range(1, groups)
    ]
    for t in tails:
        t.start()
    while steps:
        tick()
    for k in range(1, groups):
        tails[k - 1].wait()
    small_o[...] = small_s[z]
    for k in range(1, groups):
        small_o[...] += small_z[k]
    for u in units:
        w, j = u
        for n in range(2):
            c1(u, n).wait_send()
            c2(u, n).wait_send()
            if j:
                c3(u, n).wait_send()
    for w in range(count):
        for n in range(2):
            c4(w, n).wait_send()
            c5(w, n).wait_send()
        pltpu.make_async_copy(full[w], full[w], ls.at[w]).wait()
        remote(full[w], full[w], cs.at[w], cr.at[w], cn).wait()
    finish()


def backward(gw2, gw1, arrays, tables, lines, groups, blocks):
    gu, w1, wo, wq, mix, qs, kr, vb, h1, x2, x, dy, base, rest = arrays
    (own, width), clips = x.shape, dy.shape[0]
    small = jax.ShapeDtypeStruct((groups, lines + -lines % 8, width // groups), F32)
    count = len(blocks)
    dma = pltpu.SemaphoreType.DMA
    split = lambda v: (groups, 2, 2, 2, v.shape[0] // (8 * groups), v.shape[1])
    tiles = [split(wq)[4:], split(wo)[4:], gw1.shape[4:], gw2.shape[4:]]
    shapes = [
        jax.ShapeDtypeStruct((4, 2, t[0], 2 * t[1]) if b else (2, 4, 2) + t, BF)
        for t, b in zip(tiles, blocks)
    ]
    shapes += [
        jax.ShapeDtypeStruct(small.shape[1:], F32),
        jax.ShapeDtypeStruct(dy.shape, BF),
        jax.ShapeDtypeStruct(dy.shape, BF),
    ]
    scratch = [pltpu.VMEM(v.shape, v.dtype) for v in (gu, w1, wo, mix, qs, kr, vb, h1, x2, x, dy)]
    half, low = (own, width), pltpu.VMEM((2 * own, width), BF)
    scratch += [pltpu.VMEM(half, F32)] + [pltpu.VMEM(half, BF)] * 3
    scratch += [pltpu.VMEM(half, F32), low, pltpu.VMEM(mix.shape, BF)]
    scratch += [pltpu.VMEM(split(wo), BF), pltpu.VMEM(split(wq), BF)]
    scratch += [pltpu.VMEM((2 * own, HEAD), F32), pltpu.VMEM((2, 2 * own, HEAD), F32)]
    scratch += [pltpu.VMEM((2 * HEAD, 2 * own), BF)] * 2
    scratch += [pltpu.VMEM((8, width), F32), pltpu.VMEM(dy.shape, BF)]
    scratch += [dma((13,)), dma((4,)), dma((4,))]
    for lead in (
        (groups, 2),
        (groups, 2),
        (groups, 2),
        (groups, 2),
        (groups,),
        (groups,),
        (groups, 2),
        (4, 2),
    ):
        scratch += [pltpu.VMEM(lead + t, BF) for t in tiles]
    scratch += [
        pltpu.VMEM(small.shape, F32),
        pltpu.VMEM((3,) + small.shape, F32),
        pltpu.VMEM(small.shape, F32),
    ]
    pair = dma((count, groups, 2))
    scratch += [pair] * 7 + [dma((count, 2))] * 4
    scratch += [dma((count,))] * 3 + [dma((2 + groups,))] * 2 + [dma((1, clips))] * 4
    return pl.pallas_call(
        functools.partial(backward_body, groups, clips, blocks),
        out_shape=shapes,
        in_specs=[ANY] * (2 + len(arrays)) + [VM] * len(tables),
        out_specs=[ANY] * count + [VM, ANY, ANY],
        scratch_shapes=scratch,
        compiler_params=pltpu.CompilerParams(
            collective_id=1, has_side_effects=True, vmem_limit_bytes=67043328
        ),
        name="backward",
    )(gw2, gw1, *arrays, *tables)


def swap(value):
    return lax.ppermute(value, "core", [(0, 1), (1, 0)])


def both(value):
    return jnp.concatenate([value, swap(value)], axis=0)


def contract(left, right, a, b):
    return lax.dot_general(left, right, (((a,), (b,)), ((), ())), preferred_element_type=F32)


def own_sum(partial):
    half = partial.shape[0] // 2
    return partial[:half] + swap(partial[half:].astype(BF)).astype(F32)


def paired(
    tokens,
    positions,
    ln1_gain,
    ln1_bias,
    w_qkv,
    b_qkv,
    w_out,
    b_out,
    ln2_gain,
    ln2_bias,
    w_up,
    b_up,
    w_down,
    b_down,
    cotangent,
):
    groups = lax.axis_size("grp")
    clips, part, width = tokens.shape
    hidden = w_down.shape[0] * groups
    own = clips * part
    length = 2 * own
    c, z = lax.axis_index("core"), lax.axis_index("grp")
    wide = width // 2
    deep = hidden // 2
    row = width // groups

    def pick(value, axis):
        return lax.dynamic_index_in_dim(value, c, axis, keepdims=False)

    blocks = (3 * groups, 0, groups, 0)
    raw = [
        w.reshape(((4, 2) if b else (2, 4, 2)) + (w.shape[0] // (8 if b else 16), w.shape[1]))
        for w, b in zip((w_qkv, w_out, w_up, w_down), blocks)
    ]
    bq, bu = b_qkv.shape[0] // row, b_up.shape[0] // row
    vectors = [ln1_gain, ln1_bias, b_out, ln2_gain, ln2_bias, b_down]
    vectors += [b_qkv[n * row : (n + 1) * row] for n in range(bq)]
    vectors += [b_up[n * row : (n + 1) * row] for n in range(bu)]
    lines = len(vectors)
    place = lax.broadcasted_iota(jnp.int32, (lines + -lines % 8, row), 0)
    small = jnp.zeros(place.shape, F32)
    for n, v in enumerate(vectors):
        small = jnp.where(place == n, v.astype(F32)[None, :], small)
    pair = jnp.arange(HEAD // 2)
    band = (pair >= 10).astype(jnp.int32) + (pair >= 21).astype(jnp.int32)
    begin = jnp.where(band == 0, 0, jnp.where(band == 1, 10, 21))
    number = jnp.where(band == 0, 10, 11)
    freq = jnp.power(F32(10000.0), -(pair - begin).astype(F32) / number.astype(F32))
    pos = positions.astype(F32)[:, :, None, :]
    band = band[None, :, None]
    chosen = jnp.where(band == 0, pos[0], jnp.where(band == 1, pos[1], pos[2]))
    angles = chosen * freq[None, :, None]
    tab = jnp.concatenate([jnp.cos(angles), jnp.sin(angles)], axis=1)
    wq, wo, w1, w2, small, x, tab, dy, h1, qs, kr, vb, mixed, lse = forward(
        raw, blocks, small, tokens, tab, cotangent, groups
    )
    cosine, sine = tab[: HEAD // 2], tab[HEAD // 2 :]
    wq = wq.reshape(width, 3 * wide)
    wo = wo.reshape(wide, width)
    w1 = w1.reshape(width, deep)
    w2 = w2.reshape(deep, width)
    g1, b1, bo, g2, b2, bd = (small[:, n].reshape(1, width) for n in range(6))
    bu_own = pick(small[:, 6 + bq : lines].reshape(groups, 2, deep // groups), 1).reshape(1, deep)
    grad_out = dy.reshape(own, width)
    grad_all = both(grad_out)
    tokens = x.reshape(own, width)
    x = tokens.astype(F32)
    x2 = x + own_sum(contract(mixed, wo, 0, 0)) + bo
    h2 = both((normalize(x2)[0] * g2 + b2).astype(BF))
    u = contract(h2, w1, 1, 0) + bu_own
    cdf = 0.5 * (1.0 + lax.erf(u * F32(0.7071067811865476)))
    act = (u * cdf).astype(BF)
    slope = (cdf + u * jnp.exp(-0.5 * u * u) * F32(0.3989422804014327)).astype(BF)
    result = contract(act, w2, 1, 0)
    base, rest = x2 + result[:own] + bd, result[own:].astype(BF)

    gw2 = contract(act, grad_all, 0, 0).astype(BF)
    gu = (contract(grad_all, w2, 1, 1) * slope.astype(F32)).astype(BF)
    gw1 = contract(h2, gu, 0, 0).astype(BF)
    gbu = jnp.sum(gu.astype(F32), axis=0)
    gw2, gw1 = (
        g.reshape(groups, 2, 2, 2, g.shape[0] // (8 * groups), g.shape[1]) for g in (gw2, gw1)
    )
    arrays = (gu, w1, wo, wq, mixed, qs, kr, vb, h1, x2, tokens, dy, base, rest)
    tables = (lse, cosine, sine, g1, g2, gbu.reshape(1, deep))
    gwq, gwo, gw1, gw2, sums, gx, output = backward(gw2, gw1, arrays, tables, lines, groups, blocks)
    gwq, gwo, gw1, gw2 = (
        g.reshape(shard.shape).astype(F32)
        for g, shard in zip((gwq, gwo, gw1, gw2), (w_qkv, w_out, w_up, w_down))
    )
    gg1, gb1, gbo, gg2, gb2, gbd = (sums[n] for n in range(6))
    gbq, gbu = sums[6 : 6 + bq].reshape(-1), sums[6 + bq : lines].reshape(-1)
    return (output, gx, gg1, gb1, gwq, gbq, gwo, gbo, gg2, gb2, gw1, gbu, gw2, gbd)


def paired_specs():
    rep = ("rp", "core")
    ins = (P(rep, "grp", None), P(None, rep, "grp"))
    one, two = P("grp"), P("grp", None)
    ins += (one, one, two, one, two, one, one, one, two, one, two, one, P(rep, "grp", None))
    outs = (P(rep, "grp", None),) * 2
    outs += (one, one, two, one, two, one, one, one, two, one, two, one)
    return ins, outs


def rotary_angles(positions):
    pair = jnp.arange(32)
    band = (pair >= 10).astype(jnp.int32) + (pair >= 21).astype(jnp.int32)
    start = jnp.where(band == 0, 0, jnp.where(band == 1, 10, 21))
    count = jnp.where(band == 0, 10, 11)
    freq = jnp.power(
        jnp.float32(10000.0), -(pair - start).astype(jnp.float32) / count.astype(jnp.float32)
    )
    pos_f = positions.astype(jnp.float32)
    chosen = jnp.where(
        band[None, :] == 0,
        pos_f[0][:, None],
        jnp.where(band[None, :] == 1, pos_f[1][:, None], pos_f[2][:, None]),
    )
    return chosen * freq[None, :]


def rotate(field, cosine, sine):
    first = field[..., :32]
    second = field[..., 32:]
    return jnp.concatenate(
        [first * cosine - second * sine, first * sine + second * cosine], axis=-1
    )


def normalize(field):
    centred = field - jnp.mean(field, axis=-1, keepdims=True)
    variance = jnp.mean(centred * centred, axis=-1, keepdims=True)
    factor = lax.rsqrt(variance + EPS)
    return (centred * factor, factor)


def norm_back(grad_norm, normed, factor):
    return factor * (
        grad_norm
        - jnp.mean(grad_norm, axis=-1, keepdims=True)
        - normed * jnp.mean(grad_norm * normed, axis=-1, keepdims=True)
    )


def outer(left, right):
    return lax.dot_general(
        left, right, (((0,), (0,)), ((), ())), preferred_element_type=jnp.float32
    )


def back(left, right):
    return lax.dot_general(
        left, right, (((1,), (1,)), ((), ())), preferred_element_type=jnp.float32
    )


def exact_gelu(value):
    return jax.nn.gelu(value, approximate=False)


def column_sum(value):
    return jnp.sum(value.astype(jnp.float32), axis=0)


def forward_pass(params, field_in, positions):
    g1, b1, wqkv, bqkv, wo, bo, g2, b2, w1, bu, w2, bd = params
    field = field_in.astype(jnp.float32)
    count, width = field.shape
    heads = width // 64
    angles = rotary_angles(positions)
    cosine = jnp.cos(angles)[:, None, :]
    sine = jnp.sin(angles)[:, None, :]
    normed1, factor1 = normalize(field)
    h1 = (normed1 * g1.astype(jnp.float32) + b1.astype(jnp.float32)).astype(jnp.bfloat16)
    qkv = jnp.dot(h1, wqkv, preferred_element_type=jnp.float32) + bqkv.astype(jnp.float32)
    query_rot = rotate(qkv[:, :width].reshape(count, heads, 64), cosine, sine).astype(jnp.bfloat16)
    keys_rot = (
        rotate(qkv[:, width : 2 * width].reshape(count, heads, 64), cosine, sine)
        .astype(jnp.bfloat16)
        .reshape(count, width)
    )
    values = qkv[:, 2 * width :].astype(jnp.bfloat16)
    keys_all, values_all = (
        lax.all_gather(keys_rot, "grp", axis=0, tiled=True),
        lax.all_gather(values, "grp", axis=0, tiled=True),
    )
    total = keys_all.shape[0]
    keys_all = keys_all.reshape(total, heads, 64)
    values_all = values_all.reshape(total, heads, 64)
    scores = (
        jnp.einsum("thd,shd->hts", query_rot, keys_all, preferred_element_type=jnp.float32) * SCALE
    )
    top = jnp.max(scores, axis=-1, keepdims=True)
    lse = top + jnp.log(jnp.sum(jnp.exp(scores - top), axis=-1, keepdims=True))
    probs = jnp.exp(scores - lse).astype(jnp.bfloat16)
    mixed = (
        jnp.einsum("hts,shd->thd", probs, values_all, preferred_element_type=jnp.float32)
        .reshape(count, width)
        .astype(jnp.bfloat16)
    )
    second = field + jnp.dot(mixed, wo, preferred_element_type=jnp.float32) + bo.astype(jnp.float32)
    normed2, factor2 = normalize(second)
    h2 = (normed2 * g2.astype(jnp.float32) + b2.astype(jnp.float32)).astype(jnp.bfloat16)
    hidden = jnp.dot(h2, w1, preferred_element_type=jnp.float32) + bu.astype(jnp.float32)
    active = exact_gelu(hidden).astype(jnp.bfloat16)
    result = (
        second + jnp.dot(active, w2, preferred_element_type=jnp.float32) + bd.astype(jnp.float32)
    )
    saved = (
        normed1,
        factor1,
        h1,
        query_rot,
        keys_rot,
        values,
        lse,
        mixed,
        normed2,
        factor2,
        h2,
        hidden,
        active,
        cosine,
        sine,
    )
    return (saved, result.astype(jnp.bfloat16))


def backward_pass(params, saved, grad_in, totals):
    g1, b1, wqkv, bqkv, wo, bo, g2, b2, w1, bu, w2, bd = params
    (
        normed1,
        factor1,
        h1,
        query_rot,
        keys_rot,
        values,
        lse,
        mixed,
        normed2,
        factor2,
        h2,
        hidden,
        active,
        cosine,
        sine,
    ) = saved
    grad_out = grad_in.astype(jnp.float32)
    count, width = grad_out.shape
    heads = width // 64
    grad_y2 = grad_out.astype(jnp.bfloat16)
    grad_w2 = outer(active, grad_y2)
    grad_bd = column_sum(grad_y2)
    grad_act = back(grad_y2, w2)
    unused, pull = jax.vjp(exact_gelu, hidden)
    grad_hidden = pull(grad_act)[0].astype(jnp.bfloat16)
    grad_w1 = outer(h2, grad_hidden)
    grad_bu = column_sum(grad_hidden)
    grad_h2 = back(grad_hidden, w1)
    grad_g2 = jnp.sum(grad_h2 * normed2, axis=0)
    grad_b2 = jnp.sum(grad_h2, axis=0)
    grad_second = grad_out + norm_back(grad_h2 * g2.astype(jnp.float32), normed2, factor2)
    grad_y1 = grad_second.astype(jnp.bfloat16)
    grad_wo = outer(mixed, grad_y1)
    grad_bo = column_sum(grad_y1)
    grad_mixed = back(grad_y1, wo).astype(jnp.bfloat16).reshape(count, heads, 64)
    keys_all, values_all = (
        lax.all_gather(keys_rot, "grp", axis=0, tiled=True),
        lax.all_gather(values, "grp", axis=0, tiled=True),
    )
    total = keys_all.shape[0]
    keys_all = keys_all.reshape(total, heads, 64)
    values_all = values_all.reshape(total, heads, 64)
    scores = (
        jnp.einsum("thd,shd->hts", query_rot, keys_all, preferred_element_type=jnp.float32) * SCALE
    )
    probs = jnp.exp(scores - lse)
    grad_probs = jnp.einsum(
        "thd,shd->hts", grad_mixed, values_all, preferred_element_type=jnp.float32
    )
    delta = jnp.sum(probs * grad_probs, axis=-1, keepdims=True)
    grad_scores = (probs * (grad_probs - delta)).astype(jnp.bfloat16)
    grad_query = (
        jnp.einsum("hts,shd->thd", grad_scores, keys_all, preferred_element_type=jnp.float32)
        * SCALE
    )
    probs_low = probs.astype(jnp.bfloat16)
    grad_values = jnp.einsum(
        "hts,thd->shd", probs_low, grad_mixed, preferred_element_type=jnp.float32
    )
    grad_keys = (
        jnp.einsum("hts,thd->shd", grad_scores, query_rot, preferred_element_type=jnp.float32)
        * SCALE
    )
    keys_own, values_own = (
        lax.psum_scatter(
            grad_keys.reshape(total, width).astype(jnp.bfloat16),
            "grp",
            scatter_dimension=0,
            tiled=True,
        ).astype(jnp.float32),
        lax.psum_scatter(
            grad_values.reshape(total, width).astype(jnp.bfloat16),
            "grp",
            scatter_dimension=0,
            tiled=True,
        ).astype(jnp.float32),
    )
    query_back = rotate(grad_query, cosine, -sine).reshape(count, width)
    keys_back = rotate(keys_own.reshape(count, heads, 64), cosine, -sine).reshape(count, width)
    grad_qkv = jnp.concatenate([query_back, keys_back, values_own], axis=1).astype(jnp.bfloat16)
    grad_wqkv = outer(h1, grad_qkv)
    grad_bqkv = column_sum(grad_qkv)
    grad_h1 = back(grad_qkv, wqkv)
    grad_g1 = jnp.sum(grad_h1 * normed1, axis=0)
    grad_b1 = jnp.sum(grad_h1, axis=0)
    grad_field = grad_second + norm_back(grad_h1 * g1.astype(jnp.float32), normed1, factor1)
    terms = (
        grad_g1,
        grad_b1,
        grad_wqkv,
        grad_bqkv,
        grad_wo,
        grad_bo,
        grad_g2,
        grad_b2,
        grad_w1,
        grad_bu,
        grad_w2,
        grad_bd,
    )
    totals = tuple((a + b for a, b in zip(totals, terms)))
    return (grad_field.astype(jnp.bfloat16), totals)


def local(
    tokens,
    positions,
    ln1_gain,
    ln1_bias,
    w_qkv,
    b_qkv,
    w_out,
    b_out,
    ln2_gain,
    ln2_bias,
    w_up,
    b_up,
    w_down,
    b_down,
    cotangent,
):
    shards = (
        ln1_gain,
        ln1_bias,
        w_qkv,
        b_qkv,
        w_out,
        b_out,
        ln2_gain,
        ln2_bias,
        w_up,
        b_up,
        w_down,
        b_down,
    )
    groups = lax.axis_size("grp")
    totals = tuple((jnp.zeros((s.shape[0] * groups,) + s.shape[1:], jnp.float32) for s in shards))
    outputs = []
    gradients = []
    for index in range(tokens.shape[0]):
        forward_params = (
            lax.all_gather(ln1_gain, "grp", axis=0, tiled=True),
            lax.all_gather(ln1_bias, "grp", axis=0, tiled=True),
            lax.all_gather(w_qkv, "grp", axis=0, tiled=True),
            lax.all_gather(b_qkv, "grp", axis=0, tiled=True),
            lax.all_gather(w_out, "grp", axis=0, tiled=True),
            lax.all_gather(b_out, "grp", axis=0, tiled=True),
            lax.all_gather(ln2_gain, "grp", axis=0, tiled=True),
            lax.all_gather(ln2_bias, "grp", axis=0, tiled=True),
            lax.all_gather(w_up, "grp", axis=0, tiled=True),
            lax.all_gather(b_up, "grp", axis=0, tiled=True),
            lax.all_gather(w_down, "grp", axis=0, tiled=True),
            lax.all_gather(b_down, "grp", axis=0, tiled=True),
        )
        saved, result = forward_pass(forward_params, tokens[index], positions[:, index, :])
        outputs.append(result)
        backward_params = (
            lax.all_gather(ln1_gain, "grp", axis=0, tiled=True),
            lax.all_gather(ln1_bias, "grp", axis=0, tiled=True),
            lax.all_gather(w_qkv, "grp", axis=0, tiled=True),
            lax.all_gather(b_qkv, "grp", axis=0, tiled=True),
            lax.all_gather(w_out, "grp", axis=0, tiled=True),
            lax.all_gather(b_out, "grp", axis=0, tiled=True),
            lax.all_gather(ln2_gain, "grp", axis=0, tiled=True),
            lax.all_gather(ln2_bias, "grp", axis=0, tiled=True),
            lax.all_gather(w_up, "grp", axis=0, tiled=True),
            lax.all_gather(b_up, "grp", axis=0, tiled=True),
            lax.all_gather(w_down, "grp", axis=0, tiled=True),
            lax.all_gather(b_down, "grp", axis=0, tiled=True),
        )
        grad_field, totals = backward_pass(backward_params, saved, cotangent[index], totals)
        gradients.append(grad_field)
    owned = (
        lax.psum_scatter(
            totals[0].astype(jnp.bfloat16), "grp", scatter_dimension=0, tiled=True
        ).astype(jnp.float32),
        lax.psum_scatter(
            totals[1].astype(jnp.bfloat16), "grp", scatter_dimension=0, tiled=True
        ).astype(jnp.float32),
        lax.psum_scatter(
            totals[2].astype(jnp.bfloat16), "grp", scatter_dimension=0, tiled=True
        ).astype(jnp.float32),
        lax.psum_scatter(
            totals[3].astype(jnp.bfloat16), "grp", scatter_dimension=0, tiled=True
        ).astype(jnp.float32),
        lax.psum_scatter(
            totals[4].astype(jnp.bfloat16), "grp", scatter_dimension=0, tiled=True
        ).astype(jnp.float32),
        lax.psum_scatter(
            totals[5].astype(jnp.bfloat16), "grp", scatter_dimension=0, tiled=True
        ).astype(jnp.float32),
        lax.psum_scatter(
            totals[6].astype(jnp.bfloat16), "grp", scatter_dimension=0, tiled=True
        ).astype(jnp.float32),
        lax.psum_scatter(
            totals[7].astype(jnp.bfloat16), "grp", scatter_dimension=0, tiled=True
        ).astype(jnp.float32),
        lax.psum_scatter(
            totals[8].astype(jnp.bfloat16), "grp", scatter_dimension=0, tiled=True
        ).astype(jnp.float32),
        lax.psum_scatter(
            totals[9].astype(jnp.bfloat16), "grp", scatter_dimension=0, tiled=True
        ).astype(jnp.float32),
        lax.psum_scatter(
            totals[10].astype(jnp.bfloat16), "grp", scatter_dimension=0, tiled=True
        ).astype(jnp.float32),
        lax.psum_scatter(
            totals[11].astype(jnp.bfloat16), "grp", scatter_dimension=0, tiled=True
        ).astype(jnp.float32),
    )
    summed = (
        lax.psum(owned[0].astype(jnp.bfloat16), "rep").astype(jnp.float32),
        lax.psum(owned[1].astype(jnp.bfloat16), "rep").astype(jnp.float32),
        lax.psum(owned[2].astype(jnp.bfloat16), "rep").astype(jnp.float32),
        lax.psum(owned[3].astype(jnp.bfloat16), "rep").astype(jnp.float32),
        lax.psum(owned[4].astype(jnp.bfloat16), "rep").astype(jnp.float32),
        lax.psum(owned[5].astype(jnp.bfloat16), "rep").astype(jnp.float32),
        lax.psum(owned[6].astype(jnp.bfloat16), "rep").astype(jnp.float32),
        lax.psum(owned[7].astype(jnp.bfloat16), "rep").astype(jnp.float32),
        lax.psum(owned[8].astype(jnp.bfloat16), "rep").astype(jnp.float32),
        lax.psum(owned[9].astype(jnp.bfloat16), "rep").astype(jnp.float32),
        lax.psum(owned[10].astype(jnp.bfloat16), "rep").astype(jnp.float32),
        lax.psum(owned[11].astype(jnp.bfloat16), "rep").astype(jnp.float32),
    )
    output = jnp.stack(outputs, axis=0)
    grad_tokens = jnp.stack(gradients, axis=0)
    return (
        output,
        grad_tokens,
        summed[0],
        summed[1],
        summed[2],
        summed[3],
        summed[4],
        summed[5],
        summed[6],
        summed[7],
        summed[8],
        summed[9],
        summed[10],
        summed[11],
    )


def spread(mesh):
    placed = (
        P("rep", "grp", None),
        P(None, "rep", "grp"),
        P("grp"),
        P("grp"),
        P("grp", None),
        P("grp"),
        P("grp", None),
        P("grp"),
        P("grp"),
        P("grp"),
        P("grp", None),
        P("grp"),
        P("grp", None),
        P("grp"),
        P("rep", "grp", None),
    )
    return jax.shard_map(
        local,
        mesh=mesh,
        in_specs=placed,
        out_specs=(
            P("rep", "grp", None),
            P("rep", "grp", None),
            P("grp"),
            P("grp"),
            P("grp", None),
            P("grp"),
            P("grp", None),
            P("grp"),
            P("grp"),
            P("grp"),
            P("grp", None),
            P("grp"),
            P("grp", None),
            P("grp"),
        ),
        check_vma=False,
    )


def solution(mesh):
    reps, groups = mesh.devices.shape
    flat = mesh.devices.reshape(-1)

    def run(*args):
        clips = args[0].shape[0] // reps
        if reps == 8 and groups == 2 * clips:
            split = Mesh(flat.reshape(reps // 2, 2, groups), ("rp", "core", "grp"))
            ins, outs = paired_specs()
            return jax.shard_map(
                paired, mesh=split, in_specs=ins, out_specs=outs, check_vma=False
            )(*args)
        return spread(mesh)(*args)

    return run
```

```python
import functools

import jax
import jax.numpy as jnp
from jax import lax
from jax.experimental import pallas as pl
from jax.experimental.pallas import tpu as pltpu
from jax.sharding import Mesh
from jax.sharding import PartitionSpec as P

SCALE = 0.125
EPS = 1e-06
HEAD = 64
BF = jnp.bfloat16
F32 = jnp.float32
MESH = pl.DeviceIdType.MESH
ANY = pl.BlockSpec(memory_space=pl.ANY)
VM = pl.BlockSpec(memory_space=pltpu.VMEM)


def where_am_i():
    return lax.axis_index("rp"), lax.axis_index("core"), lax.axis_index("grp")


def remote(src, dst, send, recv, target):
    return pltpu.make_async_remote_copy(
        src_ref=src,
        dst_ref=dst,
        send_sem=send,
        recv_sem=recv,
        device_id=target,
        device_id_type=MESH,
    )


def enter(p, c, z, groups):
    barrier = pltpu.get_barrier_semaphore()
    for k in range(groups):
        for d in range(2):
            if k == 0 and d == 0:
                continue
            pl.semaphore_signal(
                barrier, inc=1, device_id=(p, c ^ d, lax.rem(z + k, groups)), device_id_type=MESH
            )
    for b in (1, 2):
        pl.semaphore_signal(barrier, inc=1, device_id=(p ^ b, c, z), device_id_type=MESH)
    pl.semaphore_wait(barrier, 2 * groups - 1 + 2)


def move_tokens(refs, outs, send, recv, p, c, z, clips):
    core, slot = lax.div(z, clips), lax.rem(z, clips)

    def route(i):
        return core, c * clips + i

    def here(i):
        return jnp.logical_and(core == c, c * clips + i == z)

    def start(k, pieces):
        for n, (src, dst) in enumerate(zip(refs, outs)):
            rows = src.shape[1] // pieces
            rows = pl.ds(k * rows, rows)
            for i in range(clips):
                tc, tz = route(i)

                @pl.when(here(i))
                def _():
                    pltpu.make_async_copy(
                        src.at[i, rows], dst.at[slot, rows], recv.at[n, slot]
                    ).start()

                @pl.when(jnp.logical_not(here(i)))
                def _():
                    remote(
                        src.at[i, rows],
                        dst.at[slot, rows],
                        send.at[n, i],
                        recv.at[n, slot],
                        (p, tc, tz),
                    ).start()

    def sent():
        for n, (src, dst) in enumerate(zip(refs, outs)):
            for i in range(clips):

                @pl.when(jnp.logical_not(here(i)))
                def _():
                    remote(
                        src.at[i], dst.at[slot], send.at[n, i], recv.at[n, slot], (p, c ^ 1, z)
                    ).wait_send()

    def arrive():
        for n, (src, dst) in enumerate(zip(refs, outs)):
            for m in range(clips):
                pltpu.make_async_copy(src.at[0], dst.at[m], recv.at[n, m]).wait()

    def finish():
        sent()
        arrive()

    return start, finish, sent, arrive


def turn(u, cosine, sine):
    half = HEAD // 2
    first, second = u[:half], u[half:]
    return jnp.concatenate(
        [first * cosine - second * sine, first * sine + second * cosine], axis=0
    )


def dot(a, b):
    return jnp.dot(a, b, preferred_element_type=F32)


def dot_t(a, b):
    return lax.dot_general(a, b, (((1,), (1,)), ((), ())), preferred_element_type=F32)


def tile(i, size):
    return pl.ds(pl.multiple_of(i * size, size), size)


def cuts(whole, half, c, blocks):
    if blocks == 0:
        return [(whole.at[c], half)]
    size = half.shape[3] // blocks
    return [
        (
            whole.at[:, :, :, pl.ds(pl.multiple_of((2 * b + c) * size, size), size)],
            half.at[:, :, :, pl.ds(b * size, size)],
        )
        for b in range(blocks)
    ]


def forward_body(groups, clips, blocks, *refs):
    count = len(blocks)
    raw, (small, x, tab, dy) = refs[:count], refs[count : count + 4]
    (wq_o, *outs) = refs[count + 4 : 2 * count + 4]
    (small_o, x_o, tab_o, dy_o, h1_o, qs_o, kr_o, vb_o, mix_o, lse_o) = refs[2 * count + 4 : 2 * count + 14]
    halves = refs[2 * count + 14 : 3 * count + 14]
    (wq_v, small_v, x_v, tab_v, tab_w, h1, qs, kr, vb, mix, qkv, gain, bias) = refs[
        3 * count + 14 : 3 * count + 27
    ]
    (zs, zr, xs, xr, ys, yr, fs, fr, hs, ls, ss, sr, ts, tr, us, ur, vs, vr, es, er, ks) = refs[
        3 * count + 27 :
    ]
    outs = [wq_v, *outs]
    p, c, z = where_am_i()
    for w in range(count):
        for src, dst in cuts(raw[w], halves[w], c, blocks[w]):
            pltpu.make_async_copy(src, dst, hs.at[w]).start()
    enter(p, c, z, groups)
    col = [(p, c, lax.rem(z + k, groups)) for k in range(groups)]
    org = [lax.rem(z + groups - k, groups) for k in range(groups)]
    xn, yn, cn = (p ^ 1, c, z), (p ^ 2, c, z), (p, c ^ 1, z)
    smalls = [
        remote(small, small_v.at[z], ss.at[k], sr.at[k], col[k]) for k in range(1, groups)
    ]
    for s in smalls:
        s.start()
    keep = [pltpu.make_async_copy(small, small_v.at[z], ls.at[count])]
    keep[0].start()
    start_tab, _, sent_tab, arrive_tab = move_tokens((tab,), (tab_v,), vs, vr, p, c, z, clips)
    start_x, _, sent_x, arrive_x = move_tokens((x,), (x_v,), ts, tr, p, c, z, clips)
    start_dy, finish_dy, *_ = move_tokens((dy,), (dy_o,), us, ur, p, c, z, clips)
    units = [(w, d, side) for w in range(count) for d in range(1, groups) for side in range(2)]

    def origin(d, side):
        return z - d if side == 0 else z + d

    def arrives(d, side):
        return z >= d if side == 0 else z + d < groups

    def leaves(d, side):
        if side == 0:
            return jnp.logical_and(z + 1 < groups, z + 1 >= d)
        return jnp.logical_and(z >= 1, z - 1 + d < groups)

    def hop(w, d, side, src):
        o = origin(d - 1, side)
        target = (p, c, lax.rem(z + 1 if side == 0 else z + groups - 1, groups))
        return remote(src, outs[w].at[o, p], zs.at[w, side, d], zr.at[w, side, d], target)

    def own(w):
        pltpu.make_async_copy(halves[w], halves[w], hs.at[w]).wait()
        keep.append(pltpu.make_async_copy(halves[w], outs[w].at[z], ls.at[w]))
        keep[-1].start()
        for side in range(2):

            @pl.when(leaves(1, side))
            def _():
                hop(w, 1, side, halves[w].at[p]).start()

    def links(u):
        w, d, side = u
        o = outs[w].at[lax.rem(origin(d, side) + groups, groups)]
        e, f = xs.at[w, side, d], xr.at[w, side, d]
        g, h = ys.at[w, side, d], yr.at[w, side, d]
        a, b = fs.at[w, side, d, 0], fr.at[w, side, d, 0]
        m, n = fs.at[w, side, d, 1], fr.at[w, side, d, 1]
        across = lambda q: remote(o.at[q], o.at[q], e, f, xn)
        along = lambda q: remote(o.at[q], o.at[q], g, h, yn)
        first = lambda q: remote(o.at[q, 0], o.at[q, 0], a, b, yn)
        second = lambda q: remote(o.at[q, 1], o.at[q, 1], m, n, xn)
        return o, across, along, first, second

    def plane(u):
        w, d, side = u
        o, across, along, first, second = links(u)

        @pl.when(arrives(d, side))
        def _():
            remote(o.at[p], o.at[p], zs.at[w, side, d], zr.at[w, side, d], xn).wait_recv()
            if d + 1 < groups:

                @pl.when(leaves(d + 1, side))
                def _():
                    hop(w, d + 1, side, o.at[p]).start()

            across(p).start()
            along(p).start()

    def forward(u):
        w, d, side = u
        o, across, along, first, second = links(u)

        @pl.when(arrives(d, side))
        def _():
            across(p ^ 1).wait_recv()
            first(p ^ 1).start()
            along(p ^ 2).wait_recv()
            second(p ^ 2).start()

    def complete(u):
        w, d, side = u
        o, across, along, first, second = links(u)

        @pl.when(arrives(d, side))
        def _():
            first(p ^ 3).wait_recv()
            second(p ^ 3).wait_recv()

    def settle(u):
        w, d, side = u
        o, across, along, first, second = links(u)

        @pl.when(arrives(d, side))
        def _():
            across(p).wait_send()
            along(p).wait_send()
            first(p).wait_send()
            second(p).wait_send()

        @pl.when(leaves(d, side))
        def _():
            hop(w, d, side, halves[w].at[p]).wait_send()

    own(0)
    start_tab(0, 1)
    own(1)
    moves = {2 * k: (start_x, k) for k in range(4)}
    moves.update({10 + 3 * k: (start_dy, k) for k in range(4)})
    lag = 3

    def step(n):
        if n < len(units):
            plane(units[n])
            w, d, side = units[n]
            if (d, side) == (1, 1) and w + 2 < count:
                own(w + 2)
            if n in moves:
                moves[n][0](moves[n][1], 4)
        if n >= lag:
            forward(units[n - lag])

    steps = list(range(len(units) + lag))
    early = 2 * (groups - 1) + lag
    for _ in range(early):
        step(steps.pop(0))
    for k in range(1, groups):
        remote(small, small_v.at[org[k]], ss.at[k], sr.at[k], col[k]).wait_recv()
    keep[0].wait()
    row = small_v.shape[2]
    half = row // 2
    mine = pl.ds(pl.multiple_of(c * half, half), half)
    for g in range(groups):
        gain[0:2, g * row : (g + 1) * row] = small_v[g, 0:2]
        for r in range(3):
            bias[3 * g + r : 3 * g + r + 1] = small_v[g, 6 + r : 7 + r, mine]
    small_o[...] = small_v[...]
    own_count = h1.shape[0] // 2
    arrive_x()
    saves = [pltpu.make_async_copy(x_v, x_o, ks.at[0])]
    saves[0].start()

    def norm(i, carry):
        per = own_count // clips // 128
        v = x_v[lax.div(i, per), tile(lax.rem(i, per), 128)].astype(F32)
        v = v - jnp.mean(v, axis=1, keepdims=True)
        v = v * lax.rsqrt(jnp.mean(v * v, axis=1, keepdims=True) + EPS)
        h1[tile(i, 128)] = (v * gain[0:1] + gain[1:2]).astype(BF)
        return carry

    lax.fori_loop(0, own_count // 128, norm, 0)
    swap = remote(h1.at[:own_count], h1.at[own_count:], es.at[0], er.at[0], cn)
    swap.start()
    arrive_tab()
    swap_tab = remote(tab_v, tab_w, es.at[1], er.at[1], cn)
    swap_tab.start()
    step(steps.pop(0))
    swap_tab.wait()
    part = tab_v.shape[2]
    for m in range(clips):
        tab_o[:, m * part : (m + 1) * part] = tab_v[m]
        tab_o[:, own_count + m * part : own_count + (m + 1) * part] = tab_w[m]
    for u in units[: 2 * (groups - 1)]:
        complete(u)
    keep[1].wait()
    saves.append(pltpu.make_async_copy(wq_v, wq_o, ks.at[1]))
    saves[1].start()
    swap.wait()
    saves.append(pltpu.make_async_copy(h1, h1_o, ks.at[2]))
    saves[2].start()
    inner = qs.shape[0]
    heads = inner // HEAD
    pairs = heads // 2

    def head(h, side):
        rows, place = tile(h, HEAD), tile(side, HEAD)
        co, si = tab_o[: HEAD // 2], tab_o[HEAD // 2 :]
        k = turn(qkv[1, place], co, si).astype(BF)
        v = qkv[2, place].astype(BF)
        q = (turn(qkv[0, place], co, si).astype(BF).astype(F32) * SCALE).astype(BF)
        kr[rows] = k
        vb[rows] = v
        qs[rows] = q
        keys = k.T
        size = 256
        for i in range(0, 2 * own_count, size):
            scores = dot(keys, q[:, i : i + size])
            top = jnp.max(scores, axis=0, keepdims=True)
            e = jnp.exp(scores - top)
            total = jnp.sum(e, axis=0, keepdims=True)
            mixed = dot(v, e.astype(BF))
            mix[rows, i : i + size] = (mixed / total).astype(BF)
            lse_o[h, :, i : i + size] = top + jnp.log(total)

    during = [steps.pop(0) for _ in range(heads + heads // 2)]

    def two_heads(i, carry):
        def project(n, carry):
            at = pl.ds(pl.multiple_of(n * inner + i * 2 * HEAD, 2 * HEAD), 2 * HEAD)
            w = wq_v[..., at].reshape(h1.shape[1], 2 * HEAD)
            qkv[n] = (dot(h1[...], w) + bias[pl.ds(n * pairs + i, 1)]).T
            return carry

        lax.fori_loop(0, 3, project, 0)
        for n in range(pairs):

            @pl.when(i == n)
            def _():
                step(during[3 * n])

        def one(side, carry):
            head(2 * i + side, side)
            for n in range(heads):

                @pl.when(2 * i + side == n)
                def _():
                    step(during[3 * (n // 2) + 1 + n % 2])

            return carry

        lax.fori_loop(0, 2, one, 0)
        return carry

    lax.fori_loop(0, pairs, two_heads, 0)
    for n, (a, b) in enumerate(((qs, qs_o), (kr, kr_o), (vb, vb_o), (mix, mix_o))):
        saves.append(pltpu.make_async_copy(a, b, ks.at[3 + n]))
        saves[-1].start()
    while steps:
        step(steps.pop(0))
    for u in units[2 * (groups - 1) :]:
        complete(u)
    for u in units:
        settle(u)
    for s in smalls:
        s.wait_send()
    for k in keep[2:] + saves:
        k.wait()
    sent_tab()
    sent_x()
    finish_dy()


def half_shape(raw, blocks):
    return raw.shape[1:] if blocks == 0 else raw.shape[:3] + (raw.shape[3] // 2,)


def forward(raw, blocks, small, x, tab, dy, groups):
    count, clips = len(raw), x.shape[0]
    own, width = clips * x.shape[1], x.shape[2]
    halves = [half_shape(r, b) for r, b in zip(raw, blocks)]
    inner = halves[0][-1] // 3
    dma = pltpu.SemaphoreType.DMA
    of = jax.ShapeDtypeStruct
    feature = (inner, 2 * own)
    shapes = [of((groups,) + h, BF) for h in halves]
    shapes += [of((groups,) + small.shape, F32), of(x.shape, BF), of((HEAD, 2 * own), F32)]
    shapes += [of(x.shape, BF), of((2 * own, width), BF)] + [of(feature, BF)] * 4
    shapes += [of((inner // HEAD, 1, 2 * own), F32)]
    vm = pltpu.VMEM
    scratch = [vm(h, BF) for h in halves]
    scratch += [vm((groups,) + halves[0], BF), vm((groups,) + small.shape, F32), vm(x.shape, BF)]
    scratch += [vm(tab.shape, F32)] * 2 + [vm((2 * own, width), BF)] + [vm(feature, BF)] * 4
    scratch += [vm((3, 2 * HEAD, 2 * own), F32), vm((8, width), F32)]
    scratch += [vm((3 * groups + -3 * groups % 8, width // groups // 2), F32)]
    return pl.pallas_call(
        functools.partial(forward_body, groups, clips, blocks),
        out_shape=shapes,
        in_specs=[ANY] * count + [VM, ANY, ANY, ANY],
        out_specs=[ANY] * count + [VM, ANY, VM] + [ANY] * 6 + [VM],
        scratch_shapes=scratch
        + [dma((count, 2, groups))] * 6
        + [dma((count, 2, groups, 2))] * 2
        + [dma((count,)), dma((count + 1,)), dma((groups,)), dma((groups,))]
        + [dma((1, clips))] * 6
        + [dma((2,)), dma((2,)), dma((7,))],
        compiler_params=pltpu.CompilerParams(
            collective_id=0, has_side_effects=True, vmem_limit_bytes=60 * 1024 * 1024
        ),
        name="forward",
    )(*raw, small, x, tab, dy)


def backward_body(groups, clips, blocks, *refs):
    count = len(blocks)
    (gw2, act, slope, w2, w1, wo, wq, mix, qs, kr, vb, h1, h2, x2, x, dy, dy_all) = refs[:17]
    (lse, cosine, sine, g1, g2, bd) = refs[17:23]
    outs = refs[23 : 23 + count]
    gw1, small_o, gx_o, y_o = refs[23 + count : 27 + count]
    (gu_b, w1_b, wo_b, mix_b, qs_b, kr_b, vb_b, h1_b, x2_b, x_b, dy_b) = refs[27 + count : 38 + count]
    (own_f, give, take, y_take, dx2, low, da, gwo, gwq, ak, av, dq2, dk2, acc, gx) = refs[
        38 + count : 53 + count
    ]
    (sl, gbu, stage_b) = refs[53 + count : 56 + count]
    ld, es, er, sls = refs[56 + count : 60 + count]
    grads = (gwq, gwo, gw1, gw2)
    scratch = refs[60 + count :]
    own_a, own_b, one_a, one_b, two_a, two_b, three, full = (
        scratch[i * count : (i + 1) * count] for i in range(8)
    )
    small_s, small_r, small_z = scratch[8 * count : 8 * count + 3]
    (os, s1, r1, s2, r2, s3, r3, s4, r4, s5, r5, cs, cr, ls, ss, sr, ts, tr, us, ur) = scratch[
        8 * count + 3 :
    ]
    own, width = own_f.shape
    inner = mix_b.shape[0]
    third_width = wq.shape[1]

    upper, lower = w1_b.at[:, :width], w1_b.at[:, width:]
    pairs = ((w2.at[:width], upper), (w2.at[width:], lower), (dy_all, low), (h2, h1_b))
    pairs += ((x2, x2_b), (dy, dy_b), (mix, mix_b), (wo, wo_b))
    pairs += ((qs, qs_b), (kr, kr_b), (vb, vb_b), (x, x_b))
    pairs += ((w1, w1_b), (h1, h1_b), (act, gu_b), (w2.at[:width], upper), (w2.at[width:], lower))
    pairs += ((wq, w1_b.at[:, :third_width]),)
    loads = [pltpu.make_async_copy(a, b, ld.at[n]) for n, (a, b) in enumerate(pairs)]
    first_tile = pltpu.make_async_copy(slope.at[:, :256], sl.at[0], sls.at[0])
    first_tile.start()
    for copy in loads[:12]:
        copy.start()
    p, c, z = where_am_i()
    hi, lo = lax.div(p, 2), lax.rem(p, 2)
    enter(p, c, z, groups)
    col = [(p, c, lax.rem(z + k, groups)) for k in range(groups)]
    xn, yn, cn = (p ^ 1, c, z), (p ^ 2, c, z), (p, c ^ 1, z)
    order = (3, 2, 1, 0)
    units = [(w, j) for w in order for j in [*range(1, groups), 0]]
    sides = ((own_a, one_a, two_a, hi, yn), (own_b, one_b, two_b, lo, xn))

    def c1(u, n):
        w, j = u
        g = grads[w].at[lax.rem(z + j, groups)]
        src, target = (g.at[:, 1 - lo, 0], xn) if n == 0 else (g.at[1 - hi, :, 1], yn)
        return remote(src, sides[n][1][w].at[j], s1.at[w, j, n], r1.at[w, j, n], target)

    def load(u, n):
        w, j = u
        g = grads[w].at[lax.rem(z + j, groups)]
        src = g.at[:, lo, 0] if n == 0 else g.at[hi, :, 1]
        return pltpu.make_async_copy(src, sides[n][0][w].at[j], os.at[w, j, n])

    def c2(u, n):
        w, j = u
        own, one, two, side, target = sides[n]
        return remote(own[w].at[j, 1 - side], two[w].at[j], s2.at[w, j, n], r2.at[w, j, n], target)

    def c3(u, n):
        w, j = u
        src = sides[n][0][w].at[j, sides[n][3]]
        return remote(src, three[w].at[j, n], s3.at[w, j, n], r3.at[w, j, n], col[j])

    def c4(w, n):
        f = full[w].at[p]
        return remote(f, f, s4.at[w, n], r4.at[w, n], (xn, yn)[n])

    def c5(w, n):
        f = full[w].at[(p ^ 1, p ^ 2)[n], n]
        return remote(f, f, s5.at[w, n], r5.at[w, n], (yn, xn)[n])

    def stage_zero(u):
        for n in range(2):
            c1(u, n).start()
            load(u, n).start()

    def stage_one(u):
        w, j = u
        for n, (own, one, two, side, target) in enumerate(sides):
            load(u, n).wait()
            c1(u, n).wait_recv()
            own[w][j] = (own[w][j].astype(F32) + one[w][j].astype(F32)).astype(BF)
            c2(u, n).start()

    def stage_two(u):
        w, j = u
        for n, (own, one, two, side, target) in enumerate(sides):
            c2(u, n).wait_recv()
            own[w][j, side] = (own[w][j, side].astype(F32) + two[w][j].astype(F32)).astype(BF)
            if j:
                c3(u, n).start()

    def stage_three(w):
        for n, (own, one, two, side, target) in enumerate(sides):
            total = own[w][0, side].astype(F32)
            for j in range(1, groups):
                c3((w, j), n).wait_recv()
                total = total + three[w][j, n].astype(F32)
            full[w][p, n] = total.astype(BF)
        for n in range(2):
            c4(w, n).start()

    def stage_four(w):
        for n, target in enumerate((yn, xn)):
            f = full[w].at[(p ^ 1, p ^ 2)[n]]
            remote(f, f, s4.at[w, n], r4.at[w, n], target).wait_recv()
            c5(w, n).start()

    def stage_five(w):
        for n in range(2):
            f = full[w].at[p ^ 3, n]
            remote(f, f, s5.at[w, n], r5.at[w, n], xn).wait_recv()
        for dst, src in cuts(outs[w], full[w], c, blocks[w]):
            pltpu.make_async_copy(src, dst, ls.at[w]).start()
            remote(src, dst, cs.at[w], cr.at[w], cn).start()

    ahead, lag = 3, 2
    todo = {}
    for n, u in enumerate(units):
        todo.setdefault(max(n - ahead, -1), []).append((stage_zero, u))
        todo.setdefault(n, []).append((stage_one, u))
        todo.setdefault(n + lag, []).append((stage_two, u))
    for i, w in enumerate(order):
        last = (i + 1) * groups - 1 + lag
        for at, stage in ((2, stage_three), (3, stage_four), (4, stage_five)):
            todo.setdefault(last + at, []).append((stage, w))
    steps = sorted(todo)

    def run(step):
        for stage, what in todo[step]:
            stage(what)

    def tick():
        run(steps.pop(0))

    def half_sum(n, left, right, depth):
        def other(i, carry):
            part = dot_t(left[own:, :depth], right[tile(i, 256), :depth])
            give[:, tile(i, 256)] = part.astype(BF)
            return carry

        def self(i, carry):
            own_f[:, tile(i, 256)] = dot_t(left[:own, :depth], right[tile(i, 256), :depth])
            return carry

        lax.fori_loop(0, width // 256, other, 0)
        copy = remote(give, take, es.at[n], er.at[n], cn)
        copy.start()
        lax.fori_loop(0, width // 256, self, 0)
        return copy

    def part(i):
        per = own // clips // 128
        return lax.div(i, per), tile(lax.rem(i, per), 128)

    def norm_step(i, field, gain, grad, row):
        at = tile(i, 128)
        d = own_f[at] + take[at].astype(F32)
        v = field[at].astype(F32)
        v = v - jnp.mean(v, axis=1, keepdims=True)
        r = lax.rsqrt(jnp.mean(v * v, axis=1, keepdims=True) + EPS)
        v = v * r
        acc[row : row + 1] += jnp.sum(d * v, axis=0, keepdims=True)
        acc[row + 1 : row + 2] += jnp.sum(d, axis=0, keepdims=True)
        e = d * gain[...]
        mean = jnp.mean(e, axis=1, keepdims=True)
        e = e - mean - v * jnp.mean(e * v, axis=1, keepdims=True)
        return grad + r * e

    tick()
    acc[...] = jnp.zeros_like(acc)
    for copy in loads[:3]:
        copy.wait()
    deep = slope.shape[1]
    sides_of = deep // width

    def hidden_grad(side, i):
        n = side * (width // 256) + i
        slot = lax.rem(n, 2)
        pltpu.make_async_copy(slope.at[:, :256], sl.at[slot], sls.at[slot]).wait()

        @pl.when(n + 1 < deep // 256)
        def _():
            src = slope.at[:, tile(n + 1, 256)]
            pltpu.make_async_copy(src, sl.at[1 - slot], sls.at[1 - slot]).start()

        right = w1_b[tile(i, 256), side * width : (side + 1) * width]
        line = jnp.zeros((1, 256), F32)
        for r in range(2):
            rows = slice(r * own, (r + 1) * own)
            g = dot_t(low[rows], right) * sl[slot, rows].astype(F32)
            g = g.astype(BF)
            gu_b[rows, tile(n, 256)] = g
            line = line + jnp.sum(g.astype(F32), axis=0, keepdims=True)
        gbu[:, tile(n, 256)] = line

    for side in range(sides_of):

        def columns(i, carry):
            hidden_grad(side, i)
            return carry

        lax.fori_loop(0, width // 256, columns, 0)
        if side == 0:
            tick()
    loads[12].start()
    loads[3].wait()
    row = width // groups

    def up_grad(j, carry):
        k = lax.rem(z + j, groups)
        left = h1_b[:, tile(k, row)].T

        def columns(i, carry):
            at = tile(i, 512)
            stage_b[..., at] = dot(left, gu_b[:, at]).astype(BF).reshape(stage_b.shape[:-1] + (512,))
            return carry

        lax.fori_loop(0, deep // 512, columns, 0)
        copy = pltpu.make_async_copy(stage_b, gw1.at[k], ld.at[18])
        copy.start()
        copy.wait()
        return carry

    lax.fori_loop(1, 3, up_grad, 0)
    tick()
    lax.fori_loop(3, groups + 1, up_grad, 0)
    loads[13].start()
    tick()
    loads[12].wait()
    swap = half_sum(0, gu_b, w1_b, deep)
    for copy in loads[14:17]:
        copy.start()
    tick()
    for copy in loads[4:12]:
        copy.wait()
    swap.wait()

    def second_norm(i, carry):
        at = tile(i, 128)
        g = dy_b[part(i)].astype(F32)
        d = norm_step(i, x2_b, g2, g, 3)
        dx2[at] = d
        acc[5:6] += jnp.sum(g, axis=0, keepdims=True)
        low[at] = d.astype(BF)
        acc[2:3] += jnp.sum(d.astype(BF).astype(F32), axis=0, keepdims=True)
        return carry

    lax.fori_loop(0, own // 128, second_norm, 0)
    swap = remote(low.at[:own], low.at[own:], es.at[1], er.at[1], cn)
    swap.start()
    tick()
    swap.wait()

    def out_grad(i, carry):
        at = tile(i, 256)
        gwo[..., at] = dot(mix_b[...], low[:, at]).astype(BF).reshape(gwo.shape[:-1] + (256,))
        return carry

    lax.fori_loop(0, width // 256, out_grad, 0)

    def attn_grad(i, carry):
        at = tile(i, 256)
        da[:, at] = dot_t(wo_b[...], low[at]).astype(BF)
        return carry

    lax.fori_loop(0, 2 * own // 256, attn_grad, 0)
    tick()

    for copy in loads[14:17]:
        copy.wait()

    def down(rows, i):
        left = dot(gu_b[rows, :width], w1_b[:, tile(i, 256)])
        at = pl.ds(pl.multiple_of(width + i * 256, 256), 256)
        return left + dot(gu_b[rows, width:], w1_b[:, at])

    def down_other(i, carry):
        give[:, tile(i, 256)] = down(slice(own, 2 * own), i).astype(BF)
        return carry

    def down_self(i, carry):
        own_f[:, tile(i, 256)] = down(slice(0, own), i)
        return carry

    lax.fori_loop(0, width // 256, down_other, 0)
    y_copy = remote(give, y_take, es.at[3], er.at[3], cn)
    y_copy.start()
    lax.fori_loop(0, width // 256, down_self, 0)
    loads[17].start()
    y_copy.wait()

    def last_add(i, carry):
        at = tile(i, 128)
        gx[part(i)] = (x2_b[at] + own_f[at] + bd[...] + y_take[at].astype(F32)).astype(BF)
        return carry

    lax.fori_loop(0, own // 128, last_add, 0)
    y_start, y_finish, *_ = move_tokens((gx,), (y_o,), us, ur, p, c, z, clips)
    y_start(0, 4)
    dqkv = gu_b.at[:, :third_width]

    def head(h, side):
        rows = tile(h, HEAD)
        place = tile(side, HEAD)
        co, si = cosine[...], sine[...]
        kt = kr_b[rows]
        keys, values = kt.T, vb_b[rows].T
        queries, outer_grads = qs_b[rows].T, da[rows].T
        step = 256
        for i in range(0, 2 * own, step):
            s = slice(i, i + step)
            g = da[rows, s]
            p = jnp.exp(dot(keys, qs_b[rows, s]) - lse[h, :, s])
            delta = jnp.sum(mix_b[rows, s].astype(F32) * g.astype(F32), axis=0, keepdims=True)
            ds = (p * (dot(values, g) - delta)).astype(BF)
            dq2[place, s] = turn(dot(kt, ds) * SCALE, co[:, s], -si[:, s]).astype(BF)
            dv = dot(p.astype(BF), outer_grads[s])
            dk = dot(ds, queries[s])
            if i == 0:
                ak[...] = dk
                av[side] = dv
            else:
                ak[...] += dk
                av[side] += dv
        dk2[place] = turn(ak[...].T, co, -si).astype(BF)

    heads = inner // HEAD
    during = [steps.pop(0) for _ in range(3)]

    def two_heads(i, carry):
        lax.fori_loop(0, 2, lambda side, _: head(2 * i + side, side), None)
        for n, value in enumerate(
            (dq2[...].T, dk2[...].T, jnp.concatenate([av[0], av[1]], axis=1).astype(BF))
        ):
            at = pl.ds(pl.multiple_of(n * inner + i * 2 * HEAD, 2 * HEAD), 2 * HEAD)
            dqkv[:, at] = value
        for n, step in enumerate(during):
            pl.when(i == n * heads // 8)(functools.partial(run, step))
            pl.when(i == n * heads // 8)(functools.partial(y_start, n + 1, 4))
        return carry

    lax.fori_loop(0, heads // 2, two_heads, 0)
    loads[13].wait()
    for g in range(groups):
        left = h1_b[:, g * row : (g + 1) * row].T

        def in_grad(i, carry):
            at = tile(i, 512)
            gwq[g, ..., at] = dot(left, dqkv[:, at]).astype(BF).reshape(gwq.shape[1:-1] + (512,))
            return carry

        lax.fori_loop(0, third_width // 512, in_grad, 0)
    tick()
    loads[17].wait()
    swap = half_sum(2, dqkv, w1_b, third_width)
    tick()
    swap.wait()
    y_finish()

    def first_norm(i, carry):
        gx[part(i)] = norm_step(i, x_b, g1, dx2[tile(i, 128)], 0).astype(BF)
        return carry

    lax.fori_loop(0, own // 128, first_norm, 0)
    start, finish, *_ = move_tokens((gx,), (gx_o,), ts, tr, p, c, z, clips)
    start(0, 4)
    tick()
    small_s[...] = jnp.zeros_like(small_s)
    for n in range(6):
        for g in range(groups):
            small_s[g, n : n + 1] = acc[n : n + 1, g * row : (g + 1) * row]
    half = row // 2
    mine_at = pl.ds(pl.multiple_of(c * half, half), half)
    for b in range(3 * groups):
        line = jnp.sum(dqkv[:, b * half : (b + 1) * half].astype(F32), axis=0, keepdims=True)
        small_s[b // 3, 6 + b % 3 : 7 + b % 3, mine_at] = line
    share = deep // groups
    for g in range(groups):
        for n in range(share // row):
            at = pl.ds(9 + c * (share // row) + n, 1)
            small_s[g, at] = gbu[:, g * share + n * row : g * share + (n + 1) * row]
    tick()
    for n, target in enumerate((cn, xn, yn)):
        copy = remote(small_s, small_r.at[n], ss.at[n], sr.at[n], target)
        copy.start()
        start(n + 1, 4)
        for _ in range(1 if n == 0 else 3):
            tick()
        copy.wait()
        small_s[...] += small_r[n]
    tails = [
        remote(small_s.at[col[k][2]], small_z.at[k], ss.at[2 + k], sr.at[2 + k], col[k])
        for k in range(1, groups)
    ]
    for t in tails:
        t.start()
    while steps:
        tick()
    for k in range(1, groups):
        tails[k - 1].wait()
    small_o[...] = small_s[z]
    for k in range(1, groups):
        small_o[...] += small_z[k]
    for u in units:
        w, j = u
        for n in range(2):
            c1(u, n).wait_send()
            c2(u, n).wait_send()
            if j:
                c3(u, n).wait_send()
    for w in range(count):
        for n in range(2):
            c4(w, n).wait_send()
            c5(w, n).wait_send()
        pltpu.make_async_copy(full[w], full[w], ls.at[w]).wait()
        remote(full[w], full[w], cs.at[w], cr.at[w], cn).wait()
    finish()


def backward(gw2, arrays, tables, lines, groups, blocks):
    act, slope, w2, w1, wo, wq, mix, qs, kr, vb, h1, h2, x2, x, dy, dy_all = arrays
    (own, width), clips = x.shape, dy.shape[0]
    small = jax.ShapeDtypeStruct((groups, lines + -lines % 8, width // groups), F32)
    count = len(blocks)
    dma = pltpu.SemaphoreType.DMA
    split = lambda v: (groups, 2, 2, 2, v.shape[0] // (8 * groups), v.shape[1])
    tiles = [split(v)[4:] for v in (wq, wo, w1, w2)]
    shapes = [
        jax.ShapeDtypeStruct((4, 2, t[0], 2 * t[1]) if b else (2, 4, 2) + t, BF)
        for t, b in zip(tiles, blocks)
    ]
    shapes += [
        jax.ShapeDtypeStruct(split(w1), BF),
        jax.ShapeDtypeStruct(small.shape[1:], F32),
        jax.ShapeDtypeStruct(dy.shape, BF),
        jax.ShapeDtypeStruct(dy.shape, BF),
    ]
    scratch = [pltpu.VMEM(v.shape, v.dtype) for v in (act, w1, wo, mix, qs, kr, vb, h1, x2, x, dy)]
    half, low = (own, width), pltpu.VMEM((2 * own, width), BF)
    scratch += [pltpu.VMEM(half, F32)] + [pltpu.VMEM(half, BF)] * 3
    scratch += [pltpu.VMEM(half, F32), low, pltpu.VMEM(mix.shape, BF)]
    scratch += [pltpu.VMEM(split(wo), BF), pltpu.VMEM(split(wq), BF)]
    scratch += [pltpu.VMEM((2 * own, HEAD), F32), pltpu.VMEM((2, 2 * own, HEAD), F32)]
    scratch += [pltpu.VMEM((2 * HEAD, 2 * own), BF)] * 2
    scratch += [pltpu.VMEM((8, width), F32), pltpu.VMEM(dy.shape, BF)]
    scratch += [pltpu.VMEM((2, 2 * own, 256), BF), pltpu.VMEM((1, act.shape[1]), F32)]
    scratch += [pltpu.VMEM(split(w1)[1:], BF)]
    scratch += [dma((19,)), dma((4,)), dma((4,)), dma((2,))]
    for lead in (
        (groups, 2),
        (groups, 2),
        (groups, 2),
        (groups, 2),
        (groups,),
        (groups,),
        (groups, 2),
        (4, 2),
    ):
        scratch += [pltpu.VMEM(lead + t, BF) for t in tiles]
    scratch += [
        pltpu.VMEM(small.shape, F32),
        pltpu.VMEM((3,) + small.shape, F32),
        pltpu.VMEM(small.shape, F32),
    ]
    pair = dma((count, groups, 2))
    scratch += [pair] * 7 + [dma((count, 2))] * 4
    scratch += [dma((count,))] * 3 + [dma((2 + groups,))] * 2 + [dma((1, clips))] * 4
    return pl.pallas_call(
        functools.partial(backward_body, groups, clips, blocks),
        out_shape=shapes,
        in_specs=[ANY] * (1 + len(arrays)) + [VM] * len(tables),
        out_specs=[ANY] * (count + 1) + [VM, ANY, ANY],
        scratch_shapes=scratch,
        compiler_params=pltpu.CompilerParams(
            collective_id=1, has_side_effects=True, vmem_limit_bytes=67043328
        ),
        name="backward",
    )(gw2, *arrays, *tables)


def swap(value):
    return lax.ppermute(value, "core", [(0, 1), (1, 0)])


def both(value):
    return jnp.concatenate([value, swap(value)], axis=0)


def contract(left, right, a, b):
    return lax.dot_general(left, right, (((a,), (b,)), ((), ())), preferred_element_type=F32)


def own_sum(partial):
    half = partial.shape[0] // 2
    return partial[:half] + swap(partial[half:].astype(BF)).astype(F32)


def paired(
    tokens,
    positions,
    ln1_gain,
    ln1_bias,
    w_qkv,
    b_qkv,
    w_out,
    b_out,
    ln2_gain,
    ln2_bias,
    w_up,
    b_up,
    w_down,
    b_down,
    cotangent,
):
    groups = lax.axis_size("grp")
    clips, part, width = tokens.shape
    hidden = w_down.shape[0] * groups
    own = clips * part
    length = 2 * own
    c, z = lax.axis_index("core"), lax.axis_index("grp")
    wide = width // 2
    deep = hidden // 2
    row = width // groups

    def pick(value, axis):
        return lax.dynamic_index_in_dim(value, c, axis, keepdims=False)

    blocks = (3 * groups, 0, groups, 0)
    raw = [
        w.reshape(((4, 2) if b else (2, 4, 2)) + (w.shape[0] // (8 if b else 16), w.shape[1]))
        for w, b in zip((w_qkv, w_out, w_up, w_down), blocks)
    ]
    bq, bu = b_qkv.shape[0] // row, b_up.shape[0] // row
    vectors = [ln1_gain, ln1_bias, b_out, ln2_gain, ln2_bias, b_down]
    vectors += [b_qkv[n * row : (n + 1) * row] for n in range(bq)]
    vectors += [b_up[n * row : (n + 1) * row] for n in range(bu)]
    lines = len(vectors)
    place = lax.broadcasted_iota(jnp.int32, (lines + -lines % 8, row), 0)
    small = jnp.zeros(place.shape, F32)
    for n, v in enumerate(vectors):
        small = jnp.where(place == n, v.astype(F32)[None, :], small)
    pair = jnp.arange(HEAD // 2)
    band = (pair >= 10).astype(jnp.int32) + (pair >= 21).astype(jnp.int32)
    begin = jnp.where(band == 0, 0, jnp.where(band == 1, 10, 21))
    number = jnp.where(band == 0, 10, 11)
    freq = jnp.power(F32(10000.0), -(pair - begin).astype(F32) / number.astype(F32))
    pos = positions.astype(F32)[:, :, None, :]
    band = band[None, :, None]
    chosen = jnp.where(band == 0, pos[0], jnp.where(band == 1, pos[1], pos[2]))
    angles = chosen * freq[None, :, None]
    tab = jnp.concatenate([jnp.cos(angles), jnp.sin(angles)], axis=1)
    wq, wo, w1, w2, small, x, tab, dy, h1, qs, kr, vb, mixed, lse = forward(
        raw, blocks, small, tokens, tab, cotangent, groups
    )
    cosine, sine = tab[: HEAD // 2], tab[HEAD // 2 :]
    wq = wq.reshape(width, 3 * wide)
    wo = wo.reshape(wide, width)
    w1 = w1.reshape(width, deep)
    w2 = w2.reshape(deep, width)
    g1, b1, bo, g2, b2, bd = (small[:, n].reshape(1, width) for n in range(6))
    bu_own = pick(small[:, 6 + bq : lines].reshape(groups, 2, deep // groups), 1).reshape(1, deep)
    grad_out = dy.reshape(own, width)
    grad_all = both(grad_out)
    tokens = x.reshape(own, width)
    x = tokens.astype(F32)
    x2 = x + own_sum(contract(mixed, wo, 0, 0)) + bo
    h2 = both((normalize(x2)[0] * g2 + b2).astype(BF))
    u = contract(h2, w1, 1, 0) + bu_own
    cdf = 0.5 * (1.0 + lax.erf(u * F32(0.7071067811865476)))
    act = (u * cdf).astype(BF)
    slope = (cdf + u * jnp.exp(-0.5 * u * u) * F32(0.3989422804014327)).astype(BF)

    gw2 = contract(act, grad_all, 0, 0).astype(BF)
    gw2 = gw2.reshape(groups, 2, 2, 2, gw2.shape[0] // (8 * groups), width)
    arrays = (act, slope, w2, w1, wo, wq, mixed, qs, kr, vb, h1, h2, x2, tokens, dy, grad_all)
    tables = (lse, cosine, sine, g1, g2, bd)
    gwq, gwo, gw1, gw2, _, sums, gx, output = backward(gw2, arrays, tables, lines, groups, blocks)
    gwq, gwo, gw1, gw2 = (
        g.reshape(shard.shape).astype(F32)
        for g, shard in zip((gwq, gwo, gw1, gw2), (w_qkv, w_out, w_up, w_down))
    )
    gg1, gb1, gbo, gg2, gb2, gbd = (sums[n] for n in range(6))
    gbq, gbu = sums[6 : 6 + bq].reshape(-1), sums[6 + bq : lines].reshape(-1)
    return (output, gx, gg1, gb1, gwq, gbq, gwo, gbo, gg2, gb2, gw1, gbu, gw2, gbd)


def paired_specs():
    rep = ("rp", "core")
    ins = (P(rep, "grp", None), P(None, rep, "grp"))
    one, two = P("grp"), P("grp", None)
    ins += (one, one, two, one, two, one, one, one, two, one, two, one, P(rep, "grp", None))
    outs = (P(rep, "grp", None),) * 2
    outs += (one, one, two, one, two, one, one, one, two, one, two, one)
    return ins, outs


def rotary_angles(positions):
    pair = jnp.arange(32)
    band = (pair >= 10).astype(jnp.int32) + (pair >= 21).astype(jnp.int32)
    start = jnp.where(band == 0, 0, jnp.where(band == 1, 10, 21))
    count = jnp.where(band == 0, 10, 11)
    freq = jnp.power(
        jnp.float32(10000.0), -(pair - start).astype(jnp.float32) / count.astype(jnp.float32)
    )
    pos_f = positions.astype(jnp.float32)
    chosen = jnp.where(
        band[None, :] == 0,
        pos_f[0][:, None],
        jnp.where(band[None, :] == 1, pos_f[1][:, None], pos_f[2][:, None]),
    )
    return chosen * freq[None, :]


def rotate(field, cosine, sine):
    first = field[..., :32]
    second = field[..., 32:]
    return jnp.concatenate(
        [first * cosine - second * sine, first * sine + second * cosine], axis=-1
    )


def normalize(field):
    centred = field - jnp.mean(field, axis=-1, keepdims=True)
    variance = jnp.mean(centred * centred, axis=-1, keepdims=True)
    factor = lax.rsqrt(variance + EPS)
    return (centred * factor, factor)


def norm_back(grad_norm, normed, factor):
    return factor * (
        grad_norm
        - jnp.mean(grad_norm, axis=-1, keepdims=True)
        - normed * jnp.mean(grad_norm * normed, axis=-1, keepdims=True)
    )


def outer(left, right):
    return lax.dot_general(
        left, right, (((0,), (0,)), ((), ())), preferred_element_type=jnp.float32
    )


def back(left, right):
    return lax.dot_general(
        left, right, (((1,), (1,)), ((), ())), preferred_element_type=jnp.float32
    )


def exact_gelu(value):
    return jax.nn.gelu(value, approximate=False)


def column_sum(value):
    return jnp.sum(value.astype(jnp.float32), axis=0)


def forward_pass(params, field_in, positions):
    g1, b1, wqkv, bqkv, wo, bo, g2, b2, w1, bu, w2, bd = params
    field = field_in.astype(jnp.float32)
    count, width = field.shape
    heads = width // 64
    angles = rotary_angles(positions)
    cosine = jnp.cos(angles)[:, None, :]
    sine = jnp.sin(angles)[:, None, :]
    normed1, factor1 = normalize(field)
    h1 = (normed1 * g1.astype(jnp.float32) + b1.astype(jnp.float32)).astype(jnp.bfloat16)
    qkv = jnp.dot(h1, wqkv, preferred_element_type=jnp.float32) + bqkv.astype(jnp.float32)
    query_rot = rotate(qkv[:, :width].reshape(count, heads, 64), cosine, sine).astype(jnp.bfloat16)
    keys_rot = (
        rotate(qkv[:, width : 2 * width].reshape(count, heads, 64), cosine, sine)
        .astype(jnp.bfloat16)
        .reshape(count, width)
    )
    values = qkv[:, 2 * width :].astype(jnp.bfloat16)
    keys_all, values_all = (
        lax.all_gather(keys_rot, "grp", axis=0, tiled=True),
        lax.all_gather(values, "grp", axis=0, tiled=True),
    )
    total = keys_all.shape[0]
    keys_all = keys_all.reshape(total, heads, 64)
    values_all = values_all.reshape(total, heads, 64)
    scores = (
        jnp.einsum("thd,shd->hts", query_rot, keys_all, preferred_element_type=jnp.float32) * SCALE
    )
    top = jnp.max(scores, axis=-1, keepdims=True)
    lse = top + jnp.log(jnp.sum(jnp.exp(scores - top), axis=-1, keepdims=True))
    probs = jnp.exp(scores - lse).astype(jnp.bfloat16)
    mixed = (
        jnp.einsum("hts,shd->thd", probs, values_all, preferred_element_type=jnp.float32)
        .reshape(count, width)
        .astype(jnp.bfloat16)
    )
    second = field + jnp.dot(mixed, wo, preferred_element_type=jnp.float32) + bo.astype(jnp.float32)
    normed2, factor2 = normalize(second)
    h2 = (normed2 * g2.astype(jnp.float32) + b2.astype(jnp.float32)).astype(jnp.bfloat16)
    hidden = jnp.dot(h2, w1, preferred_element_type=jnp.float32) + bu.astype(jnp.float32)
    active = exact_gelu(hidden).astype(jnp.bfloat16)
    result = (
        second + jnp.dot(active, w2, preferred_element_type=jnp.float32) + bd.astype(jnp.float32)
    )
    saved = (
        normed1,
        factor1,
        h1,
        query_rot,
        keys_rot,
        values,
        lse,
        mixed,
        normed2,
        factor2,
        h2,
        hidden,
        active,
        cosine,
        sine,
    )
    return (saved, result.astype(jnp.bfloat16))


def backward_pass(params, saved, grad_in, totals):
    g1, b1, wqkv, bqkv, wo, bo, g2, b2, w1, bu, w2, bd = params
    (
        normed1,
        factor1,
        h1,
        query_rot,
        keys_rot,
        values,
        lse,
        mixed,
        normed2,
        factor2,
        h2,
        hidden,
        active,
        cosine,
        sine,
    ) = saved
    grad_out = grad_in.astype(jnp.float32)
    count, width = grad_out.shape
    heads = width // 64
    grad_y2 = grad_out.astype(jnp.bfloat16)
    grad_w2 = outer(active, grad_y2)
    grad_bd = column_sum(grad_y2)
    grad_act = back(grad_y2, w2)
    unused, pull = jax.vjp(exact_gelu, hidden)
    grad_hidden = pull(grad_act)[0].astype(jnp.bfloat16)
    grad_w1 = outer(h2, grad_hidden)
    grad_bu = column_sum(grad_hidden)
    grad_h2 = back(grad_hidden, w1)
    grad_g2 = jnp.sum(grad_h2 * normed2, axis=0)
    grad_b2 = jnp.sum(grad_h2, axis=0)
    grad_second = grad_out + norm_back(grad_h2 * g2.astype(jnp.float32), normed2, factor2)
    grad_y1 = grad_second.astype(jnp.bfloat16)
    grad_wo = outer(mixed, grad_y1)
    grad_bo = column_sum(grad_y1)
    grad_mixed = back(grad_y1, wo).astype(jnp.bfloat16).reshape(count, heads, 64)
    keys_all, values_all = (
        lax.all_gather(keys_rot, "grp", axis=0, tiled=True),
        lax.all_gather(values, "grp", axis=0, tiled=True),
    )
    total = keys_all.shape[0]
    keys_all = keys_all.reshape(total, heads, 64)
    values_all = values_all.reshape(total, heads, 64)
    scores = (
        jnp.einsum("thd,shd->hts", query_rot, keys_all, preferred_element_type=jnp.float32) * SCALE
    )
    probs = jnp.exp(scores - lse)
    grad_probs = jnp.einsum(
        "thd,shd->hts", grad_mixed, values_all, preferred_element_type=jnp.float32
    )
    delta = jnp.sum(probs * grad_probs, axis=-1, keepdims=True)
    grad_scores = (probs * (grad_probs - delta)).astype(jnp.bfloat16)
    grad_query = (
        jnp.einsum("hts,shd->thd", grad_scores, keys_all, preferred_element_type=jnp.float32)
        * SCALE
    )
    probs_low = probs.astype(jnp.bfloat16)
    grad_values = jnp.einsum(
        "hts,thd->shd", probs_low, grad_mixed, preferred_element_type=jnp.float32
    )
    grad_keys = (
        jnp.einsum("hts,thd->shd", grad_scores, query_rot, preferred_element_type=jnp.float32)
        * SCALE
    )
    keys_own, values_own = (
        lax.psum_scatter(
            grad_keys.reshape(total, width).astype(jnp.bfloat16),
            "grp",
            scatter_dimension=0,
            tiled=True,
        ).astype(jnp.float32),
        lax.psum_scatter(
            grad_values.reshape(total, width).astype(jnp.bfloat16),
            "grp",
            scatter_dimension=0,
            tiled=True,
        ).astype(jnp.float32),
    )
    query_back = rotate(grad_query, cosine, -sine).reshape(count, width)
    keys_back = rotate(keys_own.reshape(count, heads, 64), cosine, -sine).reshape(count, width)
    grad_qkv = jnp.concatenate([query_back, keys_back, values_own], axis=1).astype(jnp.bfloat16)
    grad_wqkv = outer(h1, grad_qkv)
    grad_bqkv = column_sum(grad_qkv)
    grad_h1 = back(grad_qkv, wqkv)
    grad_g1 = jnp.sum(grad_h1 * normed1, axis=0)
    grad_b1 = jnp.sum(grad_h1, axis=0)
    grad_field = grad_second + norm_back(grad_h1 * g1.astype(jnp.float32), normed1, factor1)
    terms = (
        grad_g1,
        grad_b1,
        grad_wqkv,
        grad_bqkv,
        grad_wo,
        grad_bo,
        grad_g2,
        grad_b2,
        grad_w1,
        grad_bu,
        grad_w2,
        grad_bd,
    )
    totals = tuple((a + b for a, b in zip(totals, terms)))
    return (grad_field.astype(jnp.bfloat16), totals)


def local(
    tokens,
    positions,
    ln1_gain,
    ln1_bias,
    w_qkv,
    b_qkv,
    w_out,
    b_out,
    ln2_gain,
    ln2_bias,
    w_up,
    b_up,
    w_down,
    b_down,
    cotangent,
):
    shards = (
        ln1_gain,
        ln1_bias,
        w_qkv,
        b_qkv,
        w_out,
        b_out,
        ln2_gain,
        ln2_bias,
        w_up,
        b_up,
        w_down,
        b_down,
    )
    groups = lax.axis_size("grp")
    totals = tuple((jnp.zeros((s.shape[0] * groups,) + s.shape[1:], jnp.float32) for s in shards))
    outputs = []
    gradients = []
    for index in range(tokens.shape[0]):
        forward_params = (
            lax.all_gather(ln1_gain, "grp", axis=0, tiled=True),
            lax.all_gather(ln1_bias, "grp", axis=0, tiled=True),
            lax.all_gather(w_qkv, "grp", axis=0, tiled=True),
            lax.all_gather(b_qkv, "grp", axis=0, tiled=True),
            lax.all_gather(w_out, "grp", axis=0, tiled=True),
            lax.all_gather(b_out, "grp", axis=0, tiled=True),
            lax.all_gather(ln2_gain, "grp", axis=0, tiled=True),
            lax.all_gather(ln2_bias, "grp", axis=0, tiled=True),
            lax.all_gather(w_up, "grp", axis=0, tiled=True),
            lax.all_gather(b_up, "grp", axis=0, tiled=True),
            lax.all_gather(w_down, "grp", axis=0, tiled=True),
            lax.all_gather(b_down, "grp", axis=0, tiled=True),
        )
        saved, result = forward_pass(forward_params, tokens[index], positions[:, index, :])
        outputs.append(result)
        backward_params = (
            lax.all_gather(ln1_gain, "grp", axis=0, tiled=True),
            lax.all_gather(ln1_bias, "grp", axis=0, tiled=True),
            lax.all_gather(w_qkv, "grp", axis=0, tiled=True),
            lax.all_gather(b_qkv, "grp", axis=0, tiled=True),
            lax.all_gather(w_out, "grp", axis=0, tiled=True),
            lax.all_gather(b_out, "grp", axis=0, tiled=True),
            lax.all_gather(ln2_gain, "grp", axis=0, tiled=True),
            lax.all_gather(ln2_bias, "grp", axis=0, tiled=True),
            lax.all_gather(w_up, "grp", axis=0, tiled=True),
            lax.all_gather(b_up, "grp", axis=0, tiled=True),
            lax.all_gather(w_down, "grp", axis=0, tiled=True),
            lax.all_gather(b_down, "grp", axis=0, tiled=True),
        )
        grad_field, totals = backward_pass(backward_params, saved, cotangent[index], totals)
        gradients.append(grad_field)
    owned = (
        lax.psum_scatter(
            totals[0].astype(jnp.bfloat16), "grp", scatter_dimension=0, tiled=True
        ).astype(jnp.float32),
        lax.psum_scatter(
            totals[1].astype(jnp.bfloat16), "grp", scatter_dimension=0, tiled=True
        ).astype(jnp.float32),
        lax.psum_scatter(
            totals[2].astype(jnp.bfloat16), "grp", scatter_dimension=0, tiled=True
        ).astype(jnp.float32),
        lax.psum_scatter(
            totals[3].astype(jnp.bfloat16), "grp", scatter_dimension=0, tiled=True
        ).astype(jnp.float32),
        lax.psum_scatter(
            totals[4].astype(jnp.bfloat16), "grp", scatter_dimension=0, tiled=True
        ).astype(jnp.float32),
        lax.psum_scatter(
            totals[5].astype(jnp.bfloat16), "grp", scatter_dimension=0, tiled=True
        ).astype(jnp.float32),
        lax.psum_scatter(
            totals[6].astype(jnp.bfloat16), "grp", scatter_dimension=0, tiled=True
        ).astype(jnp.float32),
        lax.psum_scatter(
            totals[7].astype(jnp.bfloat16), "grp", scatter_dimension=0, tiled=True
        ).astype(jnp.float32),
        lax.psum_scatter(
            totals[8].astype(jnp.bfloat16), "grp", scatter_dimension=0, tiled=True
        ).astype(jnp.float32),
        lax.psum_scatter(
            totals[9].astype(jnp.bfloat16), "grp", scatter_dimension=0, tiled=True
        ).astype(jnp.float32),
        lax.psum_scatter(
            totals[10].astype(jnp.bfloat16), "grp", scatter_dimension=0, tiled=True
        ).astype(jnp.float32),
        lax.psum_scatter(
            totals[11].astype(jnp.bfloat16), "grp", scatter_dimension=0, tiled=True
        ).astype(jnp.float32),
    )
    summed = (
        lax.psum(owned[0].astype(jnp.bfloat16), "rep").astype(jnp.float32),
        lax.psum(owned[1].astype(jnp.bfloat16), "rep").astype(jnp.float32),
        lax.psum(owned[2].astype(jnp.bfloat16), "rep").astype(jnp.float32),
        lax.psum(owned[3].astype(jnp.bfloat16), "rep").astype(jnp.float32),
        lax.psum(owned[4].astype(jnp.bfloat16), "rep").astype(jnp.float32),
        lax.psum(owned[5].astype(jnp.bfloat16), "rep").astype(jnp.float32),
        lax.psum(owned[6].astype(jnp.bfloat16), "rep").astype(jnp.float32),
        lax.psum(owned[7].astype(jnp.bfloat16), "rep").astype(jnp.float32),
        lax.psum(owned[8].astype(jnp.bfloat16), "rep").astype(jnp.float32),
        lax.psum(owned[9].astype(jnp.bfloat16), "rep").astype(jnp.float32),
        lax.psum(owned[10].astype(jnp.bfloat16), "rep").astype(jnp.float32),
        lax.psum(owned[11].astype(jnp.bfloat16), "rep").astype(jnp.float32),
    )
    output = jnp.stack(outputs, axis=0)
    grad_tokens = jnp.stack(gradients, axis=0)
    return (
        output,
        grad_tokens,
        summed[0],
        summed[1],
        summed[2],
        summed[3],
        summed[4],
        summed[5],
        summed[6],
        summed[7],
        summed[8],
        summed[9],
        summed[10],
        summed[11],
    )


def spread(mesh):
    placed = (
        P("rep", "grp", None),
        P(None, "rep", "grp"),
        P("grp"),
        P("grp"),
        P("grp", None),
        P("grp"),
        P("grp", None),
        P("grp"),
        P("grp"),
        P("grp"),
        P("grp", None),
        P("grp"),
        P("grp", None),
        P("grp"),
        P("rep", "grp", None),
    )
    return jax.shard_map(
        local,
        mesh=mesh,
        in_specs=placed,
        out_specs=(
            P("rep", "grp", None),
            P("rep", "grp", None),
            P("grp"),
            P("grp"),
            P("grp", None),
            P("grp"),
            P("grp", None),
            P("grp"),
            P("grp"),
            P("grp"),
            P("grp", None),
            P("grp"),
            P("grp", None),
            P("grp"),
        ),
        check_vma=False,
    )


def solution(mesh):
    reps, groups = mesh.devices.shape
    flat = mesh.devices.reshape(-1)

    def run(*args):
        clips = args[0].shape[0] // reps
        if reps == 8 and groups == 2 * clips:
            split = Mesh(flat.reshape(reps // 2, 2, groups), ("rp", "core", "grp"))
            ins, outs = paired_specs()
            return jax.shard_map(
                paired, mesh=split, in_specs=ins, out_specs=outs, check_vma=False
            )(*args)
        return spread(mesh)(*args)

    return run
```

```python
import functools

import jax
import jax.numpy as jnp
from jax import lax
from jax.experimental import pallas as pl
from jax.experimental.pallas import tpu as pltpu
from jax.sharding import Mesh
from jax.sharding import PartitionSpec as P

SCALE = 0.125
EPS = 1e-06
HEAD = 64
BF = jnp.bfloat16
F32 = jnp.float32
MESH = pl.DeviceIdType.MESH
ANY = pl.BlockSpec(memory_space=pl.ANY)
VM = pl.BlockSpec(memory_space=pltpu.VMEM)


def where_am_i():
    return lax.axis_index("rp"), lax.axis_index("core"), lax.axis_index("grp")


def remote(src, dst, send, recv, target):
    return pltpu.make_async_remote_copy(
        src_ref=src,
        dst_ref=dst,
        send_sem=send,
        recv_sem=recv,
        device_id=target,
        device_id_type=MESH,
    )


def enter(p, c, z, groups):
    barrier = pltpu.get_barrier_semaphore()
    for k in range(groups):
        for d in range(2):
            if k == 0 and d == 0:
                continue
            pl.semaphore_signal(
                barrier, inc=1, device_id=(p, c ^ d, lax.rem(z + k, groups)), device_id_type=MESH
            )
    for b in (1, 2):
        pl.semaphore_signal(barrier, inc=1, device_id=(p ^ b, c, z), device_id_type=MESH)
    pl.semaphore_wait(barrier, 2 * groups - 1 + 2)


def move_tokens(refs, outs, send, recv, p, c, z, clips):
    core, slot = lax.div(z, clips), lax.rem(z, clips)

    def route(i):
        return core, c * clips + i

    def here(i):
        return jnp.logical_and(core == c, c * clips + i == z)

    def start(k, pieces):
        for n, (src, dst) in enumerate(zip(refs, outs)):
            rows = src.shape[1] // pieces
            rows = pl.ds(k * rows, rows)
            for i in range(clips):
                tc, tz = route(i)

                @pl.when(here(i))
                def _():
                    pltpu.make_async_copy(
                        src.at[i, rows], dst.at[slot, rows], recv.at[n, slot]
                    ).start()

                @pl.when(jnp.logical_not(here(i)))
                def _():
                    remote(
                        src.at[i, rows],
                        dst.at[slot, rows],
                        send.at[n, i],
                        recv.at[n, slot],
                        (p, tc, tz),
                    ).start()

    def sent():
        for n, (src, dst) in enumerate(zip(refs, outs)):
            for i in range(clips):

                @pl.when(jnp.logical_not(here(i)))
                def _():
                    remote(
                        src.at[i], dst.at[slot], send.at[n, i], recv.at[n, slot], (p, c ^ 1, z)
                    ).wait_send()

    def arrive():
        for n, (src, dst) in enumerate(zip(refs, outs)):
            for m in range(clips):
                pltpu.make_async_copy(src.at[0], dst.at[m], recv.at[n, m]).wait()

    def finish():
        sent()
        arrive()

    return start, finish, sent, arrive


def turn(u, cosine, sine):
    half = HEAD // 2
    first, second = u[:half], u[half:]
    return jnp.concatenate(
        [first * cosine - second * sine, first * sine + second * cosine], axis=0
    )


def dot(a, b):
    return jnp.dot(a, b, preferred_element_type=F32)


def dot_t(a, b):
    return lax.dot_general(a, b, (((1,), (1,)), ((), ())), preferred_element_type=F32)


def tile(i, size):
    return pl.ds(pl.multiple_of(i * size, size), size)


def cuts(whole, half, c, blocks):
    if blocks == 0:
        return [(whole.at[c], half)]
    size = half.shape[3] // blocks
    return [
        (
            whole.at[:, :, :, pl.ds(pl.multiple_of((2 * b + c) * size, size), size)],
            half.at[:, :, :, pl.ds(b * size, size)],
        )
        for b in range(blocks)
    ]


def forward_body(groups, clips, blocks, *refs):
    count = len(blocks)
    raw, (small, x, tab, dy) = refs[:count], refs[count : count + 4]
    (wq_o, wo_o, *outs) = refs[count + 4 : 2 * count + 4]
    (small_o, x_o, tab_o, dy_o, h1_o, qs_o, kr_o, vb_o, mix_o, lse_o, x2_o, h2_o) = refs[
        2 * count + 4 : 2 * count + 16
    ]
    halves = refs[2 * count + 16 : 3 * count + 16]
    (wq_v, small_v, x_v, tab_v, tab_w, h1, qs, kr, vb, mix, qkv, gain, bias) = refs[
        3 * count + 16 : 3 * count + 29
    ]
    (wo_v, own_f, give, take, h2) = refs[3 * count + 29 : 3 * count + 34]
    (zs, zr, xs, xr, ys, yr, fs, fr, hs, ls, ss, sr, ts, tr, us, ur, vs, vr, es, er, ks) = refs[
        3 * count + 34 :
    ]
    outs = [wq_v, wo_v, *outs]
    p, c, z = where_am_i()
    for w in range(count):
        for src, dst in cuts(raw[w], halves[w], c, blocks[w]):
            pltpu.make_async_copy(src, dst, hs.at[w]).start()
    enter(p, c, z, groups)
    col = [(p, c, lax.rem(z + k, groups)) for k in range(groups)]
    org = [lax.rem(z + groups - k, groups) for k in range(groups)]
    xn, yn, cn = (p ^ 1, c, z), (p ^ 2, c, z), (p, c ^ 1, z)
    smalls = [
        remote(small, small_v.at[z], ss.at[k], sr.at[k], col[k]) for k in range(1, groups)
    ]
    for s in smalls:
        s.start()
    keep = [pltpu.make_async_copy(small, small_v.at[z], ls.at[count])]
    keep[0].start()
    start_tab, _, sent_tab, arrive_tab = move_tokens((tab,), (tab_v,), vs, vr, p, c, z, clips)
    start_x, _, sent_x, arrive_x = move_tokens((x,), (x_v,), ts, tr, p, c, z, clips)
    start_dy, _, sent_dy, arrive_dy = move_tokens((dy,), (dy_o.at[:clips],), us, ur, p, c, z, clips)
    units = [(w, d, side) for w in range(count) for d in range(1, groups) for side in range(2)]

    def origin(d, side):
        return z - d if side == 0 else z + d

    def arrives(d, side):
        return z >= d if side == 0 else z + d < groups

    def leaves(d, side):
        if side == 0:
            return jnp.logical_and(z + 1 < groups, z + 1 >= d)
        return jnp.logical_and(z >= 1, z - 1 + d < groups)

    def hop(w, d, side, src):
        o = origin(d - 1, side)
        target = (p, c, lax.rem(z + 1 if side == 0 else z + groups - 1, groups))
        return remote(src, outs[w].at[o, p], zs.at[w, side, d], zr.at[w, side, d], target)

    def own(w):
        pltpu.make_async_copy(halves[w], halves[w], hs.at[w]).wait()
        keep.append(pltpu.make_async_copy(halves[w], outs[w].at[z], ls.at[w]))
        keep[-1].start()
        for side in range(2):

            @pl.when(leaves(1, side))
            def _():
                hop(w, 1, side, halves[w].at[p]).start()

    def links(u):
        w, d, side = u
        o = outs[w].at[lax.rem(origin(d, side) + groups, groups)]
        e, f = xs.at[w, side, d], xr.at[w, side, d]
        g, h = ys.at[w, side, d], yr.at[w, side, d]
        a, b = fs.at[w, side, d, 0], fr.at[w, side, d, 0]
        m, n = fs.at[w, side, d, 1], fr.at[w, side, d, 1]
        across = lambda q: remote(o.at[q], o.at[q], e, f, xn)
        along = lambda q: remote(o.at[q], o.at[q], g, h, yn)
        first = lambda q: remote(o.at[q, 0], o.at[q, 0], a, b, yn)
        second = lambda q: remote(o.at[q, 1], o.at[q, 1], m, n, xn)
        return o, across, along, first, second

    def plane(u):
        w, d, side = u
        o, across, along, first, second = links(u)

        @pl.when(arrives(d, side))
        def _():
            remote(o.at[p], o.at[p], zs.at[w, side, d], zr.at[w, side, d], xn).wait_recv()
            if d + 1 < groups:

                @pl.when(leaves(d + 1, side))
                def _():
                    hop(w, d + 1, side, o.at[p]).start()

            across(p).start()
            along(p).start()

    def forward(u):
        w, d, side = u
        o, across, along, first, second = links(u)

        @pl.when(arrives(d, side))
        def _():
            across(p ^ 1).wait_recv()
            first(p ^ 1).start()
            along(p ^ 2).wait_recv()
            second(p ^ 2).start()

    def complete(u):
        w, d, side = u
        o, across, along, first, second = links(u)

        @pl.when(arrives(d, side))
        def _():
            first(p ^ 3).wait_recv()
            second(p ^ 3).wait_recv()

    def settle(u):
        w, d, side = u
        o, across, along, first, second = links(u)

        @pl.when(arrives(d, side))
        def _():
            across(p).wait_send()
            along(p).wait_send()
            first(p).wait_send()
            second(p).wait_send()

        @pl.when(leaves(d, side))
        def _():
            hop(w, d, side, halves[w].at[p]).wait_send()

    own(0)
    start_tab(0, 1)
    own(1)
    moves = {2 * k: (start_x, k) for k in range(4)}
    moves.update({10 + 3 * k: (start_dy, k) for k in range(4)})
    lag = 3

    def step(n):
        if n < len(units):
            plane(units[n])
            w, d, side = units[n]
            if (d, side) == (1, 1) and w + 2 < count:
                own(w + 2)
            if n in moves:
                moves[n][0](moves[n][1], 4)
        if n >= lag:
            forward(units[n - lag])

    steps = list(range(len(units) + lag))
    early = 2 * (groups - 1) + lag
    for _ in range(early):
        step(steps.pop(0))
    for k in range(1, groups):
        remote(small, small_v.at[org[k]], ss.at[k], sr.at[k], col[k]).wait_recv()
    keep[0].wait()
    row = small_v.shape[2]
    half = row // 2
    mine = pl.ds(pl.multiple_of(c * half, half), half)
    for g in range(groups):
        gain[0:5, g * row : (g + 1) * row] = small_v[g, 0:5]
        for r in range(3):
            bias[3 * g + r : 3 * g + r + 1] = small_v[g, 6 + r : 7 + r, mine]
    small_o[...] = small_v[...]
    own_count = h1.shape[0] // 2
    arrive_x()
    saves = [pltpu.make_async_copy(x_v, x_o, ks.at[0])]
    saves[0].start()

    def norm(i, carry):
        per = own_count // clips // 128
        v = x_v[lax.div(i, per), tile(lax.rem(i, per), 128)].astype(F32)
        v = v - jnp.mean(v, axis=1, keepdims=True)
        v = v * lax.rsqrt(jnp.mean(v * v, axis=1, keepdims=True) + EPS)
        h1[tile(i, 128)] = (v * gain[0:1] + gain[1:2]).astype(BF)
        return carry

    lax.fori_loop(0, own_count // 128, norm, 0)
    swap = remote(h1.at[:own_count], h1.at[own_count:], es.at[0], er.at[0], cn)
    swap.start()
    arrive_tab()
    swap_tab = remote(tab_v, tab_w, es.at[1], er.at[1], cn)
    swap_tab.start()
    step(steps.pop(0))
    swap_tab.wait()
    part = tab_v.shape[2]
    for m in range(clips):
        tab_o[:, m * part : (m + 1) * part] = tab_v[m]
        tab_o[:, own_count + m * part : own_count + (m + 1) * part] = tab_w[m]
    for u in units[: 2 * (groups - 1)]:
        complete(u)
    keep[1].wait()
    saves.append(pltpu.make_async_copy(wq_v, wq_o, ks.at[1]))
    saves[1].start()
    swap.wait()
    saves.append(pltpu.make_async_copy(h1, h1_o, ks.at[2]))
    saves[2].start()
    inner = qs.shape[0]
    heads = inner // HEAD
    pairs = heads // 2

    def head(h, side):
        rows, place = tile(h, HEAD), tile(side, HEAD)
        co, si = tab_o[: HEAD // 2], tab_o[HEAD // 2 :]
        k = turn(qkv[1, place], co, si).astype(BF)
        v = qkv[2, place].astype(BF)
        q = (turn(qkv[0, place], co, si).astype(BF).astype(F32) * SCALE).astype(BF)
        kr[rows] = k
        vb[rows] = v
        qs[rows] = q
        keys = k.T
        size = 256
        for i in range(0, 2 * own_count, size):
            scores = dot(keys, q[:, i : i + size])
            top = jnp.max(scores, axis=0, keepdims=True)
            e = jnp.exp(scores - top)
            total = jnp.sum(e, axis=0, keepdims=True)
            mixed = dot(v, e.astype(BF))
            mix[rows, i : i + size] = (mixed / total).astype(BF)
            lse_o[h, :, i : i + size] = top + jnp.log(total)

    during = [steps.pop(0) for _ in range(heads + heads // 2)]

    def two_heads(i, carry):
        def project(n, carry):
            at = pl.ds(pl.multiple_of(n * inner + i * 2 * HEAD, 2 * HEAD), 2 * HEAD)
            w = wq_v[..., at].reshape(h1.shape[1], 2 * HEAD)
            qkv[n] = (dot(h1[...], w) + bias[pl.ds(n * pairs + i, 1)]).T
            return carry

        lax.fori_loop(0, 3, project, 0)
        for n in range(pairs):

            @pl.when(i == n)
            def _():
                step(during[3 * n])

        def one(side, carry):
            head(2 * i + side, side)
            for n in range(heads):

                @pl.when(2 * i + side == n)
                def _():
                    step(during[3 * (n // 2) + 1 + n % 2])

            return carry

        lax.fori_loop(0, 2, one, 0)
        return carry

    lax.fori_loop(0, pairs, two_heads, 0)
    for n, (a, b) in enumerate(((qs, qs_o), (kr, kr_o), (vb, vb_o), (mix, mix_o))):
        saves.append(pltpu.make_async_copy(a, b, ks.at[3 + n]))
        saves[-1].start()
    for u in units[2 * (groups - 1) : 4 * (groups - 1)]:
        complete(u)
    keep[2].wait()
    saves.append(pltpu.make_async_copy(wo_v, wo_o, ks.at[7]))
    saves[-1].start()
    width = h1.shape[1]
    left_other, left_self = mix[:, own_count:].T, mix[:, :own_count].T

    def out_other(i, carry):
        at = tile(i, 256)
        give[:, at] = dot(left_other, wo_v[..., at].reshape(inner, 256)).astype(BF)
        return carry

    def out_self(i, carry):
        at = tile(i, 256)
        own_f[:, at] = dot(left_self, wo_v[..., at].reshape(inner, 256))
        return carry

    lax.fori_loop(0, width // 256, out_other, 0)
    swap = remote(give, take, es.at[2], er.at[2], cn)
    swap.start()
    lax.fori_loop(0, width // 256, out_self, 0)
    step(steps.pop(0))
    swap.wait()

    def second_norm(i, carry):
        per = own_count // clips // 128
        at = tile(i, 128)
        v = x_v[lax.div(i, per), tile(lax.rem(i, per), 128)].astype(F32)
        v = v + (own_f[at] + take[at].astype(F32)) + gain[2:3]
        own_f[at] = v
        v = v - jnp.mean(v, axis=1, keepdims=True)
        v = v * lax.rsqrt(jnp.mean(v * v, axis=1, keepdims=True) + EPS)
        h2[at] = (v * gain[3:4] + gain[4:5]).astype(BF)
        return carry

    lax.fori_loop(0, own_count // 128, second_norm, 0)
    swap = remote(h2.at[:own_count], h2.at[own_count:], es.at[0], er.at[0], cn)
    swap.start()
    saves.append(pltpu.make_async_copy(own_f, x2_o, ks.at[8]))
    saves[-1].start()
    step(steps.pop(0))
    swap.wait()
    saves.append(pltpu.make_async_copy(h2, h2_o, ks.at[9]))
    saves[-1].start()
    while steps:
        step(steps.pop(0))
    arrive_dy()
    swap_dy = remote(dy_o.at[:clips], dy_o.at[clips:], es.at[3], er.at[3], cn)
    swap_dy.start()
    for u in units[4 * (groups - 1) :]:
        complete(u)
    for u in units:
        settle(u)
    for s in smalls:
        s.wait_send()
    for k in keep[3:] + saves:
        k.wait()
    swap_dy.wait()
    sent_dy()
    sent_tab()
    sent_x()


def half_shape(raw, blocks):
    return raw.shape[1:] if blocks == 0 else raw.shape[:3] + (raw.shape[3] // 2,)


def forward(raw, blocks, small, x, tab, dy, groups):
    count, clips = len(raw), x.shape[0]
    own, width = clips * x.shape[1], x.shape[2]
    halves = [half_shape(r, b) for r, b in zip(raw, blocks)]
    inner = halves[0][-1] // 3
    dma = pltpu.SemaphoreType.DMA
    of = jax.ShapeDtypeStruct
    feature = (inner, 2 * own)
    shapes = [of((groups,) + h, BF) for h in halves]
    shapes += [of((groups,) + small.shape, F32), of(x.shape, BF), of((HEAD, 2 * own), F32)]
    shapes += [of((2 * clips,) + x.shape[1:], BF), of((2 * own, width), BF)] + [of(feature, BF)] * 4
    shapes += [of((inner // HEAD, 1, 2 * own), F32), of((own, width), F32), of((2 * own, width), BF)]
    vm = pltpu.VMEM
    scratch = [vm(h, BF) for h in halves]
    scratch += [vm((groups,) + halves[0], BF), vm((groups,) + small.shape, F32), vm(x.shape, BF)]
    scratch += [vm(tab.shape, F32)] * 2 + [vm((2 * own, width), BF)] + [vm(feature, BF)] * 4
    scratch += [vm((3, 2 * HEAD, 2 * own), F32), vm((8, width), F32)]
    scratch += [vm((3 * groups + -3 * groups % 8, width // groups // 2), F32)]
    scratch += [vm((groups,) + halves[1], BF), vm((own, width), F32)]
    scratch += [vm((own, width), BF)] * 2 + [vm((2 * own, width), BF)]
    return pl.pallas_call(
        functools.partial(forward_body, groups, clips, blocks),
        out_shape=shapes,
        in_specs=[ANY] * count + [VM, ANY, ANY, ANY],
        out_specs=[ANY] * count + [VM, ANY, VM] + [ANY] * 6 + [VM, ANY, ANY],
        scratch_shapes=scratch
        + [dma((count, 2, groups))] * 6
        + [dma((count, 2, groups, 2))] * 2
        + [dma((count,)), dma((count + 1,)), dma((groups,)), dma((groups,))]
        + [dma((1, clips))] * 6
        + [dma((4,)), dma((4,)), dma((10,))],
        compiler_params=pltpu.CompilerParams(
            collective_id=0, has_side_effects=True, vmem_limit_bytes=60 * 1024 * 1024
        ),
        name="forward",
    )(*raw, small, x, tab, dy)


def backward_body(groups, clips, blocks, *refs):
    count = len(blocks)
    (gw2, act, slope, w2, w1, wo, wq, mix, qs, kr, vb, h1, h2, x2, x, dy, dy_all) = refs[:17]
    (lse, cosine, sine, g1, g2, bd) = refs[17:23]
    outs = refs[23 : 23 + count]
    gw1, small_o, gx_o, y_o = refs[23 + count : 27 + count]
    (gu_b, w1_b, wo_b, mix_b, qs_b, kr_b, vb_b, h1_b, x2_b, x_b, dy_b) = refs[27 + count : 38 + count]
    (own_f, give, take, y_take, dx2, low, da, gwo, gwq, ak, av, dq2, dk2, acc, gx) = refs[
        38 + count : 53 + count
    ]
    (sl, gbu, stage_b) = refs[53 + count : 56 + count]
    ld, es, er, sls = refs[56 + count : 60 + count]
    grads = (gwq, gwo, gw1, gw2)
    scratch = refs[60 + count :]
    own_a, own_b, one_a, one_b, two_a, two_b, three, full = (
        scratch[i * count : (i + 1) * count] for i in range(8)
    )
    small_s, small_r, small_z = scratch[8 * count : 8 * count + 3]
    (os, s1, r1, s2, r2, s3, r3, s4, r4, s5, r5, cs, cr, ls, ss, sr, ts, tr, us, ur) = scratch[
        8 * count + 3 :
    ]
    own, width = own_f.shape
    inner = mix_b.shape[0]
    third_width = wq.shape[1]

    upper, lower = w1_b.at[:, :width], w1_b.at[:, width:]
    pairs = ((w2.at[:width], upper), (w2.at[width:], lower), (dy_all, low), (h2, h1_b))
    pairs += ((x2, x2_b), (dy.at[:clips], dy_b), (mix, mix_b), (wo, wo_b))
    pairs += ((qs, qs_b), (kr, kr_b), (vb, vb_b), (x, x_b))
    pairs += ((w1, w1_b), (h1, h1_b), (act, gu_b), (w2.at[:width], upper), (w2.at[width:], lower))
    pairs += ((wq, w1_b.at[:, :third_width]),)
    loads = [pltpu.make_async_copy(a, b, ld.at[n]) for n, (a, b) in enumerate(pairs)]
    first_tile = pltpu.make_async_copy(slope.at[:, :256], sl.at[0], sls.at[0])
    first_tile.start()
    for copy in loads[:12]:
        copy.start()
    p, c, z = where_am_i()
    hi, lo = lax.div(p, 2), lax.rem(p, 2)
    enter(p, c, z, groups)
    col = [(p, c, lax.rem(z + k, groups)) for k in range(groups)]
    xn, yn, cn = (p ^ 1, c, z), (p ^ 2, c, z), (p, c ^ 1, z)
    order = (3, 2, 1, 0)
    units = [(w, j) for w in order for j in [*range(1, groups), 0]]
    sides = ((own_a, one_a, two_a, hi, yn), (own_b, one_b, two_b, lo, xn))

    def c1(u, n):
        w, j = u
        g = grads[w].at[lax.rem(z + j, groups)]
        src, target = (g.at[:, 1 - lo, 0], xn) if n == 0 else (g.at[1 - hi, :, 1], yn)
        return remote(src, sides[n][1][w].at[j], s1.at[w, j, n], r1.at[w, j, n], target)

    def load(u, n):
        w, j = u
        g = grads[w].at[lax.rem(z + j, groups)]
        src = g.at[:, lo, 0] if n == 0 else g.at[hi, :, 1]
        return pltpu.make_async_copy(src, sides[n][0][w].at[j], os.at[w, j, n])

    def c2(u, n):
        w, j = u
        own, one, two, side, target = sides[n]
        return remote(own[w].at[j, 1 - side], two[w].at[j], s2.at[w, j, n], r2.at[w, j, n], target)

    def c3(u, n):
        w, j = u
        src = sides[n][0][w].at[j, sides[n][3]]
        return remote(src, three[w].at[j, n], s3.at[w, j, n], r3.at[w, j, n], col[j])

    def c4(w, n):
        f = full[w].at[p]
        return remote(f, f, s4.at[w, n], r4.at[w, n], (xn, yn)[n])

    def c5(w, n):
        f = full[w].at[(p ^ 1, p ^ 2)[n], n]
        return remote(f, f, s5.at[w, n], r5.at[w, n], (yn, xn)[n])

    def stage_zero(u):
        for n in range(2):
            c1(u, n).start()
            load(u, n).start()

    def stage_one(u):
        w, j = u
        for n, (own, one, two, side, target) in enumerate(sides):
            load(u, n).wait()
            c1(u, n).wait_recv()
            own[w][j] = (own[w][j].astype(F32) + one[w][j].astype(F32)).astype(BF)
            c2(u, n).start()

    def stage_two(u):
        w, j = u
        for n, (own, one, two, side, target) in enumerate(sides):
            c2(u, n).wait_recv()
            own[w][j, side] = (own[w][j, side].astype(F32) + two[w][j].astype(F32)).astype(BF)
            if j:
                c3(u, n).start()

    def stage_three(w):
        for n, (own, one, two, side, target) in enumerate(sides):
            total = own[w][0, side].astype(F32)
            for j in range(1, groups):
                c3((w, j), n).wait_recv()
                total = total + three[w][j, n].astype(F32)
            full[w][p, n] = total.astype(BF)
        for n in range(2):
            c4(w, n).start()

    def stage_four(w):
        for n, target in enumerate((yn, xn)):
            f = full[w].at[(p ^ 1, p ^ 2)[n]]
            remote(f, f, s4.at[w, n], r4.at[w, n], target).wait_recv()
            c5(w, n).start()

    def stage_five(w):
        for n in range(2):
            f = full[w].at[p ^ 3, n]
            remote(f, f, s5.at[w, n], r5.at[w, n], xn).wait_recv()
        for dst, src in cuts(outs[w], full[w], c, blocks[w]):
            pltpu.make_async_copy(src, dst, ls.at[w]).start()
            remote(src, dst, cs.at[w], cr.at[w], cn).start()

    ahead, lag = 3, 2
    todo = {}
    for n, u in enumerate(units):
        todo.setdefault(max(n - ahead, -1), []).append((stage_zero, u))
        todo.setdefault(n, []).append((stage_one, u))
        todo.setdefault(n + lag, []).append((stage_two, u))
    for i, w in enumerate(order):
        last = (i + 1) * groups - 1 + lag
        for at, stage in ((2, stage_three), (3, stage_four), (4, stage_five)):
            todo.setdefault(last + at, []).append((stage, w))
    steps = sorted(todo)

    def run(step):
        for stage, what in todo[step]:
            stage(what)

    def tick():
        run(steps.pop(0))

    def half_sum(n, left, right, depth):
        def other(i, carry):
            part = dot_t(left[own:, :depth], right[tile(i, 256), :depth])
            give[:, tile(i, 256)] = part.astype(BF)
            return carry

        def self(i, carry):
            own_f[:, tile(i, 256)] = dot_t(left[:own, :depth], right[tile(i, 256), :depth])
            return carry

        lax.fori_loop(0, width // 256, other, 0)
        copy = remote(give, take, es.at[n], er.at[n], cn)
        copy.start()
        lax.fori_loop(0, width // 256, self, 0)
        return copy

    def part(i):
        per = own // clips // 128
        return lax.div(i, per), tile(lax.rem(i, per), 128)

    def norm_step(i, field, gain, grad, row):
        at = tile(i, 128)
        d = own_f[at] + take[at].astype(F32)
        v = field[at].astype(F32)
        v = v - jnp.mean(v, axis=1, keepdims=True)
        r = lax.rsqrt(jnp.mean(v * v, axis=1, keepdims=True) + EPS)
        v = v * r
        acc[row : row + 1] += jnp.sum(d * v, axis=0, keepdims=True)
        acc[row + 1 : row + 2] += jnp.sum(d, axis=0, keepdims=True)
        e = d * gain[...]
        mean = jnp.mean(e, axis=1, keepdims=True)
        e = e - mean - v * jnp.mean(e * v, axis=1, keepdims=True)
        return grad + r * e

    tick()
    acc[...] = jnp.zeros_like(acc)
    for copy in loads[:3]:
        copy.wait()
    deep = slope.shape[1]
    sides_of = deep // width

    def hidden_grad(side, i):
        n = side * (width // 256) + i
        slot = lax.rem(n, 2)
        pltpu.make_async_copy(slope.at[:, :256], sl.at[slot], sls.at[slot]).wait()

        @pl.when(n + 1 < deep // 256)
        def _():
            src = slope.at[:, tile(n + 1, 256)]
            pltpu.make_async_copy(src, sl.at[1 - slot], sls.at[1 - slot]).start()

        right = w1_b[tile(i, 256), side * width : (side + 1) * width]
        line = jnp.zeros((1, 256), F32)
        for r in range(2):
            rows = slice(r * own, (r + 1) * own)
            g = dot_t(low[rows], right) * sl[slot, rows].astype(F32)
            g = g.astype(BF)
            gu_b[rows, tile(n, 256)] = g
            line = line + jnp.sum(g.astype(F32), axis=0, keepdims=True)
        gbu[:, tile(n, 256)] = line

    for side in range(sides_of):

        def columns(i, carry):
            hidden_grad(side, i)
            return carry

        lax.fori_loop(0, width // 256, columns, 0)
        if side == 0:
            tick()
    loads[12].start()
    loads[3].wait()
    row = width // groups

    def up_grad(j, carry):
        k = lax.rem(z + j, groups)
        left = h1_b[:, tile(k, row)].T

        def columns(i, carry):
            at = tile(i, 512)
            stage_b[..., at] = dot(left, gu_b[:, at]).astype(BF).reshape(stage_b.shape[:-1] + (512,))
            return carry

        lax.fori_loop(0, deep // 512, columns, 0)
        copy = pltpu.make_async_copy(stage_b, gw1.at[k], ld.at[18])
        copy.start()
        copy.wait()
        return carry

    lax.fori_loop(1, 3, up_grad, 0)
    tick()
    lax.fori_loop(3, groups + 1, up_grad, 0)
    loads[13].start()
    tick()
    loads[12].wait()
    swap = half_sum(0, gu_b, w1_b, deep)
    for copy in loads[14:17]:
        copy.start()
    tick()
    for copy in loads[4:12]:
        copy.wait()
    swap.wait()

    def second_norm(i, carry):
        at = tile(i, 128)
        g = dy_b[part(i)].astype(F32)
        d = norm_step(i, x2_b, g2, g, 3)
        dx2[at] = d
        acc[5:6] += jnp.sum(g, axis=0, keepdims=True)
        low[at] = d.astype(BF)
        acc[2:3] += jnp.sum(d.astype(BF).astype(F32), axis=0, keepdims=True)
        return carry

    lax.fori_loop(0, own // 128, second_norm, 0)
    swap = remote(low.at[:own], low.at[own:], es.at[1], er.at[1], cn)
    swap.start()
    tick()
    swap.wait()

    def out_grad(i, carry):
        at = tile(i, 256)
        gwo[..., at] = dot(mix_b[...], low[:, at]).astype(BF).reshape(gwo.shape[:-1] + (256,))
        return carry

    lax.fori_loop(0, width // 256, out_grad, 0)

    def attn_grad(i, carry):
        at = tile(i, 256)
        da[:, at] = dot_t(wo_b[...], low[at]).astype(BF)
        return carry

    lax.fori_loop(0, 2 * own // 256, attn_grad, 0)
    tick()

    for copy in loads[14:17]:
        copy.wait()

    def down(rows, i):
        left = dot(gu_b[rows, :width], w1_b[:, tile(i, 256)])
        at = pl.ds(pl.multiple_of(width + i * 256, 256), 256)
        return left + dot(gu_b[rows, width:], w1_b[:, at])

    def down_other(i, carry):
        give[:, tile(i, 256)] = down(slice(own, 2 * own), i).astype(BF)
        return carry

    def down_self(i, carry):
        own_f[:, tile(i, 256)] = down(slice(0, own), i)
        return carry

    lax.fori_loop(0, width // 256, down_other, 0)
    y_copy = remote(give, y_take, es.at[3], er.at[3], cn)
    y_copy.start()
    lax.fori_loop(0, width // 256, down_self, 0)
    loads[17].start()
    y_copy.wait()

    def last_add(i, carry):
        at = tile(i, 128)
        gx[part(i)] = (x2_b[at] + own_f[at] + bd[...] + y_take[at].astype(F32)).astype(BF)
        return carry

    lax.fori_loop(0, own // 128, last_add, 0)
    y_start, y_finish, *_ = move_tokens((gx,), (y_o,), us, ur, p, c, z, clips)
    y_start(0, 4)
    dqkv = gu_b.at[:, :third_width]

    def head(h, side):
        rows = tile(h, HEAD)
        place = tile(side, HEAD)
        co, si = cosine[...], sine[...]
        kt = kr_b[rows]
        keys, values = kt.T, vb_b[rows].T
        queries, outer_grads = qs_b[rows].T, da[rows].T
        step = 256
        for i in range(0, 2 * own, step):
            s = slice(i, i + step)
            g = da[rows, s]
            p = jnp.exp(dot(keys, qs_b[rows, s]) - lse[h, :, s])
            delta = jnp.sum(mix_b[rows, s].astype(F32) * g.astype(F32), axis=0, keepdims=True)
            ds = (p * (dot(values, g) - delta)).astype(BF)
            dq2[place, s] = turn(dot(kt, ds) * SCALE, co[:, s], -si[:, s]).astype(BF)
            dv = dot(p.astype(BF), outer_grads[s])
            dk = dot(ds, queries[s])
            if i == 0:
                ak[...] = dk
                av[side] = dv
            else:
                ak[...] += dk
                av[side] += dv
        dk2[place] = turn(ak[...].T, co, -si).astype(BF)

    heads = inner // HEAD
    during = [steps.pop(0) for _ in range(3)]

    def two_heads(i, carry):
        lax.fori_loop(0, 2, lambda side, _: head(2 * i + side, side), None)
        for n, value in enumerate(
            (dq2[...].T, dk2[...].T, jnp.concatenate([av[0], av[1]], axis=1).astype(BF))
        ):
            at = pl.ds(pl.multiple_of(n * inner + i * 2 * HEAD, 2 * HEAD), 2 * HEAD)
            dqkv[:, at] = value
        for n, step in enumerate(during):
            pl.when(i == n * heads // 8)(functools.partial(run, step))
            pl.when(i == n * heads // 8)(functools.partial(y_start, n + 1, 4))
        return carry

    lax.fori_loop(0, heads // 2, two_heads, 0)
    loads[13].wait()
    for g in range(groups):
        left = h1_b[:, g * row : (g + 1) * row].T

        def in_grad(i, carry):
            at = tile(i, 512)
            gwq[g, ..., at] = dot(left, dqkv[:, at]).astype(BF).reshape(gwq.shape[1:-1] + (512,))
            return carry

        lax.fori_loop(0, third_width // 512, in_grad, 0)
    tick()
    loads[17].wait()
    swap = half_sum(2, dqkv, w1_b, third_width)
    tick()
    swap.wait()
    y_finish()

    def first_norm(i, carry):
        gx[part(i)] = norm_step(i, x_b, g1, dx2[tile(i, 128)], 0).astype(BF)
        return carry

    lax.fori_loop(0, own // 128, first_norm, 0)
    start, finish, *_ = move_tokens((gx,), (gx_o,), ts, tr, p, c, z, clips)
    start(0, 4)
    tick()
    small_s[...] = jnp.zeros_like(small_s)
    for n in range(6):
        for g in range(groups):
            small_s[g, n : n + 1] = acc[n : n + 1, g * row : (g + 1) * row]
    half = row // 2
    mine_at = pl.ds(pl.multiple_of(c * half, half), half)
    for b in range(3 * groups):
        line = jnp.sum(dqkv[:, b * half : (b + 1) * half].astype(F32), axis=0, keepdims=True)
        small_s[b // 3, 6 + b % 3 : 7 + b % 3, mine_at] = line
    share = deep // groups
    for g in range(groups):
        for n in range(share // row):
            at = pl.ds(9 + c * (share // row) + n, 1)
            small_s[g, at] = gbu[:, g * share + n * row : g * share + (n + 1) * row]
    tick()
    for n, target in enumerate((cn, xn, yn)):
        copy = remote(small_s, small_r.at[n], ss.at[n], sr.at[n], target)
        copy.start()
        start(n + 1, 4)
        for _ in range(1 if n == 0 else 3):
            tick()
        copy.wait()
        small_s[...] += small_r[n]
    tails = [
        remote(small_s.at[col[k][2]], small_z.at[k], ss.at[2 + k], sr.at[2 + k], col[k])
        for k in range(1, groups)
    ]
    for t in tails:
        t.start()
    while steps:
        tick()
    for k in range(1, groups):
        tails[k - 1].wait()
    small_o[...] = small_s[z]
    for k in range(1, groups):
        small_o[...] += small_z[k]
    for u in units:
        w, j = u
        for n in range(2):
            c1(u, n).wait_send()
            c2(u, n).wait_send()
            if j:
                c3(u, n).wait_send()
    for w in range(count):
        for n in range(2):
            c4(w, n).wait_send()
            c5(w, n).wait_send()
        pltpu.make_async_copy(full[w], full[w], ls.at[w]).wait()
        remote(full[w], full[w], cs.at[w], cr.at[w], cn).wait()
    finish()


def backward(gw2, arrays, tables, lines, groups, blocks):
    act, slope, w2, w1, wo, wq, mix, qs, kr, vb, h1, h2, x2, x, dy, dy_all = arrays
    (own, width), clips = x.shape, dy.shape[0] // 2
    moved = jax.ShapeDtypeStruct((clips,) + dy.shape[1:], BF)
    small = jax.ShapeDtypeStruct((groups, lines + -lines % 8, width // groups), F32)
    count = len(blocks)
    dma = pltpu.SemaphoreType.DMA
    split = lambda v: (groups, 2, 2, 2, v.shape[0] // (8 * groups), v.shape[1])
    tiles = [split(v)[4:] for v in (wq, wo, w1, w2)]
    shapes = [
        jax.ShapeDtypeStruct((4, 2, t[0], 2 * t[1]) if b else (2, 4, 2) + t, BF)
        for t, b in zip(tiles, blocks)
    ]
    shapes += [
        jax.ShapeDtypeStruct(split(w1), BF),
        jax.ShapeDtypeStruct(small.shape[1:], F32),
        moved,
        moved,
    ]
    scratch = [pltpu.VMEM(v.shape, v.dtype) for v in (act, w1, wo, mix, qs, kr, vb, h1, x2, x, moved)]
    half, low = (own, width), pltpu.VMEM((2 * own, width), BF)
    scratch += [pltpu.VMEM(half, F32)] + [pltpu.VMEM(half, BF)] * 3
    scratch += [pltpu.VMEM(half, F32), low, pltpu.VMEM(mix.shape, BF)]
    scratch += [pltpu.VMEM(split(wo), BF), pltpu.VMEM(split(wq), BF)]
    scratch += [pltpu.VMEM((2 * own, HEAD), F32), pltpu.VMEM((2, 2 * own, HEAD), F32)]
    scratch += [pltpu.VMEM((2 * HEAD, 2 * own), BF)] * 2
    scratch += [pltpu.VMEM((8, width), F32), pltpu.VMEM(moved.shape, BF)]
    scratch += [pltpu.VMEM((2, 2 * own, 256), BF), pltpu.VMEM((1, act.shape[1]), F32)]
    scratch += [pltpu.VMEM(split(w1)[1:], BF)]
    scratch += [dma((19,)), dma((4,)), dma((4,)), dma((2,))]
    for lead in (
        (groups, 2),
        (groups, 2),
        (groups, 2),
        (groups, 2),
        (groups,),
        (groups,),
        (groups, 2),
        (4, 2),
    ):
        scratch += [pltpu.VMEM(lead + t, BF) for t in tiles]
    scratch += [
        pltpu.VMEM(small.shape, F32),
        pltpu.VMEM((3,) + small.shape, F32),
        pltpu.VMEM(small.shape, F32),
    ]
    pair = dma((count, groups, 2))
    scratch += [pair] * 7 + [dma((count, 2))] * 4
    scratch += [dma((count,))] * 3 + [dma((2 + groups,))] * 2 + [dma((1, clips))] * 4
    return pl.pallas_call(
        functools.partial(backward_body, groups, clips, blocks),
        out_shape=shapes,
        in_specs=[ANY] * (1 + len(arrays)) + [VM] * len(tables),
        out_specs=[ANY] * (count + 1) + [VM, ANY, ANY],
        scratch_shapes=scratch,
        compiler_params=pltpu.CompilerParams(
            collective_id=1, has_side_effects=True, vmem_limit_bytes=67043328
        ),
        name="backward",
    )(gw2, *arrays, *tables)


def swap(value):
    return lax.ppermute(value, "core", [(0, 1), (1, 0)])


def both(value):
    return jnp.concatenate([value, swap(value)], axis=0)


def contract(left, right, a, b):
    return lax.dot_general(left, right, (((a,), (b,)), ((), ())), preferred_element_type=F32)


def own_sum(partial):
    half = partial.shape[0] // 2
    return partial[:half] + swap(partial[half:].astype(BF)).astype(F32)


def paired(
    tokens,
    positions,
    ln1_gain,
    ln1_bias,
    w_qkv,
    b_qkv,
    w_out,
    b_out,
    ln2_gain,
    ln2_bias,
    w_up,
    b_up,
    w_down,
    b_down,
    cotangent,
):
    groups = lax.axis_size("grp")
    clips, part, width = tokens.shape
    hidden = w_down.shape[0] * groups
    own = clips * part
    length = 2 * own
    c, z = lax.axis_index("core"), lax.axis_index("grp")
    wide = width // 2
    deep = hidden // 2
    row = width // groups

    def pick(value, axis):
        return lax.dynamic_index_in_dim(value, c, axis, keepdims=False)

    blocks = (3 * groups, 0, groups, 0)
    raw = [
        w.reshape(((4, 2) if b else (2, 4, 2)) + (w.shape[0] // (8 if b else 16), w.shape[1]))
        for w, b in zip((w_qkv, w_out, w_up, w_down), blocks)
    ]
    bq, bu = b_qkv.shape[0] // row, b_up.shape[0] // row
    vectors = [ln1_gain, ln1_bias, b_out, ln2_gain, ln2_bias, b_down]
    vectors += [b_qkv, b_up]
    lines = len(vectors) - 2 + bq + bu
    size, start = (lines + -lines % 8) * row, 0
    small = jnp.zeros((size,), F32)
    for v in vectors:
        small = small + jnp.pad(v.astype(F32), (start, size - start - v.shape[0]))
        start += v.shape[0]
    small = small.reshape(-1, row)
    pair = jnp.arange(HEAD // 2)
    band = (pair >= 10).astype(jnp.int32) + (pair >= 21).astype(jnp.int32)
    begin = jnp.where(band == 0, 0, jnp.where(band == 1, 10, 21))
    number = jnp.where(band == 0, 10, 11)
    freq = jnp.power(F32(10000.0), -(pair - begin).astype(F32) / number.astype(F32))
    pos = positions.astype(F32)[:, :, None, :]
    band = band[None, :, None]
    chosen = jnp.where(band == 0, pos[0], jnp.where(band == 1, pos[1], pos[2]))
    angles = chosen * freq[None, :, None]
    tab = jnp.concatenate([jnp.cos(angles), jnp.sin(angles)], axis=1)
    wq, wo, w1, w2, small, x, tab, dy, h1, qs, kr, vb, mixed, lse, x2, h2 = forward(
        raw, blocks, small, tokens, tab, cotangent, groups
    )
    cosine, sine = tab[: HEAD // 2], tab[HEAD // 2 :]
    wq = wq.reshape(width, 3 * wide)
    wo = wo.reshape(wide, width)
    w1 = w1.reshape(width, deep)
    w2 = w2.reshape(deep, width)
    g1, g2, bd = (small[:, n].reshape(1, width) for n in (0, 3, 5))
    bu_own = pick(small[:, 6 + bq : lines].reshape(groups, 2, deep // groups), 1).reshape(1, deep)
    grad_all = dy.reshape(length, width)
    tokens = x.reshape(own, width)
    u = contract(h2, w1, 1, 0) + bu_own
    cdf = 0.5 * (1.0 + lax.erf(u * F32(0.7071067811865476)))
    act = (u * cdf).astype(BF)
    slope = (cdf + u * jnp.exp(-0.5 * u * u) * F32(0.3989422804014327)).astype(BF)

    gw2 = contract(act, grad_all, 0, 0).astype(BF)
    gw2 = gw2.reshape(groups, 2, 2, 2, gw2.shape[0] // (8 * groups), width)
    arrays = (act, slope, w2, w1, wo, wq, mixed, qs, kr, vb, h1, h2, x2, tokens, dy, grad_all)
    tables = (lse, cosine, sine, g1, g2, bd)
    gwq, gwo, gw1, gw2, _, sums, gx, output = backward(gw2, arrays, tables, lines, groups, blocks)
    gwq, gwo, gw1, gw2 = (
        g.reshape(shard.shape).astype(F32)
        for g, shard in zip((gwq, gwo, gw1, gw2), (w_qkv, w_out, w_up, w_down))
    )
    gg1, gb1, gbo, gg2, gb2, gbd = (sums[n] for n in range(6))
    gbq, gbu = sums[6 : 6 + bq].reshape(-1), sums[6 + bq : lines].reshape(-1)
    return (output, gx, gg1, gb1, gwq, gbq, gwo, gbo, gg2, gb2, gw1, gbu, gw2, gbd)


def paired_specs():
    rep = ("rp", "core")
    ins = (P(rep, "grp", None), P(None, rep, "grp"))
    one, two = P("grp"), P("grp", None)
    ins += (one, one, two, one, two, one, one, one, two, one, two, one, P(rep, "grp", None))
    outs = (P(rep, "grp", None),) * 2
    outs += (one, one, two, one, two, one, one, one, two, one, two, one)
    return ins, outs


def rotary_angles(positions):
    pair = jnp.arange(32)
    band = (pair >= 10).astype(jnp.int32) + (pair >= 21).astype(jnp.int32)
    start = jnp.where(band == 0, 0, jnp.where(band == 1, 10, 21))
    count = jnp.where(band == 0, 10, 11)
    freq = jnp.power(
        jnp.float32(10000.0), -(pair - start).astype(jnp.float32) / count.astype(jnp.float32)
    )
    pos_f = positions.astype(jnp.float32)
    chosen = jnp.where(
        band[None, :] == 0,
        pos_f[0][:, None],
        jnp.where(band[None, :] == 1, pos_f[1][:, None], pos_f[2][:, None]),
    )
    return chosen * freq[None, :]


def rotate(field, cosine, sine):
    first = field[..., :32]
    second = field[..., 32:]
    return jnp.concatenate(
        [first * cosine - second * sine, first * sine + second * cosine], axis=-1
    )


def normalize(field):
    centred = field - jnp.mean(field, axis=-1, keepdims=True)
    variance = jnp.mean(centred * centred, axis=-1, keepdims=True)
    factor = lax.rsqrt(variance + EPS)
    return (centred * factor, factor)


def norm_back(grad_norm, normed, factor):
    return factor * (
        grad_norm
        - jnp.mean(grad_norm, axis=-1, keepdims=True)
        - normed * jnp.mean(grad_norm * normed, axis=-1, keepdims=True)
    )


def outer(left, right):
    return lax.dot_general(
        left, right, (((0,), (0,)), ((), ())), preferred_element_type=jnp.float32
    )


def back(left, right):
    return lax.dot_general(
        left, right, (((1,), (1,)), ((), ())), preferred_element_type=jnp.float32
    )


def exact_gelu(value):
    return jax.nn.gelu(value, approximate=False)


def column_sum(value):
    return jnp.sum(value.astype(jnp.float32), axis=0)


def forward_pass(params, field_in, positions):
    g1, b1, wqkv, bqkv, wo, bo, g2, b2, w1, bu, w2, bd = params
    field = field_in.astype(jnp.float32)
    count, width = field.shape
    heads = width // 64
    angles = rotary_angles(positions)
    cosine = jnp.cos(angles)[:, None, :]
    sine = jnp.sin(angles)[:, None, :]
    normed1, factor1 = normalize(field)
    h1 = (normed1 * g1.astype(jnp.float32) + b1.astype(jnp.float32)).astype(jnp.bfloat16)
    qkv = jnp.dot(h1, wqkv, preferred_element_type=jnp.float32) + bqkv.astype(jnp.float32)
    query_rot = rotate(qkv[:, :width].reshape(count, heads, 64), cosine, sine).astype(jnp.bfloat16)
    keys_rot = (
        rotate(qkv[:, width : 2 * width].reshape(count, heads, 64), cosine, sine)
        .astype(jnp.bfloat16)
        .reshape(count, width)
    )
    values = qkv[:, 2 * width :].astype(jnp.bfloat16)
    keys_all, values_all = (
        lax.all_gather(keys_rot, "grp", axis=0, tiled=True),
        lax.all_gather(values, "grp", axis=0, tiled=True),
    )
    total = keys_all.shape[0]
    keys_all = keys_all.reshape(total, heads, 64)
    values_all = values_all.reshape(total, heads, 64)
    scores = (
        jnp.einsum("thd,shd->hts", query_rot, keys_all, preferred_element_type=jnp.float32) * SCALE
    )
    top = jnp.max(scores, axis=-1, keepdims=True)
    lse = top + jnp.log(jnp.sum(jnp.exp(scores - top), axis=-1, keepdims=True))
    probs = jnp.exp(scores - lse).astype(jnp.bfloat16)
    mixed = (
        jnp.einsum("hts,shd->thd", probs, values_all, preferred_element_type=jnp.float32)
        .reshape(count, width)
        .astype(jnp.bfloat16)
    )
    second = field + jnp.dot(mixed, wo, preferred_element_type=jnp.float32) + bo.astype(jnp.float32)
    normed2, factor2 = normalize(second)
    h2 = (normed2 * g2.astype(jnp.float32) + b2.astype(jnp.float32)).astype(jnp.bfloat16)
    hidden = jnp.dot(h2, w1, preferred_element_type=jnp.float32) + bu.astype(jnp.float32)
    active = exact_gelu(hidden).astype(jnp.bfloat16)
    result = (
        second + jnp.dot(active, w2, preferred_element_type=jnp.float32) + bd.astype(jnp.float32)
    )
    saved = (
        normed1,
        factor1,
        h1,
        query_rot,
        keys_rot,
        values,
        lse,
        mixed,
        normed2,
        factor2,
        h2,
        hidden,
        active,
        cosine,
        sine,
    )
    return (saved, result.astype(jnp.bfloat16))


def backward_pass(params, saved, grad_in, totals):
    g1, b1, wqkv, bqkv, wo, bo, g2, b2, w1, bu, w2, bd = params
    (
        normed1,
        factor1,
        h1,
        query_rot,
        keys_rot,
        values,
        lse,
        mixed,
        normed2,
        factor2,
        h2,
        hidden,
        active,
        cosine,
        sine,
    ) = saved
    grad_out = grad_in.astype(jnp.float32)
    count, width = grad_out.shape
    heads = width // 64
    grad_y2 = grad_out.astype(jnp.bfloat16)
    grad_w2 = outer(active, grad_y2)
    grad_bd = column_sum(grad_y2)
    grad_act = back(grad_y2, w2)
    unused, pull = jax.vjp(exact_gelu, hidden)
    grad_hidden = pull(grad_act)[0].astype(jnp.bfloat16)
    grad_w1 = outer(h2, grad_hidden)
    grad_bu = column_sum(grad_hidden)
    grad_h2 = back(grad_hidden, w1)
    grad_g2 = jnp.sum(grad_h2 * normed2, axis=0)
    grad_b2 = jnp.sum(grad_h2, axis=0)
    grad_second = grad_out + norm_back(grad_h2 * g2.astype(jnp.float32), normed2, factor2)
    grad_y1 = grad_second.astype(jnp.bfloat16)
    grad_wo = outer(mixed, grad_y1)
    grad_bo = column_sum(grad_y1)
    grad_mixed = back(grad_y1, wo).astype(jnp.bfloat16).reshape(count, heads, 64)
    keys_all, values_all = (
        lax.all_gather(keys_rot, "grp", axis=0, tiled=True),
        lax.all_gather(values, "grp", axis=0, tiled=True),
    )
    total = keys_all.shape[0]
    keys_all = keys_all.reshape(total, heads, 64)
    values_all = values_all.reshape(total, heads, 64)
    scores = (
        jnp.einsum("thd,shd->hts", query_rot, keys_all, preferred_element_type=jnp.float32) * SCALE
    )
    probs = jnp.exp(scores - lse)
    grad_probs = jnp.einsum(
        "thd,shd->hts", grad_mixed, values_all, preferred_element_type=jnp.float32
    )
    delta = jnp.sum(probs * grad_probs, axis=-1, keepdims=True)
    grad_scores = (probs * (grad_probs - delta)).astype(jnp.bfloat16)
    grad_query = (
        jnp.einsum("hts,shd->thd", grad_scores, keys_all, preferred_element_type=jnp.float32)
        * SCALE
    )
    probs_low = probs.astype(jnp.bfloat16)
    grad_values = jnp.einsum(
        "hts,thd->shd", probs_low, grad_mixed, preferred_element_type=jnp.float32
    )
    grad_keys = (
        jnp.einsum("hts,thd->shd", grad_scores, query_rot, preferred_element_type=jnp.float32)
        * SCALE
    )
    keys_own, values_own = (
        lax.psum_scatter(
            grad_keys.reshape(total, width).astype(jnp.bfloat16),
            "grp",
            scatter_dimension=0,
            tiled=True,
        ).astype(jnp.float32),
        lax.psum_scatter(
            grad_values.reshape(total, width).astype(jnp.bfloat16),
            "grp",
            scatter_dimension=0,
            tiled=True,
        ).astype(jnp.float32),
    )
    query_back = rotate(grad_query, cosine, -sine).reshape(count, width)
    keys_back = rotate(keys_own.reshape(count, heads, 64), cosine, -sine).reshape(count, width)
    grad_qkv = jnp.concatenate([query_back, keys_back, values_own], axis=1).astype(jnp.bfloat16)
    grad_wqkv = outer(h1, grad_qkv)
    grad_bqkv = column_sum(grad_qkv)
    grad_h1 = back(grad_qkv, wqkv)
    grad_g1 = jnp.sum(grad_h1 * normed1, axis=0)
    grad_b1 = jnp.sum(grad_h1, axis=0)
    grad_field = grad_second + norm_back(grad_h1 * g1.astype(jnp.float32), normed1, factor1)
    terms = (
        grad_g1,
        grad_b1,
        grad_wqkv,
        grad_bqkv,
        grad_wo,
        grad_bo,
        grad_g2,
        grad_b2,
        grad_w1,
        grad_bu,
        grad_w2,
        grad_bd,
    )
    totals = tuple((a + b for a, b in zip(totals, terms)))
    return (grad_field.astype(jnp.bfloat16), totals)


def local(
    tokens,
    positions,
    ln1_gain,
    ln1_bias,
    w_qkv,
    b_qkv,
    w_out,
    b_out,
    ln2_gain,
    ln2_bias,
    w_up,
    b_up,
    w_down,
    b_down,
    cotangent,
):
    shards = (
        ln1_gain,
        ln1_bias,
        w_qkv,
        b_qkv,
        w_out,
        b_out,
        ln2_gain,
        ln2_bias,
        w_up,
        b_up,
        w_down,
        b_down,
    )
    groups = lax.axis_size("grp")
    totals = tuple((jnp.zeros((s.shape[0] * groups,) + s.shape[1:], jnp.float32) for s in shards))
    outputs = []
    gradients = []
    for index in range(tokens.shape[0]):
        forward_params = (
            lax.all_gather(ln1_gain, "grp", axis=0, tiled=True),
            lax.all_gather(ln1_bias, "grp", axis=0, tiled=True),
            lax.all_gather(w_qkv, "grp", axis=0, tiled=True),
            lax.all_gather(b_qkv, "grp", axis=0, tiled=True),
            lax.all_gather(w_out, "grp", axis=0, tiled=True),
            lax.all_gather(b_out, "grp", axis=0, tiled=True),
            lax.all_gather(ln2_gain, "grp", axis=0, tiled=True),
            lax.all_gather(ln2_bias, "grp", axis=0, tiled=True),
            lax.all_gather(w_up, "grp", axis=0, tiled=True),
            lax.all_gather(b_up, "grp", axis=0, tiled=True),
            lax.all_gather(w_down, "grp", axis=0, tiled=True),
            lax.all_gather(b_down, "grp", axis=0, tiled=True),
        )
        saved, result = forward_pass(forward_params, tokens[index], positions[:, index, :])
        outputs.append(result)
        backward_params = (
            lax.all_gather(ln1_gain, "grp", axis=0, tiled=True),
            lax.all_gather(ln1_bias, "grp", axis=0, tiled=True),
            lax.all_gather(w_qkv, "grp", axis=0, tiled=True),
            lax.all_gather(b_qkv, "grp", axis=0, tiled=True),
            lax.all_gather(w_out, "grp", axis=0, tiled=True),
            lax.all_gather(b_out, "grp", axis=0, tiled=True),
            lax.all_gather(ln2_gain, "grp", axis=0, tiled=True),
            lax.all_gather(ln2_bias, "grp", axis=0, tiled=True),
            lax.all_gather(w_up, "grp", axis=0, tiled=True),
            lax.all_gather(b_up, "grp", axis=0, tiled=True),
            lax.all_gather(w_down, "grp", axis=0, tiled=True),
            lax.all_gather(b_down, "grp", axis=0, tiled=True),
        )
        grad_field, totals = backward_pass(backward_params, saved, cotangent[index], totals)
        gradients.append(grad_field)
    owned = (
        lax.psum_scatter(
            totals[0].astype(jnp.bfloat16), "grp", scatter_dimension=0, tiled=True
        ).astype(jnp.float32),
        lax.psum_scatter(
            totals[1].astype(jnp.bfloat16), "grp", scatter_dimension=0, tiled=True
        ).astype(jnp.float32),
        lax.psum_scatter(
            totals[2].astype(jnp.bfloat16), "grp", scatter_dimension=0, tiled=True
        ).astype(jnp.float32),
        lax.psum_scatter(
            totals[3].astype(jnp.bfloat16), "grp", scatter_dimension=0, tiled=True
        ).astype(jnp.float32),
        lax.psum_scatter(
            totals[4].astype(jnp.bfloat16), "grp", scatter_dimension=0, tiled=True
        ).astype(jnp.float32),
        lax.psum_scatter(
            totals[5].astype(jnp.bfloat16), "grp", scatter_dimension=0, tiled=True
        ).astype(jnp.float32),
        lax.psum_scatter(
            totals[6].astype(jnp.bfloat16), "grp", scatter_dimension=0, tiled=True
        ).astype(jnp.float32),
        lax.psum_scatter(
            totals[7].astype(jnp.bfloat16), "grp", scatter_dimension=0, tiled=True
        ).astype(jnp.float32),
        lax.psum_scatter(
            totals[8].astype(jnp.bfloat16), "grp", scatter_dimension=0, tiled=True
        ).astype(jnp.float32),
        lax.psum_scatter(
            totals[9].astype(jnp.bfloat16), "grp", scatter_dimension=0, tiled=True
        ).astype(jnp.float32),
        lax.psum_scatter(
            totals[10].astype(jnp.bfloat16), "grp", scatter_dimension=0, tiled=True
        ).astype(jnp.float32),
        lax.psum_scatter(
            totals[11].astype(jnp.bfloat16), "grp", scatter_dimension=0, tiled=True
        ).astype(jnp.float32),
    )
    summed = (
        lax.psum(owned[0].astype(jnp.bfloat16), "rep").astype(jnp.float32),
        lax.psum(owned[1].astype(jnp.bfloat16), "rep").astype(jnp.float32),
        lax.psum(owned[2].astype(jnp.bfloat16), "rep").astype(jnp.float32),
        lax.psum(owned[3].astype(jnp.bfloat16), "rep").astype(jnp.float32),
        lax.psum(owned[4].astype(jnp.bfloat16), "rep").astype(jnp.float32),
        lax.psum(owned[5].astype(jnp.bfloat16), "rep").astype(jnp.float32),
        lax.psum(owned[6].astype(jnp.bfloat16), "rep").astype(jnp.float32),
        lax.psum(owned[7].astype(jnp.bfloat16), "rep").astype(jnp.float32),
        lax.psum(owned[8].astype(jnp.bfloat16), "rep").astype(jnp.float32),
        lax.psum(owned[9].astype(jnp.bfloat16), "rep").astype(jnp.float32),
        lax.psum(owned[10].astype(jnp.bfloat16), "rep").astype(jnp.float32),
        lax.psum(owned[11].astype(jnp.bfloat16), "rep").astype(jnp.float32),
    )
    output = jnp.stack(outputs, axis=0)
    grad_tokens = jnp.stack(gradients, axis=0)
    return (
        output,
        grad_tokens,
        summed[0],
        summed[1],
        summed[2],
        summed[3],
        summed[4],
        summed[5],
        summed[6],
        summed[7],
        summed[8],
        summed[9],
        summed[10],
        summed[11],
    )


def spread(mesh):
    placed = (
        P("rep", "grp", None),
        P(None, "rep", "grp"),
        P("grp"),
        P("grp"),
        P("grp", None),
        P("grp"),
        P("grp", None),
        P("grp"),
        P("grp"),
        P("grp"),
        P("grp", None),
        P("grp"),
        P("grp", None),
        P("grp"),
        P("rep", "grp", None),
    )
    return jax.shard_map(
        local,
        mesh=mesh,
        in_specs=placed,
        out_specs=(
            P("rep", "grp", None),
            P("rep", "grp", None),
            P("grp"),
            P("grp"),
            P("grp", None),
            P("grp"),
            P("grp", None),
            P("grp"),
            P("grp"),
            P("grp"),
            P("grp", None),
            P("grp"),
            P("grp", None),
            P("grp"),
        ),
        check_vma=False,
    )


def solution(mesh):
    reps, groups = mesh.devices.shape
    flat = mesh.devices.reshape(-1)

    def run(*args):
        clips = args[0].shape[0] // reps
        if reps == 8 and groups == 2 * clips:
            split = Mesh(flat.reshape(reps // 2, 2, groups), ("rp", "core", "grp"))
            ins, outs = paired_specs()
            return jax.shard_map(
                paired, mesh=split, in_specs=ins, out_specs=outs, check_vma=False
            )(*args)
        return spread(mesh)(*args)

    return run
```

```python
import functools

import jax
import jax.numpy as jnp
from jax import lax
from jax.experimental import pallas as pl
from jax.experimental.pallas import tpu as pltpu
from jax.sharding import Mesh
from jax.sharding import PartitionSpec as P

SCALE = 0.125
EPS = 1e-06
HEAD = 64
BF = jnp.bfloat16
F32 = jnp.float32
MESH = pl.DeviceIdType.MESH
ANY = pl.BlockSpec(memory_space=pl.ANY)
VM = pl.BlockSpec(memory_space=pltpu.VMEM)


def where_am_i():
    return lax.axis_index("rp"), lax.axis_index("core"), lax.axis_index("grp")


def remote(src, dst, send, recv, target):
    return pltpu.make_async_remote_copy(
        src_ref=src,
        dst_ref=dst,
        send_sem=send,
        recv_sem=recv,
        device_id=target,
        device_id_type=MESH,
    )


def enter(p, c, z, groups):
    barrier = pltpu.get_barrier_semaphore()
    for k in range(groups):
        for d in range(2):
            if k == 0 and d == 0:
                continue
            pl.semaphore_signal(
                barrier, inc=1, device_id=(p, c ^ d, lax.rem(z + k, groups)), device_id_type=MESH
            )
    for b in (1, 2):
        pl.semaphore_signal(barrier, inc=1, device_id=(p ^ b, c, z), device_id_type=MESH)
    pl.semaphore_wait(barrier, 2 * groups - 1 + 2)


def move_tokens(refs, outs, send, recv, p, c, z, clips):
    core, slot = lax.div(z, clips), lax.rem(z, clips)

    def route(i):
        return core, c * clips + i

    def here(i):
        return jnp.logical_and(core == c, c * clips + i == z)

    def start(k, pieces):
        for n, (src, dst) in enumerate(zip(refs, outs)):
            rows = src.shape[1] // pieces
            rows = pl.ds(k * rows, rows)
            for i in range(clips):
                tc, tz = route(i)

                @pl.when(here(i))
                def _():
                    pltpu.make_async_copy(
                        src.at[i, rows], dst.at[slot, rows], recv.at[n, slot]
                    ).start()

                @pl.when(jnp.logical_not(here(i)))
                def _():
                    remote(
                        src.at[i, rows],
                        dst.at[slot, rows],
                        send.at[n, i],
                        recv.at[n, slot],
                        (p, tc, tz),
                    ).start()

    def sent():
        for n, (src, dst) in enumerate(zip(refs, outs)):
            for i in range(clips):

                @pl.when(jnp.logical_not(here(i)))
                def _():
                    remote(
                        src.at[i], dst.at[slot], send.at[n, i], recv.at[n, slot], (p, c ^ 1, z)
                    ).wait_send()

    def arrive():
        for n, (src, dst) in enumerate(zip(refs, outs)):
            for m in range(clips):
                pltpu.make_async_copy(src.at[0], dst.at[m], recv.at[n, m]).wait()

    def finish():
        sent()
        arrive()

    return start, finish, sent, arrive


def turn(u, cosine, sine):
    half = HEAD // 2
    first, second = u[:half], u[half:]
    return jnp.concatenate(
        [first * cosine - second * sine, first * sine + second * cosine], axis=0
    )


def dot(a, b):
    return jnp.dot(a, b, preferred_element_type=F32)


def dot_t(a, b):
    return lax.dot_general(a, b, (((1,), (1,)), ((), ())), preferred_element_type=F32)


def tile(i, size):
    return pl.ds(pl.multiple_of(i * size, size), size)


def cuts(whole, half, c, blocks):
    if blocks == 0:
        return [(whole.at[c], half)]
    size = half.shape[3] // blocks
    return [
        (
            whole.at[:, :, :, pl.ds(pl.multiple_of((2 * b + c) * size, size), size)],
            half.at[:, :, :, pl.ds(b * size, size)],
        )
        for b in range(blocks)
    ]


def forward_body(groups, clips, blocks, *refs):
    count = len(blocks)
    raw, (small, x, tab, dy) = refs[:count], refs[count : count + 4]
    (wq_o, wo_o, *outs) = refs[count + 4 : 2 * count + 4]
    (gain, bu, x_o, tab_o, dy_o, h1_o, qs_o, kr_o, vb_o, mix_o, lse_o, x2_o, h2_o) = refs[
        2 * count + 4 : 2 * count + 17
    ]
    halves = refs[2 * count + 17 : 3 * count + 17]
    (wq_v, small_v, x_v, tab_v, tab_w, h1, qs, kr, vb, mix, qkv, bias) = refs[
        3 * count + 17 : 3 * count + 29
    ]
    (wo_v, own_f, give, take, h2) = refs[3 * count + 29 : 3 * count + 34]
    (zs, zr, xs, xr, ys, yr, fs, fr, hs, ls, ss, sr, ts, tr, us, ur, vs, vr, es, er, ks) = refs[
        3 * count + 34 :
    ]
    outs = [wq_v, wo_v, *outs]
    p, c, z = where_am_i()
    for w in range(count):
        for src, dst in cuts(raw[w], halves[w], c, blocks[w]):
            pltpu.make_async_copy(src, dst, hs.at[w]).start()
    enter(p, c, z, groups)
    col = [(p, c, lax.rem(z + k, groups)) for k in range(groups)]
    org = [lax.rem(z + groups - k, groups) for k in range(groups)]
    xn, yn, cn = (p ^ 1, c, z), (p ^ 2, c, z), (p, c ^ 1, z)
    smalls = [
        remote(small, small_v.at[z], ss.at[k], sr.at[k], col[k]) for k in range(1, groups)
    ]
    for s in smalls:
        s.start()
    keep = [pltpu.make_async_copy(small, small_v.at[z], ls.at[count])]
    keep[0].start()
    start_tab, _, sent_tab, arrive_tab = move_tokens((tab,), (tab_v,), vs, vr, p, c, z, clips)
    start_x, _, sent_x, arrive_x = move_tokens((x,), (x_v,), ts, tr, p, c, z, clips)
    start_dy, _, sent_dy, arrive_dy = move_tokens((dy,), (dy_o.at[:clips],), us, ur, p, c, z, clips)
    units = [(w, d, side) for w in range(count) for d in range(1, groups) for side in range(2)]

    def origin(d, side):
        return z - d if side == 0 else z + d

    def arrives(d, side):
        return z >= d if side == 0 else z + d < groups

    def leaves(d, side):
        if side == 0:
            return jnp.logical_and(z + 1 < groups, z + 1 >= d)
        return jnp.logical_and(z >= 1, z - 1 + d < groups)

    def hop(w, d, side, src):
        o = origin(d - 1, side)
        target = (p, c, lax.rem(z + 1 if side == 0 else z + groups - 1, groups))
        return remote(src, outs[w].at[o, p], zs.at[w, side, d], zr.at[w, side, d], target)

    def own(w):
        pltpu.make_async_copy(halves[w], halves[w], hs.at[w]).wait()
        keep.append(pltpu.make_async_copy(halves[w], outs[w].at[z], ls.at[w]))
        keep[-1].start()
        for side in range(2):

            @pl.when(leaves(1, side))
            def _():
                hop(w, 1, side, halves[w].at[p]).start()

    def links(u):
        w, d, side = u
        o = outs[w].at[lax.rem(origin(d, side) + groups, groups)]
        e, f = xs.at[w, side, d], xr.at[w, side, d]
        g, h = ys.at[w, side, d], yr.at[w, side, d]
        a, b = fs.at[w, side, d, 0], fr.at[w, side, d, 0]
        m, n = fs.at[w, side, d, 1], fr.at[w, side, d, 1]
        across = lambda q: remote(o.at[q], o.at[q], e, f, xn)
        along = lambda q: remote(o.at[q], o.at[q], g, h, yn)
        first = lambda q: remote(o.at[q, 0], o.at[q, 0], a, b, yn)
        second = lambda q: remote(o.at[q, 1], o.at[q, 1], m, n, xn)
        return o, across, along, first, second

    def plane(u):
        w, d, side = u
        o, across, along, first, second = links(u)

        @pl.when(arrives(d, side))
        def _():
            remote(o.at[p], o.at[p], zs.at[w, side, d], zr.at[w, side, d], xn).wait_recv()
            if d + 1 < groups:

                @pl.when(leaves(d + 1, side))
                def _():
                    hop(w, d + 1, side, o.at[p]).start()

            across(p).start()
            along(p).start()

    def forward(u):
        w, d, side = u
        o, across, along, first, second = links(u)

        @pl.when(arrives(d, side))
        def _():
            across(p ^ 1).wait_recv()
            first(p ^ 1).start()
            along(p ^ 2).wait_recv()
            second(p ^ 2).start()

    def complete(u):
        w, d, side = u
        o, across, along, first, second = links(u)

        @pl.when(arrives(d, side))
        def _():
            first(p ^ 3).wait_recv()
            second(p ^ 3).wait_recv()

    def settle(u):
        w, d, side = u
        o, across, along, first, second = links(u)

        @pl.when(arrives(d, side))
        def _():
            across(p).wait_send()
            along(p).wait_send()
            first(p).wait_send()
            second(p).wait_send()

        @pl.when(leaves(d, side))
        def _():
            hop(w, d, side, halves[w].at[p]).wait_send()

    own(0)
    start_tab(0, 1)
    own(1)
    moves = {2 * k: (start_x, k) for k in range(4)}
    moves.update({10 + 3 * k: (start_dy, k) for k in range(4)})
    lag = 3

    def step(n):
        if n < len(units):
            plane(units[n])
            w, d, side = units[n]
            if (d, side) == (1, 1) and w + 2 < count:
                own(w + 2)
            if n in moves:
                moves[n][0](moves[n][1], 4)
        if n >= lag:
            forward(units[n - lag])

    steps = list(range(len(units) + lag))
    early = 2 * (groups - 1) + lag
    for _ in range(early):
        step(steps.pop(0))
    for k in range(1, groups):
        remote(small, small_v.at[org[k]], ss.at[k], sr.at[k], col[k]).wait_recv()
    keep[0].wait()
    row = small_v.shape[2]
    half = row // 2
    mine = pl.ds(pl.multiple_of(c * half, half), half)
    for g in range(groups):
        gain[0:6, g * row : (g + 1) * row] = small_v[g, 0:6]
        share = bu.shape[1] // groups
        for n in range(share // row):
            line = small_v[g, pl.ds(9 + c * (share // row) + n, 1)]
            bu[:, g * share + n * row : g * share + (n + 1) * row] = line
        for r in range(3):
            bias[3 * g + r : 3 * g + r + 1] = small_v[g, 6 + r : 7 + r, mine]
    own_count = h1.shape[0] // 2
    arrive_x()
    saves = [pltpu.make_async_copy(x_v, x_o, ks.at[0])]
    saves[0].start()

    def norm(i, carry):
        per = own_count // clips // 128
        v = x_v[lax.div(i, per), tile(lax.rem(i, per), 128)].astype(F32)
        v = v - jnp.mean(v, axis=1, keepdims=True)
        v = v * lax.rsqrt(jnp.mean(v * v, axis=1, keepdims=True) + EPS)
        h1[tile(i, 128)] = (v * gain[0:1] + gain[1:2]).astype(BF)
        return carry

    lax.fori_loop(0, own_count // 128, norm, 0)
    swap = remote(h1.at[:own_count], h1.at[own_count:], es.at[0], er.at[0], cn)
    swap.start()
    arrive_tab()
    swap_tab = remote(tab_v, tab_w, es.at[1], er.at[1], cn)
    swap_tab.start()
    step(steps.pop(0))
    swap_tab.wait()
    part = tab_v.shape[2]
    for m in range(clips):
        tab_o[:, m * part : (m + 1) * part] = tab_v[m]
        tab_o[:, own_count + m * part : own_count + (m + 1) * part] = tab_w[m]
    for u in units[: 2 * (groups - 1)]:
        complete(u)
    keep[1].wait()
    saves.append(pltpu.make_async_copy(wq_v, wq_o, ks.at[1]))
    saves[1].start()
    swap.wait()
    saves.append(pltpu.make_async_copy(h1, h1_o, ks.at[2]))
    saves[2].start()
    inner = qs.shape[0]
    heads = inner // HEAD
    pairs = heads // 2

    def head(h, side):
        rows, place = tile(h, HEAD), tile(side, HEAD)
        co, si = tab_o[: HEAD // 2], tab_o[HEAD // 2 :]
        k = turn(qkv[1, place], co, si).astype(BF)
        v = qkv[2, place].astype(BF)
        q = (turn(qkv[0, place], co, si).astype(BF).astype(F32) * SCALE).astype(BF)
        kr[rows] = k
        vb[rows] = v
        qs[rows] = q
        keys = k.T
        size = 256
        for i in range(0, 2 * own_count, size):
            scores = dot(keys, q[:, i : i + size])
            top = jnp.max(scores, axis=0, keepdims=True)
            e = jnp.exp(scores - top)
            total = jnp.sum(e, axis=0, keepdims=True)
            mixed = dot(v, e.astype(BF))
            mix[rows, i : i + size] = (mixed / total).astype(BF)
            lse_o[h, :, i : i + size] = top + jnp.log(total)

    during = [steps.pop(0) for _ in range(heads + heads // 2)]

    def two_heads(i, carry):
        def project(n, carry):
            at = pl.ds(pl.multiple_of(n * inner + i * 2 * HEAD, 2 * HEAD), 2 * HEAD)
            w = wq_v[..., at].reshape(h1.shape[1], 2 * HEAD)
            qkv[n] = (dot(h1[...], w) + bias[pl.ds(n * pairs + i, 1)]).T
            return carry

        lax.fori_loop(0, 3, project, 0)
        for n in range(pairs):

            @pl.when(i == n)
            def _():
                step(during[3 * n])

        def one(side, carry):
            head(2 * i + side, side)
            for n in range(heads):

                @pl.when(2 * i + side == n)
                def _():
                    step(during[3 * (n // 2) + 1 + n % 2])

            return carry

        lax.fori_loop(0, 2, one, 0)
        return carry

    lax.fori_loop(0, pairs, two_heads, 0)
    for n, (a, b) in enumerate(((qs, qs_o), (kr, kr_o), (vb, vb_o), (mix, mix_o))):
        saves.append(pltpu.make_async_copy(a, b, ks.at[3 + n]))
        saves[-1].start()
    for u in units[2 * (groups - 1) : 4 * (groups - 1)]:
        complete(u)
    keep[2].wait()
    saves.append(pltpu.make_async_copy(wo_v, wo_o, ks.at[7]))
    saves[-1].start()
    width = h1.shape[1]
    left_other, left_self = mix[:, own_count:].T, mix[:, :own_count].T

    def out_other(i, carry):
        at = tile(i, 256)
        give[:, at] = dot(left_other, wo_v[..., at].reshape(inner, 256)).astype(BF)
        return carry

    def out_self(i, carry):
        at = tile(i, 256)
        own_f[:, at] = dot(left_self, wo_v[..., at].reshape(inner, 256))
        return carry

    lax.fori_loop(0, width // 256, out_other, 0)
    swap = remote(give, take, es.at[2], er.at[2], cn)
    swap.start()
    lax.fori_loop(0, width // 256, out_self, 0)
    step(steps.pop(0))
    swap.wait()

    def second_norm(i, carry):
        per = own_count // clips // 128
        at = tile(i, 128)
        v = x_v[lax.div(i, per), tile(lax.rem(i, per), 128)].astype(F32)
        v = v + (own_f[at] + take[at].astype(F32)) + gain[2:3]
        own_f[at] = v
        v = v - jnp.mean(v, axis=1, keepdims=True)
        v = v * lax.rsqrt(jnp.mean(v * v, axis=1, keepdims=True) + EPS)
        h2[at] = (v * gain[3:4] + gain[4:5]).astype(BF)
        return carry

    lax.fori_loop(0, own_count // 128, second_norm, 0)
    swap = remote(h2.at[:own_count], h2.at[own_count:], es.at[0], er.at[0], cn)
    swap.start()
    saves.append(pltpu.make_async_copy(own_f, x2_o, ks.at[8]))
    saves[-1].start()
    step(steps.pop(0))
    swap.wait()
    saves.append(pltpu.make_async_copy(h2, h2_o, ks.at[9]))
    saves[-1].start()
    while steps:
        step(steps.pop(0))
    arrive_dy()
    swap_dy = remote(dy_o.at[:clips], dy_o.at[clips:], es.at[3], er.at[3], cn)
    swap_dy.start()
    for u in units[4 * (groups - 1) :]:
        complete(u)
    for u in units:
        settle(u)
    for s in smalls:
        s.wait_send()
    for k in keep[3:] + saves:
        k.wait()
    swap_dy.wait()
    sent_dy()
    sent_tab()
    sent_x()


def half_shape(raw, blocks):
    return raw.shape[1:] if blocks == 0 else raw.shape[:3] + (raw.shape[3] // 2,)


def forward(raw, blocks, small, x, tab, dy, groups):
    count, clips = len(raw), x.shape[0]
    own, width = clips * x.shape[1], x.shape[2]
    halves = [half_shape(r, b) for r, b in zip(raw, blocks)]
    inner = halves[0][-1] // 3
    dma = pltpu.SemaphoreType.DMA
    of = jax.ShapeDtypeStruct
    feature = (inner, 2 * own)
    shapes = [of((groups,) + h, BF) for h in halves]
    shapes += [of((8, width), F32), of((1, halves[2][-1]), F32)]
    shapes += [of(x.shape, BF), of((HEAD, 2 * own), F32)]
    shapes += [of((2 * clips,) + x.shape[1:], BF), of((2 * own, width), BF)] + [of(feature, BF)] * 4
    shapes += [of((inner // HEAD, 1, 2 * own), F32), of((own, width), F32), of((2 * own, width), BF)]
    vm = pltpu.VMEM
    scratch = [vm(h, BF) for h in halves]
    scratch += [vm((groups,) + halves[0], BF), vm((groups,) + small.shape, F32), vm(x.shape, BF)]
    scratch += [vm(tab.shape, F32)] * 2 + [vm((2 * own, width), BF)] + [vm(feature, BF)] * 4
    scratch += [vm((3, 2 * HEAD, 2 * own), F32)]
    scratch += [vm((3 * groups + -3 * groups % 8, width // groups // 2), F32)]
    scratch += [vm((groups,) + halves[1], BF), vm((own, width), F32)]
    scratch += [vm((own, width), BF)] * 2 + [vm((2 * own, width), BF)]
    return pl.pallas_call(
        functools.partial(forward_body, groups, clips, blocks),
        out_shape=shapes,
        in_specs=[ANY] * count + [VM, ANY, ANY, ANY],
        out_specs=[ANY] * count + [VM, VM, ANY, VM] + [ANY] * 6 + [VM, ANY, ANY],
        scratch_shapes=scratch
        + [dma((count, 2, groups))] * 6
        + [dma((count, 2, groups, 2))] * 2
        + [dma((count,)), dma((count + 1,)), dma((groups,)), dma((groups,))]
        + [dma((1, clips))] * 6
        + [dma((4,)), dma((4,)), dma((10,))],
        compiler_params=pltpu.CompilerParams(
            collective_id=0, has_side_effects=True, vmem_limit_bytes=60 * 1024 * 1024
        ),
        name="forward",
    )(*raw, small, x, tab, dy)


def backward_body(groups, clips, blocks, *refs):
    count = len(blocks)
    (gw2, act, slope, w2, w1, wo, wq, mix, qs, kr, vb, h1, h2, x2, x, dy, dy_all) = refs[:17]
    lse, tab, gain = refs[17:20]
    cosine, sine = tab.at[: HEAD // 2], tab.at[HEAD // 2 :]
    g1, g2, bd = (gain.at[n : n + 1] for n in (0, 3, 5))
    outs = refs[20 : 20 + count]
    gw1, small_o, gx_o, y_o = refs[20 + count : 24 + count]
    (gu_b, w1_b, wo_b, mix_b, qs_b, kr_b, vb_b, h1_b, x2_b, x_b, dy_b) = refs[24 + count : 35 + count]
    (own_f, give, take, y_take, dx2, low, da, gwo, gwq, ak, av, dq2, dk2, acc, gx) = refs[
        35 + count : 50 + count
    ]
    (sl, gbu, stage_b) = refs[50 + count : 53 + count]
    ld, es, er, sls = refs[53 + count : 57 + count]
    grads = (gwq, gwo, gw1, gw2)
    scratch = refs[57 + count :]
    own_a, own_b, one_a, one_b, two_a, two_b, three, full = (
        scratch[i * count : (i + 1) * count] for i in range(8)
    )
    small_s, small_r, small_z = scratch[8 * count : 8 * count + 3]
    (os, s1, r1, s2, r2, s3, r3, s4, r4, s5, r5, cs, cr, ls, ss, sr, ts, tr, us, ur) = scratch[
        8 * count + 3 :
    ]
    own, width = own_f.shape
    inner = mix_b.shape[0]
    third_width = wq.shape[1]

    upper, lower = w1_b.at[:, :width], w1_b.at[:, width:]
    pairs = ((w2.at[:width], upper), (w2.at[width:], lower), (dy_all, low), (h2, h1_b))
    pairs += ((x2, x2_b), (dy.at[:clips], dy_b), (mix, mix_b), (wo, wo_b))
    pairs += ((qs, qs_b), (kr, kr_b), (vb, vb_b), (x, x_b))
    pairs += ((w1, w1_b), (h1, h1_b), (act, gu_b), (w2.at[:width], upper), (w2.at[width:], lower))
    pairs += ((wq, w1_b.at[:, :third_width]),)
    loads = [pltpu.make_async_copy(a, b, ld.at[n]) for n, (a, b) in enumerate(pairs)]
    first_tile = pltpu.make_async_copy(slope.at[:, :256], sl.at[0], sls.at[0])
    first_tile.start()
    for copy in loads[:12]:
        copy.start()
    p, c, z = where_am_i()
    hi, lo = lax.div(p, 2), lax.rem(p, 2)
    enter(p, c, z, groups)
    col = [(p, c, lax.rem(z + k, groups)) for k in range(groups)]
    xn, yn, cn = (p ^ 1, c, z), (p ^ 2, c, z), (p, c ^ 1, z)
    order = (3, 2, 1, 0)
    units = [(w, j) for w in order for j in [*range(1, groups), 0]]
    sides = ((own_a, one_a, two_a, hi, yn), (own_b, one_b, two_b, lo, xn))

    def c1(u, n):
        w, j = u
        g = grads[w].at[lax.rem(z + j, groups)]
        src, target = (g.at[:, 1 - lo, 0], xn) if n == 0 else (g.at[1 - hi, :, 1], yn)
        return remote(src, sides[n][1][w].at[j], s1.at[w, j, n], r1.at[w, j, n], target)

    def load(u, n):
        w, j = u
        g = grads[w].at[lax.rem(z + j, groups)]
        src = g.at[:, lo, 0] if n == 0 else g.at[hi, :, 1]
        return pltpu.make_async_copy(src, sides[n][0][w].at[j], os.at[w, j, n])

    def c2(u, n):
        w, j = u
        own, one, two, side, target = sides[n]
        return remote(own[w].at[j, 1 - side], two[w].at[j], s2.at[w, j, n], r2.at[w, j, n], target)

    def c3(u, n):
        w, j = u
        src = sides[n][0][w].at[j, sides[n][3]]
        return remote(src, three[w].at[j, n], s3.at[w, j, n], r3.at[w, j, n], col[j])

    def c4(w, n):
        f = full[w].at[p]
        return remote(f, f, s4.at[w, n], r4.at[w, n], (xn, yn)[n])

    def c5(w, n):
        f = full[w].at[(p ^ 1, p ^ 2)[n], n]
        return remote(f, f, s5.at[w, n], r5.at[w, n], (yn, xn)[n])

    def stage_zero(u):
        for n in range(2):
            c1(u, n).start()
            load(u, n).start()

    def stage_one(u):
        w, j = u
        for n, (own, one, two, side, target) in enumerate(sides):
            load(u, n).wait()
            c1(u, n).wait_recv()
            own[w][j] = (own[w][j].astype(F32) + one[w][j].astype(F32)).astype(BF)
            c2(u, n).start()

    def stage_two(u):
        w, j = u
        for n, (own, one, two, side, target) in enumerate(sides):
            c2(u, n).wait_recv()
            own[w][j, side] = (own[w][j, side].astype(F32) + two[w][j].astype(F32)).astype(BF)
            if j:
                c3(u, n).start()

    def stage_three(w):
        for n, (own, one, two, side, target) in enumerate(sides):
            total = own[w][0, side].astype(F32)
            for j in range(1, groups):
                c3((w, j), n).wait_recv()
                total = total + three[w][j, n].astype(F32)
            full[w][p, n] = total.astype(BF)
        for n in range(2):
            c4(w, n).start()

    def stage_four(w):
        for n, target in enumerate((yn, xn)):
            f = full[w].at[(p ^ 1, p ^ 2)[n]]
            remote(f, f, s4.at[w, n], r4.at[w, n], target).wait_recv()
            c5(w, n).start()

    def stage_five(w):
        for n in range(2):
            f = full[w].at[p ^ 3, n]
            remote(f, f, s5.at[w, n], r5.at[w, n], xn).wait_recv()
        for dst, src in cuts(outs[w], full[w], c, blocks[w]):
            pltpu.make_async_copy(src, dst, ls.at[w]).start()
            remote(src, dst, cs.at[w], cr.at[w], cn).start()

    ahead, lag = 3, 2
    todo = {}
    for n, u in enumerate(units):
        todo.setdefault(max(n - ahead, -1), []).append((stage_zero, u))
        todo.setdefault(n, []).append((stage_one, u))
        todo.setdefault(n + lag, []).append((stage_two, u))
    for i, w in enumerate(order):
        last = (i + 1) * groups - 1 + lag
        for at, stage in ((2, stage_three), (3, stage_four), (4, stage_five)):
            todo.setdefault(last + at, []).append((stage, w))
    steps = sorted(todo)

    def run(step):
        for stage, what in todo[step]:
            stage(what)

    def tick(times=1):
        for _ in range(times):
            run(steps.pop(0))

    def half_sum(n, left, right, depth):
        def other(i, carry):
            part = dot_t(left[own:, :depth], right[tile(i, 256), :depth])
            give[:, tile(i, 256)] = part.astype(BF)
            return carry

        def self(i, carry):
            own_f[:, tile(i, 256)] = dot_t(left[:own, :depth], right[tile(i, 256), :depth])
            return carry

        lax.fori_loop(0, width // 256, other, 0)
        copy = remote(give, take, es.at[n], er.at[n], cn)
        copy.start()
        lax.fori_loop(0, width // 256, self, 0)
        return copy

    def part(i):
        per = own // clips // 128
        return lax.div(i, per), tile(lax.rem(i, per), 128)

    def norm_step(i, field, gain, grad, row):
        at = tile(i, 128)
        d = own_f[at] + take[at].astype(F32)
        v = field[at].astype(F32)
        v = v - jnp.mean(v, axis=1, keepdims=True)
        r = lax.rsqrt(jnp.mean(v * v, axis=1, keepdims=True) + EPS)
        v = v * r
        acc[row : row + 1] += jnp.sum(d * v, axis=0, keepdims=True)
        acc[row + 1 : row + 2] += jnp.sum(d, axis=0, keepdims=True)
        e = d * gain[...]
        mean = jnp.mean(e, axis=1, keepdims=True)
        e = e - mean - v * jnp.mean(e * v, axis=1, keepdims=True)
        return grad + r * e

    tick()
    acc[...] = jnp.zeros_like(acc)
    for copy in loads[:3]:
        copy.wait()
    deep = slope.shape[1]
    sides_of = deep // width

    def hidden_grad(side, i):
        n = side * (width // 256) + i
        slot = lax.rem(n, 2)
        pltpu.make_async_copy(slope.at[:, :256], sl.at[slot], sls.at[slot]).wait()

        @pl.when(n + 1 < deep // 256)
        def _():
            src = slope.at[:, tile(n + 1, 256)]
            pltpu.make_async_copy(src, sl.at[1 - slot], sls.at[1 - slot]).start()

        right = w1_b[tile(i, 256), side * width : (side + 1) * width]
        line = jnp.zeros((1, 256), F32)
        for r in range(2):
            rows = slice(r * own, (r + 1) * own)
            g = dot_t(low[rows], right) * sl[slot, rows].astype(F32)
            g = g.astype(BF)
            gu_b[rows, tile(n, 256)] = g
            line = line + jnp.sum(g.astype(F32), axis=0, keepdims=True)
        gbu[:, tile(n, 256)] = line

    for side in range(sides_of):

        def columns(i, carry):
            hidden_grad(side, i)
            return carry

        lax.fori_loop(0, width // 256, columns, 0)
        if side == 0:
            tick()
    loads[12].start()
    loads[3].wait()
    row = width // groups

    def up_grad(j, carry):
        k = lax.rem(z + j, groups)
        left = h1_b[:, tile(k, row)].T

        def columns(i, carry):
            at = tile(i, 512)
            stage_b[..., at] = dot(left, gu_b[:, at]).astype(BF).reshape(stage_b.shape[:-1] + (512,))
            return carry

        lax.fori_loop(0, deep // 512, columns, 0)
        copy = pltpu.make_async_copy(stage_b, gw1.at[k], ld.at[18])
        copy.start()
        copy.wait()
        return carry

    lax.fori_loop(1, 3, up_grad, 0)
    tick()
    lax.fori_loop(3, groups + 1, up_grad, 0)
    loads[13].start()
    tick()
    loads[12].wait()
    swap = half_sum(0, gu_b, w1_b, deep)
    for copy in loads[14:17]:
        copy.start()
    tick()
    for copy in loads[4:12]:
        copy.wait()
    swap.wait()

    def second_norm(i, carry):
        at = tile(i, 128)
        g = dy_b[part(i)].astype(F32)
        d = norm_step(i, x2_b, g2, g, 3)
        dx2[at] = d
        acc[5:6] += jnp.sum(g, axis=0, keepdims=True)
        low[at] = d.astype(BF)
        acc[2:3] += jnp.sum(d.astype(BF).astype(F32), axis=0, keepdims=True)
        return carry

    lax.fori_loop(0, own // 128, second_norm, 0)
    swap = remote(low.at[:own], low.at[own:], es.at[1], er.at[1], cn)
    swap.start()
    tick()
    swap.wait()

    def out_grad(i, carry):
        at = tile(i, 256)
        gwo[..., at] = dot(mix_b[...], low[:, at]).astype(BF).reshape(gwo.shape[:-1] + (256,))
        return carry

    lax.fori_loop(0, width // 256, out_grad, 0)

    def attn_grad(i, carry):
        at = tile(i, 256)
        da[:, at] = dot_t(wo_b[...], low[at]).astype(BF)
        return carry

    lax.fori_loop(0, 2 * own // 256, attn_grad, 0)
    tick()

    for copy in loads[14:17]:
        copy.wait()

    def down(rows, i):
        left = dot(gu_b[rows, :width], w1_b[:, tile(i, 256)])
        at = pl.ds(pl.multiple_of(width + i * 256, 256), 256)
        return left + dot(gu_b[rows, width:], w1_b[:, at])

    def down_other(i, carry):
        give[:, tile(i, 256)] = down(slice(own, 2 * own), i).astype(BF)
        return carry

    def down_self(i, carry):
        own_f[:, tile(i, 256)] = down(slice(0, own), i)
        return carry

    lax.fori_loop(0, width // 256, down_other, 0)
    y_copy = remote(give, y_take, es.at[3], er.at[3], cn)
    y_copy.start()
    lax.fori_loop(0, width // 256, down_self, 0)
    loads[17].start()
    y_copy.wait()

    def last_add(i, carry):
        at = tile(i, 128)
        gx[part(i)] = (x2_b[at] + own_f[at] + bd[...] + y_take[at].astype(F32)).astype(BF)
        return carry

    lax.fori_loop(0, own // 128, last_add, 0)
    y_start, y_finish, *_ = move_tokens((gx,), (y_o,), us, ur, p, c, z, clips)
    y_start(0, 4)
    dqkv = gu_b.at[:, :third_width]

    def head(h, side):
        rows = tile(h, HEAD)
        place = tile(side, HEAD)
        co, si = cosine[...], sine[...]
        kt = kr_b[rows]
        keys, values = kt.T, vb_b[rows].T
        queries, outer_grads = qs_b[rows].T, da[rows].T
        step = 256
        for i in range(0, 2 * own, step):
            s = slice(i, i + step)
            g = da[rows, s]
            p = jnp.exp(dot(keys, qs_b[rows, s]) - lse[h, :, s])
            delta = jnp.sum(mix_b[rows, s].astype(F32) * g.astype(F32), axis=0, keepdims=True)
            ds = (p * (dot(values, g) - delta)).astype(BF)
            dq2[place, s] = turn(dot(kt, ds) * SCALE, co[:, s], -si[:, s]).astype(BF)
            dv = dot(p.astype(BF), outer_grads[s])
            dk = dot(ds, queries[s])
            if i == 0:
                ak[...] = dk
                av[side] = dv
            else:
                ak[...] += dk
                av[side] += dv
        dk2[place] = turn(ak[...].T, co, -si).astype(BF)

    heads = inner // HEAD
    during = [steps.pop(0) for _ in range(3)]

    def two_heads(i, carry):
        lax.fori_loop(0, 2, lambda side, _: head(2 * i + side, side), None)
        for n, value in enumerate(
            (dq2[...].T, dk2[...].T, jnp.concatenate([av[0], av[1]], axis=1).astype(BF))
        ):
            at = pl.ds(pl.multiple_of(n * inner + i * 2 * HEAD, 2 * HEAD), 2 * HEAD)
            dqkv[:, at] = value
        for n, step in enumerate(during):
            pl.when(i == n * heads // 8)(functools.partial(run, step))
            pl.when(i == n * heads // 8)(functools.partial(y_start, n + 1, 4))
        return carry

    lax.fori_loop(0, heads // 2, two_heads, 0)
    loads[13].wait()
    for g in range(groups):
        left = h1_b[:, g * row : (g + 1) * row].T

        def in_grad(i, carry):
            at = tile(i, 512)
            gwq[g, ..., at] = dot(left, dqkv[:, at]).astype(BF).reshape(gwq.shape[1:-1] + (512,))
            return carry

        lax.fori_loop(0, third_width // 512, in_grad, 0)
    tick(3)
    loads[17].wait()
    swap = half_sum(2, dqkv, w1_b, third_width)
    tick(2)
    swap.wait()
    y_finish()

    def first_norm(i, carry):
        gx[part(i)] = norm_step(i, x_b, g1, dx2[tile(i, 128)], 0).astype(BF)
        return carry

    lax.fori_loop(0, own // 128, first_norm, 0)
    start, finish, *_ = move_tokens((gx,), (gx_o,), ts, tr, p, c, z, clips)
    start(0, 4)
    tick()
    small_s[...] = jnp.zeros_like(small_s)
    for n in range(6):
        for g in range(groups):
            small_s[g, n : n + 1] = acc[n : n + 1, g * row : (g + 1) * row]
    half = row // 2
    mine_at = pl.ds(pl.multiple_of(c * half, half), half)
    for b in range(3 * groups):
        line = jnp.sum(dqkv[:, b * half : (b + 1) * half].astype(F32), axis=0, keepdims=True)
        small_s[b // 3, 6 + b % 3 : 7 + b % 3, mine_at] = line
    share = deep // groups
    for g in range(groups):
        for n in range(share // row):
            at = pl.ds(9 + c * (share // row) + n, 1)
            small_s[g, at] = gbu[:, g * share + n * row : g * share + (n + 1) * row]
    tick()
    for n, target in enumerate((cn, xn, yn)):
        copy = remote(small_s, small_r.at[n], ss.at[n], sr.at[n], target)
        copy.start()
        start(n + 1, 4)
        tick()
        copy.wait()
        small_s[...] += small_r[n]
    tails = [
        remote(small_s.at[col[k][2]], small_z.at[k], ss.at[2 + k], sr.at[2 + k], col[k])
        for k in range(1, groups)
    ]
    for t in tails:
        t.start()
    while steps:
        tick()
    for k in range(1, groups):
        tails[k - 1].wait()
    small_o[...] = small_s[z]
    for k in range(1, groups):
        small_o[...] += small_z[k]
    for u in units:
        w, j = u
        for n in range(2):
            c1(u, n).wait_send()
            c2(u, n).wait_send()
            if j:
                c3(u, n).wait_send()
    for w in range(count):
        for n in range(2):
            c4(w, n).wait_send()
            c5(w, n).wait_send()
        pltpu.make_async_copy(full[w], full[w], ls.at[w]).wait()
        remote(full[w], full[w], cs.at[w], cr.at[w], cn).wait()
    finish()


def backward(gw2, arrays, tables, lines, groups, blocks):
    act, slope, w2, w1, wo, wq, mix, qs, kr, vb, h1, h2, x2, x, dy, dy_all = arrays
    (own, width), clips = x.shape, dy.shape[0] // 2
    moved = jax.ShapeDtypeStruct((clips,) + dy.shape[1:], BF)
    small = jax.ShapeDtypeStruct((groups, lines + -lines % 8, width // groups), F32)
    count = len(blocks)
    dma = pltpu.SemaphoreType.DMA
    split = lambda v: (groups, 2, 2, 2, v.shape[0] // (8 * groups), v.shape[1])
    tiles = [split(v)[4:] for v in (wq, wo, w1, w2)]
    shapes = [
        jax.ShapeDtypeStruct((4, 2, t[0], 2 * t[1]) if b else (2, 4, 2) + t, BF)
        for t, b in zip(tiles, blocks)
    ]
    shapes += [
        jax.ShapeDtypeStruct(split(w1), BF),
        jax.ShapeDtypeStruct(small.shape[1:], F32),
        moved,
        moved,
    ]
    scratch = [pltpu.VMEM(v.shape, v.dtype) for v in (act, w1, wo, mix, qs, kr, vb, h1, x2, x, moved)]
    half, low = (own, width), pltpu.VMEM((2 * own, width), BF)
    scratch += [pltpu.VMEM(half, F32)] + [pltpu.VMEM(half, BF)] * 3
    scratch += [pltpu.VMEM(half, F32), low, pltpu.VMEM(mix.shape, BF)]
    scratch += [pltpu.VMEM(split(wo), BF), pltpu.VMEM(split(wq), BF)]
    scratch += [pltpu.VMEM((2 * own, HEAD), F32), pltpu.VMEM((2, 2 * own, HEAD), F32)]
    scratch += [pltpu.VMEM((2 * HEAD, 2 * own), BF)] * 2
    scratch += [pltpu.VMEM((8, width), F32), pltpu.VMEM(moved.shape, BF)]
    scratch += [pltpu.VMEM((2, 2 * own, 256), BF), pltpu.VMEM((1, act.shape[1]), F32)]
    scratch += [pltpu.VMEM(split(w1)[1:], BF)]
    scratch += [dma((19,)), dma((4,)), dma((4,)), dma((2,))]
    for lead in (
        (groups, 2),
        (groups, 2),
        (groups, 2),
        (groups, 2),
        (groups,),
        (groups,),
        (groups, 2),
        (4, 2),
    ):
        scratch += [pltpu.VMEM(lead + t, BF) for t in tiles]
    scratch += [
        pltpu.VMEM(small.shape, F32),
        pltpu.VMEM((3,) + small.shape, F32),
        pltpu.VMEM(small.shape, F32),
    ]
    pair = dma((count, groups, 2))
    scratch += [pair] * 7 + [dma((count, 2))] * 4
    scratch += [dma((count,))] * 3 + [dma((2 + groups,))] * 2 + [dma((1, clips))] * 4
    return pl.pallas_call(
        functools.partial(backward_body, groups, clips, blocks),
        out_shape=shapes,
        in_specs=[ANY] * (1 + len(arrays)) + [VM] * len(tables),
        out_specs=[ANY] * (count + 1) + [VM, ANY, ANY],
        scratch_shapes=scratch,
        compiler_params=pltpu.CompilerParams(
            collective_id=1, has_side_effects=True, vmem_limit_bytes=67043328
        ),
        name="backward",
    )(gw2, *arrays, *tables)


def contract(left, right, a, b):
    return lax.dot_general(left, right, (((a,), (b,)), ((), ())), preferred_element_type=F32)


def paired(
    tokens,
    positions,
    ln1_gain,
    ln1_bias,
    w_qkv,
    b_qkv,
    w_out,
    b_out,
    ln2_gain,
    ln2_bias,
    w_up,
    b_up,
    w_down,
    b_down,
    cotangent,
):
    groups = lax.axis_size("grp")
    clips, part, width = tokens.shape
    hidden = w_down.shape[0] * groups
    own = clips * part
    length = 2 * own
    c, z = lax.axis_index("core"), lax.axis_index("grp")
    wide = width // 2
    deep = hidden // 2
    row = width // groups

    def pick(value, axis):
        return lax.dynamic_index_in_dim(value, c, axis, keepdims=False)

    blocks = (3 * groups, 0, groups, 0)
    raw = [
        w.reshape(((4, 2) if b else (2, 4, 2)) + (w.shape[0] // (8 if b else 16), w.shape[1]))
        for w, b in zip((w_qkv, w_out, w_up, w_down), blocks)
    ]
    bq, bu = b_qkv.shape[0] // row, b_up.shape[0] // row
    vectors = [ln1_gain, ln1_bias, b_out, ln2_gain, ln2_bias, b_down]
    vectors += [b_qkv, b_up]
    lines = len(vectors) - 2 + bq + bu
    size, start = (lines + -lines % 8) * row, 0
    small = jnp.zeros((size,), F32)
    for v in vectors:
        small = small + jnp.pad(v.astype(F32), (start, size - start - v.shape[0]))
        start += v.shape[0]
    small = small.reshape(-1, row)
    pair = jnp.arange(HEAD // 2)
    band = (pair >= 10).astype(jnp.int32) + (pair >= 21).astype(jnp.int32)
    begin = jnp.where(band == 0, 0, jnp.where(band == 1, 10, 21))
    number = jnp.where(band == 0, 10, 11)
    freq = jnp.power(F32(10000.0), -(pair - begin).astype(F32) / number.astype(F32))
    pos = positions.astype(F32)[:, :, None, :]
    band = band[None, :, None]
    chosen = jnp.where(band == 0, pos[0], jnp.where(band == 1, pos[1], pos[2]))
    angles = chosen * freq[None, :, None]
    tab = jnp.concatenate([jnp.cos(angles), jnp.sin(angles)], axis=1)
    wq, wo, w1, w2, gain, bu_own, x, tab, dy, h1, qs, kr, vb, mixed, lse, x2, h2 = forward(
        raw, blocks, small, tokens, tab, cotangent, groups
    )
    wq = wq.reshape(width, 3 * wide)
    wo = wo.reshape(wide, width)
    w1 = w1.reshape(width, deep)
    w2 = w2.reshape(deep, width)
    grad_all = dy.reshape(length, width)
    tokens = x.reshape(own, width)
    u = contract(h2, w1, 1, 0) + bu_own
    cdf = 0.5 * (1.0 + lax.erf(u * F32(0.7071067811865476)))
    act = (u * cdf).astype(BF)
    slope = (cdf + u * jnp.exp(-0.5 * u * u) * F32(0.3989422804014327)).astype(BF)

    gw2 = contract(act, grad_all, 0, 0).astype(BF)
    gw2 = gw2.reshape(groups, 2, 2, 2, gw2.shape[0] // (8 * groups), width)
    arrays = (act, slope, w2, w1, wo, wq, mixed, qs, kr, vb, h1, h2, x2, tokens, dy, grad_all)
    tables = (lse, tab, gain)
    gwq, gwo, gw1, gw2, _, sums, gx, output = backward(gw2, arrays, tables, lines, groups, blocks)
    gwq, gwo, gw1, gw2 = (
        g.reshape(shard.shape).astype(F32)
        for g, shard in zip((gwq, gwo, gw1, gw2), (w_qkv, w_out, w_up, w_down))
    )
    gg1, gb1, gbo, gg2, gb2, gbd = (sums[n] for n in range(6))
    gbq, gbu = sums[6 : 6 + bq].reshape(-1), sums[6 + bq : lines].reshape(-1)
    return (output, gx, gg1, gb1, gwq, gbq, gwo, gbo, gg2, gb2, gw1, gbu, gw2, gbd)


def paired_specs():
    rep = ("rp", "core")
    ins = (P(rep, "grp", None), P(None, rep, "grp"))
    one, two = P("grp"), P("grp", None)
    ins += (one, one, two, one, two, one, one, one, two, one, two, one, P(rep, "grp", None))
    outs = (P(rep, "grp", None),) * 2
    outs += (one, one, two, one, two, one, one, one, two, one, two, one)
    return ins, outs


def rotary_angles(positions):
    pair = jnp.arange(32)
    band = (pair >= 10).astype(jnp.int32) + (pair >= 21).astype(jnp.int32)
    start = jnp.where(band == 0, 0, jnp.where(band == 1, 10, 21))
    count = jnp.where(band == 0, 10, 11)
    freq = jnp.power(
        jnp.float32(10000.0), -(pair - start).astype(jnp.float32) / count.astype(jnp.float32)
    )
    pos_f = positions.astype(jnp.float32)
    chosen = jnp.where(
        band[None, :] == 0,
        pos_f[0][:, None],
        jnp.where(band[None, :] == 1, pos_f[1][:, None], pos_f[2][:, None]),
    )
    return chosen * freq[None, :]


def rotate(field, cosine, sine):
    first = field[..., :32]
    second = field[..., 32:]
    return jnp.concatenate(
        [first * cosine - second * sine, first * sine + second * cosine], axis=-1
    )


def normalize(field):
    centred = field - jnp.mean(field, axis=-1, keepdims=True)
    variance = jnp.mean(centred * centred, axis=-1, keepdims=True)
    factor = lax.rsqrt(variance + EPS)
    return (centred * factor, factor)


def norm_back(grad_norm, normed, factor):
    return factor * (
        grad_norm
        - jnp.mean(grad_norm, axis=-1, keepdims=True)
        - normed * jnp.mean(grad_norm * normed, axis=-1, keepdims=True)
    )


def outer(left, right):
    return lax.dot_general(
        left, right, (((0,), (0,)), ((), ())), preferred_element_type=jnp.float32
    )


def back(left, right):
    return lax.dot_general(
        left, right, (((1,), (1,)), ((), ())), preferred_element_type=jnp.float32
    )


def exact_gelu(value):
    return jax.nn.gelu(value, approximate=False)


def column_sum(value):
    return jnp.sum(value.astype(jnp.float32), axis=0)


def forward_pass(params, field_in, positions):
    g1, b1, wqkv, bqkv, wo, bo, g2, b2, w1, bu, w2, bd = params
    field = field_in.astype(jnp.float32)
    count, width = field.shape
    heads = width // 64
    angles = rotary_angles(positions)
    cosine = jnp.cos(angles)[:, None, :]
    sine = jnp.sin(angles)[:, None, :]
    normed1, factor1 = normalize(field)
    h1 = (normed1 * g1.astype(jnp.float32) + b1.astype(jnp.float32)).astype(jnp.bfloat16)
    qkv = jnp.dot(h1, wqkv, preferred_element_type=jnp.float32) + bqkv.astype(jnp.float32)
    query_rot = rotate(qkv[:, :width].reshape(count, heads, 64), cosine, sine).astype(jnp.bfloat16)
    keys_rot = (
        rotate(qkv[:, width : 2 * width].reshape(count, heads, 64), cosine, sine)
        .astype(jnp.bfloat16)
        .reshape(count, width)
    )
    values = qkv[:, 2 * width :].astype(jnp.bfloat16)
    keys_all, values_all = (
        lax.all_gather(keys_rot, "grp", axis=0, tiled=True),
        lax.all_gather(values, "grp", axis=0, tiled=True),
    )
    total = keys_all.shape[0]
    keys_all = keys_all.reshape(total, heads, 64)
    values_all = values_all.reshape(total, heads, 64)
    scores = (
        jnp.einsum("thd,shd->hts", query_rot, keys_all, preferred_element_type=jnp.float32) * SCALE
    )
    top = jnp.max(scores, axis=-1, keepdims=True)
    lse = top + jnp.log(jnp.sum(jnp.exp(scores - top), axis=-1, keepdims=True))
    probs = jnp.exp(scores - lse).astype(jnp.bfloat16)
    mixed = (
        jnp.einsum("hts,shd->thd", probs, values_all, preferred_element_type=jnp.float32)
        .reshape(count, width)
        .astype(jnp.bfloat16)
    )
    second = field + jnp.dot(mixed, wo, preferred_element_type=jnp.float32) + bo.astype(jnp.float32)
    normed2, factor2 = normalize(second)
    h2 = (normed2 * g2.astype(jnp.float32) + b2.astype(jnp.float32)).astype(jnp.bfloat16)
    hidden = jnp.dot(h2, w1, preferred_element_type=jnp.float32) + bu.astype(jnp.float32)
    active = exact_gelu(hidden).astype(jnp.bfloat16)
    result = (
        second + jnp.dot(active, w2, preferred_element_type=jnp.float32) + bd.astype(jnp.float32)
    )
    saved = (
        normed1,
        factor1,
        h1,
        query_rot,
        keys_rot,
        values,
        lse,
        mixed,
        normed2,
        factor2,
        h2,
        hidden,
        active,
        cosine,
        sine,
    )
    return (saved, result.astype(jnp.bfloat16))


def backward_pass(params, saved, grad_in, totals):
    g1, b1, wqkv, bqkv, wo, bo, g2, b2, w1, bu, w2, bd = params
    (
        normed1,
        factor1,
        h1,
        query_rot,
        keys_rot,
        values,
        lse,
        mixed,
        normed2,
        factor2,
        h2,
        hidden,
        active,
        cosine,
        sine,
    ) = saved
    grad_out = grad_in.astype(jnp.float32)
    count, width = grad_out.shape
    heads = width // 64
    grad_y2 = grad_out.astype(jnp.bfloat16)
    grad_w2 = outer(active, grad_y2)
    grad_bd = column_sum(grad_y2)
    grad_act = back(grad_y2, w2)
    unused, pull = jax.vjp(exact_gelu, hidden)
    grad_hidden = pull(grad_act)[0].astype(jnp.bfloat16)
    grad_w1 = outer(h2, grad_hidden)
    grad_bu = column_sum(grad_hidden)
    grad_h2 = back(grad_hidden, w1)
    grad_g2 = jnp.sum(grad_h2 * normed2, axis=0)
    grad_b2 = jnp.sum(grad_h2, axis=0)
    grad_second = grad_out + norm_back(grad_h2 * g2.astype(jnp.float32), normed2, factor2)
    grad_y1 = grad_second.astype(jnp.bfloat16)
    grad_wo = outer(mixed, grad_y1)
    grad_bo = column_sum(grad_y1)
    grad_mixed = back(grad_y1, wo).astype(jnp.bfloat16).reshape(count, heads, 64)
    keys_all, values_all = (
        lax.all_gather(keys_rot, "grp", axis=0, tiled=True),
        lax.all_gather(values, "grp", axis=0, tiled=True),
    )
    total = keys_all.shape[0]
    keys_all = keys_all.reshape(total, heads, 64)
    values_all = values_all.reshape(total, heads, 64)
    scores = (
        jnp.einsum("thd,shd->hts", query_rot, keys_all, preferred_element_type=jnp.float32) * SCALE
    )
    probs = jnp.exp(scores - lse)
    grad_probs = jnp.einsum(
        "thd,shd->hts", grad_mixed, values_all, preferred_element_type=jnp.float32
    )
    delta = jnp.sum(probs * grad_probs, axis=-1, keepdims=True)
    grad_scores = (probs * (grad_probs - delta)).astype(jnp.bfloat16)
    grad_query = (
        jnp.einsum("hts,shd->thd", grad_scores, keys_all, preferred_element_type=jnp.float32)
        * SCALE
    )
    probs_low = probs.astype(jnp.bfloat16)
    grad_values = jnp.einsum(
        "hts,thd->shd", probs_low, grad_mixed, preferred_element_type=jnp.float32
    )
    grad_keys = (
        jnp.einsum("hts,thd->shd", grad_scores, query_rot, preferred_element_type=jnp.float32)
        * SCALE
    )
    keys_own, values_own = (
        lax.psum_scatter(
            grad_keys.reshape(total, width).astype(jnp.bfloat16),
            "grp",
            scatter_dimension=0,
            tiled=True,
        ).astype(jnp.float32),
        lax.psum_scatter(
            grad_values.reshape(total, width).astype(jnp.bfloat16),
            "grp",
            scatter_dimension=0,
            tiled=True,
        ).astype(jnp.float32),
    )
    query_back = rotate(grad_query, cosine, -sine).reshape(count, width)
    keys_back = rotate(keys_own.reshape(count, heads, 64), cosine, -sine).reshape(count, width)
    grad_qkv = jnp.concatenate([query_back, keys_back, values_own], axis=1).astype(jnp.bfloat16)
    grad_wqkv = outer(h1, grad_qkv)
    grad_bqkv = column_sum(grad_qkv)
    grad_h1 = back(grad_qkv, wqkv)
    grad_g1 = jnp.sum(grad_h1 * normed1, axis=0)
    grad_b1 = jnp.sum(grad_h1, axis=0)
    grad_field = grad_second + norm_back(grad_h1 * g1.astype(jnp.float32), normed1, factor1)
    terms = (
        grad_g1,
        grad_b1,
        grad_wqkv,
        grad_bqkv,
        grad_wo,
        grad_bo,
        grad_g2,
        grad_b2,
        grad_w1,
        grad_bu,
        grad_w2,
        grad_bd,
    )
    totals = tuple((a + b for a, b in zip(totals, terms)))
    return (grad_field.astype(jnp.bfloat16), totals)


def local(
    tokens,
    positions,
    ln1_gain,
    ln1_bias,
    w_qkv,
    b_qkv,
    w_out,
    b_out,
    ln2_gain,
    ln2_bias,
    w_up,
    b_up,
    w_down,
    b_down,
    cotangent,
):
    shards = (
        ln1_gain,
        ln1_bias,
        w_qkv,
        b_qkv,
        w_out,
        b_out,
        ln2_gain,
        ln2_bias,
        w_up,
        b_up,
        w_down,
        b_down,
    )
    groups = lax.axis_size("grp")
    totals = tuple((jnp.zeros((s.shape[0] * groups,) + s.shape[1:], jnp.float32) for s in shards))
    outputs = []
    gradients = []
    for index in range(tokens.shape[0]):
        forward_params = (
            lax.all_gather(ln1_gain, "grp", axis=0, tiled=True),
            lax.all_gather(ln1_bias, "grp", axis=0, tiled=True),
            lax.all_gather(w_qkv, "grp", axis=0, tiled=True),
            lax.all_gather(b_qkv, "grp", axis=0, tiled=True),
            lax.all_gather(w_out, "grp", axis=0, tiled=True),
            lax.all_gather(b_out, "grp", axis=0, tiled=True),
            lax.all_gather(ln2_gain, "grp", axis=0, tiled=True),
            lax.all_gather(ln2_bias, "grp", axis=0, tiled=True),
            lax.all_gather(w_up, "grp", axis=0, tiled=True),
            lax.all_gather(b_up, "grp", axis=0, tiled=True),
            lax.all_gather(w_down, "grp", axis=0, tiled=True),
            lax.all_gather(b_down, "grp", axis=0, tiled=True),
        )
        saved, result = forward_pass(forward_params, tokens[index], positions[:, index, :])
        outputs.append(result)
        backward_params = (
            lax.all_gather(ln1_gain, "grp", axis=0, tiled=True),
            lax.all_gather(ln1_bias, "grp", axis=0, tiled=True),
            lax.all_gather(w_qkv, "grp", axis=0, tiled=True),
            lax.all_gather(b_qkv, "grp", axis=0, tiled=True),
            lax.all_gather(w_out, "grp", axis=0, tiled=True),
            lax.all_gather(b_out, "grp", axis=0, tiled=True),
            lax.all_gather(ln2_gain, "grp", axis=0, tiled=True),
            lax.all_gather(ln2_bias, "grp", axis=0, tiled=True),
            lax.all_gather(w_up, "grp", axis=0, tiled=True),
            lax.all_gather(b_up, "grp", axis=0, tiled=True),
            lax.all_gather(w_down, "grp", axis=0, tiled=True),
            lax.all_gather(b_down, "grp", axis=0, tiled=True),
        )
        grad_field, totals = backward_pass(backward_params, saved, cotangent[index], totals)
        gradients.append(grad_field)
    owned = (
        lax.psum_scatter(
            totals[0].astype(jnp.bfloat16), "grp", scatter_dimension=0, tiled=True
        ).astype(jnp.float32),
        lax.psum_scatter(
            totals[1].astype(jnp.bfloat16), "grp", scatter_dimension=0, tiled=True
        ).astype(jnp.float32),
        lax.psum_scatter(
            totals[2].astype(jnp.bfloat16), "grp", scatter_dimension=0, tiled=True
        ).astype(jnp.float32),
        lax.psum_scatter(
            totals[3].astype(jnp.bfloat16), "grp", scatter_dimension=0, tiled=True
        ).astype(jnp.float32),
        lax.psum_scatter(
            totals[4].astype(jnp.bfloat16), "grp", scatter_dimension=0, tiled=True
        ).astype(jnp.float32),
        lax.psum_scatter(
            totals[5].astype(jnp.bfloat16), "grp", scatter_dimension=0, tiled=True
        ).astype(jnp.float32),
        lax.psum_scatter(
            totals[6].astype(jnp.bfloat16), "grp", scatter_dimension=0, tiled=True
        ).astype(jnp.float32),
        lax.psum_scatter(
            totals[7].astype(jnp.bfloat16), "grp", scatter_dimension=0, tiled=True
        ).astype(jnp.float32),
        lax.psum_scatter(
            totals[8].astype(jnp.bfloat16), "grp", scatter_dimension=0, tiled=True
        ).astype(jnp.float32),
        lax.psum_scatter(
            totals[9].astype(jnp.bfloat16), "grp", scatter_dimension=0, tiled=True
        ).astype(jnp.float32),
        lax.psum_scatter(
            totals[10].astype(jnp.bfloat16), "grp", scatter_dimension=0, tiled=True
        ).astype(jnp.float32),
        lax.psum_scatter(
            totals[11].astype(jnp.bfloat16), "grp", scatter_dimension=0, tiled=True
        ).astype(jnp.float32),
    )
    summed = (
        lax.psum(owned[0].astype(jnp.bfloat16), "rep").astype(jnp.float32),
        lax.psum(owned[1].astype(jnp.bfloat16), "rep").astype(jnp.float32),
        lax.psum(owned[2].astype(jnp.bfloat16), "rep").astype(jnp.float32),
        lax.psum(owned[3].astype(jnp.bfloat16), "rep").astype(jnp.float32),
        lax.psum(owned[4].astype(jnp.bfloat16), "rep").astype(jnp.float32),
        lax.psum(owned[5].astype(jnp.bfloat16), "rep").astype(jnp.float32),
        lax.psum(owned[6].astype(jnp.bfloat16), "rep").astype(jnp.float32),
        lax.psum(owned[7].astype(jnp.bfloat16), "rep").astype(jnp.float32),
        lax.psum(owned[8].astype(jnp.bfloat16), "rep").astype(jnp.float32),
        lax.psum(owned[9].astype(jnp.bfloat16), "rep").astype(jnp.float32),
        lax.psum(owned[10].astype(jnp.bfloat16), "rep").astype(jnp.float32),
        lax.psum(owned[11].astype(jnp.bfloat16), "rep").astype(jnp.float32),
    )
    output = jnp.stack(outputs, axis=0)
    grad_tokens = jnp.stack(gradients, axis=0)
    return (
        output,
        grad_tokens,
        summed[0],
        summed[1],
        summed[2],
        summed[3],
        summed[4],
        summed[5],
        summed[6],
        summed[7],
        summed[8],
        summed[9],
        summed[10],
        summed[11],
    )


def spread(mesh):
    placed = (
        P("rep", "grp", None),
        P(None, "rep", "grp"),
        P("grp"),
        P("grp"),
        P("grp", None),
        P("grp"),
        P("grp", None),
        P("grp"),
        P("grp"),
        P("grp"),
        P("grp", None),
        P("grp"),
        P("grp", None),
        P("grp"),
        P("rep", "grp", None),
    )
    return jax.shard_map(
        local,
        mesh=mesh,
        in_specs=placed,
        out_specs=(
            P("rep", "grp", None),
            P("rep", "grp", None),
            P("grp"),
            P("grp"),
            P("grp", None),
            P("grp"),
            P("grp", None),
            P("grp"),
            P("grp"),
            P("grp"),
            P("grp", None),
            P("grp"),
            P("grp", None),
            P("grp"),
        ),
        check_vma=False,
    )


def solution(mesh):
    reps, groups = mesh.devices.shape
    flat = mesh.devices.reshape(-1)

    def run(*args):
        clips = args[0].shape[0] // reps
        if reps == 8 and groups == 2 * clips:
            split = Mesh(flat.reshape(reps // 2, 2, groups), ("rp", "core", "grp"))
            ins, outs = paired_specs()
            return jax.shard_map(
                paired, mesh=split, in_specs=ins, out_specs=outs, check_vma=False
            )(*args)
        return spread(mesh)(*args)

    return run
```

```python
import functools

import jax
import jax.numpy as jnp
from jax import lax
from jax.experimental import pallas as pl
from jax.experimental.pallas import tpu as pltpu
from jax.sharding import Mesh
from jax.sharding import PartitionSpec as P

SCALE = 0.125
EPS = 1e-06
HEAD = 64
BF = jnp.bfloat16
F32 = jnp.float32
MESH = pl.DeviceIdType.MESH
ANY = pl.BlockSpec(memory_space=pl.ANY)
VM = pl.BlockSpec(memory_space=pltpu.VMEM)


def where_am_i():
    return lax.axis_index("rp"), lax.axis_index("core"), lax.axis_index("grp")


def remote(src, dst, send, recv, target):
    return pltpu.make_async_remote_copy(
        src_ref=src,
        dst_ref=dst,
        send_sem=send,
        recv_sem=recv,
        device_id=target,
        device_id_type=MESH,
    )


def enter(p, c, z, groups):
    barrier = pltpu.get_barrier_semaphore()
    for k in range(groups):
        for d in range(2):
            if k == 0 and d == 0:
                continue
            pl.semaphore_signal(
                barrier, inc=1, device_id=(p, c ^ d, lax.rem(z + k, groups)), device_id_type=MESH
            )
    for b in (1, 2):
        pl.semaphore_signal(barrier, inc=1, device_id=(p ^ b, c, z), device_id_type=MESH)
    pl.semaphore_wait(barrier, 2 * groups - 1 + 2)


def move_tokens(refs, outs, send, recv, p, c, z, clips):
    core, slot = lax.div(z, clips), lax.rem(z, clips)

    def route(i):
        return core, c * clips + i

    def here(i):
        return jnp.logical_and(core == c, c * clips + i == z)

    def start(k, pieces):
        for n, (src, dst) in enumerate(zip(refs, outs)):
            rows = src.shape[1] // pieces
            rows = pl.ds(k * rows, rows)
            for i in range(clips):
                tc, tz = route(i)

                @pl.when(here(i))
                def _():
                    pltpu.make_async_copy(
                        src.at[i, rows], dst.at[slot, rows], recv.at[n, slot]
                    ).start()

                @pl.when(jnp.logical_not(here(i)))
                def _():
                    remote(
                        src.at[i, rows],
                        dst.at[slot, rows],
                        send.at[n, i],
                        recv.at[n, slot],
                        (p, tc, tz),
                    ).start()

    def sent():
        for n, (src, dst) in enumerate(zip(refs, outs)):
            for i in range(clips):

                @pl.when(jnp.logical_not(here(i)))
                def _():
                    remote(
                        src.at[i], dst.at[slot], send.at[n, i], recv.at[n, slot], (p, c ^ 1, z)
                    ).wait_send()

    def arrive():
        for n, (src, dst) in enumerate(zip(refs, outs)):
            for m in range(clips):
                pltpu.make_async_copy(src.at[0], dst.at[m], recv.at[n, m]).wait()

    def finish():
        sent()
        arrive()

    return start, finish, sent, arrive


def turn(u, cosine, sine):
    half = HEAD // 2
    first, second = u[:half], u[half:]
    return jnp.concatenate(
        [first * cosine - second * sine, first * sine + second * cosine], axis=0
    )


def dot(a, b):
    return jnp.dot(a, b, preferred_element_type=F32)


def dot_t(a, b):
    return lax.dot_general(a, b, (((1,), (1,)), ((), ())), preferred_element_type=F32)


def tile(i, size):
    return pl.ds(pl.multiple_of(i * size, size), size)


def cuts(whole, half, c, blocks):
    if blocks == 0:
        return [(whole.at[c], half)]
    size = half.shape[3] // blocks
    return [
        (
            whole.at[:, :, :, pl.ds(pl.multiple_of((2 * b + c) * size, size), size)],
            half.at[:, :, :, pl.ds(b * size, size)],
        )
        for b in range(blocks)
    ]


def forward_body(groups, clips, blocks, *refs):
    count = len(blocks)
    raw, (small, x, tab, dy) = refs[:count], refs[count : count + 4]
    (wq_o, wo_o, *outs) = refs[count + 4 : 2 * count + 4]
    (gain, bu, x_o, tab_o, dy_o, h1_o, qs_o, kr_o, vb_o, mix_o, lse_o, x2_o, h2_o) = refs[
        2 * count + 4 : 2 * count + 17
    ]
    halves = refs[2 * count + 17 : 3 * count + 17]
    (wq_v, small_v, x_v, tab_v, tab_w, h1, qs, kr, vb, mix, qkv, bias) = refs[
        3 * count + 17 : 3 * count + 29
    ]
    (wo_v, own_f, give, take, h2) = refs[3 * count + 29 : 3 * count + 34]
    (zs, zr, xs, xr, ys, yr, fs, fr, hs, ls, ss, sr, ts, tr, us, ur, vs, vr, es, er, ks) = refs[
        3 * count + 34 :
    ]
    outs = [wq_v, wo_v, *outs]
    p, c, z = where_am_i()
    for w in range(count):
        for src, dst in cuts(raw[w], halves[w], c, blocks[w]):
            pltpu.make_async_copy(src, dst, hs.at[w]).start()
    enter(p, c, z, groups)
    col = [(p, c, lax.rem(z + k, groups)) for k in range(groups)]
    org = [lax.rem(z + groups - k, groups) for k in range(groups)]
    xn, yn, cn = (p ^ 1, c, z), (p ^ 2, c, z), (p, c ^ 1, z)
    smalls = [
        remote(small, small_v.at[z], ss.at[k], sr.at[k], col[k]) for k in range(1, groups)
    ]
    for s in smalls:
        s.start()
    keep = [pltpu.make_async_copy(small, small_v.at[z], ls.at[count])]
    keep[0].start()
    start_tab, _, sent_tab, arrive_tab = move_tokens((tab,), (tab_v,), vs, vr, p, c, z, clips)
    start_x, _, sent_x, arrive_x = move_tokens((x,), (x_v,), ts, tr, p, c, z, clips)
    start_dy, _, sent_dy, arrive_dy = move_tokens((dy,), (dy_o.at[:clips],), us, ur, p, c, z, clips)
    units = [(w, d, side) for w in range(count) for d in range(1, groups) for side in range(2)]

    def origin(d, side):
        return z - d if side == 0 else z + d

    def arrives(d, side):
        return z >= d if side == 0 else z + d < groups

    def leaves(d, side):
        if side == 0:
            return jnp.logical_and(z + 1 < groups, z + 1 >= d)
        return jnp.logical_and(z >= 1, z - 1 + d < groups)

    def hop(w, d, side, src):
        o = origin(d - 1, side)
        target = (p, c, lax.rem(z + 1 if side == 0 else z + groups - 1, groups))
        return remote(src, outs[w].at[o, p], zs.at[w, side, d], zr.at[w, side, d], target)

    def own(w):
        pltpu.make_async_copy(halves[w], halves[w], hs.at[w]).wait()
        keep.append(pltpu.make_async_copy(halves[w], outs[w].at[z], ls.at[w]))
        keep[-1].start()
        for side in range(2):

            @pl.when(leaves(1, side))
            def _():
                hop(w, 1, side, halves[w].at[p]).start()

    def links(u):
        w, d, side = u
        o = outs[w].at[lax.rem(origin(d, side) + groups, groups)]
        e, f = xs.at[w, side, d], xr.at[w, side, d]
        g, h = ys.at[w, side, d], yr.at[w, side, d]
        a, b = fs.at[w, side, d, 0], fr.at[w, side, d, 0]
        m, n = fs.at[w, side, d, 1], fr.at[w, side, d, 1]
        across = lambda q: remote(o.at[q], o.at[q], e, f, xn)
        along = lambda q: remote(o.at[q], o.at[q], g, h, yn)
        first = lambda q: remote(o.at[q, 0], o.at[q, 0], a, b, yn)
        second = lambda q: remote(o.at[q, 1], o.at[q, 1], m, n, xn)
        return o, across, along, first, second

    def plane(u):
        w, d, side = u
        o, across, along, first, second = links(u)

        @pl.when(arrives(d, side))
        def _():
            remote(o.at[p], o.at[p], zs.at[w, side, d], zr.at[w, side, d], xn).wait_recv()
            if d + 1 < groups:

                @pl.when(leaves(d + 1, side))
                def _():
                    hop(w, d + 1, side, o.at[p]).start()

            across(p).start()
            along(p).start()

    def forward(u):
        w, d, side = u
        o, across, along, first, second = links(u)

        @pl.when(arrives(d, side))
        def _():
            across(p ^ 1).wait_recv()
            first(p ^ 1).start()
            along(p ^ 2).wait_recv()
            second(p ^ 2).start()

    def complete(u):
        w, d, side = u
        o, across, along, first, second = links(u)

        @pl.when(arrives(d, side))
        def _():
            first(p ^ 3).wait_recv()
            second(p ^ 3).wait_recv()

    def settle(u):
        w, d, side = u
        o, across, along, first, second = links(u)

        @pl.when(arrives(d, side))
        def _():
            across(p).wait_send()
            along(p).wait_send()
            first(p).wait_send()
            second(p).wait_send()

        @pl.when(leaves(d, side))
        def _():
            hop(w, d, side, halves[w].at[p]).wait_send()

    own(0)
    start_tab(0, 1)
    own(1)
    moves = {2 * k: (start_x, k) for k in range(4)}
    moves.update({10 + 3 * k: (start_dy, k) for k in range(4)})
    lag = 3

    def step(n):
        if n < len(units):
            plane(units[n])
            w, d, side = units[n]
            if (d, side) == (1, 1) and w + 2 < count:
                own(w + 2)
            if n in moves:
                moves[n][0](moves[n][1], 4)
        if n >= lag:
            forward(units[n - lag])

    steps = list(range(len(units) + lag))
    early = 2 * (groups - 1) + lag
    for _ in range(early):
        step(steps.pop(0))
    for k in range(1, groups):
        remote(small, small_v.at[org[k]], ss.at[k], sr.at[k], col[k]).wait_recv()
    keep[0].wait()
    row = small_v.shape[2]
    half = row // 2
    mine = pl.ds(pl.multiple_of(c * half, half), half)
    for g in range(groups):
        gain[0:6, g * row : (g + 1) * row] = small_v[g, 0:6]
        share = bu.shape[1] // groups
        for n in range(share // row):
            line = small_v[g, pl.ds(9 + c * (share // row) + n, 1)]
            bu[:, g * share + n * row : g * share + (n + 1) * row] = line
        for r in range(3):
            bias[3 * g + r : 3 * g + r + 1] = small_v[g, 6 + r : 7 + r, mine]
    own_count = h1.shape[0] // 2
    arrive_x()
    saves = [pltpu.make_async_copy(x_v, x_o, ks.at[0])]
    saves[0].start()

    def norm(i, carry):
        per = own_count // clips // 128
        v = x_v[lax.div(i, per), tile(lax.rem(i, per), 128)].astype(F32)
        v = v - jnp.mean(v, axis=1, keepdims=True)
        v = v * lax.rsqrt(jnp.mean(v * v, axis=1, keepdims=True) + EPS)
        h1[tile(i, 128)] = (v * gain[0:1] + gain[1:2]).astype(BF)
        return carry

    lax.fori_loop(0, own_count // 128, norm, 0)
    swap = remote(h1.at[:own_count], h1.at[own_count:], es.at[0], er.at[0], cn)
    swap.start()
    arrive_tab()
    swap_tab = remote(tab_v, tab_w, es.at[1], er.at[1], cn)
    swap_tab.start()
    step(steps.pop(0))
    swap_tab.wait()
    part = tab_v.shape[2]
    for m in range(clips):
        tab_o[:, m * part : (m + 1) * part] = tab_v[m]
        tab_o[:, own_count + m * part : own_count + (m + 1) * part] = tab_w[m]
    for u in units[: 2 * (groups - 1)]:
        complete(u)
    keep[1].wait()
    saves.append(pltpu.make_async_copy(wq_v, wq_o, ks.at[1]))
    saves[1].start()
    swap.wait()
    saves.append(pltpu.make_async_copy(h1, h1_o, ks.at[2]))
    saves[2].start()
    inner = qs.shape[0]
    heads = inner // HEAD
    pairs = heads // 2

    def head(h, side):
        rows, place = tile(h, HEAD), tile(side, HEAD)
        co, si = tab_o[: HEAD // 2], tab_o[HEAD // 2 :]
        k = turn(qkv[1, place], co, si).astype(BF)
        v = qkv[2, place].astype(BF)
        q = (turn(qkv[0, place], co, si).astype(BF).astype(F32) * SCALE).astype(BF)
        kr[rows] = k
        vb[rows] = v
        qs[rows] = q
        keys = k.T
        size = 256
        for i in range(0, 2 * own_count, size):
            scores = dot(keys, q[:, i : i + size])
            top = jnp.max(scores, axis=0, keepdims=True)
            e = jnp.exp(scores - top)
            total = jnp.sum(e, axis=0, keepdims=True)
            mixed = dot(v, e.astype(BF))
            mix[rows, i : i + size] = (mixed / total).astype(BF)
            lse_o[h, :, i : i + size] = top + jnp.log(total)

    during = [steps.pop(0) for _ in range(heads + heads // 2)]

    def two_heads(i, carry):
        def project(n, carry):
            at = pl.ds(pl.multiple_of(n * inner + i * 2 * HEAD, 2 * HEAD), 2 * HEAD)
            w = wq_v[..., at].reshape(h1.shape[1], 2 * HEAD)
            qkv[n] = (dot(h1[...], w) + bias[pl.ds(n * pairs + i, 1)]).T
            return carry

        lax.fori_loop(0, 3, project, 0)
        for n in range(pairs):

            @pl.when(i == n)
            def _():
                step(during[3 * n])

        def one(side, carry):
            head(2 * i + side, side)
            for n in range(heads):

                @pl.when(2 * i + side == n)
                def _():
                    step(during[3 * (n // 2) + 1 + n % 2])

            return carry

        lax.fori_loop(0, 2, one, 0)
        return carry

    lax.fori_loop(0, pairs, two_heads, 0)
    for n, (a, b) in enumerate(((qs, qs_o), (kr, kr_o), (vb, vb_o), (mix, mix_o))):
        saves.append(pltpu.make_async_copy(a, b, ks.at[3 + n]))
        saves[-1].start()
    for u in units[2 * (groups - 1) : 4 * (groups - 1)]:
        complete(u)
    keep[2].wait()
    saves.append(pltpu.make_async_copy(wo_v, wo_o, ks.at[7]))
    saves[-1].start()
    width = h1.shape[1]
    left_other, left_self = mix[:, own_count:].T, mix[:, :own_count].T

    def out_other(i, carry):
        at = tile(i, 256)
        give[:, at] = dot(left_other, wo_v[..., at].reshape(inner, 256)).astype(BF)
        return carry

    def out_self(i, carry):
        at = tile(i, 256)
        own_f[:, at] = dot(left_self, wo_v[..., at].reshape(inner, 256))
        return carry

    lax.fori_loop(0, width // 256, out_other, 0)
    swap = remote(give, take, es.at[2], er.at[2], cn)
    swap.start()
    lax.fori_loop(0, width // 256, out_self, 0)
    step(steps.pop(0))
    swap.wait()

    def second_norm(i, carry):
        per = own_count // clips // 128
        at = tile(i, 128)
        v = x_v[lax.div(i, per), tile(lax.rem(i, per), 128)].astype(F32)
        v = v + (own_f[at] + take[at].astype(F32)) + gain[2:3]
        own_f[at] = v
        v = v - jnp.mean(v, axis=1, keepdims=True)
        v = v * lax.rsqrt(jnp.mean(v * v, axis=1, keepdims=True) + EPS)
        h2[at] = (v * gain[3:4] + gain[4:5]).astype(BF)
        return carry

    lax.fori_loop(0, own_count // 128, second_norm, 0)
    swap = remote(h2.at[:own_count], h2.at[own_count:], es.at[0], er.at[0], cn)
    swap.start()
    saves.append(pltpu.make_async_copy(own_f, x2_o, ks.at[8]))
    saves[-1].start()
    step(steps.pop(0))
    swap.wait()
    saves.append(pltpu.make_async_copy(h2, h2_o, ks.at[9]))
    saves[-1].start()
    while steps:
        step(steps.pop(0))
    arrive_dy()
    swap_dy = remote(dy_o.at[:clips], dy_o.at[clips:], es.at[3], er.at[3], cn)
    swap_dy.start()
    for u in units[4 * (groups - 1) :]:
        complete(u)
    for u in units:
        settle(u)
    for s in smalls:
        s.wait_send()
    for k in keep[3:] + saves:
        k.wait()
    swap_dy.wait()
    sent_dy()
    sent_tab()
    sent_x()


def half_shape(raw, blocks):
    return raw.shape[1:] if blocks == 0 else raw.shape[:3] + (raw.shape[3] // 2,)


def forward(raw, blocks, small, x, tab, dy, groups):
    count, clips = len(raw), x.shape[0]
    own, width = clips * x.shape[1], x.shape[2]
    halves = [half_shape(r, b) for r, b in zip(raw, blocks)]
    inner = halves[0][-1] // 3
    dma = pltpu.SemaphoreType.DMA
    of = jax.ShapeDtypeStruct
    feature = (inner, 2 * own)
    shapes = [of((groups,) + h, BF) for h in halves]
    shapes += [of((8, width), F32), of((1, halves[2][-1]), F32)]
    shapes += [of(x.shape, BF), of((HEAD, 2 * own), F32)]
    shapes += [of((2 * clips,) + x.shape[1:], BF), of((2 * own, width), BF)] + [of(feature, BF)] * 4
    shapes += [of((inner // HEAD, 1, 2 * own), F32), of((own, width), F32), of((2 * own, width), BF)]
    vm = pltpu.VMEM
    scratch = [vm(h, BF) for h in halves]
    scratch += [vm((groups,) + halves[0], BF), vm((groups,) + small.shape, F32), vm(x.shape, BF)]
    scratch += [vm(tab.shape, F32)] * 2 + [vm((2 * own, width), BF)] + [vm(feature, BF)] * 4
    scratch += [vm((3, 2 * HEAD, 2 * own), F32)]
    scratch += [vm((3 * groups + -3 * groups % 8, width // groups // 2), F32)]
    scratch += [vm((groups,) + halves[1], BF), vm((own, width), F32)]
    scratch += [vm((own, width), BF)] * 2 + [vm((2 * own, width), BF)]
    return pl.pallas_call(
        functools.partial(forward_body, groups, clips, blocks),
        out_shape=shapes,
        in_specs=[ANY] * count + [VM, ANY, ANY, ANY],
        out_specs=[ANY] * count + [VM, VM, ANY, VM] + [ANY] * 6 + [VM, ANY, ANY],
        scratch_shapes=scratch
        + [dma((count, 2, groups))] * 6
        + [dma((count, 2, groups, 2))] * 2
        + [dma((count,)), dma((count + 1,)), dma((groups,)), dma((groups,))]
        + [dma((1, clips))] * 6
        + [dma((4,)), dma((4,)), dma((10,))],
        compiler_params=pltpu.CompilerParams(
            collective_id=0, has_side_effects=True, vmem_limit_bytes=60 * 1024 * 1024
        ),
        name="forward",
    )(*raw, small, x, tab, dy)


def backward_body(groups, clips, blocks, *refs):
    count = len(blocks)
    (gw2, act, slope, w2, w1, wo, wq, mix, qs, kr, vb, h1, h2, x2, x, dy, dy_all) = refs[:17]
    lse, tab, gain = refs[17:20]
    cosine, sine = tab.at[: HEAD // 2], tab.at[HEAD // 2 :]
    g1, g2, bd = (gain.at[n : n + 1] for n in (0, 3, 5))
    outs = refs[20 : 20 + count]
    gw1, small_o, gx_o, y_o = refs[20 + count : 24 + count]
    (gu_b, w1_b, wo_b, mix_b, qs_b, kr_b, vb_b, h1_b, x2_b, x_b, dy_b) = refs[24 + count : 35 + count]
    (own_f, give, take, y_take, dx2, low, da, gwo, gwq, ak, av, dq2, dk2, acc, gx) = refs[
        35 + count : 50 + count
    ]
    (sl, gbu, stage_b) = refs[50 + count : 53 + count]
    ld, es, er, sls = refs[53 + count : 57 + count]
    grads = (gwq, gwo, gw1, gw2)
    scratch = refs[57 + count :]
    own_a, own_b, one_a, one_b, two_a, two_b, three, full = (
        scratch[i * count : (i + 1) * count] for i in range(8)
    )
    small_s, small_r, small_z = scratch[8 * count : 8 * count + 3]
    (os, s1, r1, s2, r2, s3, r3, s4, r4, s5, r5, cs, cr, ls, ss, sr, ts, tr, us, ur) = scratch[
        8 * count + 3 :
    ]
    own, width = own_f.shape
    inner = mix_b.shape[0]
    third_width = wq.shape[1]

    upper, lower = w1_b.at[:, :width], w1_b.at[:, width:]
    pairs = ((w2.at[:width], upper), (w2.at[width:], lower), (dy_all, low), (h2, h1_b))
    pairs += ((x2, x2_b), (dy.at[:clips], dy_b), (mix, mix_b), (wo, wo_b))
    pairs += ((qs, qs_b), (kr, kr_b), (vb, vb_b), (x, x_b))
    pairs += ((w1, w1_b), (h1, h1_b), (act, gu_b), (w2.at[:width], upper), (w2.at[width:], lower))
    pairs += ((wq, w1_b.at[:, :third_width]),)
    loads = [pltpu.make_async_copy(a, b, ld.at[n]) for n, (a, b) in enumerate(pairs)]
    first_tile = pltpu.make_async_copy(slope.at[:, :256], sl.at[0], sls.at[0])
    first_tile.start()
    for copy in loads[:12]:
        copy.start()
    p, c, z = where_am_i()
    hi, lo = lax.div(p, 2), lax.rem(p, 2)
    enter(p, c, z, groups)
    col = [(p, c, lax.rem(z + k, groups)) for k in range(groups)]
    xn, yn, cn = (p ^ 1, c, z), (p ^ 2, c, z), (p, c ^ 1, z)
    order = (3, 2, 1, 0)
    units = [(w, j) for w in order for j in [*range(1, groups), 0]]
    sides = ((own_a, one_a, two_a, hi, yn), (own_b, one_b, two_b, lo, xn))

    def c1(u, n):
        w, j = u
        g = grads[w].at[lax.rem(z + j, groups)]
        src, target = (g.at[:, 1 - lo, 0], xn) if n == 0 else (g.at[1 - hi, :, 1], yn)
        return remote(src, sides[n][1][w].at[j], s1.at[w, j, n], r1.at[w, j, n], target)

    def load(u, n):
        w, j = u
        g = grads[w].at[lax.rem(z + j, groups)]
        src = g.at[:, lo, 0] if n == 0 else g.at[hi, :, 1]
        return pltpu.make_async_copy(src, sides[n][0][w].at[j], os.at[w, j, n])

    def c2(u, n):
        w, j = u
        own, one, two, side, target = sides[n]
        return remote(own[w].at[j, 1 - side], two[w].at[j], s2.at[w, j, n], r2.at[w, j, n], target)

    def c3(u, n):
        w, j = u
        src = sides[n][0][w].at[j, sides[n][3]]
        return remote(src, three[w].at[j, n], s3.at[w, j, n], r3.at[w, j, n], col[j])

    def c4(w, n):
        f = full[w].at[p]
        return remote(f, f, s4.at[w, n], r4.at[w, n], (xn, yn)[n])

    def c5(w, n):
        f = full[w].at[(p ^ 1, p ^ 2)[n], n]
        return remote(f, f, s5.at[w, n], r5.at[w, n], (yn, xn)[n])

    def stage_zero(u):
        for n in range(2):
            c1(u, n).start()
            load(u, n).start()

    def stage_one(u):
        w, j = u
        for n, (own, one, two, side, target) in enumerate(sides):
            load(u, n).wait()
            c1(u, n).wait_recv()
            own[w][j] = (own[w][j].astype(F32) + one[w][j].astype(F32)).astype(BF)
            c2(u, n).start()

    def stage_two(u):
        w, j = u
        for n, (own, one, two, side, target) in enumerate(sides):
            c2(u, n).wait_recv()
            own[w][j, side] = (own[w][j, side].astype(F32) + two[w][j].astype(F32)).astype(BF)
            if j:
                c3(u, n).start()

    def stage_three(w):
        for n, (own, one, two, side, target) in enumerate(sides):
            total = own[w][0, side].astype(F32)
            for j in range(1, groups):
                c3((w, j), n).wait_recv()
                total = total + three[w][j, n].astype(F32)
            full[w][p, n] = total.astype(BF)
        for n in range(2):
            c4(w, n).start()

    def stage_four(w):
        for n, target in enumerate((yn, xn)):
            f = full[w].at[(p ^ 1, p ^ 2)[n]]
            remote(f, f, s4.at[w, n], r4.at[w, n], target).wait_recv()
            c5(w, n).start()

    def stage_five(w):
        for n in range(2):
            f = full[w].at[p ^ 3, n]
            remote(f, f, s5.at[w, n], r5.at[w, n], xn).wait_recv()
        for dst, src in cuts(outs[w], full[w], c, blocks[w]):
            pltpu.make_async_copy(src, dst, ls.at[w]).start()
            remote(src, dst, cs.at[w], cr.at[w], cn).start()

    ahead, lag = 3, 3
    todo = {}
    for n, u in enumerate(units):
        todo.setdefault(max(n - ahead, -1), []).append((stage_zero, u))
        todo.setdefault(n, []).append((stage_one, u))
        todo.setdefault(n + lag, []).append((stage_two, u))
    for i, w in enumerate(order):
        last = (i + 1) * groups - 1 + lag
        for at, stage in ((2, stage_three), (3, stage_four), (4, stage_five)):
            todo.setdefault(last + at, []).append((stage, w))
    steps = sorted(todo)

    def run(step):
        for stage, what in todo[step]:
            stage(what)

    def tick(times=1):
        for _ in range(times):
            run(steps.pop(0))

    def half_sum(n, left, right, depth):
        def other(i, carry):
            part = dot_t(left[own:, :depth], right[tile(i, 256), :depth])
            give[:, tile(i, 256)] = part.astype(BF)
            return carry

        def self(i, carry):
            own_f[:, tile(i, 256)] = dot_t(left[:own, :depth], right[tile(i, 256), :depth])
            return carry

        lax.fori_loop(0, width // 256, other, 0)
        copy = remote(give, take, es.at[n], er.at[n], cn)
        copy.start()
        lax.fori_loop(0, width // 256, self, 0)
        return copy

    def part(i):
        per = own // clips // 128
        return lax.div(i, per), tile(lax.rem(i, per), 128)

    def norm_step(i, field, gain, grad, row):
        at = tile(i, 128)
        d = own_f[at] + take[at].astype(F32)
        v = field[at].astype(F32)
        v = v - jnp.mean(v, axis=1, keepdims=True)
        r = lax.rsqrt(jnp.mean(v * v, axis=1, keepdims=True) + EPS)
        v = v * r
        acc[row : row + 1] += jnp.sum(d * v, axis=0, keepdims=True)
        acc[row + 1 : row + 2] += jnp.sum(d, axis=0, keepdims=True)
        e = d * gain[...]
        mean = jnp.mean(e, axis=1, keepdims=True)
        e = e - mean - v * jnp.mean(e * v, axis=1, keepdims=True)
        return grad + r * e

    tick()
    acc[...] = jnp.zeros_like(acc)
    for copy in loads[:3]:
        copy.wait()
    deep = slope.shape[1]
    sides_of = deep // width

    def hidden_grad(side, i):
        n = side * (width // 256) + i
        slot = lax.rem(n, 2)
        pltpu.make_async_copy(slope.at[:, :256], sl.at[slot], sls.at[slot]).wait()

        @pl.when(n + 1 < deep // 256)
        def _():
            src = slope.at[:, tile(n + 1, 256)]
            pltpu.make_async_copy(src, sl.at[1 - slot], sls.at[1 - slot]).start()

        right = w1_b[tile(i, 256), side * width : (side + 1) * width]
        line = jnp.zeros((1, 256), F32)
        for r in range(2):
            rows = slice(r * own, (r + 1) * own)
            g = dot_t(low[rows], right) * sl[slot, rows].astype(F32)
            g = g.astype(BF)
            gu_b[rows, tile(n, 256)] = g
            line = line + jnp.sum(g.astype(F32), axis=0, keepdims=True)
        gbu[:, tile(n, 256)] = line

    for side in range(sides_of):

        def columns(i, carry):
            hidden_grad(side, i)
            return carry

        lax.fori_loop(0, width // 256, columns, 0)
        if side == 0:
            tick()
    loads[12].start()
    loads[3].wait()
    row = width // groups

    def up_grad(j, carry):
        k = lax.rem(z + j, groups)
        left = h1_b[:, tile(k, row)].T

        def columns(i, carry):
            at = tile(i, 512)
            stage_b[..., at] = dot(left, gu_b[:, at]).astype(BF).reshape(stage_b.shape[:-1] + (512,))
            return carry

        lax.fori_loop(0, deep // 512, columns, 0)
        copy = pltpu.make_async_copy(stage_b, gw1.at[k], ld.at[18])
        copy.start()
        copy.wait()
        return carry

    lax.fori_loop(1, 3, up_grad, 0)
    tick()
    lax.fori_loop(3, groups + 1, up_grad, 0)
    loads[13].start()
    tick()
    loads[12].wait()
    swap = half_sum(0, gu_b, w1_b, deep)
    for copy in loads[14:17]:
        copy.start()
    tick()
    for copy in loads[4:12]:
        copy.wait()
    swap.wait()

    def second_norm(i, carry):
        at = tile(i, 128)
        g = dy_b[part(i)].astype(F32)
        d = norm_step(i, x2_b, g2, g, 3)
        dx2[at] = d
        acc[5:6] += jnp.sum(g, axis=0, keepdims=True)
        low[at] = d.astype(BF)
        acc[2:3] += jnp.sum(d.astype(BF).astype(F32), axis=0, keepdims=True)
        return carry

    lax.fori_loop(0, own // 128, second_norm, 0)
    swap = remote(low.at[:own], low.at[own:], es.at[1], er.at[1], cn)
    swap.start()
    tick()
    swap.wait()

    def out_grad(i, carry):
        at = tile(i, 256)
        gwo[..., at] = dot(mix_b[...], low[:, at]).astype(BF).reshape(gwo.shape[:-1] + (256,))
        return carry

    lax.fori_loop(0, width // 256, out_grad, 0)

    def attn_grad(i, carry):
        at = tile(i, 256)
        da[:, at] = dot_t(wo_b[...], low[at]).astype(BF)
        return carry

    lax.fori_loop(0, 2 * own // 256, attn_grad, 0)
    tick()

    for copy in loads[14:17]:
        copy.wait()

    def down(rows, i):
        left = dot(gu_b[rows, :width], w1_b[:, tile(i, 256)])
        at = pl.ds(pl.multiple_of(width + i * 256, 256), 256)
        return left + dot(gu_b[rows, width:], w1_b[:, at])

    def down_other(i, carry):
        give[:, tile(i, 256)] = down(slice(own, 2 * own), i).astype(BF)
        return carry

    def down_self(i, carry):
        own_f[:, tile(i, 256)] = down(slice(0, own), i)
        return carry

    lax.fori_loop(0, width // 256, down_other, 0)
    y_copy = remote(give, y_take, es.at[3], er.at[3], cn)
    y_copy.start()
    lax.fori_loop(0, width // 256, down_self, 0)
    loads[17].start()
    y_copy.wait()

    def last_add(i, carry):
        at = tile(i, 128)
        gx[part(i)] = (x2_b[at] + own_f[at] + bd[...] + y_take[at].astype(F32)).astype(BF)
        return carry

    lax.fori_loop(0, own // 128, last_add, 0)
    y_start, y_finish, *_ = move_tokens((gx,), (y_o,), us, ur, p, c, z, clips)
    y_start(0, 4)
    dqkv = gu_b.at[:, :third_width]

    def head(h, side):
        rows = tile(h, HEAD)
        place = tile(side, HEAD)
        co, si = cosine[...], sine[...]
        kt = kr_b[rows]
        keys, values = kt.T, vb_b[rows].T
        queries, outer_grads = qs_b[rows].T, da[rows].T
        step = 256
        for i in range(0, 2 * own, step):
            s = slice(i, i + step)
            g = da[rows, s]
            p = jnp.exp(dot(keys, qs_b[rows, s]) - lse[h, :, s])
            delta = jnp.sum(mix_b[rows, s].astype(F32) * g.astype(F32), axis=0, keepdims=True)
            ds = (p * (dot(values, g) - delta)).astype(BF)
            dq2[place, s] = turn(dot(kt, ds) * SCALE, co[:, s], -si[:, s]).astype(BF)
            dv = dot(p.astype(BF), outer_grads[s])
            dk = dot(ds, queries[s])
            if i == 0:
                ak[...] = dk
                av[side] = dv
            else:
                ak[...] += dk
                av[side] += dv
        dk2[place] = turn(ak[...].T, co, -si).astype(BF)

    heads = inner // HEAD
    during = [steps.pop(0) for _ in range(3)]

    def two_heads(i, carry):
        lax.fori_loop(0, 2, lambda side, _: head(2 * i + side, side), None)
        for n, value in enumerate(
            (dq2[...].T, dk2[...].T, jnp.concatenate([av[0], av[1]], axis=1).astype(BF))
        ):
            at = pl.ds(pl.multiple_of(n * inner + i * 2 * HEAD, 2 * HEAD), 2 * HEAD)
            dqkv[:, at] = value
        for n, step in enumerate(during):
            pl.when(i == n * heads // 8)(functools.partial(run, step))
            pl.when(i == n * heads // 8)(functools.partial(y_start, n + 1, 4))
        return carry

    lax.fori_loop(0, heads // 2, two_heads, 0)
    loads[13].wait()
    for g in range(groups):
        left = h1_b[:, g * row : (g + 1) * row].T

        def in_grad(i, carry):
            at = tile(i, 512)
            gwq[g, ..., at] = dot(left, dqkv[:, at]).astype(BF).reshape(gwq.shape[1:-1] + (512,))
            return carry

        lax.fori_loop(0, third_width // 512, in_grad, 0)
    tick()
    loads[17].wait()
    swap = half_sum(2, dqkv, w1_b, third_width)
    tick()
    swap.wait()
    y_finish()

    def first_norm(i, carry):
        gx[part(i)] = norm_step(i, x_b, g1, dx2[tile(i, 128)], 0).astype(BF)
        return carry

    lax.fori_loop(0, own // 128, first_norm, 0)
    start, finish, *_ = move_tokens((gx,), (gx_o,), ts, tr, p, c, z, clips)
    start(0, 4)
    tick()
    small_s[...] = jnp.zeros_like(small_s)
    for n in range(6):
        for g in range(groups):
            small_s[g, n : n + 1] = acc[n : n + 1, g * row : (g + 1) * row]
    half = row // 2
    mine_at = pl.ds(pl.multiple_of(c * half, half), half)
    for b in range(3 * groups):
        line = jnp.sum(dqkv[:, b * half : (b + 1) * half].astype(F32), axis=0, keepdims=True)
        small_s[b // 3, 6 + b % 3 : 7 + b % 3, mine_at] = line
    share = deep // groups
    for g in range(groups):
        for n in range(share // row):
            at = pl.ds(9 + c * (share // row) + n, 1)
            small_s[g, at] = gbu[:, g * share + n * row : g * share + (n + 1) * row]
    tick()
    for n, target in enumerate((cn, xn, yn)):
        copy = remote(small_s, small_r.at[n], ss.at[n], sr.at[n], target)
        copy.start()
        start(n + 1, 4)
        tick(1 if n == 0 else 3)
        copy.wait()
        small_s[...] += small_r[n]
    tails = [
        remote(small_s.at[col[k][2]], small_z.at[k], ss.at[2 + k], sr.at[2 + k], col[k])
        for k in range(1, groups)
    ]
    for t in tails:
        t.start()
    while steps:
        tick()
    for k in range(1, groups):
        tails[k - 1].wait()
    small_o[...] = small_s[z]
    for k in range(1, groups):
        small_o[...] += small_z[k]
    for u in units:
        w, j = u
        for n in range(2):
            c1(u, n).wait_send()
            c2(u, n).wait_send()
            if j:
                c3(u, n).wait_send()
    for w in range(count):
        for n in range(2):
            c4(w, n).wait_send()
            c5(w, n).wait_send()
        pltpu.make_async_copy(full[w], full[w], ls.at[w]).wait()
        remote(full[w], full[w], cs.at[w], cr.at[w], cn).wait()
    finish()


def backward(gw2, arrays, tables, lines, groups, blocks):
    act, slope, w2, w1, wo, wq, mix, qs, kr, vb, h1, h2, x2, x, dy, dy_all = arrays
    (own, width), clips = x.shape, dy.shape[0] // 2
    moved = jax.ShapeDtypeStruct((clips,) + dy.shape[1:], BF)
    small = jax.ShapeDtypeStruct((groups, lines + -lines % 8, width // groups), F32)
    count = len(blocks)
    dma = pltpu.SemaphoreType.DMA
    split = lambda v: (groups, 2, 2, 2, v.shape[0] // (8 * groups), v.shape[1])
    tiles = [split(v)[4:] for v in (wq, wo, w1, w2)]
    shapes = [
        jax.ShapeDtypeStruct((4, 2, t[0], 2 * t[1]) if b else (2, 4, 2) + t, BF)
        for t, b in zip(tiles, blocks)
    ]
    shapes += [
        jax.ShapeDtypeStruct(split(w1), BF),
        jax.ShapeDtypeStruct(small.shape[1:], F32),
        moved,
        moved,
    ]
    scratch = [pltpu.VMEM(v.shape, v.dtype) for v in (act, w1, wo, mix, qs, kr, vb, h1, x2, x, moved)]
    half, low = (own, width), pltpu.VMEM((2 * own, width), BF)
    scratch += [pltpu.VMEM(half, F32)] + [pltpu.VMEM(half, BF)] * 3
    scratch += [pltpu.VMEM(half, F32), low, pltpu.VMEM(mix.shape, BF)]
    scratch += [pltpu.VMEM(split(wo), BF), pltpu.VMEM(split(wq), BF)]
    scratch += [pltpu.VMEM((2 * own, HEAD), F32), pltpu.VMEM((2, 2 * own, HEAD), F32)]
    scratch += [pltpu.VMEM((2 * HEAD, 2 * own), BF)] * 2
    scratch += [pltpu.VMEM((8, width), F32), pltpu.VMEM(moved.shape, BF)]
    scratch += [pltpu.VMEM((2, 2 * own, 256), BF), pltpu.VMEM((1, act.shape[1]), F32)]
    scratch += [pltpu.VMEM(split(w1)[1:], BF)]
    scratch += [dma((19,)), dma((4,)), dma((4,)), dma((2,))]
    for lead in (
        (groups, 2),
        (groups, 2),
        (groups, 2),
        (groups, 2),
        (groups,),
        (groups,),
        (groups, 2),
        (4, 2),
    ):
        scratch += [pltpu.VMEM(lead + t, BF) for t in tiles]
    scratch += [
        pltpu.VMEM(small.shape, F32),
        pltpu.VMEM((3,) + small.shape, F32),
        pltpu.VMEM(small.shape, F32),
    ]
    pair = dma((count, groups, 2))
    scratch += [pair] * 7 + [dma((count, 2))] * 4
    scratch += [dma((count,))] * 3 + [dma((2 + groups,))] * 2 + [dma((1, clips))] * 4
    return pl.pallas_call(
        functools.partial(backward_body, groups, clips, blocks),
        out_shape=shapes,
        in_specs=[ANY] * (1 + len(arrays)) + [VM] * len(tables),
        out_specs=[ANY] * (count + 1) + [VM, ANY, ANY],
        scratch_shapes=scratch,
        compiler_params=pltpu.CompilerParams(
            collective_id=1, has_side_effects=True, vmem_limit_bytes=67043328
        ),
        name="backward",
    )(gw2, *arrays, *tables)


def contract(left, right, a, b):
    return lax.dot_general(left, right, (((a,), (b,)), ((), ())), preferred_element_type=F32)


def paired(
    tokens,
    positions,
    ln1_gain,
    ln1_bias,
    w_qkv,
    b_qkv,
    w_out,
    b_out,
    ln2_gain,
    ln2_bias,
    w_up,
    b_up,
    w_down,
    b_down,
    cotangent,
):
    groups = lax.axis_size("grp")
    clips, part, width = tokens.shape
    hidden = w_down.shape[0] * groups
    own = clips * part
    length = 2 * own
    c, z = lax.axis_index("core"), lax.axis_index("grp")
    wide = width // 2
    deep = hidden // 2
    row = width // groups

    def pick(value, axis):
        return lax.dynamic_index_in_dim(value, c, axis, keepdims=False)

    blocks = (3 * groups, 0, groups, 0)
    raw = [
        w.reshape(((4, 2) if b else (2, 4, 2)) + (w.shape[0] // (8 if b else 16), w.shape[1]))
        for w, b in zip((w_qkv, w_out, w_up, w_down), blocks)
    ]
    bq, bu = b_qkv.shape[0] // row, b_up.shape[0] // row
    vectors = [ln1_gain, ln1_bias, b_out, ln2_gain, ln2_bias, b_down]
    vectors += [b_qkv, b_up]
    lines = len(vectors) - 2 + bq + bu
    size, start = (lines + -lines % 8) * row, 0
    small = jnp.zeros((size,), F32)
    for v in vectors:
        small = small + jnp.pad(v.astype(F32), (start, size - start - v.shape[0]))
        start += v.shape[0]
    small = small.reshape(-1, row)
    pair = jnp.arange(HEAD // 2)
    band = (pair >= 10).astype(jnp.int32) + (pair >= 21).astype(jnp.int32)
    begin = jnp.where(band == 0, 0, jnp.where(band == 1, 10, 21))
    number = jnp.where(band == 0, 10, 11)
    freq = jnp.power(F32(10000.0), -(pair - begin).astype(F32) / number.astype(F32))
    pos = positions.astype(F32)[:, :, None, :]
    band = band[None, :, None]
    chosen = jnp.where(band == 0, pos[0], jnp.where(band == 1, pos[1], pos[2]))
    angles = chosen * freq[None, :, None]
    tab = jnp.concatenate([jnp.cos(angles), jnp.sin(angles)], axis=1)
    wq, wo, w1, w2, gain, bu_own, x, tab, dy, h1, qs, kr, vb, mixed, lse, x2, h2 = forward(
        raw, blocks, small, tokens, tab, cotangent, groups
    )
    wq = wq.reshape(width, 3 * wide)
    wo = wo.reshape(wide, width)
    w1 = w1.reshape(width, deep)
    w2 = w2.reshape(deep, width)
    grad_all = dy.reshape(length, width)
    tokens = x.reshape(own, width)
    u = contract(h2, w1, 1, 0) + bu_own
    cdf = 0.5 * (1.0 + lax.erf(u * F32(0.7071067811865476)))
    act = (u * cdf).astype(BF)
    slope = (cdf + u * jnp.exp(-0.5 * u * u) * F32(0.3989422804014327)).astype(BF)

    gw2 = contract(act, grad_all, 0, 0).astype(BF)
    gw2 = gw2.reshape(groups, 2, 2, 2, gw2.shape[0] // (8 * groups), width)
    arrays = (act, slope, w2, w1, wo, wq, mixed, qs, kr, vb, h1, h2, x2, tokens, dy, grad_all)
    tables = (lse, tab, gain)
    gwq, gwo, gw1, gw2, _, sums, gx, output = backward(gw2, arrays, tables, lines, groups, blocks)
    gwq, gwo, gw1, gw2 = (
        g.reshape(shard.shape).astype(F32)
        for g, shard in zip((gwq, gwo, gw1, gw2), (w_qkv, w_out, w_up, w_down))
    )
    gg1, gb1, gbo, gg2, gb2, gbd = (sums[n] for n in range(6))
    gbq, gbu = sums[6 : 6 + bq].reshape(-1), sums[6 + bq : lines].reshape(-1)
    return (output, gx, gg1, gb1, gwq, gbq, gwo, gbo, gg2, gb2, gw1, gbu, gw2, gbd)


def paired_specs():
    rep = ("rp", "core")
    ins = (P(rep, "grp", None), P(None, rep, "grp"))
    one, two = P("grp"), P("grp", None)
    ins += (one, one, two, one, two, one, one, one, two, one, two, one, P(rep, "grp", None))
    outs = (P(rep, "grp", None),) * 2
    outs += (one, one, two, one, two, one, one, one, two, one, two, one)
    return ins, outs


def rotary_angles(positions):
    pair = jnp.arange(32)
    band = (pair >= 10).astype(jnp.int32) + (pair >= 21).astype(jnp.int32)
    start = jnp.where(band == 0, 0, jnp.where(band == 1, 10, 21))
    count = jnp.where(band == 0, 10, 11)
    freq = jnp.power(
        jnp.float32(10000.0), -(pair - start).astype(jnp.float32) / count.astype(jnp.float32)
    )
    pos_f = positions.astype(jnp.float32)
    chosen = jnp.where(
        band[None, :] == 0,
        pos_f[0][:, None],
        jnp.where(band[None, :] == 1, pos_f[1][:, None], pos_f[2][:, None]),
    )
    return chosen * freq[None, :]


def rotate(field, cosine, sine):
    first = field[..., :32]
    second = field[..., 32:]
    return jnp.concatenate(
        [first * cosine - second * sine, first * sine + second * cosine], axis=-1
    )


def normalize(field):
    centred = field - jnp.mean(field, axis=-1, keepdims=True)
    variance = jnp.mean(centred * centred, axis=-1, keepdims=True)
    factor = lax.rsqrt(variance + EPS)
    return (centred * factor, factor)


def norm_back(grad_norm, normed, factor):
    return factor * (
        grad_norm
        - jnp.mean(grad_norm, axis=-1, keepdims=True)
        - normed * jnp.mean(grad_norm * normed, axis=-1, keepdims=True)
    )


def outer(left, right):
    return lax.dot_general(
        left, right, (((0,), (0,)), ((), ())), preferred_element_type=jnp.float32
    )


def back(left, right):
    return lax.dot_general(
        left, right, (((1,), (1,)), ((), ())), preferred_element_type=jnp.float32
    )


def exact_gelu(value):
    return jax.nn.gelu(value, approximate=False)


def column_sum(value):
    return jnp.sum(value.astype(jnp.float32), axis=0)


def forward_pass(params, field_in, positions):
    g1, b1, wqkv, bqkv, wo, bo, g2, b2, w1, bu, w2, bd = params
    field = field_in.astype(jnp.float32)
    count, width = field.shape
    heads = width // 64
    angles = rotary_angles(positions)
    cosine = jnp.cos(angles)[:, None, :]
    sine = jnp.sin(angles)[:, None, :]
    normed1, factor1 = normalize(field)
    h1 = (normed1 * g1.astype(jnp.float32) + b1.astype(jnp.float32)).astype(jnp.bfloat16)
    qkv = jnp.dot(h1, wqkv, preferred_element_type=jnp.float32) + bqkv.astype(jnp.float32)
    query_rot = rotate(qkv[:, :width].reshape(count, heads, 64), cosine, sine).astype(jnp.bfloat16)
    keys_rot = (
        rotate(qkv[:, width : 2 * width].reshape(count, heads, 64), cosine, sine)
        .astype(jnp.bfloat16)
        .reshape(count, width)
    )
    values = qkv[:, 2 * width :].astype(jnp.bfloat16)
    keys_all, values_all = (
        lax.all_gather(keys_rot, "grp", axis=0, tiled=True),
        lax.all_gather(values, "grp", axis=0, tiled=True),
    )
    total = keys_all.shape[0]
    keys_all = keys_all.reshape(total, heads, 64)
    values_all = values_all.reshape(total, heads, 64)
    scores = (
        jnp.einsum("thd,shd->hts", query_rot, keys_all, preferred_element_type=jnp.float32) * SCALE
    )
    top = jnp.max(scores, axis=-1, keepdims=True)
    lse = top + jnp.log(jnp.sum(jnp.exp(scores - top), axis=-1, keepdims=True))
    probs = jnp.exp(scores - lse).astype(jnp.bfloat16)
    mixed = (
        jnp.einsum("hts,shd->thd", probs, values_all, preferred_element_type=jnp.float32)
        .reshape(count, width)
        .astype(jnp.bfloat16)
    )
    second = field + jnp.dot(mixed, wo, preferred_element_type=jnp.float32) + bo.astype(jnp.float32)
    normed2, factor2 = normalize(second)
    h2 = (normed2 * g2.astype(jnp.float32) + b2.astype(jnp.float32)).astype(jnp.bfloat16)
    hidden = jnp.dot(h2, w1, preferred_element_type=jnp.float32) + bu.astype(jnp.float32)
    active = exact_gelu(hidden).astype(jnp.bfloat16)
    result = (
        second + jnp.dot(active, w2, preferred_element_type=jnp.float32) + bd.astype(jnp.float32)
    )
    saved = (
        normed1,
        factor1,
        h1,
        query_rot,
        keys_rot,
        values,
        lse,
        mixed,
        normed2,
        factor2,
        h2,
        hidden,
        active,
        cosine,
        sine,
    )
    return (saved, result.astype(jnp.bfloat16))


def backward_pass(params, saved, grad_in, totals):
    g1, b1, wqkv, bqkv, wo, bo, g2, b2, w1, bu, w2, bd = params
    (
        normed1,
        factor1,
        h1,
        query_rot,
        keys_rot,
        values,
        lse,
        mixed,
        normed2,
        factor2,
        h2,
        hidden,
        active,
        cosine,
        sine,
    ) = saved
    grad_out = grad_in.astype(jnp.float32)
    count, width = grad_out.shape
    heads = width // 64
    grad_y2 = grad_out.astype(jnp.bfloat16)
    grad_w2 = outer(active, grad_y2)
    grad_bd = column_sum(grad_y2)
    grad_act = back(grad_y2, w2)
    unused, pull = jax.vjp(exact_gelu, hidden)
    grad_hidden = pull(grad_act)[0].astype(jnp.bfloat16)
    grad_w1 = outer(h2, grad_hidden)
    grad_bu = column_sum(grad_hidden)
    grad_h2 = back(grad_hidden, w1)
    grad_g2 = jnp.sum(grad_h2 * normed2, axis=0)
    grad_b2 = jnp.sum(grad_h2, axis=0)
    grad_second = grad_out + norm_back(grad_h2 * g2.astype(jnp.float32), normed2, factor2)
    grad_y1 = grad_second.astype(jnp.bfloat16)
    grad_wo = outer(mixed, grad_y1)
    grad_bo = column_sum(grad_y1)
    grad_mixed = back(grad_y1, wo).astype(jnp.bfloat16).reshape(count, heads, 64)
    keys_all, values_all = (
        lax.all_gather(keys_rot, "grp", axis=0, tiled=True),
        lax.all_gather(values, "grp", axis=0, tiled=True),
    )
    total = keys_all.shape[0]
    keys_all = keys_all.reshape(total, heads, 64)
    values_all = values_all.reshape(total, heads, 64)
    scores = (
        jnp.einsum("thd,shd->hts", query_rot, keys_all, preferred_element_type=jnp.float32) * SCALE
    )
    probs = jnp.exp(scores - lse)
    grad_probs = jnp.einsum(
        "thd,shd->hts", grad_mixed, values_all, preferred_element_type=jnp.float32
    )
    delta = jnp.sum(probs * grad_probs, axis=-1, keepdims=True)
    grad_scores = (probs * (grad_probs - delta)).astype(jnp.bfloat16)
    grad_query = (
        jnp.einsum("hts,shd->thd", grad_scores, keys_all, preferred_element_type=jnp.float32)
        * SCALE
    )
    probs_low = probs.astype(jnp.bfloat16)
    grad_values = jnp.einsum(
        "hts,thd->shd", probs_low, grad_mixed, preferred_element_type=jnp.float32
    )
    grad_keys = (
        jnp.einsum("hts,thd->shd", grad_scores, query_rot, preferred_element_type=jnp.float32)
        * SCALE
    )
    keys_own, values_own = (
        lax.psum_scatter(
            grad_keys.reshape(total, width).astype(jnp.bfloat16),
            "grp",
            scatter_dimension=0,
            tiled=True,
        ).astype(jnp.float32),
        lax.psum_scatter(
            grad_values.reshape(total, width).astype(jnp.bfloat16),
            "grp",
            scatter_dimension=0,
            tiled=True,
        ).astype(jnp.float32),
    )
    query_back = rotate(grad_query, cosine, -sine).reshape(count, width)
    keys_back = rotate(keys_own.reshape(count, heads, 64), cosine, -sine).reshape(count, width)
    grad_qkv = jnp.concatenate([query_back, keys_back, values_own], axis=1).astype(jnp.bfloat16)
    grad_wqkv = outer(h1, grad_qkv)
    grad_bqkv = column_sum(grad_qkv)
    grad_h1 = back(grad_qkv, wqkv)
    grad_g1 = jnp.sum(grad_h1 * normed1, axis=0)
    grad_b1 = jnp.sum(grad_h1, axis=0)
    grad_field = grad_second + norm_back(grad_h1 * g1.astype(jnp.float32), normed1, factor1)
    terms = (
        grad_g1,
        grad_b1,
        grad_wqkv,
        grad_bqkv,
        grad_wo,
        grad_bo,
        grad_g2,
        grad_b2,
        grad_w1,
        grad_bu,
        grad_w2,
        grad_bd,
    )
    totals = tuple((a + b for a, b in zip(totals, terms)))
    return (grad_field.astype(jnp.bfloat16), totals)


def local(
    tokens,
    positions,
    ln1_gain,
    ln1_bias,
    w_qkv,
    b_qkv,
    w_out,
    b_out,
    ln2_gain,
    ln2_bias,
    w_up,
    b_up,
    w_down,
    b_down,
    cotangent,
):
    shards = (
        ln1_gain,
        ln1_bias,
        w_qkv,
        b_qkv,
        w_out,
        b_out,
        ln2_gain,
        ln2_bias,
        w_up,
        b_up,
        w_down,
        b_down,
    )
    groups = lax.axis_size("grp")
    totals = tuple((jnp.zeros((s.shape[0] * groups,) + s.shape[1:], jnp.float32) for s in shards))
    outputs = []
    gradients = []
    for index in range(tokens.shape[0]):
        forward_params = (
            lax.all_gather(ln1_gain, "grp", axis=0, tiled=True),
            lax.all_gather(ln1_bias, "grp", axis=0, tiled=True),
            lax.all_gather(w_qkv, "grp", axis=0, tiled=True),
            lax.all_gather(b_qkv, "grp", axis=0, tiled=True),
            lax.all_gather(w_out, "grp", axis=0, tiled=True),
            lax.all_gather(b_out, "grp", axis=0, tiled=True),
            lax.all_gather(ln2_gain, "grp", axis=0, tiled=True),
            lax.all_gather(ln2_bias, "grp", axis=0, tiled=True),
            lax.all_gather(w_up, "grp", axis=0, tiled=True),
            lax.all_gather(b_up, "grp", axis=0, tiled=True),
            lax.all_gather(w_down, "grp", axis=0, tiled=True),
            lax.all_gather(b_down, "grp", axis=0, tiled=True),
        )
        saved, result = forward_pass(forward_params, tokens[index], positions[:, index, :])
        outputs.append(result)
        backward_params = (
            lax.all_gather(ln1_gain, "grp", axis=0, tiled=True),
            lax.all_gather(ln1_bias, "grp", axis=0, tiled=True),
            lax.all_gather(w_qkv, "grp", axis=0, tiled=True),
            lax.all_gather(b_qkv, "grp", axis=0, tiled=True),
            lax.all_gather(w_out, "grp", axis=0, tiled=True),
            lax.all_gather(b_out, "grp", axis=0, tiled=True),
            lax.all_gather(ln2_gain, "grp", axis=0, tiled=True),
            lax.all_gather(ln2_bias, "grp", axis=0, tiled=True),
            lax.all_gather(w_up, "grp", axis=0, tiled=True),
            lax.all_gather(b_up, "grp", axis=0, tiled=True),
            lax.all_gather(w_down, "grp", axis=0, tiled=True),
            lax.all_gather(b_down, "grp", axis=0, tiled=True),
        )
        grad_field, totals = backward_pass(backward_params, saved, cotangent[index], totals)
        gradients.append(grad_field)
    owned = (
        lax.psum_scatter(
            totals[0].astype(jnp.bfloat16), "grp", scatter_dimension=0, tiled=True
        ).astype(jnp.float32),
        lax.psum_scatter(
            totals[1].astype(jnp.bfloat16), "grp", scatter_dimension=0, tiled=True
        ).astype(jnp.float32),
        lax.psum_scatter(
            totals[2].astype(jnp.bfloat16), "grp", scatter_dimension=0, tiled=True
        ).astype(jnp.float32),
        lax.psum_scatter(
            totals[3].astype(jnp.bfloat16), "grp", scatter_dimension=0, tiled=True
        ).astype(jnp.float32),
        lax.psum_scatter(
            totals[4].astype(jnp.bfloat16), "grp", scatter_dimension=0, tiled=True
        ).astype(jnp.float32),
        lax.psum_scatter(
            totals[5].astype(jnp.bfloat16), "grp", scatter_dimension=0, tiled=True
        ).astype(jnp.float32),
        lax.psum_scatter(
            totals[6].astype(jnp.bfloat16), "grp", scatter_dimension=0, tiled=True
        ).astype(jnp.float32),
        lax.psum_scatter(
            totals[7].astype(jnp.bfloat16), "grp", scatter_dimension=0, tiled=True
        ).astype(jnp.float32),
        lax.psum_scatter(
            totals[8].astype(jnp.bfloat16), "grp", scatter_dimension=0, tiled=True
        ).astype(jnp.float32),
        lax.psum_scatter(
            totals[9].astype(jnp.bfloat16), "grp", scatter_dimension=0, tiled=True
        ).astype(jnp.float32),
        lax.psum_scatter(
            totals[10].astype(jnp.bfloat16), "grp", scatter_dimension=0, tiled=True
        ).astype(jnp.float32),
        lax.psum_scatter(
            totals[11].astype(jnp.bfloat16), "grp", scatter_dimension=0, tiled=True
        ).astype(jnp.float32),
    )
    summed = (
        lax.psum(owned[0].astype(jnp.bfloat16), "rep").astype(jnp.float32),
        lax.psum(owned[1].astype(jnp.bfloat16), "rep").astype(jnp.float32),
        lax.psum(owned[2].astype(jnp.bfloat16), "rep").astype(jnp.float32),
        lax.psum(owned[3].astype(jnp.bfloat16), "rep").astype(jnp.float32),
        lax.psum(owned[4].astype(jnp.bfloat16), "rep").astype(jnp.float32),
        lax.psum(owned[5].astype(jnp.bfloat16), "rep").astype(jnp.float32),
        lax.psum(owned[6].astype(jnp.bfloat16), "rep").astype(jnp.float32),
        lax.psum(owned[7].astype(jnp.bfloat16), "rep").astype(jnp.float32),
        lax.psum(owned[8].astype(jnp.bfloat16), "rep").astype(jnp.float32),
        lax.psum(owned[9].astype(jnp.bfloat16), "rep").astype(jnp.float32),
        lax.psum(owned[10].astype(jnp.bfloat16), "rep").astype(jnp.float32),
        lax.psum(owned[11].astype(jnp.bfloat16), "rep").astype(jnp.float32),
    )
    output = jnp.stack(outputs, axis=0)
    grad_tokens = jnp.stack(gradients, axis=0)
    return (
        output,
        grad_tokens,
        summed[0],
        summed[1],
        summed[2],
        summed[3],
        summed[4],
        summed[5],
        summed[6],
        summed[7],
        summed[8],
        summed[9],
        summed[10],
        summed[11],
    )


def spread(mesh):
    placed = (
        P("rep", "grp", None),
        P(None, "rep", "grp"),
        P("grp"),
        P("grp"),
        P("grp", None),
        P("grp"),
        P("grp", None),
        P("grp"),
        P("grp"),
        P("grp"),
        P("grp", None),
        P("grp"),
        P("grp", None),
        P("grp"),
        P("rep", "grp", None),
    )
    return jax.shard_map(
        local,
        mesh=mesh,
        in_specs=placed,
        out_specs=(
            P("rep", "grp", None),
            P("rep", "grp", None),
            P("grp"),
            P("grp"),
            P("grp", None),
            P("grp"),
            P("grp", None),
            P("grp"),
            P("grp"),
            P("grp"),
            P("grp", None),
            P("grp"),
            P("grp", None),
            P("grp"),
        ),
        check_vma=False,
    )


def solution(mesh):
    reps, groups = mesh.devices.shape
    flat = mesh.devices.reshape(-1)

    def run(*args):
        clips = args[0].shape[0] // reps
        if reps == 8 and groups == 2 * clips:
            split = Mesh(flat.reshape(reps // 2, 2, groups), ("rp", "core", "grp"))
            ins, outs = paired_specs()
            return jax.shard_map(
                paired, mesh=split, in_specs=ins, out_specs=outs, check_vma=False
            )(*args)
        return spread(mesh)(*args)

    return run
```

```python
import functools

import jax
import jax.numpy as jnp
from jax import lax
from jax.experimental import pallas as pl
from jax.experimental.pallas import tpu as pltpu
from jax.sharding import Mesh
from jax.sharding import PartitionSpec as P

SCALE = 0.125
EPS = 1e-06
HEAD = 64
BF = jnp.bfloat16
F32 = jnp.float32
MESH = pl.DeviceIdType.MESH
ANY = pl.BlockSpec(memory_space=pl.ANY)
VM = pl.BlockSpec(memory_space=pltpu.VMEM)


def where_am_i():
    return lax.axis_index("rp"), lax.axis_index("core"), lax.axis_index("grp")


def remote(src, dst, send, recv, target):
    return pltpu.make_async_remote_copy(
        src_ref=src,
        dst_ref=dst,
        send_sem=send,
        recv_sem=recv,
        device_id=target,
        device_id_type=MESH,
    )


def enter(p, c, z, groups):
    barrier = pltpu.get_barrier_semaphore()
    for k in range(groups):
        for d in range(2):
            if k == 0 and d == 0:
                continue
            pl.semaphore_signal(
                barrier, inc=1, device_id=(p, c ^ d, lax.rem(z + k, groups)), device_id_type=MESH
            )
    for b in (1, 2):
        pl.semaphore_signal(barrier, inc=1, device_id=(p ^ b, c, z), device_id_type=MESH)
    pl.semaphore_wait(barrier, 2 * groups - 1 + 2)


def move_tokens(refs, outs, send, recv, p, c, z, clips):
    core, slot = lax.div(z, clips), lax.rem(z, clips)

    def route(i):
        return core, c * clips + i

    def here(i):
        return jnp.logical_and(core == c, c * clips + i == z)

    def start(k, pieces):
        for n, (src, dst) in enumerate(zip(refs, outs)):
            rows = src.shape[1] // pieces
            rows = pl.ds(k * rows, rows)
            for i in range(clips):
                tc, tz = route(i)

                @pl.when(here(i))
                def _():
                    pltpu.make_async_copy(
                        src.at[i, rows], dst.at[slot, rows], recv.at[n, slot]
                    ).start()

                @pl.when(jnp.logical_not(here(i)))
                def _():
                    remote(
                        src.at[i, rows],
                        dst.at[slot, rows],
                        send.at[n, i],
                        recv.at[n, slot],
                        (p, tc, tz),
                    ).start()

    def sent():
        for n, (src, dst) in enumerate(zip(refs, outs)):
            for i in range(clips):

                @pl.when(jnp.logical_not(here(i)))
                def _():
                    remote(
                        src.at[i], dst.at[slot], send.at[n, i], recv.at[n, slot], (p, c ^ 1, z)
                    ).wait_send()

    def arrive():
        for n, (src, dst) in enumerate(zip(refs, outs)):
            for m in range(clips):
                pltpu.make_async_copy(src.at[0], dst.at[m], recv.at[n, m]).wait()

    def finish():
        sent()
        arrive()

    return start, finish, sent, arrive


def turn(u, cosine, sine):
    half = HEAD // 2
    first, second = u[:half], u[half:]
    return jnp.concatenate(
        [first * cosine - second * sine, first * sine + second * cosine], axis=0
    )


def dot(a, b):
    return jnp.dot(a, b, preferred_element_type=F32)


def dot_t(a, b):
    return lax.dot_general(a, b, (((1,), (1,)), ((), ())), preferred_element_type=F32)


def tile(i, size):
    return pl.ds(pl.multiple_of(i * size, size), size)


def cuts(whole, half, c, blocks):
    if blocks == 0:
        return [(whole.at[c], half)]
    size = half.shape[3] // blocks
    return [
        (
            whole.at[:, :, :, pl.ds(pl.multiple_of((2 * b + c) * size, size), size)],
            half.at[:, :, :, pl.ds(b * size, size)],
        )
        for b in range(blocks)
    ]


def forward_body(groups, clips, blocks, *refs):
    count = len(blocks)
    raw, (small, x, tab, dy) = refs[:count], refs[count : count + 4]
    (wq_o, wo_o, *outs) = refs[count + 4 : 2 * count + 4]
    (gain, bu, x_o, tab_o, dy_o, h1_o, qs_o, kr_o, vb_o, mix_o, lse_o, x2_o, h2_o) = refs[
        2 * count + 4 : 2 * count + 17
    ]
    halves = refs[2 * count + 17 : 3 * count + 17]
    (wq_v, small_v, x_v, tab_v, tab_w, h1, qs, kr, vb, mix, qkv, bias) = refs[
        3 * count + 17 : 3 * count + 29
    ]
    (wo_v, own_f, give, take, h2) = refs[3 * count + 29 : 3 * count + 34]
    (zs, zr, xs, xr, ys, yr, fs, fr, hs, ls, ss, sr, ts, tr, us, ur, vs, vr, es, er, ks) = refs[
        3 * count + 34 :
    ]
    outs = [wq_v, wo_v, *outs]
    p, c, z = where_am_i()
    for w in range(count):
        for src, dst in cuts(raw[w], halves[w], c, blocks[w]):
            pltpu.make_async_copy(src, dst, hs.at[w]).start()
    enter(p, c, z, groups)
    col = [(p, c, lax.rem(z + k, groups)) for k in range(groups)]
    org = [lax.rem(z + groups - k, groups) for k in range(groups)]
    xn, yn, cn = (p ^ 1, c, z), (p ^ 2, c, z), (p, c ^ 1, z)
    smalls = [
        remote(small, small_v.at[z], ss.at[k], sr.at[k], col[k]) for k in range(1, groups)
    ]
    for s in smalls:
        s.start()
    keep = [pltpu.make_async_copy(small, small_v.at[z], ls.at[count])]
    keep[0].start()
    start_tab, _, sent_tab, arrive_tab = move_tokens((tab,), (tab_v,), vs, vr, p, c, z, clips)
    start_x, _, sent_x, arrive_x = move_tokens((x,), (x_v,), ts, tr, p, c, z, clips)
    start_dy, _, sent_dy, arrive_dy = move_tokens((dy,), (dy_o.at[:clips],), us, ur, p, c, z, clips)
    units = [(w, d, side) for w in range(count) for d in range(1, groups) for side in range(2)]

    def origin(d, side):
        return z - d if side == 0 else z + d

    def arrives(d, side):
        return z >= d if side == 0 else z + d < groups

    def leaves(d, side):
        if side == 0:
            return jnp.logical_and(z + 1 < groups, z + 1 >= d)
        return jnp.logical_and(z >= 1, z - 1 + d < groups)

    def hop(w, d, side, src):
        o = origin(d - 1, side)
        target = (p, c, lax.rem(z + 1 if side == 0 else z + groups - 1, groups))
        return remote(src, outs[w].at[o, p], zs.at[w, side, d], zr.at[w, side, d], target)

    def own(w):
        pltpu.make_async_copy(halves[w], halves[w], hs.at[w]).wait()
        keep.append(pltpu.make_async_copy(halves[w], outs[w].at[z], ls.at[w]))
        keep[-1].start()
        for side in range(2):

            @pl.when(leaves(1, side))
            def _():
                hop(w, 1, side, halves[w].at[p]).start()

    def links(u):
        w, d, side = u
        o = outs[w].at[lax.rem(origin(d, side) + groups, groups)]
        e, f = xs.at[w, side, d], xr.at[w, side, d]
        g, h = ys.at[w, side, d], yr.at[w, side, d]
        a, b = fs.at[w, side, d, 0], fr.at[w, side, d, 0]
        m, n = fs.at[w, side, d, 1], fr.at[w, side, d, 1]
        across = lambda q: remote(o.at[q], o.at[q], e, f, xn)
        along = lambda q: remote(o.at[q], o.at[q], g, h, yn)
        first = lambda q: remote(o.at[q, 0], o.at[q, 0], a, b, yn)
        second = lambda q: remote(o.at[q, 1], o.at[q, 1], m, n, xn)
        return o, across, along, first, second

    def plane(u):
        w, d, side = u
        o, across, along, first, second = links(u)

        @pl.when(arrives(d, side))
        def _():
            remote(o.at[p], o.at[p], zs.at[w, side, d], zr.at[w, side, d], xn).wait_recv()
            if d + 1 < groups:

                @pl.when(leaves(d + 1, side))
                def _():
                    hop(w, d + 1, side, o.at[p]).start()

            across(p).start()
            along(p).start()

    def forward(u):
        w, d, side = u
        o, across, along, first, second = links(u)

        @pl.when(arrives(d, side))
        def _():
            across(p ^ 1).wait_recv()
            first(p ^ 1).start()
            along(p ^ 2).wait_recv()
            second(p ^ 2).start()

    def complete(u):
        w, d, side = u
        o, across, along, first, second = links(u)

        @pl.when(arrives(d, side))
        def _():
            first(p ^ 3).wait_recv()
            second(p ^ 3).wait_recv()

    def settle(u):
        w, d, side = u
        o, across, along, first, second = links(u)

        @pl.when(arrives(d, side))
        def _():
            across(p).wait_send()
            along(p).wait_send()
            first(p).wait_send()
            second(p).wait_send()

        @pl.when(leaves(d, side))
        def _():
            hop(w, d, side, halves[w].at[p]).wait_send()

    own(0)
    start_tab(0, 1)
    own(1)
    moves = {2 * k: (start_x, k) for k in range(4)}
    moves.update({10 + 3 * k: (start_dy, k) for k in range(4)})
    lag = 3

    def step(n):
        if n < len(units):
            plane(units[n])
            w, d, side = units[n]
            if (d, side) == (1, 1) and w + 2 < count:
                own(w + 2)
            if n in moves:
                moves[n][0](moves[n][1], 4)
        if n >= lag:
            forward(units[n - lag])

    steps = list(range(len(units) + lag))
    early = 2 * (groups - 1) + lag
    for _ in range(early):
        step(steps.pop(0))
    for k in range(1, groups):
        remote(small, small_v.at[org[k]], ss.at[k], sr.at[k], col[k]).wait_recv()
    keep[0].wait()
    row = small_v.shape[2]
    half = row // 2
    mine = pl.ds(pl.multiple_of(c * half, half), half)
    for g in range(groups):
        gain[0:6, g * row : (g + 1) * row] = small_v[g, 0:6]
        share = bu.shape[1] // groups
        for n in range(share // row):
            line = small_v[g, pl.ds(9 + c * (share // row) + n, 1)]
            bu[:, g * share + n * row : g * share + (n + 1) * row] = line
        for r in range(3):
            bias[3 * g + r : 3 * g + r + 1] = small_v[g, 6 + r : 7 + r, mine]
    own_count = h1.shape[0] // 2
    arrive_x()
    saves = [pltpu.make_async_copy(x_v, x_o, ks.at[0])]
    saves[0].start()

    def norm(i, carry):
        per = own_count // clips // 128
        v = x_v[lax.div(i, per), tile(lax.rem(i, per), 128)].astype(F32)
        v = v - jnp.mean(v, axis=1, keepdims=True)
        v = v * lax.rsqrt(jnp.mean(v * v, axis=1, keepdims=True) + EPS)
        h1[tile(i, 128)] = (v * gain[0:1] + gain[1:2]).astype(BF)
        return carry

    lax.fori_loop(0, own_count // 128, norm, 0)
    swap = remote(h1.at[:own_count], h1.at[own_count:], es.at[0], er.at[0], cn)
    swap.start()
    arrive_tab()
    swap_tab = remote(tab_v, tab_w, es.at[1], er.at[1], cn)
    swap_tab.start()
    step(steps.pop(0))
    swap_tab.wait()
    part = tab_v.shape[2]
    for m in range(clips):
        tab_o[:, m * part : (m + 1) * part] = tab_v[m]
        tab_o[:, own_count + m * part : own_count + (m + 1) * part] = tab_w[m]
    for u in units[: 2 * (groups - 1)]:
        complete(u)
    keep[1].wait()
    saves.append(pltpu.make_async_copy(wq_v, wq_o, ks.at[1]))
    saves[1].start()
    swap.wait()
    saves.append(pltpu.make_async_copy(h1, h1_o, ks.at[2]))
    saves[2].start()
    inner = qs.shape[0]
    heads = inner // HEAD
    pairs = heads // 2

    def head(h, side):
        rows, place = tile(h, HEAD), tile(side, HEAD)
        co, si = tab_o[: HEAD // 2], tab_o[HEAD // 2 :]
        k = turn(qkv[1, place], co, si).astype(BF)
        v = qkv[2, place].astype(BF)
        q = (turn(qkv[0, place], co, si).astype(BF).astype(F32) * SCALE).astype(BF)
        kr[rows] = k
        vb[rows] = v
        qs[rows] = q
        keys = k.T
        size = 256
        for i in range(0, 2 * own_count, size):
            scores = dot(keys, q[:, i : i + size])
            top = jnp.max(scores, axis=0, keepdims=True)
            e = jnp.exp(scores - top)
            total = jnp.sum(e, axis=0, keepdims=True)
            mixed = dot(v, e.astype(BF))
            mix[rows, i : i + size] = (mixed / total).astype(BF)
            lse_o[h, :, i : i + size] = top + jnp.log(total)

    during = [steps.pop(0) for _ in range(heads + heads // 2)]

    def two_heads(i, carry):
        def project(n, carry):
            at = pl.ds(pl.multiple_of(n * inner + i * 2 * HEAD, 2 * HEAD), 2 * HEAD)
            w = wq_v[..., at].reshape(h1.shape[1], 2 * HEAD)
            qkv[n] = (dot(h1[...], w) + bias[pl.ds(n * pairs + i, 1)]).T
            return carry

        lax.fori_loop(0, 3, project, 0)
        for n in range(pairs):

            @pl.when(i == n)
            def _():
                step(during[3 * n])

        def one(side, carry):
            head(2 * i + side, side)
            for n in range(heads):

                @pl.when(2 * i + side == n)
                def _():
                    step(during[3 * (n // 2) + 1 + n % 2])

            return carry

        lax.fori_loop(0, 2, one, 0)
        return carry

    lax.fori_loop(0, pairs, two_heads, 0)
    for n, (a, b) in enumerate(((qs, qs_o), (kr, kr_o), (vb, vb_o), (mix, mix_o))):
        saves.append(pltpu.make_async_copy(a, b, ks.at[3 + n]))
        saves[-1].start()
    for u in units[2 * (groups - 1) : 4 * (groups - 1)]:
        complete(u)
    keep[2].wait()
    saves.append(pltpu.make_async_copy(wo_v, wo_o, ks.at[7]))
    saves[-1].start()
    width = h1.shape[1]
    left_other, left_self = mix[:, own_count:].T, mix[:, :own_count].T

    def out_other(i, carry):
        at = tile(i, 256)
        give[:, at] = dot(left_other, wo_v[..., at].reshape(inner, 256)).astype(BF)
        return carry

    def out_self(i, carry):
        at = tile(i, 256)
        own_f[:, at] = dot(left_self, wo_v[..., at].reshape(inner, 256))
        return carry

    lax.fori_loop(0, width // 256, out_other, 0)
    swap = remote(give, take, es.at[2], er.at[2], cn)
    swap.start()
    lax.fori_loop(0, width // 256, out_self, 0)
    step(steps.pop(0))
    swap.wait()

    def second_norm(i, carry):
        per = own_count // clips // 128
        at = tile(i, 128)
        v = x_v[lax.div(i, per), tile(lax.rem(i, per), 128)].astype(F32)
        v = v + (own_f[at] + take[at].astype(F32)) + gain[2:3]
        own_f[at] = v
        v = v - jnp.mean(v, axis=1, keepdims=True)
        v = v * lax.rsqrt(jnp.mean(v * v, axis=1, keepdims=True) + EPS)
        h2[at] = (v * gain[3:4] + gain[4:5]).astype(BF)
        return carry

    lax.fori_loop(0, own_count // 128, second_norm, 0)
    swap = remote(h2.at[:own_count], h2.at[own_count:], es.at[0], er.at[0], cn)
    swap.start()
    saves.append(pltpu.make_async_copy(own_f, x2_o, ks.at[8]))
    saves[-1].start()
    step(steps.pop(0))
    swap.wait()
    saves.append(pltpu.make_async_copy(h2, h2_o, ks.at[9]))
    saves[-1].start()
    while steps:
        step(steps.pop(0))
    arrive_dy()
    swap_dy = remote(dy_o.at[:clips], dy_o.at[clips:], es.at[3], er.at[3], cn)
    swap_dy.start()
    for u in units[4 * (groups - 1) :]:
        complete(u)
    for u in units:
        settle(u)
    for s in smalls:
        s.wait_send()
    for k in keep[3:] + saves:
        k.wait()
    swap_dy.wait()
    sent_dy()
    sent_tab()
    sent_x()


def half_shape(raw, blocks):
    return raw.shape[1:] if blocks == 0 else raw.shape[:3] + (raw.shape[3] // 2,)


def forward(raw, blocks, small, x, tab, dy, groups):
    count, clips = len(raw), x.shape[0]
    own, width = clips * x.shape[1], x.shape[2]
    halves = [half_shape(r, b) for r, b in zip(raw, blocks)]
    inner = halves[0][-1] // 3
    dma = pltpu.SemaphoreType.DMA
    of = jax.ShapeDtypeStruct
    feature = (inner, 2 * own)
    shapes = [of((groups,) + h, BF) for h in halves]
    shapes += [of((8, width), F32), of((1, halves[2][-1]), F32)]
    shapes += [of(x.shape, BF), of((HEAD, 2 * own), F32)]
    shapes += [of((2 * clips,) + x.shape[1:], BF), of((2 * own, width), BF)] + [of(feature, BF)] * 4
    shapes += [of((inner // HEAD, 1, 2 * own), F32), of((own, width), F32), of((2 * own, width), BF)]
    vm = pltpu.VMEM
    scratch = [vm(h, BF) for h in halves]
    scratch += [vm((groups,) + halves[0], BF), vm((groups,) + small.shape, F32), vm(x.shape, BF)]
    scratch += [vm(tab.shape, F32)] * 2 + [vm((2 * own, width), BF)] + [vm(feature, BF)] * 4
    scratch += [vm((3, 2 * HEAD, 2 * own), F32)]
    scratch += [vm((3 * groups + -3 * groups % 8, width // groups // 2), F32)]
    scratch += [vm((groups,) + halves[1], BF), vm((own, width), F32)]
    scratch += [vm((own, width), BF)] * 2 + [vm((2 * own, width), BF)]
    return pl.pallas_call(
        functools.partial(forward_body, groups, clips, blocks),
        out_shape=shapes,
        in_specs=[ANY] * count + [VM, ANY, ANY, ANY],
        out_specs=[ANY] * count + [VM, VM, ANY, VM] + [ANY] * 6 + [VM, ANY, ANY],
        scratch_shapes=scratch
        + [dma((count, 2, groups))] * 6
        + [dma((count, 2, groups, 2))] * 2
        + [dma((count,)), dma((count + 1,)), dma((groups,)), dma((groups,))]
        + [dma((1, clips))] * 6
        + [dma((4,)), dma((4,)), dma((10,))],
        compiler_params=pltpu.CompilerParams(
            collective_id=0, has_side_effects=True, vmem_limit_bytes=60 * 1024 * 1024
        ),
        name="forward",
    )(*raw, small, x, tab, dy)


def backward_body(groups, clips, blocks, *refs):
    count = len(blocks)
    (gw2, act, slope, w2, w1, wo, wq, mix, qs, kr, vb, h1, h2, x2, x, dy, dy_all) = refs[:17]
    lse, tab, gain = refs[17:20]
    cosine, sine = tab.at[: HEAD // 2], tab.at[HEAD // 2 :]
    g1, g2, bd = (gain.at[n : n + 1] for n in (0, 3, 5))
    outs = refs[20 : 20 + count]
    gw1, small_o, gx_o, y_o = refs[20 + count : 24 + count]
    (gu_b, w1_b, wo_b, mix_b, qs_b, kr_b, vb_b, h1_b, x2_b, x_b, dy_b) = refs[24 + count : 35 + count]
    (own_f, give, take, y_take, dx2, low, da, gwo, gwq, ak, av, dq2, dk2, acc, gx) = refs[
        35 + count : 50 + count
    ]
    (sl, gbu, stage_b) = refs[50 + count : 53 + count]
    ld, es, er, sls = refs[53 + count : 57 + count]
    grads = (gwq, gwo, gw1, gw2)
    scratch = refs[57 + count :]
    own_a, own_b, one_a, one_b, two_a, two_b, three, full = (
        scratch[i * count : (i + 1) * count] for i in range(8)
    )
    small_s, small_r, small_z = scratch[8 * count : 8 * count + 3]
    (os, s1, r1, s2, r2, s3, r3, s4, r4, s5, r5, cs, cr, ls, ss, sr, ts, tr, us, ur) = scratch[
        8 * count + 3 :
    ]
    own, width = own_f.shape
    inner = mix_b.shape[0]
    third_width = wq.shape[1]

    upper, lower = w1_b.at[:, :width], w1_b.at[:, width:]
    pairs = ((w2.at[:width], upper), (w2.at[width:], lower), (dy_all, low), (h2, h1_b))
    pairs += ((x2, x2_b), (dy.at[:clips], dy_b), (mix, mix_b), (wo, wo_b))
    pairs += ((qs, qs_b), (kr, kr_b), (vb, vb_b), (x, x_b))
    pairs += ((w1, w1_b), (h1, h1_b), (act, gu_b), (w2.at[:width], upper), (w2.at[width:], lower))
    pairs += ((wq, w1_b.at[:, :third_width]),)
    loads = [pltpu.make_async_copy(a, b, ld.at[n]) for n, (a, b) in enumerate(pairs)]
    first_tile = pltpu.make_async_copy(slope.at[:, :256], sl.at[0], sls.at[0])
    first_tile.start()
    for copy in loads[:12]:
        copy.start()
    p, c, z = where_am_i()
    hi, lo = lax.div(p, 2), lax.rem(p, 2)
    enter(p, c, z, groups)
    col = [(p, c, lax.rem(z + k, groups)) for k in range(groups)]
    xn, yn, cn = (p ^ 1, c, z), (p ^ 2, c, z), (p, c ^ 1, z)
    order = (3, 2, 1, 0)
    units = [(w, j) for w in order for j in [*range(1, groups), 0]]
    sides = ((own_a, one_a, two_a, hi, yn), (own_b, one_b, two_b, lo, xn))

    def c1(u, n):
        w, j = u
        g = grads[w].at[lax.rem(z + j, groups)]
        src, target = (g.at[:, 1 - lo, 0], xn) if n == 0 else (g.at[1 - hi, :, 1], yn)
        return remote(src, sides[n][1][w].at[j], s1.at[w, j, n], r1.at[w, j, n], target)

    def load(u, n):
        w, j = u
        g = grads[w].at[lax.rem(z + j, groups)]
        src = g.at[:, lo, 0] if n == 0 else g.at[hi, :, 1]
        return pltpu.make_async_copy(src, sides[n][0][w].at[j], os.at[w, j, n])

    def c2(u, n):
        w, j = u
        own, one, two, side, target = sides[n]
        return remote(own[w].at[j, 1 - side], two[w].at[j], s2.at[w, j, n], r2.at[w, j, n], target)

    def c3(u, n):
        w, j = u
        src = sides[n][0][w].at[j, sides[n][3]]
        return remote(src, three[w].at[j, n], s3.at[w, j, n], r3.at[w, j, n], col[j])

    def c4(w, n):
        f = full[w].at[p]
        return remote(f, f, s4.at[w, n], r4.at[w, n], (xn, yn)[n])

    def c5(w, n):
        f = full[w].at[(p ^ 1, p ^ 2)[n], n]
        return remote(f, f, s5.at[w, n], r5.at[w, n], (yn, xn)[n])

    def stage_zero(u):
        for n in range(2):
            c1(u, n).start()
            load(u, n).start()

    def stage_one(u):
        w, j = u
        for n, (own, one, two, side, target) in enumerate(sides):
            load(u, n).wait()
            c1(u, n).wait_recv()
            own[w][j] = (own[w][j].astype(F32) + one[w][j].astype(F32)).astype(BF)
            c2(u, n).start()

    def stage_two(u):
        w, j = u
        for n, (own, one, two, side, target) in enumerate(sides):
            c2(u, n).wait_recv()
            own[w][j, side] = (own[w][j, side].astype(F32) + two[w][j].astype(F32)).astype(BF)
            if j:
                c3(u, n).start()

    def stage_three(w):
        for n, (own, one, two, side, target) in enumerate(sides):
            total = own[w][0, side].astype(F32)
            for j in range(1, groups):
                c3((w, j), n).wait_recv()
                total = total + three[w][j, n].astype(F32)
            full[w][p, n] = total.astype(BF)
        for n in range(2):
            c4(w, n).start()

    def stage_four(w):
        for n, target in enumerate((yn, xn)):
            f = full[w].at[(p ^ 1, p ^ 2)[n]]
            remote(f, f, s4.at[w, n], r4.at[w, n], target).wait_recv()
            c5(w, n).start()

    def stage_five(w):
        for n in range(2):
            f = full[w].at[p ^ 3, n]
            remote(f, f, s5.at[w, n], r5.at[w, n], xn).wait_recv()
        for dst, src in cuts(outs[w], full[w], c, blocks[w]):
            pltpu.make_async_copy(src, dst, ls.at[w]).start()
            remote(src, dst, cs.at[w], cr.at[w], cn).start()

    ahead, lag = 3, 3
    todo = {}
    for n, u in enumerate(units):
        todo.setdefault(max(n - ahead, -1), []).append((stage_zero, u))
        todo.setdefault(n, []).append((stage_one, u))
        todo.setdefault(n + lag, []).append((stage_two, u))
    for i, w in enumerate(order):
        last = (i + 1) * groups - 1 + lag
        for at, stage in ((2, stage_three), (3, stage_four), (4, stage_five)):
            todo.setdefault(last + at, []).append((stage, w))
    steps = sorted(todo)

    def run(step):
        for stage, what in todo[step]:
            stage(what)

    def tick(times=1):
        for _ in range(times):
            run(steps.pop(0))

    def half_sum(n, left, right, depth):
        def other(i, carry):
            part = dot_t(left[own:, :depth], right[tile(i, 256), :depth])
            give[:, tile(i, 256)] = part.astype(BF)
            return carry

        def self(i, carry):
            own_f[:, tile(i, 256)] = dot_t(left[:own, :depth], right[tile(i, 256), :depth])
            return carry

        lax.fori_loop(0, width // 256, other, 0)
        copy = remote(give, take, es.at[n], er.at[n], cn)
        copy.start()
        lax.fori_loop(0, width // 256, self, 0)
        return copy

    def part(i):
        per = own // clips // 128
        return lax.div(i, per), tile(lax.rem(i, per), 128)

    def norm_step(i, field, gain, grad, row):
        at = tile(i, 128)
        d = own_f[at] + take[at].astype(F32)
        v = field[at].astype(F32)
        v = v - jnp.mean(v, axis=1, keepdims=True)
        r = lax.rsqrt(jnp.mean(v * v, axis=1, keepdims=True) + EPS)
        v = v * r
        acc[row : row + 1] += jnp.sum(d * v, axis=0, keepdims=True)
        acc[row + 1 : row + 2] += jnp.sum(d, axis=0, keepdims=True)
        e = d * gain[...]
        mean = jnp.mean(e, axis=1, keepdims=True)
        e = e - mean - v * jnp.mean(e * v, axis=1, keepdims=True)
        return grad + r * e

    tick()
    acc[...] = jnp.zeros_like(acc)
    for copy in loads[:3]:
        copy.wait()
    deep = slope.shape[1]
    sides_of = deep // width

    def hidden_grad(side, i):
        n = side * (width // 256) + i
        slot = lax.rem(n, 2)
        pltpu.make_async_copy(slope.at[:, :256], sl.at[slot], sls.at[slot]).wait()

        @pl.when(n + 1 < deep // 256)
        def _():
            src = slope.at[:, tile(n + 1, 256)]
            pltpu.make_async_copy(src, sl.at[1 - slot], sls.at[1 - slot]).start()

        right = w1_b[tile(i, 256), side * width : (side + 1) * width]
        line = jnp.zeros((1, 256), F32)
        for r in range(2):
            rows = slice(r * own, (r + 1) * own)
            g = dot_t(low[rows], right) * sl[slot, rows].astype(F32)
            g = g.astype(BF)
            gu_b[rows, tile(n, 256)] = g
            line = line + jnp.sum(g.astype(F32), axis=0, keepdims=True)
        gbu[:, tile(n, 256)] = line

    for side in range(sides_of):

        def columns(i, carry):
            hidden_grad(side, i)
            return carry

        lax.fori_loop(0, width // 256, columns, 0)
        if side == 0:
            tick()
    loads[12].start()
    loads[3].wait()
    row = width // groups

    def up_grad(j, carry):
        k = lax.rem(z + j, groups)
        left = h1_b[:, tile(k, row)].T

        def columns(i, carry):
            at = tile(i, 512)
            stage_b[..., at] = dot(left, gu_b[:, at]).astype(BF).reshape(stage_b.shape[:-1] + (512,))
            return carry

        lax.fori_loop(0, deep // 512, columns, 0)
        copy = pltpu.make_async_copy(stage_b, gw1.at[k], ld.at[18])
        copy.start()
        copy.wait()
        return carry

    lax.fori_loop(1, 3, up_grad, 0)
    tick()
    lax.fori_loop(3, groups + 1, up_grad, 0)
    loads[13].start()
    tick()
    loads[12].wait()
    swap = half_sum(0, gu_b, w1_b, deep)
    for copy in loads[14:17]:
        copy.start()
    tick()
    for copy in loads[4:12]:
        copy.wait()
    swap.wait()

    def second_norm(i, carry):
        at = tile(i, 128)
        g = dy_b[part(i)].astype(F32)
        d = norm_step(i, x2_b, g2, g, 3)
        dx2[at] = d
        acc[5:6] += jnp.sum(g, axis=0, keepdims=True)
        low[at] = d.astype(BF)
        acc[2:3] += jnp.sum(d.astype(BF).astype(F32), axis=0, keepdims=True)
        return carry

    lax.fori_loop(0, own // 128, second_norm, 0)
    swap = remote(low.at[:own], low.at[own:], es.at[1], er.at[1], cn)
    swap.start()
    tick()
    swap.wait()

    def out_grad(i, carry):
        at = tile(i, 256)
        gwo[..., at] = dot(mix_b[...], low[:, at]).astype(BF).reshape(gwo.shape[:-1] + (256,))
        return carry

    lax.fori_loop(0, width // 256, out_grad, 0)

    def attn_grad(i, carry):
        at = tile(i, 256)
        da[:, at] = dot_t(wo_b[...], low[at]).astype(BF)
        return carry

    lax.fori_loop(0, 2 * own // 256, attn_grad, 0)
    tick()

    for copy in loads[14:17]:
        copy.wait()

    def down(rows, i):
        left = dot(gu_b[rows, :width], w1_b[:, tile(i, 256)])
        at = pl.ds(pl.multiple_of(width + i * 256, 256), 256)
        return left + dot(gu_b[rows, width:], w1_b[:, at])

    def down_other(i, carry):
        give[:, tile(i, 256)] = down(slice(own, 2 * own), i).astype(BF)
        return carry

    def down_self(i, carry):
        own_f[:, tile(i, 256)] = down(slice(0, own), i)
        return carry

    lax.fori_loop(0, width // 256, down_other, 0)
    y_copy = remote(give, y_take, es.at[3], er.at[3], cn)
    y_copy.start()
    lax.fori_loop(0, width // 256, down_self, 0)
    loads[17].start()
    y_copy.wait()

    def last_add(i, carry):
        at = tile(i, 128)
        gx[part(i)] = (x2_b[at] + own_f[at] + bd[...] + y_take[at].astype(F32)).astype(BF)
        return carry

    lax.fori_loop(0, own // 128, last_add, 0)
    y_start, y_finish, *_ = move_tokens((gx,), (y_o,), us, ur, p, c, z, clips)
    y_start(0, 4)
    dqkv = gu_b.at[:, :third_width]

    def head(h, side):
        rows = tile(h, HEAD)
        place = tile(side, HEAD)
        co, si = cosine[...], sine[...]
        kt = kr_b[rows]
        keys, values = kt.T, vb_b[rows].T
        queries, outer_grads = qs_b[rows].T, da[rows].T
        step = 256
        for i in range(0, 2 * own, step):
            s = slice(i, i + step)
            g = da[rows, s]
            p = jnp.exp(dot(keys, qs_b[rows, s]) - lse[h, :, s])
            delta = jnp.sum(mix_b[rows, s].astype(F32) * g.astype(F32), axis=0, keepdims=True)
            ds = (p * (dot(values, g) - delta)).astype(BF)
            dq2[place, s] = turn(dot(kt, ds) * SCALE, co[:, s], -si[:, s]).astype(BF)
            dv = dot(p.astype(BF), outer_grads[s])
            dk = dot(ds, queries[s])
            if i == 0:
                ak[...] = dk
                av[side] = dv
            else:
                ak[...] += dk
                av[side] += dv
        dk2[place] = turn(ak[...].T, co, -si).astype(BF)

    heads = inner // HEAD
    during = [steps.pop(0) for _ in range(3)]

    def two_heads(i, carry):
        lax.fori_loop(0, 2, lambda side, _: head(2 * i + side, side), None)
        for n, value in enumerate(
            (dq2[...].T, dk2[...].T, jnp.concatenate([av[0], av[1]], axis=1).astype(BF))
        ):
            at = pl.ds(pl.multiple_of(n * inner + i * 2 * HEAD, 2 * HEAD), 2 * HEAD)
            dqkv[:, at] = value
        for n, step in enumerate(during):
            pl.when(i == n * heads // 8)(functools.partial(run, step))
            pl.when(i == n * heads // 8)(functools.partial(y_start, n + 1, 4))
        return carry

    lax.fori_loop(0, heads // 2, two_heads, 0)
    loads[13].wait()
    for g in range(groups):
        left = h1_b[:, g * row : (g + 1) * row].T

        def in_grad(i, carry):
            at = tile(i, 512)
            gwq[g, ..., at] = dot(left, dqkv[:, at]).astype(BF).reshape(gwq.shape[1:-1] + (512,))
            return carry

        lax.fori_loop(0, third_width // 512, in_grad, 0)
    tick()
    loads[17].wait()
    swap = half_sum(2, dqkv, w1_b, third_width)
    tick()
    swap.wait()
    y_finish()

    def first_norm(i, carry):
        gx[part(i)] = norm_step(i, x_b, g1, dx2[tile(i, 128)], 0).astype(BF)
        return carry

    lax.fori_loop(0, own // 128, first_norm, 0)
    start, finish, *_ = move_tokens((gx,), (gx_o,), ts, tr, p, c, z, clips)
    start(0, 4)
    tick()
    small_s[...] = jnp.zeros_like(small_s)
    for n in range(6):
        for g in range(groups):
            small_s[g, n : n + 1] = acc[n : n + 1, g * row : (g + 1) * row]
    half = row // 2
    mine_at = pl.ds(pl.multiple_of(c * half, half), half)
    for b in range(3 * groups):
        line = jnp.sum(dqkv[:, b * half : (b + 1) * half].astype(F32), axis=0, keepdims=True)
        small_s[b // 3, 6 + b % 3 : 7 + b % 3, mine_at] = line
    share = deep // groups
    for g in range(groups):
        for n in range(share // row):
            at = pl.ds(9 + c * (share // row) + n, 1)
            small_s[g, at] = gbu[:, g * share + n * row : g * share + (n + 1) * row]
    tick()
    for n, target in enumerate((cn, xn, yn)):
        copy = remote(small_s, small_r.at[n], ss.at[n], sr.at[n], target)
        copy.start()
        start(n + 1, 4)
        tick(1 if n == 0 else 2)
        copy.wait()
        small_s[...] += small_r[n]
    tails = [
        remote(small_s.at[col[k][2]], small_z.at[k], ss.at[2 + k], sr.at[2 + k], col[k])
        for k in range(1, groups)
    ]
    for t in tails:
        t.start()
    while steps:
        tick()
    for k in range(1, groups):
        tails[k - 1].wait()
    small_o[...] = small_s[z]
    for k in range(1, groups):
        small_o[...] += small_z[k]
    for u in units:
        w, j = u
        for n in range(2):
            c1(u, n).wait_send()
            c2(u, n).wait_send()
            if j:
                c3(u, n).wait_send()
    for w in range(count):
        for n in range(2):
            c4(w, n).wait_send()
            c5(w, n).wait_send()
        pltpu.make_async_copy(full[w], full[w], ls.at[w]).wait()
        remote(full[w], full[w], cs.at[w], cr.at[w], cn).wait()
    finish()


def backward(gw2, arrays, tables, lines, groups, blocks):
    act, slope, w2, w1, wo, wq, mix, qs, kr, vb, h1, h2, x2, x, dy, dy_all = arrays
    (own, width), clips = x.shape, dy.shape[0] // 2
    moved = jax.ShapeDtypeStruct((clips,) + dy.shape[1:], BF)
    small = jax.ShapeDtypeStruct((groups, lines + -lines % 8, width // groups), F32)
    count = len(blocks)
    dma = pltpu.SemaphoreType.DMA
    split = lambda v: (groups, 2, 2, 2, v.shape[0] // (8 * groups), v.shape[1])
    tiles = [split(v)[4:] for v in (wq, wo, w1, w2)]
    shapes = [
        jax.ShapeDtypeStruct((4, 2, t[0], 2 * t[1]) if b else (2, 4, 2) + t, BF)
        for t, b in zip(tiles, blocks)
    ]
    shapes += [
        jax.ShapeDtypeStruct(split(w1), BF),
        jax.ShapeDtypeStruct(small.shape[1:], F32),
        moved,
        moved,
    ]
    scratch = [pltpu.VMEM(v.shape, v.dtype) for v in (act, w1, wo, mix, qs, kr, vb, h1, x2, x, moved)]
    half, low = (own, width), pltpu.VMEM((2 * own, width), BF)
    scratch += [pltpu.VMEM(half, F32)] + [pltpu.VMEM(half, BF)] * 3
    scratch += [pltpu.VMEM(half, F32), low, pltpu.VMEM(mix.shape, BF)]
    scratch += [pltpu.VMEM(split(wo), BF), pltpu.VMEM(split(wq), BF)]
    scratch += [pltpu.VMEM((2 * own, HEAD), F32), pltpu.VMEM((2, 2 * own, HEAD), F32)]
    scratch += [pltpu.VMEM((2 * HEAD, 2 * own), BF)] * 2
    scratch += [pltpu.VMEM((8, width), F32), pltpu.VMEM(moved.shape, BF)]
    scratch += [pltpu.VMEM((2, 2 * own, 256), BF), pltpu.VMEM((1, act.shape[1]), F32)]
    scratch += [pltpu.VMEM(split(w1)[1:], BF)]
    scratch += [dma((19,)), dma((4,)), dma((4,)), dma((2,))]
    for lead in (
        (groups, 2),
        (groups, 2),
        (groups, 2),
        (groups, 2),
        (groups,),
        (groups,),
        (groups, 2),
        (4, 2),
    ):
        scratch += [pltpu.VMEM(lead + t, BF) for t in tiles]
    scratch += [
        pltpu.VMEM(small.shape, F32),
        pltpu.VMEM((3,) + small.shape, F32),
        pltpu.VMEM(small.shape, F32),
    ]
    pair = dma((count, groups, 2))
    scratch += [pair] * 7 + [dma((count, 2))] * 4
    scratch += [dma((count,))] * 3 + [dma((2 + groups,))] * 2 + [dma((1, clips))] * 4
    return pl.pallas_call(
        functools.partial(backward_body, groups, clips, blocks),
        out_shape=shapes,
        in_specs=[ANY] * (1 + len(arrays)) + [VM] * len(tables),
        out_specs=[ANY] * (count + 1) + [VM, ANY, ANY],
        scratch_shapes=scratch,
        compiler_params=pltpu.CompilerParams(
            collective_id=1, has_side_effects=True, vmem_limit_bytes=67043328
        ),
        name="backward",
    )(gw2, *arrays, *tables)


def contract(left, right, a, b):
    return lax.dot_general(left, right, (((a,), (b,)), ((), ())), preferred_element_type=F32)


def paired(
    tokens,
    positions,
    ln1_gain,
    ln1_bias,
    w_qkv,
    b_qkv,
    w_out,
    b_out,
    ln2_gain,
    ln2_bias,
    w_up,
    b_up,
    w_down,
    b_down,
    cotangent,
):
    groups = lax.axis_size("grp")
    clips, part, width = tokens.shape
    hidden = w_down.shape[0] * groups
    own = clips * part
    length = 2 * own
    c, z = lax.axis_index("core"), lax.axis_index("grp")
    wide = width // 2
    deep = hidden // 2
    row = width // groups

    def pick(value, axis):
        return lax.dynamic_index_in_dim(value, c, axis, keepdims=False)

    blocks = (3 * groups, 0, groups, 0)
    raw = [
        w.reshape(((4, 2) if b else (2, 4, 2)) + (w.shape[0] // (8 if b else 16), w.shape[1]))
        for w, b in zip((w_qkv, w_out, w_up, w_down), blocks)
    ]
    bq, bu = b_qkv.shape[0] // row, b_up.shape[0] // row
    vectors = [ln1_gain, ln1_bias, b_out, ln2_gain, ln2_bias, b_down]
    vectors += [b_qkv, b_up]
    lines = len(vectors) - 2 + bq + bu
    size, start = (lines + -lines % 8) * row, 0
    small = jnp.zeros((size,), F32)
    for v in vectors:
        small = small + jnp.pad(v.astype(F32), (start, size - start - v.shape[0]))
        start += v.shape[0]
    small = small.reshape(-1, row)
    pair = jnp.arange(HEAD // 2)
    band = (pair >= 10).astype(jnp.int32) + (pair >= 21).astype(jnp.int32)
    begin = jnp.where(band == 0, 0, jnp.where(band == 1, 10, 21))
    number = jnp.where(band == 0, 10, 11)
    freq = jnp.power(F32(10000.0), -(pair - begin).astype(F32) / number.astype(F32))
    pos = positions.astype(F32)[:, :, None, :]
    band = band[None, :, None]
    chosen = jnp.where(band == 0, pos[0], jnp.where(band == 1, pos[1], pos[2]))
    angles = chosen * freq[None, :, None]
    tab = jnp.concatenate([jnp.cos(angles), jnp.sin(angles)], axis=1)
    wq, wo, w1, w2, gain, bu_own, x, tab, dy, h1, qs, kr, vb, mixed, lse, x2, h2 = forward(
        raw, blocks, small, tokens, tab, cotangent, groups
    )
    wq = wq.reshape(width, 3 * wide)
    wo = wo.reshape(wide, width)
    w1 = w1.reshape(width, deep)
    w2 = w2.reshape(deep, width)
    grad_all = dy.reshape(length, width)
    tokens = x.reshape(own, width)
    u = contract(h2, w1, 1, 0) + bu_own
    cdf = 0.5 * (1.0 + lax.erf(u * F32(0.7071067811865476)))
    act = (u * cdf).astype(BF)
    slope = (cdf + u * jnp.exp(-0.5 * u * u) * F32(0.3989422804014327)).astype(BF)

    gw2 = contract(act, grad_all, 0, 0).astype(BF)
    gw2 = gw2.reshape(groups, 2, 2, 2, gw2.shape[0] // (8 * groups), width)
    arrays = (act, slope, w2, w1, wo, wq, mixed, qs, kr, vb, h1, h2, x2, tokens, dy, grad_all)
    tables = (lse, tab, gain)
    gwq, gwo, gw1, gw2, _, sums, gx, output = backward(gw2, arrays, tables, lines, groups, blocks)
    gwq, gwo, gw1, gw2 = (
        g.reshape(shard.shape).astype(F32)
        for g, shard in zip((gwq, gwo, gw1, gw2), (w_qkv, w_out, w_up, w_down))
    )
    gg1, gb1, gbo, gg2, gb2, gbd = (sums[n] for n in range(6))
    gbq, gbu = sums[6 : 6 + bq].reshape(-1), sums[6 + bq : lines].reshape(-1)
    return (output, gx, gg1, gb1, gwq, gbq, gwo, gbo, gg2, gb2, gw1, gbu, gw2, gbd)


def paired_specs():
    rep = ("rp", "core")
    ins = (P(rep, "grp", None), P(None, rep, "grp"))
    one, two = P("grp"), P("grp", None)
    ins += (one, one, two, one, two, one, one, one, two, one, two, one, P(rep, "grp", None))
    outs = (P(rep, "grp", None),) * 2
    outs += (one, one, two, one, two, one, one, one, two, one, two, one)
    return ins, outs


def rotary_angles(positions):
    pair = jnp.arange(32)
    band = (pair >= 10).astype(jnp.int32) + (pair >= 21).astype(jnp.int32)
    start = jnp.where(band == 0, 0, jnp.where(band == 1, 10, 21))
    count = jnp.where(band == 0, 10, 11)
    freq = jnp.power(
        jnp.float32(10000.0), -(pair - start).astype(jnp.float32) / count.astype(jnp.float32)
    )
    pos_f = positions.astype(jnp.float32)
    chosen = jnp.where(
        band[None, :] == 0,
        pos_f[0][:, None],
        jnp.where(band[None, :] == 1, pos_f[1][:, None], pos_f[2][:, None]),
    )
    return chosen * freq[None, :]


def rotate(field, cosine, sine):
    first = field[..., :32]
    second = field[..., 32:]
    return jnp.concatenate(
        [first * cosine - second * sine, first * sine + second * cosine], axis=-1
    )


def normalize(field):
    centred = field - jnp.mean(field, axis=-1, keepdims=True)
    variance = jnp.mean(centred * centred, axis=-1, keepdims=True)
    factor = lax.rsqrt(variance + EPS)
    return (centred * factor, factor)


def norm_back(grad_norm, normed, factor):
    return factor * (
        grad_norm
        - jnp.mean(grad_norm, axis=-1, keepdims=True)
        - normed * jnp.mean(grad_norm * normed, axis=-1, keepdims=True)
    )


def outer(left, right):
    return lax.dot_general(
        left, right, (((0,), (0,)), ((), ())), preferred_element_type=jnp.float32
    )


def back(left, right):
    return lax.dot_general(
        left, right, (((1,), (1,)), ((), ())), preferred_element_type=jnp.float32
    )


def exact_gelu(value):
    return jax.nn.gelu(value, approximate=False)


def column_sum(value):
    return jnp.sum(value.astype(jnp.float32), axis=0)


def forward_pass(params, field_in, positions):
    g1, b1, wqkv, bqkv, wo, bo, g2, b2, w1, bu, w2, bd = params
    field = field_in.astype(jnp.float32)
    count, width = field.shape
    heads = width // 64
    angles = rotary_angles(positions)
    cosine = jnp.cos(angles)[:, None, :]
    sine = jnp.sin(angles)[:, None, :]
    normed1, factor1 = normalize(field)
    h1 = (normed1 * g1.astype(jnp.float32) + b1.astype(jnp.float32)).astype(jnp.bfloat16)
    qkv = jnp.dot(h1, wqkv, preferred_element_type=jnp.float32) + bqkv.astype(jnp.float32)
    query_rot = rotate(qkv[:, :width].reshape(count, heads, 64), cosine, sine).astype(jnp.bfloat16)
    keys_rot = (
        rotate(qkv[:, width : 2 * width].reshape(count, heads, 64), cosine, sine)
        .astype(jnp.bfloat16)
        .reshape(count, width)
    )
    values = qkv[:, 2 * width :].astype(jnp.bfloat16)
    keys_all, values_all = (
        lax.all_gather(keys_rot, "grp", axis=0, tiled=True),
        lax.all_gather(values, "grp", axis=0, tiled=True),
    )
    total = keys_all.shape[0]
    keys_all = keys_all.reshape(total, heads, 64)
    values_all = values_all.reshape(total, heads, 64)
    scores = (
        jnp.einsum("thd,shd->hts", query_rot, keys_all, preferred_element_type=jnp.float32) * SCALE
    )
    top = jnp.max(scores, axis=-1, keepdims=True)
    lse = top + jnp.log(jnp.sum(jnp.exp(scores - top), axis=-1, keepdims=True))
    probs = jnp.exp(scores - lse).astype(jnp.bfloat16)
    mixed = (
        jnp.einsum("hts,shd->thd", probs, values_all, preferred_element_type=jnp.float32)
        .reshape(count, width)
        .astype(jnp.bfloat16)
    )
    second = field + jnp.dot(mixed, wo, preferred_element_type=jnp.float32) + bo.astype(jnp.float32)
    normed2, factor2 = normalize(second)
    h2 = (normed2 * g2.astype(jnp.float32) + b2.astype(jnp.float32)).astype(jnp.bfloat16)
    hidden = jnp.dot(h2, w1, preferred_element_type=jnp.float32) + bu.astype(jnp.float32)
    active = exact_gelu(hidden).astype(jnp.bfloat16)
    result = (
        second + jnp.dot(active, w2, preferred_element_type=jnp.float32) + bd.astype(jnp.float32)
    )
    saved = (
        normed1,
        factor1,
        h1,
        query_rot,
        keys_rot,
        values,
        lse,
        mixed,
        normed2,
        factor2,
        h2,
        hidden,
        active,
        cosine,
        sine,
    )
    return (saved, result.astype(jnp.bfloat16))


def backward_pass(params, saved, grad_in, totals):
    g1, b1, wqkv, bqkv, wo, bo, g2, b2, w1, bu, w2, bd = params
    (
        normed1,
        factor1,
        h1,
        query_rot,
        keys_rot,
        values,
        lse,
        mixed,
        normed2,
        factor2,
        h2,
        hidden,
        active,
        cosine,
        sine,
    ) = saved
    grad_out = grad_in.astype(jnp.float32)
    count, width = grad_out.shape
    heads = width // 64
    grad_y2 = grad_out.astype(jnp.bfloat16)
    grad_w2 = outer(active, grad_y2)
    grad_bd = column_sum(grad_y2)
    grad_act = back(grad_y2, w2)
    unused, pull = jax.vjp(exact_gelu, hidden)
    grad_hidden = pull(grad_act)[0].astype(jnp.bfloat16)
    grad_w1 = outer(h2, grad_hidden)
    grad_bu = column_sum(grad_hidden)
    grad_h2 = back(grad_hidden, w1)
    grad_g2 = jnp.sum(grad_h2 * normed2, axis=0)
    grad_b2 = jnp.sum(grad_h2, axis=0)
    grad_second = grad_out + norm_back(grad_h2 * g2.astype(jnp.float32), normed2, factor2)
    grad_y1 = grad_second.astype(jnp.bfloat16)
    grad_wo = outer(mixed, grad_y1)
    grad_bo = column_sum(grad_y1)
    grad_mixed = back(grad_y1, wo).astype(jnp.bfloat16).reshape(count, heads, 64)
    keys_all, values_all = (
        lax.all_gather(keys_rot, "grp", axis=0, tiled=True),
        lax.all_gather(values, "grp", axis=0, tiled=True),
    )
    total = keys_all.shape[0]
    keys_all = keys_all.reshape(total, heads, 64)
    values_all = values_all.reshape(total, heads, 64)
    scores = (
        jnp.einsum("thd,shd->hts", query_rot, keys_all, preferred_element_type=jnp.float32) * SCALE
    )
    probs = jnp.exp(scores - lse)
    grad_probs = jnp.einsum(
        "thd,shd->hts", grad_mixed, values_all, preferred_element_type=jnp.float32
    )
    delta = jnp.sum(probs * grad_probs, axis=-1, keepdims=True)
    grad_scores = (probs * (grad_probs - delta)).astype(jnp.bfloat16)
    grad_query = (
        jnp.einsum("hts,shd->thd", grad_scores, keys_all, preferred_element_type=jnp.float32)
        * SCALE
    )
    probs_low = probs.astype(jnp.bfloat16)
    grad_values = jnp.einsum(
        "hts,thd->shd", probs_low, grad_mixed, preferred_element_type=jnp.float32
    )
    grad_keys = (
        jnp.einsum("hts,thd->shd", grad_scores, query_rot, preferred_element_type=jnp.float32)
        * SCALE
    )
    keys_own, values_own = (
        lax.psum_scatter(
            grad_keys.reshape(total, width).astype(jnp.bfloat16),
            "grp",
            scatter_dimension=0,
            tiled=True,
        ).astype(jnp.float32),
        lax.psum_scatter(
            grad_values.reshape(total, width).astype(jnp.bfloat16),
            "grp",
            scatter_dimension=0,
            tiled=True,
        ).astype(jnp.float32),
    )
    query_back = rotate(grad_query, cosine, -sine).reshape(count, width)
    keys_back = rotate(keys_own.reshape(count, heads, 64), cosine, -sine).reshape(count, width)
    grad_qkv = jnp.concatenate([query_back, keys_back, values_own], axis=1).astype(jnp.bfloat16)
    grad_wqkv = outer(h1, grad_qkv)
    grad_bqkv = column_sum(grad_qkv)
    grad_h1 = back(grad_qkv, wqkv)
    grad_g1 = jnp.sum(grad_h1 * normed1, axis=0)
    grad_b1 = jnp.sum(grad_h1, axis=0)
    grad_field = grad_second + norm_back(grad_h1 * g1.astype(jnp.float32), normed1, factor1)
    terms = (
        grad_g1,
        grad_b1,
        grad_wqkv,
        grad_bqkv,
        grad_wo,
        grad_bo,
        grad_g2,
        grad_b2,
        grad_w1,
        grad_bu,
        grad_w2,
        grad_bd,
    )
    totals = tuple((a + b for a, b in zip(totals, terms)))
    return (grad_field.astype(jnp.bfloat16), totals)


def local(
    tokens,
    positions,
    ln1_gain,
    ln1_bias,
    w_qkv,
    b_qkv,
    w_out,
    b_out,
    ln2_gain,
    ln2_bias,
    w_up,
    b_up,
    w_down,
    b_down,
    cotangent,
):
    shards = (
        ln1_gain,
        ln1_bias,
        w_qkv,
        b_qkv,
        w_out,
        b_out,
        ln2_gain,
        ln2_bias,
        w_up,
        b_up,
        w_down,
        b_down,
    )
    groups = lax.axis_size("grp")
    totals = tuple((jnp.zeros((s.shape[0] * groups,) + s.shape[1:], jnp.float32) for s in shards))
    outputs = []
    gradients = []
    for index in range(tokens.shape[0]):
        forward_params = (
            lax.all_gather(ln1_gain, "grp", axis=0, tiled=True),
            lax.all_gather(ln1_bias, "grp", axis=0, tiled=True),
            lax.all_gather(w_qkv, "grp", axis=0, tiled=True),
            lax.all_gather(b_qkv, "grp", axis=0, tiled=True),
            lax.all_gather(w_out, "grp", axis=0, tiled=True),
            lax.all_gather(b_out, "grp", axis=0, tiled=True),
            lax.all_gather(ln2_gain, "grp", axis=0, tiled=True),
            lax.all_gather(ln2_bias, "grp", axis=0, tiled=True),
            lax.all_gather(w_up, "grp", axis=0, tiled=True),
            lax.all_gather(b_up, "grp", axis=0, tiled=True),
            lax.all_gather(w_down, "grp", axis=0, tiled=True),
            lax.all_gather(b_down, "grp", axis=0, tiled=True),
        )
        saved, result = forward_pass(forward_params, tokens[index], positions[:, index, :])
        outputs.append(result)
        backward_params = (
            lax.all_gather(ln1_gain, "grp", axis=0, tiled=True),
            lax.all_gather(ln1_bias, "grp", axis=0, tiled=True),
            lax.all_gather(w_qkv, "grp", axis=0, tiled=True),
            lax.all_gather(b_qkv, "grp", axis=0, tiled=True),
            lax.all_gather(w_out, "grp", axis=0, tiled=True),
            lax.all_gather(b_out, "grp", axis=0, tiled=True),
            lax.all_gather(ln2_gain, "grp", axis=0, tiled=True),
            lax.all_gather(ln2_bias, "grp", axis=0, tiled=True),
            lax.all_gather(w_up, "grp", axis=0, tiled=True),
            lax.all_gather(b_up, "grp", axis=0, tiled=True),
            lax.all_gather(w_down, "grp", axis=0, tiled=True),
            lax.all_gather(b_down, "grp", axis=0, tiled=True),
        )
        grad_field, totals = backward_pass(backward_params, saved, cotangent[index], totals)
        gradients.append(grad_field)
    owned = (
        lax.psum_scatter(
            totals[0].astype(jnp.bfloat16), "grp", scatter_dimension=0, tiled=True
        ).astype(jnp.float32),
        lax.psum_scatter(
            totals[1].astype(jnp.bfloat16), "grp", scatter_dimension=0, tiled=True
        ).astype(jnp.float32),
        lax.psum_scatter(
            totals[2].astype(jnp.bfloat16), "grp", scatter_dimension=0, tiled=True
        ).astype(jnp.float32),
        lax.psum_scatter(
            totals[3].astype(jnp.bfloat16), "grp", scatter_dimension=0, tiled=True
        ).astype(jnp.float32),
        lax.psum_scatter(
            totals[4].astype(jnp.bfloat16), "grp", scatter_dimension=0, tiled=True
        ).astype(jnp.float32),
        lax.psum_scatter(
            totals[5].astype(jnp.bfloat16), "grp", scatter_dimension=0, tiled=True
        ).astype(jnp.float32),
        lax.psum_scatter(
            totals[6].astype(jnp.bfloat16), "grp", scatter_dimension=0, tiled=True
        ).astype(jnp.float32),
        lax.psum_scatter(
            totals[7].astype(jnp.bfloat16), "grp", scatter_dimension=0, tiled=True
        ).astype(jnp.float32),
        lax.psum_scatter(
            totals[8].astype(jnp.bfloat16), "grp", scatter_dimension=0, tiled=True
        ).astype(jnp.float32),
        lax.psum_scatter(
            totals[9].astype(jnp.bfloat16), "grp", scatter_dimension=0, tiled=True
        ).astype(jnp.float32),
        lax.psum_scatter(
            totals[10].astype(jnp.bfloat16), "grp", scatter_dimension=0, tiled=True
        ).astype(jnp.float32),
        lax.psum_scatter(
            totals[11].astype(jnp.bfloat16), "grp", scatter_dimension=0, tiled=True
        ).astype(jnp.float32),
    )
    summed = (
        lax.psum(owned[0].astype(jnp.bfloat16), "rep").astype(jnp.float32),
        lax.psum(owned[1].astype(jnp.bfloat16), "rep").astype(jnp.float32),
        lax.psum(owned[2].astype(jnp.bfloat16), "rep").astype(jnp.float32),
        lax.psum(owned[3].astype(jnp.bfloat16), "rep").astype(jnp.float32),
        lax.psum(owned[4].astype(jnp.bfloat16), "rep").astype(jnp.float32),
        lax.psum(owned[5].astype(jnp.bfloat16), "rep").astype(jnp.float32),
        lax.psum(owned[6].astype(jnp.bfloat16), "rep").astype(jnp.float32),
        lax.psum(owned[7].astype(jnp.bfloat16), "rep").astype(jnp.float32),
        lax.psum(owned[8].astype(jnp.bfloat16), "rep").astype(jnp.float32),
        lax.psum(owned[9].astype(jnp.bfloat16), "rep").astype(jnp.float32),
        lax.psum(owned[10].astype(jnp.bfloat16), "rep").astype(jnp.float32),
        lax.psum(owned[11].astype(jnp.bfloat16), "rep").astype(jnp.float32),
    )
    output = jnp.stack(outputs, axis=0)
    grad_tokens = jnp.stack(gradients, axis=0)
    return (
        output,
        grad_tokens,
        summed[0],
        summed[1],
        summed[2],
        summed[3],
        summed[4],
        summed[5],
        summed[6],
        summed[7],
        summed[8],
        summed[9],
        summed[10],
        summed[11],
    )


def spread(mesh):
    placed = (
        P("rep", "grp", None),
        P(None, "rep", "grp"),
        P("grp"),
        P("grp"),
        P("grp", None),
        P("grp"),
        P("grp", None),
        P("grp"),
        P("grp"),
        P("grp"),
        P("grp", None),
        P("grp"),
        P("grp", None),
        P("grp"),
        P("rep", "grp", None),
    )
    return jax.shard_map(
        local,
        mesh=mesh,
        in_specs=placed,
        out_specs=(
            P("rep", "grp", None),
            P("rep", "grp", None),
            P("grp"),
            P("grp"),
            P("grp", None),
            P("grp"),
            P("grp", None),
            P("grp"),
            P("grp"),
            P("grp"),
            P("grp", None),
            P("grp"),
            P("grp", None),
            P("grp"),
        ),
        check_vma=False,
    )


def solution(mesh):
    reps, groups = mesh.devices.shape
    flat = mesh.devices.reshape(-1)

    def run(*args):
        clips = args[0].shape[0] // reps
        if reps == 8 and groups == 2 * clips:
            split = Mesh(flat.reshape(reps // 2, 2, groups), ("rp", "core", "grp"))
            ins, outs = paired_specs()
            return jax.shard_map(
                paired, mesh=split, in_specs=ins, out_specs=outs, check_vma=False
            )(*args)
        return spread(mesh)(*args)

    return run
```
